32 devices in a mesh: dp: 8 (over z, x), fsdp: 4 (over y, core).
Axes of the slice: x: 2, y: 2, z: 4, core: 2. Of those that a mesh axis runs over, the one named last changes fastest.
Arguments:
- tokens: bfloat16 [32768, 1024], P(('dp', 'fsdp')), may hold values from -6 to 6
- lengths: int32 [32], P(('dp', 'fsdp')), may hold values from 64 to 1024, as said below
- cotangent: bfloat16 [32768, 1024], P(('dp', 'fsdp')), may hold values from -6 to 6
- w_qkv: float32 [1024, 3072], P(('dp', 'fsdp')), may hold values from -0.1875 to 0.1875
- w_out: float32 [1024, 1024], P(('dp', 'fsdp')), may hold values from -0.1875 to 0.1875
- w_fc1: float32 [1024, 4096], P(('dp', 'fsdp')), may hold values from -0.1875 to 0.1875
- w_fc2: float32 [4096, 1024], P(('dp', 'fsdp')), may hold values from -0.09375 to 0.09375
- norm_gain: float32 [3, 1024], P(None, ('dp', 'fsdp')), may hold values from 0.25 to 1.75
- norm_bias: float32 [7, 1024], P(None, ('dp', 'fsdp')), may hold values from -3 to 3
- mid_gain: float32 [4096], P(('dp', 'fsdp')), may hold values from 0.25 to 1.75
- ff_bias: float32 [2, 4096], P(None, ('dp', 'fsdp')), may hold values from -3 to 3
- head_scale: float32 [16], replicated, may hold values from 0.5 to 2
Outputs:
- out: bfloat16 [32768, 1024], P(('dp', 'fsdp'))
- grad_tokens: bfloat16 [32768, 1024], P(('dp', 'fsdp'))
- grad_qkv: float32 [1024, 3072], P(('dp', 'fsdp'))
- grad_out: float32 [1024, 1024], P(('dp', 'fsdp'))
- grad_fc1: float32 [1024, 4096], P(('dp', 'fsdp'))
- grad_fc2: float32 [4096, 1024], P(('dp', 'fsdp'))
- grad_norm_gain: float32 [3, 1024], P(None, ('dp', 'fsdp'))
- grad_norm_bias: float32 [7, 1024], P(None, ('dp', 'fsdp'))
- grad_mid_gain: float32 [4096], P(('dp', 'fsdp'))
- grad_ff_bias: float32 [2, 4096], P(None, ('dp', 'fsdp'))
- grad_head_scale: float32 [16], replicated
The draws below stay inside these ranges and needn't reach their ends.
Inputs may be any that keep to these rules, and one draw needn't show every extreme that they name: `lengths`: every sequence's valid length; at least one sequence has exactly 1024 valid tokens and one exactly 64.
All inputs are finite; a program needn't handle non-finite values.
Results may differ from the reference program's by a relative error of at most 0.012.
Values may be sent and summed in bfloat16 or wider, within the bound.
A program may use at most 320 MiB of HBM per device.

```python
import math
import jax
import jax.numpy as jnp
from jax import lax

D = 1024
H = 16
HD = 64
FF = 4096
PAD = 1024
MIN_LEN = 64
SEQS = 32
TOKENS = 32768


def draw_lengths(key, part):
    subkeys = jax.random.split(key, 4)
    factor_one = jax.random.randint(subkeys[0], (SEQS,), 0, 1025)
    factor_two = jax.random.randint(subkeys[1], (SEQS,), 768, 1281)
    spread = PAD - MIN_LEN
    drawn_len = MIN_LEN + jnp.minimum(spread, spread * factor_one // 1024 * factor_two // 1024)
    longest = jax.random.randint(subkeys[2], (), 0, SEQS)
    shortest = (longest + 1 + jax.random.randint(subkeys[3], (), 0, SEQS - 1)) % SEQS
    position = jnp.arange(SEQS)
    drawn_len = jnp.where(position == longest, PAD, drawn_len)
    drawn_len = jnp.where(position == shortest, MIN_LEN, drawn_len)
    return drawn_len.astype(jnp.int32)


def spiked(values, stream_key, source, target, blocks, factor):
    owner, partner = [(jnp.arange(values.shape[dim]) // (values.shape[dim] // blocks)).reshape([-1 if axis == dim else 1 for axis in range(values.ndim)]) for dim in (source, target)]
    chosen = jax.random.permutation(stream_key, blocks)[partner]
    strong = (owner == chosen) | (owner == (partner + blocks // 2) % blocks)
    return jnp.where(strong, factor * values, values)


def block_scale(own_key, extent, cuts, low, largest):
    def one(dim, parts):
        draws = jax.random.uniform(jax.random.fold_in(jax.random.fold_in(own_key, 6), dim), (parts,), jnp.float32, low / len(cuts), largest / len(cuts))
        return jnp.repeat(jnp.exp(draws), extent[dim] // parts).reshape((-1,) + (1,) * (len(extent) - dim - 1))

    gain = one(*cuts[0])
    for cut in cuts[1:]:
        gain = gain * one(*cut)
    return gain


def bell_draw(rng, extent, scale, most, shards=(), kind=jnp.bfloat16):
    values = jax.random.normal(rng, extent, jnp.float32) * scale
    if len(shards) > 0:
        values = block_scale(rng, extent, shards, -0.22, 0.18) * values
    return jnp.clip(values, min=-most, max=most).astype(kind)


def noise_with(rng, shape, scale, bound, cuts, heavy, held_as=jnp.bfloat16):
    result = scale * jax.random.normal(rng, shape, jnp.float32)
    if cuts:
        result = result * block_scale(rng, shape, cuts, -0.22, 0.18)
    return jnp.clip(spiked(result, jax.random.fold_in(rng, 3), *heavy), -bound, bound).astype(held_as)


def setup_inputs(seed: int = 0) -> dict:
    seeds = jax.random.split(jax.random.key(seed), 13)
    return {
        "tokens": bell_draw(seeds[0], (TOKENS, D), 1.0, 6.0, ((0, 32),)),
        "lengths": draw_lengths(jax.random.fold_in(seeds[12], 71), 0),
        "cotangent": noise_with(seeds[2], (TOKENS, D), 1.0, 6.0, ((0, 32),), (0, 1, 32, 2.75)),
        "w_qkv": bell_draw(seeds[3], (D, 3 * D), D ** -0.5, 0.1875, ((0, 32),), jnp.float32),
        "w_out": bell_draw(seeds[4], (D, D), D ** -0.5, 0.1875, ((0, 32),), jnp.float32),
        "w_fc1": bell_draw(seeds[5], (D, FF), D ** -0.5, 0.1875, ((0, 32),), jnp.float32),
        "w_fc2": bell_draw(seeds[6], (FF, D), FF ** -0.5, 0.09375, ((0, 32),), jnp.float32),
        "norm_gain": jnp.clip(1.0 + 0.15 * jax.random.normal(seeds[7], (3, D), jnp.float32), 0.25, 1.75),
        "norm_bias": bell_draw(seeds[8], (7, D), 0.5, 3.0, ((1, 32),), jnp.float32),
        "mid_gain": jnp.clip(1.0 + 0.15 * jax.random.normal(seeds[9], (FF,), jnp.float32), 0.25, 1.75),
        "ff_bias": bell_draw(seeds[10], (2, FF), 0.5, 3.0, ((1, 32),), jnp.float32),
        "head_scale": jnp.clip(jnp.exp(jax.random.uniform(seeds[11], (H,), jnp.float32, math.log(0.5), math.log(2.0))), 0.5, 2.0),
    }


@jax.custom_vjp
def low(v):
    return lax.optimization_barrier(v.astype(jnp.bfloat16)).astype(jnp.float32)

@jax.custom_vjp
def low_back(v):
    return v

def low_keep(v):
    return (low(v), None)

def low_pass(kept, grad):
    return (grad,)

def back_keep(v):
    return (v, None)

def back_low(kept, grad):
    return (low(grad),)
low.defvjp(low_keep, low_pass)
low_back.defvjp(back_keep, back_low)
epsilon = 1e-05
mask_fill = -1e+30

def layer_norm(values):
    average = lax.optimization_barrier(jnp.mean(values, axis=-1, keepdims=True))
    centered = values - average
    variance = lax.optimization_barrier(jnp.mean(centered * centered, axis=-1, keepdims=True))
    return centered * lax.rsqrt(variance + epsilon)

def matmul_high(left, right):
    return jnp.dot(left, right, precision=lax.Precision.HIGHEST)

def sequence_layer(x_seq, seq_len, params):
    w_qkv, w_out, w_fc1, w_fc2, norm_gain, norm_bias, mid_gain, ff_bias, head_scale = params
    positions = jnp.arange(PAD, dtype=jnp.int32)
    allowed = (positions[None, :] <= positions[:, None]) & (positions[None, :] < seq_len)
    normed_in = low(layer_norm(x_seq) * norm_gain[0] + norm_bias[0])
    projected = matmul_high(normed_in, w_qkv)
    queries = low(low_back(projected[:, :D] + norm_bias[1])).reshape(PAD, H, HD)
    key_rows = low(low_back(projected[:, D:2 * D])).reshape(PAD, H, HD)
    value_rows = low(low_back(projected[:, 2 * D:] + norm_bias[2])).reshape(PAD, H, HD)
    scores = jnp.einsum('qhd,khd->hqk', queries, key_rows, precision=lax.Precision.HIGHEST) * HD ** (-0.5)
    scores = jnp.where(allowed[None], low_back(scores), mask_fill)
    softmaxed = low(jax.nn.softmax(scores, axis=-1))
    attended = low_back(jnp.einsum('hqk,khd->qhd', softmaxed, value_rows, precision=lax.Precision.HIGHEST))
    mixed = low((attended * head_scale[None, :, None]).reshape(PAD, D))
    projection = low_back(matmul_high(mixed, w_out) + norm_bias[3])
    residual = x_seq + (layer_norm(projection) * norm_gain[1] + norm_bias[4])
    normed_ff = low(layer_norm(residual) * norm_gain[2] + norm_bias[5])
    pre_act = low_back(matmul_high(normed_ff, w_fc1) + ff_bias[0])
    activated = jax.nn.gelu(pre_act, approximate=False)
    normed_mid = low(layer_norm(activated) * mid_gain + ff_bias[1])
    branch = low_back(matmul_high(normed_mid, w_fc2) + norm_bias[6])
    return residual + branch

def reference(tokens, lengths, cotangent, w_qkv, w_out, w_fc1, w_fc2, norm_gain, norm_bias, mid_gain, ff_bias, head_scale):
    inputs = tokens.astype(jnp.float32).reshape(SEQS, PAD, D)
    masters = (w_qkv, w_out, w_fc1, w_fc2, norm_gain, norm_bias, mid_gain, ff_bias, head_scale)
    layer_step = jax.checkpoint(sequence_layer)

    def forward(inputs, masters):
        copies = tuple((low(master) for master in masters[:8])) + (masters[8],)

        def scan_step(scan_carry, pieces):
            return (scan_carry, layer_step(pieces[0], pieces[1], copies))
        _, results = lax.scan(scan_step, jnp.zeros((), jnp.float32), (inputs, lengths))
        return results
    results, pullback = jax.vjp(forward, inputs, masters)
    positions = jnp.arange(PAD, dtype=jnp.int32)
    valid = (positions[None, :] < lengths[:, None]).astype(jnp.float32)
    grad_seed = cotangent.astype(jnp.float32).reshape(SEQS, PAD, D) * valid[:, :, None]
    grad_inputs, grad_masters = pullback(grad_seed)
    return (results.reshape(TOKENS, D).astype(jnp.bfloat16), grad_inputs.reshape(TOKENS, D).astype(jnp.bfloat16), grad_masters[0], grad_masters[1], grad_masters[2], grad_masters[3], grad_masters[4], grad_masters[5], grad_masters[6], grad_masters[7], grad_masters[8])
```

```python
import functools

import jax
import jax.numpy as jnp
from jax import lax
from jax.experimental import pallas as pl
from jax.experimental.pallas import tpu as pltpu
from jax.sharding import PartitionSpec as P

epsilon = 1e-05
mask_fill = -1e30
MESH = pl.DeviceIdType.MESH
ORDERS = ((1, 2, 0), (2, 1, 0), (0, 1, 2), (0, 2, 1))


def digits_of(mesh):
    dp, fsdp = mesh.shape["dp"], mesh.shape["fsdp"]
    minor = 2 if dp <= 8 else 8
    return (dp // minor, minor, fsdp // 2, 2)


class Place:
    def __init__(self, digits):
        self.digits = digits
        dp, fs = lax.axis_index("dp"), lax.axis_index("fsdp")
        self.at = (dp // digits[1], dp % digits[1], fs // digits[3], fs % digits[3])

    def digit(self, axis, shift):
        n = self.digits[axis]
        return (self.at[axis] + shift + n) % n

    def peer(self, axis, shift):
        at = list(self.at)
        at[axis] = self.digit(axis, shift)
        return (at[0] * self.digits[1] + at[1], at[2] * self.digits[3] + at[3])

    def greet(self):
        barrier = pltpu.get_barrier_semaphore()
        peers = []
        for axis, n in enumerate(self.digits):
            if n > 1:
                peers.append(self.peer(axis, 1))
            if n > 2:
                peers.append(self.peer(axis, -1))
        for peer in peers:
            pl.semaphore_signal(barrier, inc=1, device_id=peer, device_id_type=MESH)
        pl.semaphore_wait(barrier, len(peers))


class Sems:
    def __init__(self, send, recv, local):
        self.send, self.recv, self.local = send, recv, local
        self.remotes = self.locals = 0

    def remote(self, src, dst, peer):
        copy = pltpu.make_async_remote_copy(
            src_ref=src,
            dst_ref=dst,
            send_sem=self.send.at[self.remotes],
            recv_sem=self.recv.at[self.remotes],
            device_id=peer,
            device_id_type=MESH,
        )
        self.remotes += 1
        copy.start()
        return copy

    def copy(self, src, dst):
        copy = pltpu.make_async_copy(src, dst, self.local.at[self.locals])
        self.locals += 1
        copy.start()
        return copy


def hops(n):
    if n == 1:
        return []
    if n == 2:
        return [(0, (1,), False)]
    return [(s, (1, -1), s == n // 2 - 1) for s in range(n // 2)]


def column_part(start, size, direction, halved):
    if not halved:
        return start, size
    first = size // 256 * 128
    if first == 0:
        return (start, size) if direction > 0 else (start, 0)
    return (start, first) if direction > 0 else (start + first, size - first)


def slots(place, view, axis, slot, part):
    index = []
    for other, n in enumerate(place.digits):
        if other == axis:
            index.append(slot)
        elif other in view:
            index.append(pl.ds(0, n))
        else:
            index.append(place.at[other])
    return tuple(index) + (slice(None), pl.ds(*part))


def gather_piece(place, sems, shard, full, start, size, order):
    held, sends, cores = set(), [], []
    own = sems.copy(
        shard.at[:, pl.ds(start, size)], full.at[slots(place, (), None, None, (start, size))]
    )
    core = place.peer(3, 1)

    def forward(axis, slot, part):
        view = full.at[slots(place, held, axis, slot, part)]
        cores.append(sems.remote(view, view, core))

    first = True
    for axis in order:
        n = place.digits[axis]
        for step, directions, last in hops(n):
            started = []
            for direction in directions:
                part = column_part(start, size, direction, last)
                if part[1] == 0:
                    continue
                index = slots(place, held, axis, place.digit(axis, -step * direction), part)
                src = shard.at[:, pl.ds(*part)] if first and step == 0 else full.at[index]
                started.append(
                    (direction, sems.remote(src, full.at[index], place.peer(axis, direction)))
                )
            yield
            for direction, copy in started:
                copy.wait_recv()
                sends.append(copy)
                if not first and not last and n > 2:
                    forward(axis, place.digit(axis, -(step + 1) * direction), (start, size))
            if not first and (last or n == 2):
                forward(axis, place.digit(axis, n // 2), (start, size))
        if n > 1:
            held.add(axis)
            if first:
                own.wait()
                forward(None, None, (start, size))
                first = False
    if first:
        own.wait()
        forward(None, None, (start, size))
    yield
    for copy in cores:
        copy.wait()
    for copy in sends:
        copy.wait_send()


def accumulate(target, source, result=None):
    lead, dims = target.shape[:-2], target.shape
    count = 1
    for n in lead:
        count *= n

    def index_of(flat):
        index = []
        for n in reversed(lead):
            index.append(flat % n)
            flat = flat // n
        return tuple(reversed(index)) + (slice(None), slice(None))

    def body(flat, carry):
        index = index_of(flat)
        total = target[index].astype(jnp.float32) + source[index].astype(jnp.float32)
        target[index] = total.astype(target.dtype)
        return carry

    if lead:
        lax.fori_loop(0, count, body, 0)
    else:
        body(0, 0)


def reduce_steps(digits, start, size, order):
    left, plan = [0, 1, 2], []
    for axis in order:
        n = digits[axis]
        left.remove(axis)
        lead = tuple(digits[a] for a in left)
        for step, directions, last in reversed(hops(n)):
            batch = []
            for direction in directions:
                part = column_part(start, size, direction, last)
                if part[1] > 0:
                    batch.append((axis, direction, step, part, lead))
            plan.append((tuple(left), batch))
    return plan


def reduce_piece(place, sems, grad, acc, landed, slabs, out, start, size, order):
    sends = []
    lead = (slice(None),) * 3
    whole = (slice(None), pl.ds(start, size))
    mine = acc.at[lead + whole]
    other = landed.at[lead + whole]
    own = sems.copy(grad.at[lead + (place.at[3],) + whole], mine)
    sent = sems.remote(grad.at[lead + (place.digit(3, 1),) + whole], other, place.peer(3, 1))
    yield
    own.wait()
    sent.wait_recv()
    sends.append(sent)
    accumulate(mine, other)
    slabs = iter(slabs)
    for left, batch in reduce_steps(place.digits, start, size, order):
        started = []
        for axis, direction, step, part, _ in batch:
            slot = place.digit(axis, (step + 1) * direction)
            src = acc.at[slots(place, left, axis, slot, part)[:3] + (slice(None), pl.ds(*part))]
            dst = next(slabs)
            sent = sems.remote(src, dst, place.peer(axis, direction))
            started.append((axis, direction * step, part, dst, sent))
        yield
        for axis, shift, part, dst, sent in started:
            sent.wait_recv()
            sends.append(sent)
            slot = place.digit(axis, shift)
            view = slots(place, left, axis, slot, part)[:3] + (slice(None), pl.ds(*part))
            accumulate(acc.at[view], dst)
    out[:, pl.ds(start, size)] = acc[place.at[:3] + whole].astype(jnp.float32)
    for sent in sends:
        sent.wait_send()
    yield


def pieces_of(cols, wanted=4):
    tiles = cols // 128
    count = wanted
    while tiles % count:
        count -= 1
    size = tiles // count * 128
    return [(k * size, size) for k in range(count)]


def run_all(generators):
    live = list(generators)
    while live:
        still = []
        for generator in live:
            try:
                next(generator)
                still.append(generator)
            except StopIteration:
                pass
        live = still


def gather_kernel(digits, count, *refs):
    shards, fulls = refs[:count], refs[count : 2 * count]
    send, recv, local = refs[2 * count :]
    place = Place(digits)
    sems = Sems(send, recv, local)
    place.greet()
    run_all(
        gather_piece(place, sems, shard, full, start, size, ORDERS[k % 4])
        for shard, full in zip(shards, fulls)
        for k, (start, size) in enumerate(pieces_of(shard.shape[1]))
    )


def gather_all(digits, shards):
    count = len(shards)
    copies = 16 * 4 * count * max(1, max(digits) // 4)
    whole = [jax.ShapeDtypeStruct(digits + s.shape, s.dtype) for s in shards]
    return pl.pallas_call(
        functools.partial(gather_kernel, digits, count),
        out_shape=whole,
        in_specs=[pl.BlockSpec(memory_space=pl.ANY)] * count,
        out_specs=[pl.BlockSpec(memory_space=pl.ANY)] * count,
        scratch_shapes=[
            pltpu.SemaphoreType.DMA((copies,)),
            pltpu.SemaphoreType.DMA((copies,)),
            pltpu.SemaphoreType.DMA((4 * count,)),
        ],
        compiler_params=pltpu.CompilerParams(collective_id=0, has_side_effects=True),
        name="gather_all",
    )(*shards)


def reduce_plan(digits, grads):
    plan = []
    for g, grad in enumerate(grads):
        for k, (start, size) in enumerate(pieces_of(grad.shape[-1])):
            plan.append((g, start, size, ORDERS[k % 4]))
    return plan


def reduce_kernel(digits, plan, slab_counts, count, *refs):
    grads, outs = refs[:count], refs[count : 2 * count]
    accs, landed = refs[2 * count : 3 * count], refs[3 * count : 4 * count]
    slabs = refs[4 * count : -3]
    send, recv, local = refs[-3:]
    place = Place(digits)
    sems = Sems(send, recv, local)
    place.greet()
    generators, used = [], 0
    for (g, start, size, order), many in zip(plan, slab_counts):
        own = slabs[used : used + many]
        used += many
        generators.append(
            reduce_piece(place, sems, grads[g], accs[g], landed[g], own, outs[g], start, size, order)
        )
    run_all(generators)


def reduce_all(digits, grads):
    count = len(grads)
    plan = reduce_plan(digits, grads)
    slabs, slab_counts = [], []
    for g, start, size, order in plan:
        shapes = [
            pltpu.VMEM(lead + (grads[g].shape[-2], part[1]), grads[g].dtype)
            for _, batch in reduce_steps(digits, start, size, order)
            for _, _, _, part, lead in batch
        ]
        slabs += shapes
        slab_counts.append(len(shapes))
    blocks = [pltpu.VMEM(digits[:3] + g.shape[-2:], g.dtype) for g in grads]
    copies = len(slabs) + len(plan)
    return pl.pallas_call(
        functools.partial(reduce_kernel, digits, plan, slab_counts, count),
        out_shape=[jax.ShapeDtypeStruct(g.shape[-2:], jnp.float32) for g in grads],
        in_specs=[pl.BlockSpec(memory_space=pl.ANY)] * count,
        out_specs=[pl.BlockSpec(memory_space=pltpu.VMEM)] * count,
        scratch_shapes=blocks
        + blocks
        + slabs
        + [
            pltpu.SemaphoreType.DMA((copies,)),
            pltpu.SemaphoreType.DMA((copies,)),
            pltpu.SemaphoreType.DMA((len(plan),)),
        ],
        compiler_params=pltpu.CompilerParams(
            collective_id=1, has_side_effects=True, vmem_limit_bytes=58 << 20
        ),
        name="reduce_all",
    )(*grads)


def tiled_rows(rows, cols):
    return (rows, cols) if rows % 16 == 0 else (16, rows * cols // 16)


def layer_norm(values):
    average = jnp.mean(values, axis=-1, keepdims=True)
    centered = values - average
    variance = jnp.mean(centered * centered, axis=-1, keepdims=True)
    return centered * lax.rsqrt(variance + epsilon)


def norm_affine(values, gain, offset):
    return layer_norm(values) * gain + offset


def gelu_exact(values):
    return jax.nn.gelu(values, approximate=False)


def to_bf16(values):
    return values.astype(jnp.bfloat16)


def plain_product(left, right):
    return jnp.dot(left, right, preferred_element_type=jnp.float32)


def row_contract(left, right):
    return lax.dot_general(
        left, right, (((0,), (0,)), ((), ())), preferred_element_type=jnp.float32
    )


def col_contract(left, right):
    return lax.dot_general(
        left, right, (((1,), (1,)), ((), ())), preferred_element_type=jnp.float32
    )


def score_block(query_block, key_rows, offset, seq_len):
    query_pos = offset + jnp.arange(query_block.shape[0], dtype=jnp.int32)
    key_pos = jnp.arange(key_rows.shape[0], dtype=jnp.int32)
    allowed = (key_pos[None, :] <= query_pos[:, None]) & (key_pos[None, :] < seq_len)
    scores = jnp.einsum("qhd,khd->hqk", query_block, key_rows, preferred_element_type=jnp.float32)
    scores = scores * query_block.shape[2] ** (-0.5)
    return jnp.where(allowed[None], scores, mask_fill)


def attend_block(query_block, key_rows, value_rows, offset, seq_len):
    scores = score_block(query_block, key_rows, offset, seq_len)
    row_max = jnp.max(scores, axis=-1, keepdims=True)
    shifted = jnp.exp(scores - row_max)
    row_sum = jnp.sum(shifted, axis=-1, keepdims=True)
    weights = to_bf16(shifted / row_sum)
    attended = jnp.einsum("hqk,khd->qhd", weights, value_rows, preferred_element_type=jnp.float32)
    return (attended, (row_max + jnp.log(row_sum))[..., 0])


def attend_sequence(query_rows, key_rows, value_rows, seq_len):
    padded = query_rows.shape[0]
    block_rows = min(512, padded)
    blocks = padded // block_rows
    query_blocks = query_rows.reshape((blocks, block_rows) + query_rows.shape[1:])
    offsets = jnp.arange(blocks, dtype=jnp.int32) * block_rows

    def one_block(pieces):
        return attend_block(pieces[0], key_rows, value_rows, pieces[1], seq_len)

    attended, log_totals = lax.map(one_block, (query_blocks, offsets))
    return (attended.reshape(query_rows.shape), log_totals)


def attend_block_back(query_block, key_rows, value_rows, grad_block, log_total, offset, seq_len):
    scores = score_block(query_block, key_rows, offset, seq_len)
    softmaxed = jnp.exp(scores - log_total[..., None])
    grad_weights = jnp.einsum(
        "qhd,khd->hqk", grad_block, value_rows, preferred_element_type=jnp.float32
    )
    grad_values = jnp.einsum(
        "hqk,qhd->khd", to_bf16(softmaxed), grad_block, preferred_element_type=jnp.float32
    )
    centered = grad_weights - jnp.sum(softmaxed * grad_weights, axis=-1, keepdims=True)
    grad_scores = to_bf16(softmaxed * centered)
    scaling = query_block.shape[2] ** (-0.5)
    grad_queries = (
        jnp.einsum("hqk,khd->qhd", grad_scores, key_rows, preferred_element_type=jnp.float32)
        * scaling
    )
    grad_keys = (
        jnp.einsum("hqk,qhd->khd", grad_scores, query_block, preferred_element_type=jnp.float32)
        * scaling
    )
    return (grad_queries, grad_keys, grad_values)


def attend_sequence_back(query_rows, key_rows, value_rows, grad_rows, log_totals, seq_len):
    padded = query_rows.shape[0]
    block_rows = min(512, padded)
    blocks = padded // block_rows
    query_blocks = query_rows.reshape((blocks, block_rows) + query_rows.shape[1:])
    grad_blocks = grad_rows.reshape((blocks, block_rows) + grad_rows.shape[1:])
    offsets = jnp.arange(blocks, dtype=jnp.int32) * block_rows

    def step_block(totals, pieces):
        grad_queries, grad_keys, grad_values = attend_block_back(
            pieces[0], key_rows, value_rows, pieces[1], pieces[2], pieces[3], seq_len
        )
        return ((totals[0] + grad_keys, totals[1] + grad_values), grad_queries)

    zeros_kv = jnp.zeros(key_rows.shape, jnp.float32)
    (grad_keys, grad_values), grad_queries = lax.scan(
        step_block, (zeros_kv, zeros_kv), (query_blocks, grad_blocks, log_totals, offsets)
    )
    return (grad_queries.reshape(query_rows.shape), grad_keys, grad_values)


def shards(
    digits,
    tokens,
    lengths,
    cotangent,
    w_qkv,
    w_out,
    w_fc1,
    w_fc2,
    norm_gain,
    norm_bias,
    mid_gain,
    ff_bias,
    head_scale,
):
    weights = (w_qkv, w_out, w_fc1, w_fc2)
    small = jnp.concatenate([v.reshape(-1) for v in (norm_gain, norm_bias, mid_gain, ff_bias)])
    small = jnp.pad(to_bf16(small), (0, 2048 - small.shape[0])).reshape(16, 128)
    shards_in = [to_bf16(w).reshape(tiled_rows(*w.shape)) for w in weights] + [small]
    gathered = gather_all(digits, shards_in)
    full_qkv, full_out, full_fc1, full_fc2 = (
        g.reshape((-1, w.shape[1])) for g, w in zip(gathered, weights)
    )
    smalls = gathered[4].reshape(-1, 2048)
    parts, used = [], 0
    for v in (norm_gain, norm_bias, mid_gain, ff_bias):
        block = smalls[:, used : used + v.size].reshape((-1,) + (v.shape if v.ndim == 2 else (1,) + v.shape))
        parts.append(block.transpose(1, 0, 2).reshape(block.shape[1], -1))
        used += v.size
    gain_copy, bias_copy, mid_copy, ff_copy = parts[0], parts[1], parts[2][0], parts[3]
    gains = gain_copy.astype(jnp.float32)
    biases = bias_copy.astype(jnp.float32)
    mid_gains = mid_copy.astype(jnp.float32)
    ff_biases = ff_copy.astype(jnp.float32)
    seq_total = lengths.shape[0]
    row_total = tokens.shape[0]
    padded = row_total // seq_total
    width = tokens.shape[1]
    heads = head_scale.shape[0]
    head_dim = width // heads
    seq_shape = (seq_total, padded, heads, head_dim)
    x_in = tokens.astype(jnp.float32)
    normed_in = to_bf16(norm_affine(x_in, gains[0], biases[0]))
    projected = plain_product(normed_in, full_qkv)
    queries = to_bf16(projected[:, :width] + biases[1])
    key_rows = to_bf16(projected[:, width : 2 * width])
    value_rows = to_bf16(projected[:, 2 * width :] + biases[2])

    def forward_sequence(pieces):
        return attend_sequence(pieces[0], pieces[1], pieces[2], pieces[3])

    attended, log_totals = lax.map(
        forward_sequence,
        (
            queries.reshape(seq_shape),
            key_rows.reshape(seq_shape),
            value_rows.reshape(seq_shape),
            lengths,
        ),
    )
    attended = attended.reshape(row_total, heads, head_dim)
    mixed = to_bf16((attended * head_scale[None, :, None]).reshape(row_total, width))
    projection = plain_product(mixed, full_out) + biases[3]
    residual = x_in + norm_affine(projection, gains[1], biases[4])
    normed_ff = to_bf16(norm_affine(residual, gains[2], biases[5]))
    pre_act = plain_product(normed_ff, full_fc1) + ff_biases[0]
    activated = gelu_exact(pre_act)
    normed_mid = to_bf16(norm_affine(activated, mid_gains, ff_biases[1]))
    result = residual + (plain_product(normed_mid, full_fc2) + biases[6])
    positions = jnp.arange(padded, dtype=jnp.int32)
    valid = (positions[None, :] < lengths[:, None]).astype(jnp.float32).reshape(row_total, 1)
    grad_result = cotangent.astype(jnp.float32) * valid
    grad_branch = to_bf16(grad_result)
    grad_fc2 = row_contract(normed_mid, grad_branch)
    grad_bias_fc2 = jnp.sum(grad_branch.astype(jnp.float32), axis=0)
    grad_mid = col_contract(grad_branch, full_fc2)
    _, mid_pull = jax.vjp(norm_affine, activated, mid_gains, ff_biases[1])
    grad_activated, grad_mid_gain, grad_mid_bias = mid_pull(grad_mid)
    _, gelu_pull = jax.vjp(gelu_exact, pre_act)
    grad_pre = to_bf16(gelu_pull(grad_activated)[0])
    grad_fc1 = row_contract(normed_ff, grad_pre)
    grad_bias_fc1 = jnp.sum(grad_pre.astype(jnp.float32), axis=0)
    grad_ff_biases = jnp.stack((grad_bias_fc1, grad_mid_bias))
    grad_normed_ff = col_contract(grad_pre, full_fc1)
    _, ff_pull = jax.vjp(norm_affine, residual, gains[2], biases[5])
    grad_res_part, grad_gain_ff, grad_bias_ff = ff_pull(grad_normed_ff)
    grad_residual = grad_result + grad_res_part
    _, post_pull = jax.vjp(norm_affine, projection, gains[1], biases[4])
    grad_projection, grad_gain_post, grad_bias_post = post_pull(grad_residual)
    grad_projection = to_bf16(grad_projection)
    grad_out_w = row_contract(mixed, grad_projection)
    grad_bias_out = jnp.sum(grad_projection.astype(jnp.float32), axis=0)
    grad_mixed = col_contract(grad_projection, full_out).reshape(row_total, heads, head_dim)
    grad_scale_local = jnp.sum(grad_mixed * attended, axis=(0, 2))
    grad_attended = to_bf16(grad_mixed * head_scale[None, :, None])

    def backward_sequence(pieces):
        return attend_sequence_back(
            pieces[0], pieces[1], pieces[2], pieces[3], pieces[4], pieces[5]
        )

    grad_queries, grad_keys, grad_values = lax.map(
        backward_sequence,
        (
            queries.reshape(seq_shape),
            key_rows.reshape(seq_shape),
            value_rows.reshape(seq_shape),
            grad_attended.reshape(seq_shape),
            log_totals,
            lengths,
        ),
    )
    grad_projected = to_bf16(
        jnp.concatenate(
            (
                grad_queries.reshape(row_total, width),
                grad_keys.reshape(row_total, width),
                grad_values.reshape(row_total, width),
            ),
            axis=1,
        )
    )
    grad_qkv = row_contract(normed_in, grad_projected)
    grad_bias_q = jnp.sum(grad_projected[:, :width].astype(jnp.float32), axis=0)
    grad_bias_v = jnp.sum(grad_projected[:, 2 * width :].astype(jnp.float32), axis=0)
    grad_normed_in = col_contract(grad_projected, full_qkv)
    _, in_pull = jax.vjp(norm_affine, x_in, gains[0], biases[0])
    grad_x_part, grad_gain_in, grad_bias_in = in_pull(grad_normed_in)
    grad_tokens = (grad_residual + grad_x_part).astype(jnp.bfloat16)
    grad_gains = jnp.stack((grad_gain_in, grad_gain_post, grad_gain_ff))
    grad_biases = jnp.stack(
        (
            grad_bias_in,
            grad_bias_q,
            grad_bias_v,
            grad_bias_out,
            grad_bias_post,
            grad_bias_ff,
            grad_bias_fc2,
        )
    )
    total = digits[0] * digits[1] * digits[2] * digits[3]
    block = []
    for v in (grad_gains, grad_biases, grad_mid_gain[None], grad_ff_biases):
        block.append(v.reshape(v.shape[0], total, -1).transpose(1, 0, 2).reshape(total, -1))
    block.append(jnp.broadcast_to(grad_scale_local[None], (total, heads)))
    block = jnp.concatenate(block, axis=1)
    block = jnp.pad(block, ((0, 0), (0, 1024 - block.shape[1]))).reshape(digits + (8, 128))
    grads = [
        to_bf16(g).reshape(digits + tiled_rows(*w.shape))
        for g, w in zip((grad_qkv, grad_out_w, grad_fc1, grad_fc2), weights)
    ]
    summed = reduce_all(digits, grads + [block])
    flat, used, owned = summed[4].reshape(-1), 0, []
    for v in (norm_gain, norm_bias, mid_gain, ff_bias, head_scale):
        owned.append(flat[used : used + v.size].reshape(v.shape))
        used += v.size
    summed = [g.reshape(w.shape) for g, w in zip(summed[:4], weights)] + owned
    grad_scale = summed[8]
    return (
        result.astype(jnp.bfloat16),
        grad_tokens,
        summed[0],
        summed[1],
        summed[2],
        summed[3],
        summed[4],
        summed[5],
        summed[6],
        summed[7],
        grad_scale,
    )


def solution(mesh):
    placed = (
        P(("dp", "fsdp"), None),
        P(("dp", "fsdp")),
        P(("dp", "fsdp"), None),
        P(("dp", "fsdp"), None),
        P(("dp", "fsdp"), None),
        P(("dp", "fsdp"), None),
        P(("dp", "fsdp"), None),
        P(None, ("dp", "fsdp")),
        P(None, ("dp", "fsdp")),
        P(("dp", "fsdp")),
        P(None, ("dp", "fsdp")),
        P(),
    )
    return jax.shard_map(
        functools.partial(shards, digits_of(mesh)),
        mesh=mesh,
        in_specs=placed,
        out_specs=(
            P(("dp", "fsdp"), None),
            P(("dp", "fsdp"), None),
            P(("dp", "fsdp"), None),
            P(("dp", "fsdp"), None),
            P(("dp", "fsdp"), None),
            P(("dp", "fsdp"), None),
            P(None, ("dp", "fsdp")),
            P(None, ("dp", "fsdp")),
            P(("dp", "fsdp")),
            P(None, ("dp", "fsdp")),
            P(),
        ),
        check_vma=False,
    )
```

```python
import functools

import jax
import jax.numpy as jnp
from jax import lax
from jax.experimental import pallas as pl
from jax.experimental.pallas import tpu as pltpu
from jax.sharding import PartitionSpec as P

epsilon = 1e-05
mask_fill = -1e30
MESH = pl.DeviceIdType.MESH
ORDERS = ((1, 2, 0), (2, 1, 0), (0, 1, 2), (0, 2, 1))


def digits_of(mesh):
    dp, fsdp = mesh.shape["dp"], mesh.shape["fsdp"]
    minor = 2 if dp <= 8 else 8
    return (dp // minor, minor, fsdp // 2, 2)


class Place:
    def __init__(self, digits):
        self.digits = digits
        dp, fs = lax.axis_index("dp"), lax.axis_index("fsdp")
        self.at = (dp // digits[1], dp % digits[1], fs // digits[3], fs % digits[3])

    def digit(self, axis, shift):
        n = self.digits[axis]
        return (self.at[axis] + shift + n) % n

    def peer(self, axis, shift):
        at = list(self.at)
        at[axis] = self.digit(axis, shift)
        return (at[0] * self.digits[1] + at[1], at[2] * self.digits[3] + at[3])

    def greet(self):
        barrier = pltpu.get_barrier_semaphore()
        peers = []
        for axis, n in enumerate(self.digits):
            if n > 1:
                peers.append(self.peer(axis, 1))
            if n > 2:
                peers.append(self.peer(axis, -1))
        for peer in peers:
            pl.semaphore_signal(barrier, inc=1, device_id=peer, device_id_type=MESH)
        pl.semaphore_wait(barrier, len(peers))


class Sems:
    def __init__(self, send, recv, local):
        self.send, self.recv, self.local = send, recv, local
        self.remotes = self.locals = 0

    def remote(self, src, dst, peer):
        copy = pltpu.make_async_remote_copy(
            src_ref=src,
            dst_ref=dst,
            send_sem=self.send.at[self.remotes],
            recv_sem=self.recv.at[self.remotes],
            device_id=peer,
            device_id_type=MESH,
        )
        self.remotes += 1
        copy.start()
        return copy

    def copy(self, src, dst):
        copy = pltpu.make_async_copy(src, dst, self.local.at[self.locals])
        self.locals += 1
        copy.start()
        return copy


def hops(n):
    if n == 1:
        return []
    if n == 2:
        return [(0, (1,), False)]
    return [(s, (1, -1), s == n // 2 - 1) for s in range(n // 2)]


def column_part(start, size, direction, halved):
    if not halved:
        return start, size
    first = size // 256 * 128
    if first == 0:
        return (start, size) if direction > 0 else (start, 0)
    return (start, first) if direction > 0 else (start + first, size - first)


def slots(place, view, axis, slot, part):
    index = []
    for other, n in enumerate(place.digits):
        if other == axis:
            index.append(slot)
        elif other in view:
            index.append(pl.ds(0, n))
        else:
            index.append(place.at[other])
    return tuple(index) + (slice(None), pl.ds(*part))


def gather_piece(place, sems, shard, full, start, size, order):
    held, sends, cores = set(), [], []
    own = sems.copy(
        shard.at[:, pl.ds(start, size)], full.at[slots(place, (), None, None, (start, size))]
    )
    core = place.peer(3, 1)

    def forward(axis, slot, part):
        view = full.at[slots(place, held, axis, slot, part)]
        cores.append(sems.remote(view, view, core))

    first = True
    for axis in order:
        n = place.digits[axis]
        for step, directions, last in hops(n):
            started = []
            for direction in directions:
                part = column_part(start, size, direction, last)
                if part[1] == 0:
                    continue
                index = slots(place, held, axis, place.digit(axis, -step * direction), part)
                src = shard.at[:, pl.ds(*part)] if first and step == 0 else full.at[index]
                started.append(
                    (direction, sems.remote(src, full.at[index], place.peer(axis, direction)))
                )
            yield
            for direction, copy in started:
                copy.wait_recv()
                sends.append(copy)
                if not first and not last and n > 2:
                    forward(axis, place.digit(axis, -(step + 1) * direction), (start, size))
            if not first and (last or n == 2):
                forward(axis, place.digit(axis, n // 2), (start, size))
        if n > 1:
            held.add(axis)
            if first:
                own.wait()
                forward(None, None, (start, size))
                first = False
    if first:
        own.wait()
        forward(None, None, (start, size))
    yield
    for copy in cores:
        copy.wait()
    for copy in sends:
        copy.wait_send()


def accumulate(target, source, result=None):
    lead, dims = target.shape[:-2], target.shape
    count = 1
    for n in lead:
        count *= n

    def index_of(flat):
        index = []
        for n in reversed(lead):
            index.append(flat % n)
            flat = flat // n
        return tuple(reversed(index)) + (slice(None), slice(None))

    def body(flat, carry):
        index = index_of(flat)
        total = target[index].astype(jnp.float32) + source[index].astype(jnp.float32)
        target[index] = total.astype(target.dtype)
        return carry

    if lead:
        lax.fori_loop(0, count, body, 0)
    else:
        body(0, 0)


def reduce_steps(digits, start, size, order):
    left, plan = [0, 1, 2], []
    for axis in order:
        n = digits[axis]
        left.remove(axis)
        lead = tuple(digits[a] for a in left)
        for step, directions, last in reversed(hops(n)):
            batch = []
            for direction in directions:
                part = column_part(start, size, direction, last)
                if part[1] > 0:
                    batch.append((axis, direction, step, part, lead))
            plan.append((tuple(left), batch))
    return plan


def reduce_piece(place, sems, grad, acc, landed, slabs, out, start, size, order):
    sends = []
    lead = (slice(None),) * 3
    whole = (slice(None), pl.ds(start, size))
    mine = acc.at[lead + whole]
    other = landed.at[lead + whole]
    own = sems.copy(grad.at[lead + (place.at[3],) + whole], mine)
    sent = sems.remote(grad.at[lead + (place.digit(3, 1),) + whole], other, place.peer(3, 1))
    yield
    own.wait()
    sent.wait_recv()
    sends.append(sent)
    accumulate(mine, other)
    slabs = iter(slabs)
    for left, batch in reduce_steps(place.digits, start, size, order):
        started = []
        for axis, direction, step, part, _ in batch:
            slot = place.digit(axis, (step + 1) * direction)
            src = acc.at[slots(place, left, axis, slot, part)[:3] + (slice(None), pl.ds(*part))]
            dst = next(slabs)
            sent = sems.remote(src, dst, place.peer(axis, direction))
            started.append((axis, direction * step, part, dst, sent))
        yield
        for axis, shift, part, dst, sent in started:
            sent.wait_recv()
            sends.append(sent)
            slot = place.digit(axis, shift)
            view = slots(place, left, axis, slot, part)[:3] + (slice(None), pl.ds(*part))
            accumulate(acc.at[view], dst)
    out[:, pl.ds(start, size)] = acc[place.at[:3] + whole].astype(jnp.float32)
    for sent in sends:
        sent.wait_send()
    yield


def pieces_of(cols, wanted=4):
    tiles = cols // 128
    count = wanted
    while tiles % count:
        count -= 1
    size = tiles // count * 128
    return [(k * size, size) for k in range(count)]


def run_all(generators):
    live = list(generators)
    while live:
        still = []
        for generator in live:
            try:
                next(generator)
                still.append(generator)
            except StopIteration:
                pass
        live = still


def gather_kernel(digits, count, *refs):
    shards, fulls = refs[:count], refs[count : 2 * count]
    send, recv, local = refs[2 * count :]
    place = Place(digits)
    sems = Sems(send, recv, local)
    place.greet()
    run_all(
        gather_piece(place, sems, shard, full, start, size, ORDERS[k % 4])
        for shard, full in zip(shards, fulls)
        for k, (start, size) in enumerate(pieces_of(shard.shape[1]))
    )


def gather_all(digits, shards):
    count = len(shards)
    copies = 16 * 4 * count * max(1, max(digits) // 4)
    whole = [jax.ShapeDtypeStruct(digits + s.shape, s.dtype) for s in shards]
    return pl.pallas_call(
        functools.partial(gather_kernel, digits, count),
        out_shape=whole,
        in_specs=[pl.BlockSpec(memory_space=pl.ANY)] * count,
        out_specs=[pl.BlockSpec(memory_space=pl.ANY)] * count,
        scratch_shapes=[
            pltpu.SemaphoreType.DMA((copies,)),
            pltpu.SemaphoreType.DMA((copies,)),
            pltpu.SemaphoreType.DMA((4 * count,)),
        ],
        compiler_params=pltpu.CompilerParams(collective_id=0, has_side_effects=True),
        name="gather_all",
    )(*shards)


def reduce_plan(digits, grads):
    plan = []
    for g, grad in enumerate(grads):
        for k, (start, size) in enumerate(pieces_of(grad.shape[-1])):
            plan.append((g, start, size, ORDERS[k % 4]))
    return plan


def reduce_kernel(digits, plan, slab_counts, count, *refs):
    grads, outs = refs[:count], refs[count : 2 * count]
    accs, landed = refs[2 * count : 3 * count], refs[3 * count : 4 * count]
    slabs = refs[4 * count : -3]
    send, recv, local = refs[-3:]
    place = Place(digits)
    sems = Sems(send, recv, local)
    place.greet()
    generators, used = [], 0
    for (g, start, size, order), many in zip(plan, slab_counts):
        own = slabs[used : used + many]
        used += many
        generators.append(
            reduce_piece(place, sems, grads[g], accs[g], landed[g], own, outs[g], start, size, order)
        )
    run_all(generators)


def reduce_all(digits, grads):
    count = len(grads)
    plan = reduce_plan(digits, grads)
    slabs, slab_counts = [], []
    for g, start, size, order in plan:
        shapes = [
            pltpu.VMEM(lead + (grads[g].shape[-2], part[1]), grads[g].dtype)
            for _, batch in reduce_steps(digits, start, size, order)
            for _, _, _, part, lead in batch
        ]
        slabs += shapes
        slab_counts.append(len(shapes))
    blocks = [pltpu.VMEM(digits[:3] + g.shape[-2:], g.dtype) for g in grads]
    copies = len(slabs) + len(plan)
    return pl.pallas_call(
        functools.partial(reduce_kernel, digits, plan, slab_counts, count),
        out_shape=[jax.ShapeDtypeStruct(g.shape[-2:], jnp.float32) for g in grads],
        in_specs=[pl.BlockSpec(memory_space=pl.ANY)] * count,
        out_specs=[pl.BlockSpec(memory_space=pltpu.VMEM)] * count,
        scratch_shapes=blocks
        + blocks
        + slabs
        + [
            pltpu.SemaphoreType.DMA((copies,)),
            pltpu.SemaphoreType.DMA((copies,)),
            pltpu.SemaphoreType.DMA((len(plan),)),
        ],
        compiler_params=pltpu.CompilerParams(
            collective_id=1, has_side_effects=True, vmem_limit_bytes=58 << 20
        ),
        name="reduce_all",
    )(*grads)


def tiled_rows(rows, cols):
    return (rows, cols) if rows % 16 == 0 else (16, rows * cols // 16)


def to_bf16(values):
    return values.astype(jnp.bfloat16)


def dot_nn(a, b):
    return lax.dot_general(a, b, (((1,), (0,)), ((), ())), preferred_element_type=jnp.float32)


def dot_nt(a, b):
    return lax.dot_general(a, b, (((1,), (1,)), ((), ())), preferred_element_type=jnp.float32)


def dot_tn(a, b):
    return lax.dot_general(a, b, (((0,), (0,)), ((), ())), preferred_element_type=jnp.float32)


def row_mean(v):
    return jnp.mean(v, axis=-1, keepdims=True)


def norm_parts(v):
    centered = v - row_mean(v)
    inverse = lax.rsqrt(row_mean(centered * centered) + epsilon)
    return centered * inverse, inverse


def norm_back(grad, gain, normed, inverse):
    scaled = grad * gain
    return (scaled - row_mean(scaled) - normed * row_mean(scaled * normed)) * inverse


def fold(v):
    return v.reshape(v.shape[0] // 8, 8, v.shape[1]).sum(0)


def ffn_kernel(
    chunk, unrolled,
    len_ref, scale_ref, x_ref, z_ref, cot_ref, wo_ref, w1_ref, w2_ref, gain_ref, bias_ref, mid_ref, ffb_ref,
    out_ref, c_ref, m_ref, df_ref, dy_ref, dr_ref, do_ref, sums_ref, wide_ref,
    act_ref, slope_ref, dm_ref,
):
    step = pl.program_id(0)
    rows, width = x_ref.shape
    hidden = w1_ref.shape[1]
    f32, bf16 = jnp.float32, jnp.bfloat16

    @pl.when(step == 0)
    def _():
        sums_ref[...] = jnp.zeros_like(sums_ref)
        wide_ref[...] = jnp.zeros_like(wide_ref)

    def each(body, carry):
        if unrolled:
            for j in range(hidden // chunk):
                carry = body(slice(j * chunk, (j + 1) * chunk), carry)
            return carry
        return lax.fori_loop(
            0, hidden // chunk, lambda j, c: body(pl.ds(pl.multiple_of(j * chunk, chunk), chunk), c), carry
        )

    gain = lambda k: gain_ref[k : k + 1, :]
    bias = lambda k: bias_ref[k : k + 1, :]
    y_norm, y_inv = norm_parts(dot_nn(z_ref[...], wo_ref[...]) + bias(3))
    residual = x_ref[...].astype(f32) + (y_norm * gain(1) + bias(4))
    r_norm, r_inv = norm_parts(residual)
    normed = (r_norm * gain(2) + bias(5)).astype(bf16)
    c_ref[...] = normed

    def expand(at, total):
        pre = dot_nn(normed, w1_ref[:, at]) + ffb_ref[0:1, at]
        cdf = 0.5 * (1.0 + lax.erf(pre * (0.5**0.5)))
        pdf = jnp.exp(pre * pre * -0.5) * 0.3989422804014327
        act = pre * cdf
        act_ref[:, at] = act
        slope_ref[:, at] = cdf + pre * pdf
        return total + jnp.sum(act, axis=-1, keepdims=True)

    zero = jnp.zeros((rows, 1), f32)
    average = each(expand, zero) / hidden

    def spread(at, total):
        centered = act_ref[:, at] - average
        return total + jnp.sum(centered * centered, axis=-1, keepdims=True)

    m_inv = lax.rsqrt(each(spread, zero) / hidden + epsilon)

    def contract(at, total):
        n = (act_ref[:, at] - average) * m_inv
        act_ref[:, at] = n
        m = (n * mid_ref[0:1, at] + ffb_ref[1:2, at]).astype(bf16)
        m_ref[:, at] = m
        return total + dot_nn(m, w2_ref[at, :])

    branch = each(contract, jnp.zeros((rows, width), f32))
    out_ref[...] = (residual + (branch + bias(6))).astype(bf16)

    position = step * rows + lax.broadcasted_iota(jnp.int32, (rows, 1), 0)
    d_out = jnp.where(position < len_ref[0], cot_ref[...].astype(f32), 0.0)
    d_w = d_out.astype(bf16)
    sums_ref[6] += fold(d_out)

    def back_mid(at, totals):
        dm = dot_nt(d_w, w2_ref[at, :])
        n = act_ref[:, at]
        dn = dm * n
        wide_ref[0, :, at] += fold(dn)
        wide_ref[2, :, at] += fold(dm)
        g = mid_ref[0:1, at]
        dm_ref[:, at] = dm
        return (
            totals[0] + jnp.sum(dm * g, axis=-1, keepdims=True),
            totals[1] + jnp.sum(dn * g, axis=-1, keepdims=True),
        )

    first, second = each(back_mid, (zero, zero))
    first, second = first / hidden, second / hidden

    def back_act(at, total):
        du = (dm_ref[:, at] * mid_ref[0:1, at] - first - act_ref[:, at] * second) * m_inv
        df = (du * slope_ref[:, at]).astype(bf16)
        df_ref[:, at] = df
        wide_ref[1, :, at] += fold(df.astype(f32))
        return total + dot_nt(df, w1_ref[:, at])

    d_c = each(back_act, jnp.zeros((rows, width), f32))
    sums_ref[2] += fold(d_c * r_norm)
    sums_ref[5] += fold(d_c)
    d_r = d_out + norm_back(d_c, gain(2), r_norm, r_inv)
    dr_ref[...] = d_r
    sums_ref[1] += fold(d_r * y_norm)
    sums_ref[4] += fold(d_r)
    d_y = norm_back(d_r, gain(1), y_norm, y_inv).astype(bf16)
    dy_ref[...] = d_y
    sums_ref[3] += fold(d_y.astype(f32))
    do_ref[...] = (dot_nt(d_y, wo_ref[...]) * scale_ref[...]).astype(bf16)


def ffn(lengths, scale_row, x, z, cot, wo, w1, w2, gains, biases, mid, ffb, rows=256, chunk=512, unrolled=True):
    tokens, width = x.shape
    hidden = w1.shape[1]
    by_row = lambda n: pl.BlockSpec((rows, n), lambda i: (i, 0))
    whole = lambda a: pl.BlockSpec(a.shape, lambda i: (0,) * a.ndim, pipeline_mode=pl.Buffered(1))
    sds = jax.ShapeDtypeStruct
    bf16, f32 = jnp.bfloat16, jnp.float32
    outs = [(width, bf16), (width, bf16), (hidden, bf16), (hidden, bf16), (width, bf16), (width, f32), (width, bf16)]
    return pl.pallas_call(
        functools.partial(ffn_kernel, chunk, unrolled),
        grid=(tokens // rows,),
        in_specs=[pl.BlockSpec(memory_space=pltpu.SMEM), whole(scale_row)]
        + [by_row(width)] * 3
        + [whole(a) for a in (wo, w1, w2, gains, biases, mid, ffb)],
        out_specs=[by_row(n) for n, _ in outs]
        + [pl.BlockSpec((7, 8, width), lambda i: (0, 0, 0)), pl.BlockSpec((3, 8, hidden), lambda i: (0, 0, 0))],
        out_shape=[sds((tokens, n), d) for n, d in outs] + [sds((7, 8, width), f32), sds((3, 8, hidden), f32)],
        scratch_shapes=[pltpu.VMEM((rows, hidden), f32)] * 3,
        compiler_params=pltpu.CompilerParams(vmem_limit_bytes=60 << 20),
        name="ffn_both",
    )(lengths, scale_row, x, z, cot, wo, w1, w2, gains, biases, mid, ffb)


head_size = 64


def head_lanes(values, second):
    lane = lax.broadcasted_iota(jnp.int32, values.shape, 1)
    keep = lane >= head_size if second else lane < head_size
    return jnp.where(keep, values, jnp.zeros_like(values))


def masked_scores(keys, queries, first, length):
    scores = dot_nt(keys, queries)
    key_pos = lax.broadcasted_iota(jnp.int32, scores.shape, 0)
    near = key_pos[first:]
    query_pos = first + lax.broadcasted_iota(jnp.int32, near.shape, 1)
    last = jnp.where((near <= query_pos) & (near < length), scores[first:], mask_fill)
    if first == 0:
        return last
    return jnp.concatenate((jnp.where(key_pos[:first] < length, scores[:first], mask_fill), last), axis=0)


def attend_kernel(block, scaling, len_ref, scale_ref, q_ref, k_ref, v_ref, z_ref, log_ref):
    length, pair = len_ref[0], pl.program_id(0)
    tokens, lanes = q_ref.shape
    for first in range(0, tokens, block):
        rows, seen = slice(first, first + block), first + block
        keys, values = k_ref[:seen, :], v_ref[:seen, :]
        mixed = []
        for h in range(2):
            queries = head_lanes(q_ref[rows, :], h) * jnp.bfloat16(scaling)
            scores = masked_scores(keys, queries, first, length)
            top = jnp.max(scores, axis=0, keepdims=True)
            shifted = jnp.exp(scores - top)
            total = jnp.sum(shifted, axis=0, keepdims=True)
            log_ref[0, h : h + 1, rows] = top + jnp.log(total)
            attended = dot_tn(shifted.astype(jnp.bfloat16), values)
            mixed.append(attended * (scale_ref[pair * 2 + h] / total).T)
        lane = lax.broadcasted_iota(jnp.int32, (block, lanes), 1)
        z_ref[rows, :] = jnp.where(lane < head_size, mixed[0], mixed[1]).astype(jnp.bfloat16)


def attend(lengths, head_scale, qkv, block=256):
    tokens, width = qkv.shape[0], qkv.shape[1] // 3
    pairs = width // 128
    cols = lambda part: pl.BlockSpec((tokens, 128), lambda p: (0, p + part * pairs))
    smem = pl.BlockSpec(memory_space=pltpu.SMEM)
    return pl.pallas_call(
        functools.partial(attend_kernel, min(block, tokens), head_size**-0.5),
        grid=(pairs,),
        in_specs=[smem, smem, cols(0), cols(1), cols(2)],
        out_specs=[cols(0), pl.BlockSpec((1, 2, tokens), lambda p: (p, 0, 0))],
        out_shape=[
            jax.ShapeDtypeStruct((tokens, width), jnp.bfloat16),
            jax.ShapeDtypeStruct((pairs, 2, tokens), jnp.float32),
        ],
        compiler_params=pltpu.CompilerParams(vmem_limit_bytes=56 << 20),
        name="attend",
    )(lengths, head_scale, qkv, qkv, qkv)


def attend_back_kernel(block, scaling, len_ref, q_ref, k_ref, v_ref, do_ref, log_ref, dqkv_ref, dot_ref, dk_ref, dv_ref):
    length = len_ref[0]
    tokens, lanes = q_ref.shape
    bf16 = jnp.bfloat16
    for first in range(0, tokens, block):
        rows, seen = slice(first, first + block), first + block
        keys, values = k_ref[:seen, :], v_ref[:seen, :]
        mixed = []
        for h in range(2):
            queries = head_lanes(q_ref[rows, :], h) * bf16(scaling)
            grads = head_lanes(do_ref[rows, :], h)
            scores = masked_scores(keys, queries, first, length)
            weights = jnp.exp(scores - log_ref[0, h : h + 1, rows])
            products = weights * dot_nt(values, grads)
            total = jnp.sum(products, axis=0, keepdims=True)
            dot_ref[0, h : h + 1, rows] = total
            d_scores = (products - weights * total).astype(bf16)
            for ref, left, right in ((dv_ref, weights.astype(bf16), grads), (dk_ref, d_scores, queries)):
                part = dot_nn(left, right)
                if h == 0:
                    ref[rows, :] = part[first:]
                    if first:
                        ref[:first, :] += part[:first]
                else:
                    ref[:seen, :] += part
            mixed.append(dot_tn(d_scores, keys))
        lane = lax.broadcasted_iota(jnp.int32, (block, lanes), 1)
        dqkv_ref[0, rows, :] = (jnp.where(lane < head_size, mixed[0], mixed[1]) * scaling).astype(bf16)
    dqkv_ref[1] = dk_ref[...].astype(bf16)
    dqkv_ref[2] = dv_ref[...].astype(bf16)


def attend_back(lengths, qkv, d_attended, logs, block=256):
    tokens, width = qkv.shape[0], qkv.shape[1] // 3
    pairs = width // 128
    cols = lambda part: pl.BlockSpec((tokens, 128), lambda p: (0, p + part * pairs))
    per_pair = pl.BlockSpec((1, 2, tokens), lambda p: (p, 0, 0))
    return pl.pallas_call(
        functools.partial(attend_back_kernel, min(block, tokens), head_size**-0.5),
        grid=(pairs,),
        in_specs=[pl.BlockSpec(memory_space=pltpu.SMEM), cols(0), cols(1), cols(2), cols(0), per_pair],
        out_specs=[pl.BlockSpec((3, tokens, 128), lambda p: (0, 0, p)), per_pair],
        out_shape=[
            jax.ShapeDtypeStruct((3, tokens, width), jnp.bfloat16),
            jax.ShapeDtypeStruct((pairs, 2, tokens), jnp.float32),
        ],
        scratch_shapes=[pltpu.VMEM((tokens, 128), jnp.float32)] * 2,
        compiler_params=pltpu.CompilerParams(vmem_limit_bytes=56 << 20),
        name="attend_back",
    )(lengths, qkv, qkv, qkv, d_attended, logs)


def project_kernel(x_ref, w_ref, gain_ref, bias_ref, a_ref, qkv_ref):
    width = x_ref.shape[1]
    normed, _ = norm_parts(x_ref[...].astype(jnp.float32))
    a = (normed * gain_ref[0:1, :] + bias_ref[0:1, :]).astype(jnp.bfloat16)
    a_ref[...] = a
    for part, row in ((0, 1), (1, None), (2, 2)):
        at = slice(part * width, (part + 1) * width)
        value = dot_nn(a, w_ref[:, at])
        if row is not None:
            value = value + bias_ref[row : row + 1, :]
        qkv_ref[:, at] = value.astype(jnp.bfloat16)


def project(x, w, gains, biases, rows=256):
    tokens, width = x.shape
    by_row = lambda n: pl.BlockSpec((rows, n), lambda i: (i, 0))
    whole = lambda a: pl.BlockSpec(a.shape, lambda i: (0,) * a.ndim, pipeline_mode=pl.Buffered(1))
    return pl.pallas_call(
        project_kernel,
        grid=(tokens // rows,),
        in_specs=[by_row(width), whole(w), whole(gains), whole(biases)],
        out_specs=[by_row(width), by_row(3 * width)],
        out_shape=[
            jax.ShapeDtypeStruct((tokens, width), jnp.bfloat16),
            jax.ShapeDtypeStruct((tokens, 3 * width), jnp.bfloat16),
        ],
        compiler_params=pltpu.CompilerParams(vmem_limit_bytes=56 << 20),
        name="project",
    )(x, w, gains, biases)


def project_back_kernel(d_ref, x_ref, dr_ref, w_ref, gain_ref, dx_ref, sums_ref):
    @pl.when(pl.program_id(0) == 0)
    def _():
        sums_ref[...] = jnp.zeros_like(sums_ref)

    width = x_ref.shape[1]
    d_a = sum(dot_nt(d_ref[k], w_ref[:, k * width : (k + 1) * width]) for k in range(3))
    normed, inverse = norm_parts(x_ref[...].astype(jnp.float32))
    sums_ref[0] += fold(d_a * normed)
    sums_ref[1] += fold(d_a)
    sums_ref[2] += fold(d_ref[0].astype(jnp.float32))
    sums_ref[3] += fold(d_ref[2].astype(jnp.float32))
    back = norm_back(d_a, gain_ref[0:1, :], normed, inverse)
    dx_ref[...] = (dr_ref[...] + back).astype(jnp.bfloat16)


def project_back(d_qkv, x, d_r, w, gains, rows=256):
    tokens, width = x.shape
    by_row = pl.BlockSpec((rows, width), lambda i: (i, 0))
    whole = lambda a: pl.BlockSpec(a.shape, lambda i: (0,) * a.ndim, pipeline_mode=pl.Buffered(1))
    return pl.pallas_call(
        project_back_kernel,
        grid=(tokens // rows,),
        in_specs=[pl.BlockSpec((3, rows, width), lambda i: (0, i, 0)), by_row, by_row, whole(w), whole(gains)],
        out_specs=[by_row, pl.BlockSpec((4, 8, width), lambda i: (0, 0, 0))],
        out_shape=[
            jax.ShapeDtypeStruct((tokens, width), jnp.bfloat16),
            jax.ShapeDtypeStruct((4, 8, width), jnp.float32),
        ],
        compiler_params=pltpu.CompilerParams(vmem_limit_bytes=56 << 20),
        name="project_back",
    )(d_qkv, x, d_r, w, gains)


def shards(
    digits,
    tokens,
    lengths,
    cotangent,
    w_qkv,
    w_out,
    w_fc1,
    w_fc2,
    norm_gain,
    norm_bias,
    mid_gain,
    ff_bias,
    head_scale,
):
    weights = (w_qkv, w_out, w_fc1, w_fc2)
    small = jnp.concatenate([v.reshape(-1) for v in (norm_gain, norm_bias, mid_gain, ff_bias)])
    small = jnp.pad(to_bf16(small), (0, 2048 - small.shape[0])).reshape(16, 128)
    shards_in = [to_bf16(w).reshape(tiled_rows(*w.shape)) for w in weights] + [small]
    gathered = gather_all(digits, shards_in)
    full_qkv, full_out, full_fc1, full_fc2 = (
        g.reshape((-1, w.shape[1])) for g, w in zip(gathered, weights)
    )
    smalls = gathered[4].reshape(-1, 2048)
    parts, used = [], 0
    for v in (norm_gain, norm_bias, mid_gain, ff_bias):
        block = smalls[:, used : used + v.size].reshape((-1,) + (v.shape if v.ndim == 2 else (1,) + v.shape))
        parts.append(block.transpose(1, 0, 2).reshape(block.shape[1], -1))
        used += v.size
    gain_copy, bias_copy, mid_copy, ff_copy = parts[0], parts[1], parts[2][0], parts[3]
    f32 = jnp.float32
    gains, biases = gain_copy.astype(f32), bias_copy.astype(f32)
    mid_gains, ff_biases = mid_copy[None].astype(f32), ff_copy.astype(f32)
    heads = head_scale.shape[0]
    scale_row = jnp.repeat(head_scale, tokens.shape[1] // heads)[None]
    normed_in, qkv = project(tokens, full_qkv, gains, biases)
    mixed, logs = attend(lengths, head_scale, qkv)
    result, normed_ff, normed_mid, grad_pre, grad_projection, grad_residual, grad_attended, sums, wide = ffn(
        lengths, scale_row, tokens, mixed, cotangent, full_out, full_fc1, full_fc2, gains, biases, mid_gains, ff_biases
    )
    positions = jnp.arange(tokens.shape[0], dtype=jnp.int32)[:, None]
    grad_branch = jnp.where(positions < lengths, cotangent, jnp.zeros_like(cotangent))
    grad_fc2 = dot_tn(normed_mid, grad_branch)
    grad_fc1 = dot_tn(normed_ff, grad_pre)
    grad_out_w = dot_tn(mixed, grad_projection)
    d_qkv, dots = attend_back(lengths, qkv, grad_attended, logs)
    grad_tokens, first_sums = project_back(d_qkv, tokens, grad_residual, full_qkv, gains)
    grad_qkv = jnp.concatenate([dot_tn(normed_in, d_qkv[k]) for k in range(3)], axis=1)
    sums, wide, first_sums = sums.sum(1), wide.sum(1), first_sums.sum(1)
    grad_scale_local = dots.sum(-1).reshape(heads) / head_scale
    grad_gains = jnp.concatenate((first_sums[0:1], sums[1:3]))
    grad_biases = jnp.concatenate((first_sums[1:4], sums[3:7]))
    grad_mid_gain, grad_ff_biases = wide[0], wide[1:3]
    total = digits[0] * digits[1] * digits[2] * digits[3]
    block = []
    for v in (grad_gains, grad_biases, grad_mid_gain[None], grad_ff_biases):
        block.append(v.reshape(v.shape[0], total, -1).transpose(1, 0, 2).reshape(total, -1))
    block.append(jnp.broadcast_to(grad_scale_local[None], (total, heads)))
    block = jnp.concatenate(block, axis=1)
    block = jnp.pad(block, ((0, 0), (0, 1024 - block.shape[1]))).reshape(digits + (8, 128))
    grads = [
        to_bf16(g).reshape(digits + tiled_rows(*w.shape))
        for g, w in zip((grad_qkv, grad_out_w, grad_fc1, grad_fc2), weights)
    ]
    summed = reduce_all(digits, grads + [block])
    flat, used, owned = summed[4].reshape(-1), 0, []
    for v in (norm_gain, norm_bias, mid_gain, ff_bias, head_scale):
        owned.append(flat[used : used + v.size].reshape(v.shape))
        used += v.size
    summed = [g.reshape(w.shape) for g, w in zip(summed[:4], weights)] + owned
    grad_scale = summed[8]
    return (
        result,
        grad_tokens,
        summed[0],
        summed[1],
        summed[2],
        summed[3],
        summed[4],
        summed[5],
        summed[6],
        summed[7],
        grad_scale,
    )


def solution(mesh):
    placed = (
        P(("dp", "fsdp"), None),
        P(("dp", "fsdp")),
        P(("dp", "fsdp"), None),
        P(("dp", "fsdp"), None),
        P(("dp", "fsdp"), None),
        P(("dp", "fsdp"), None),
        P(("dp", "fsdp"), None),
        P(None, ("dp", "fsdp")),
        P(None, ("dp", "fsdp")),
        P(("dp", "fsdp")),
        P(None, ("dp", "fsdp")),
        P(),
    )
    return jax.shard_map(
        functools.partial(shards, digits_of(mesh)),
        mesh=mesh,
        in_specs=placed,
        out_specs=(
            P(("dp", "fsdp"), None),
            P(("dp", "fsdp"), None),
            P(("dp", "fsdp"), None),
            P(("dp", "fsdp"), None),
            P(("dp", "fsdp"), None),
            P(("dp", "fsdp"), None),
            P(None, ("dp", "fsdp")),
            P(None, ("dp", "fsdp")),
            P(("dp", "fsdp")),
            P(None, ("dp", "fsdp")),
            P(),
        ),
        check_vma=False,
    )
```

```python
import functools
import heapq

import jax
import jax.numpy as jnp
from jax import lax
from jax.experimental import pallas as pl
from jax.experimental.pallas import tpu as pltpu
from jax.sharding import PartitionSpec as P

epsilon = 1e-05
mask_fill = -1e30
MESH = pl.DeviceIdType.MESH
ORDERS = ((1, 2, 0), (2, 1, 0), (0, 1, 2), (0, 2, 1))


def digits_of(mesh):
    dp, fsdp = mesh.shape["dp"], mesh.shape["fsdp"]
    minor = 2 if dp <= 8 else 8
    return (dp // minor, minor, fsdp // 2, 2)


class Place:
    def __init__(self, digits):
        self.digits = digits
        dp, fs = lax.axis_index("dp"), lax.axis_index("fsdp")
        self.at = (dp // digits[1], dp % digits[1], fs // digits[3], fs % digits[3])

    def digit(self, axis, shift):
        n = self.digits[axis]
        return (self.at[axis] + shift + n) % n

    def peer(self, axis, shift):
        at = list(self.at)
        at[axis] = self.digit(axis, shift)
        return (at[0] * self.digits[1] + at[1], at[2] * self.digits[3] + at[3])

    def greet(self):
        barrier = pltpu.get_barrier_semaphore()
        peers = []
        for axis, n in enumerate(self.digits):
            if n > 1:
                peers.append(self.peer(axis, 1))
            if n > 2:
                peers.append(self.peer(axis, -1))
        for peer in peers:
            pl.semaphore_signal(barrier, inc=1, device_id=peer, device_id_type=MESH)
        pl.semaphore_wait(barrier, len(peers))


class Sems:
    def __init__(self, send, recv, local):
        self.send, self.recv, self.local = send, recv, local
        self.remotes = self.locals = 0

    def remote(self, src, dst, peer):
        copy = pltpu.make_async_remote_copy(
            src_ref=src,
            dst_ref=dst,
            send_sem=self.send.at[self.remotes],
            recv_sem=self.recv.at[self.remotes],
            device_id=peer,
            device_id_type=MESH,
        )
        self.remotes += 1
        copy.start()
        return copy

    def copy(self, src, dst):
        copy = pltpu.make_async_copy(src, dst, self.local.at[self.locals])
        self.locals += 1
        copy.start()
        return copy


def hops(n):
    if n == 1:
        return []
    if n == 2:
        return [(0, (1,), False)]
    return [(s, (1, -1), s == n // 2 - 1) for s in range(n // 2)]


def column_part(start, size, direction, halved):
    if not halved:
        return start, size
    first = size // 256 * 128
    if first == 0:
        return (start, size) if direction > 0 else (start, 0)
    return (start, first) if direction > 0 else (start + first, size - first)


def slots(place, view, axis, slot, part):
    index = []
    for other, n in enumerate(place.digits):
        if other == axis:
            index.append(slot)
        elif other in view:
            index.append(pl.ds(0, n))
        else:
            index.append(place.at[other])
    return tuple(index) + (slice(None), pl.ds(*part))


def gather_piece(place, sems, shard, full, start, size, order):
    held, sends, cores = set(), [], []
    own = sems.copy(
        shard.at[:, pl.ds(start, size)], full.at[slots(place, (), None, None, (start, size))]
    )
    core = place.peer(3, 1)

    def forward(axis, slot, part):
        view = full.at[slots(place, held, axis, slot, part)]
        cores.append(sems.remote(view, view, core))

    first = True
    for axis in order:
        n = place.digits[axis]
        for step, directions, last in hops(n):
            started = []
            for direction in directions:
                part = column_part(start, size, direction, last)
                if part[1] == 0:
                    continue
                index = slots(place, held, axis, place.digit(axis, -step * direction), part)
                src = shard.at[:, pl.ds(*part)] if first and step == 0 else full.at[index]
                started.append(
                    (direction, sems.remote(src, full.at[index], place.peer(axis, direction)))
                )
            yield
            for direction, copy in started:
                copy.wait_recv()
                sends.append(copy)
                if not first and not last and n > 2:
                    forward(axis, place.digit(axis, -(step + 1) * direction), (start, size))
            if not first and (last or n == 2):
                forward(axis, place.digit(axis, n // 2), (start, size))
        if n > 1:
            held.add(axis)
            if first:
                own.wait()
                forward(None, None, (start, size))
                first = False
    if first:
        own.wait()
        forward(None, None, (start, size))
    yield
    for copy in cores:
        copy.wait()
    for copy in sends:
        copy.wait_send()


def accumulate(target, source, result=None):
    lead, dims = target.shape[:-2], target.shape
    count = 1
    for n in lead:
        count *= n

    def index_of(flat):
        index = []
        for n in reversed(lead):
            index.append(flat % n)
            flat = flat // n
        return tuple(reversed(index)) + (slice(None), slice(None))

    def body(flat, carry):
        index = index_of(flat)
        total = target[index].astype(jnp.float32) + source[index].astype(jnp.float32)
        target[index] = total.astype(target.dtype)
        return carry

    if lead:
        lax.fori_loop(0, count, body, 0)
    else:
        body(0, 0)


def reduce_steps(digits, start, size, order):
    left, plan = [0, 1, 2], []
    for axis in order:
        n = digits[axis]
        left.remove(axis)
        lead = tuple(digits[a] for a in left)
        for step, directions, last in reversed(hops(n)):
            batch = []
            for direction in directions:
                part = column_part(start, size, direction, last)
                if part[1] > 0:
                    batch.append((axis, direction, step, part, lead))
            plan.append((tuple(left), batch))
    return plan


def reduce_piece(place, sems, grad, acc, landed, slabs, out, start, size, order):
    sends = []
    lead = (slice(None),) * 3
    whole = (slice(None), pl.ds(start, size))
    mine = acc.at[lead + whole]
    other = landed.at[lead + whole]
    own = sems.copy(grad.at[lead + (place.at[3],) + whole], mine)
    sent = sems.remote(grad.at[lead + (place.digit(3, 1),) + whole], other, place.peer(3, 1))
    yield
    own.wait()
    sent.wait_recv()
    sends.append(sent)
    accumulate(mine, other)
    slabs = iter(slabs)
    for left, batch in reduce_steps(place.digits, start, size, order):
        started = []
        for axis, direction, step, part, _ in batch:
            slot = place.digit(axis, (step + 1) * direction)
            src = acc.at[slots(place, left, axis, slot, part)[:3] + (slice(None), pl.ds(*part))]
            dst = next(slabs)
            sent = sems.remote(src, dst, place.peer(axis, direction))
            started.append((axis, direction * step, part, dst, sent))
        yield
        for axis, shift, part, dst, sent in started:
            sent.wait_recv()
            sends.append(sent)
            slot = place.digit(axis, shift)
            view = slots(place, left, axis, slot, part)[:3] + (slice(None), pl.ds(*part))
            accumulate(acc.at[view], dst)
    out[:, pl.ds(start, size)] = acc[place.at[:3] + whole].astype(jnp.float32)
    for sent in sends:
        sent.wait_send()
    yield


def pieces_of(cols, wanted=4):
    tiles = cols // 128
    count = wanted
    while tiles % count:
        count -= 1
    size = tiles // count * 128
    return [(k * size, size) for k in range(count)]


def run_all(generators):
    live = list(generators)
    while live:
        still = []
        for generator in live:
            try:
                next(generator)
                still.append(generator)
            except StopIteration:
                pass
        live = still


def gather_kernel(digits, count, *refs):
    shards, fulls = refs[:count], refs[count : 2 * count]
    send, recv, local = refs[2 * count :]
    place = Place(digits)
    sems = Sems(send, recv, local)
    place.greet()
    run_all(
        gather_piece(place, sems, shard, full, start, size, ORDERS[k % 4])
        for shard, full in zip(shards, fulls)
        for k, (start, size) in enumerate(pieces_of(shard.shape[1]))
    )


def gather_all(digits, shards):
    count = len(shards)
    copies = 16 * 4 * count * max(1, max(digits) // 4)
    whole = [jax.ShapeDtypeStruct(digits + s.shape, s.dtype) for s in shards]
    return pl.pallas_call(
        functools.partial(gather_kernel, digits, count),
        out_shape=whole,
        in_specs=[pl.BlockSpec(memory_space=pl.ANY)] * count,
        out_specs=[pl.BlockSpec(memory_space=pl.ANY)] * count,
        scratch_shapes=[
            pltpu.SemaphoreType.DMA((copies,)),
            pltpu.SemaphoreType.DMA((copies,)),
            pltpu.SemaphoreType.DMA((4 * count,)),
        ],
        compiler_params=pltpu.CompilerParams(collective_id=0, has_side_effects=True),
        name="gather_all",
    )(*shards)


def reduce_plan(digits, grads):
    plan = []
    for g, grad in enumerate(grads):
        for k, (start, size) in enumerate(pieces_of(grad.shape[-1])):
            plan.append((g, start, size, ORDERS[k % 4]))
    return plan


def reduce_kernel(digits, plan, slab_counts, count, *refs):
    grads, outs = refs[:count], refs[count : 2 * count]
    accs, landed = refs[2 * count : 3 * count], refs[3 * count : 4 * count]
    slabs = refs[4 * count : -3]
    send, recv, local = refs[-3:]
    place = Place(digits)
    sems = Sems(send, recv, local)
    place.greet()
    generators, used = [], 0
    for (g, start, size, order), many in zip(plan, slab_counts):
        own = slabs[used : used + many]
        used += many
        generators.append(
            reduce_piece(place, sems, grads[g], accs[g], landed[g], own, outs[g], start, size, order)
        )
    run_all(generators)


def reduce_all(digits, grads):
    count = len(grads)
    plan = reduce_plan(digits, grads)
    slabs, slab_counts = [], []
    for g, start, size, order in plan:
        shapes = [
            pltpu.VMEM(lead + (grads[g].shape[-2], part[1]), grads[g].dtype)
            for _, batch in reduce_steps(digits, start, size, order)
            for _, _, _, part, lead in batch
        ]
        slabs += shapes
        slab_counts.append(len(shapes))
    blocks = [pltpu.VMEM(digits[:3] + g.shape[-2:], g.dtype) for g in grads]
    copies = len(slabs) + len(plan)
    return pl.pallas_call(
        functools.partial(reduce_kernel, digits, plan, slab_counts, count),
        out_shape=[jax.ShapeDtypeStruct(g.shape[-2:], jnp.float32) for g in grads],
        in_specs=[pl.BlockSpec(memory_space=pl.ANY)] * count,
        out_specs=[pl.BlockSpec(memory_space=pltpu.VMEM)] * count,
        scratch_shapes=blocks
        + blocks
        + slabs
        + [
            pltpu.SemaphoreType.DMA((copies,)),
            pltpu.SemaphoreType.DMA((copies,)),
            pltpu.SemaphoreType.DMA((len(plan),)),
        ],
        compiler_params=pltpu.CompilerParams(
            collective_id=1, has_side_effects=True, vmem_limit_bytes=58 << 20
        ),
        name="reduce_all",
    )(*grads)


def tiled_rows(rows, cols):
    return (rows, cols) if rows % 16 == 0 else (16, rows * cols // 16)


def to_bf16(values):
    return values.astype(jnp.bfloat16)


def dot_nn(a, b):
    return lax.dot_general(a, b, (((1,), (0,)), ((), ())), preferred_element_type=jnp.float32)


def dot_nt(a, b):
    return lax.dot_general(a, b, (((1,), (1,)), ((), ())), preferred_element_type=jnp.float32)


def dot_tn(a, b):
    return lax.dot_general(a, b, (((0,), (0,)), ((), ())), preferred_element_type=jnp.float32)


def row_mean(v):
    return jnp.mean(v, axis=-1, keepdims=True)


def norm_parts(v):
    centered = v - row_mean(v)
    inverse = lax.rsqrt(row_mean(centered * centered) + epsilon)
    return centered * inverse, inverse


def norm_back(grad, gain, normed, inverse):
    scaled = grad * gain
    return (scaled - row_mean(scaled) - normed * row_mean(scaled * normed)) * inverse


def fold(v):
    return v.reshape(v.shape[0] // 8, 8, v.shape[1]).sum(0)


def ffn_kernel(
    chunk, unrolled,
    len_ref, scale_ref, x_ref, z_ref, cot_ref, wo_ref, w1_ref, w2_ref, par_ref, table_ref,
    out_ref, c_ref, m_ref, df_ref, dy_ref, dr_ref, do_ref, sums_ref, wide_ref,
    act_ref, slope_ref, dm_ref,
):
    step = pl.program_id(0)
    rows, width = x_ref.shape
    hidden = w1_ref.shape[1]
    f32, bf16 = jnp.float32, jnp.bfloat16

    @pl.when(step == 0)
    def _():
        sums_ref[...] = jnp.zeros_like(sums_ref)
        wide_ref[...] = jnp.zeros_like(wide_ref)

    def each(body, carry):
        if unrolled:
            for j in range(hidden // chunk):
                carry = body(slice(j * chunk, (j + 1) * chunk), carry)
            return carry
        return lax.fori_loop(
            0, hidden // chunk, lambda j, c: body(pl.ds(pl.multiple_of(j * chunk, chunk), chunk), c), carry
        )

    gain = lambda k: par_ref[k : k + 1, :]
    bias = lambda k: par_ref[3 + k : 4 + k, :]
    y_norm, y_inv = norm_parts(dot_nn(z_ref[...], wo_ref[...]) + bias(3))
    residual = x_ref[...].astype(f32) + (y_norm * gain(1) + bias(4))
    r_norm, r_inv = norm_parts(residual)
    normed = (r_norm * gain(2) + bias(5)).astype(bf16)
    c_ref[...] = normed

    def expand(at, total):
        pre = dot_nn(normed, w1_ref[:, at]) + table_ref[11:12, at]
        cdf = 0.5 * (1.0 + lax.erf(pre * (0.5**0.5)))
        pdf = jnp.exp(pre * pre * -0.5) * 0.3989422804014327
        act = pre * cdf
        act_ref[:, at] = act
        slope_ref[:, at] = cdf + pre * pdf
        return total + jnp.sum(act, axis=-1, keepdims=True)

    zero = jnp.zeros((rows, 1), f32)
    average = each(expand, zero) / hidden

    def spread(at, total):
        centered = act_ref[:, at] - average
        return total + jnp.sum(centered * centered, axis=-1, keepdims=True)

    m_inv = lax.rsqrt(each(spread, zero) / hidden + epsilon)

    def contract(at, total):
        n = (act_ref[:, at] - average) * m_inv
        act_ref[:, at] = n
        m = (n * table_ref[10:11, at] + table_ref[12:13, at]).astype(bf16)
        m_ref[:, at] = m
        return total + dot_nn(m, w2_ref[at, :])

    branch = each(contract, jnp.zeros((rows, width), f32))
    out_ref[...] = (residual + (branch + bias(6))).astype(bf16)

    position = step * rows + lax.broadcasted_iota(jnp.int32, (rows, 1), 0)
    d_out = jnp.where(position < len_ref[0], cot_ref[...].astype(f32), 0.0)
    d_w = d_out.astype(bf16)
    sums_ref[6] += fold(d_out)

    def back_mid(at, totals):
        dm = dot_nt(d_w, w2_ref[at, :])
        n = act_ref[:, at]
        dn = dm * n
        wide_ref[0, :, at] += fold(dn)
        wide_ref[2, :, at] += fold(dm)
        g = table_ref[10:11, at]
        dm_ref[:, at] = dm
        return (
            totals[0] + jnp.sum(dm * g, axis=-1, keepdims=True),
            totals[1] + jnp.sum(dn * g, axis=-1, keepdims=True),
        )

    first, second = each(back_mid, (zero, zero))
    first, second = first / hidden, second / hidden

    def back_act(at, total):
        du = (dm_ref[:, at] * table_ref[10:11, at] - first - act_ref[:, at] * second) * m_inv
        df = (du * slope_ref[:, at]).astype(bf16)
        df_ref[:, at] = df
        wide_ref[1, :, at] += fold(df.astype(f32))
        return total + dot_nt(df, w1_ref[:, at])

    d_c = each(back_act, jnp.zeros((rows, width), f32))
    sums_ref[2] += fold(d_c * r_norm)
    sums_ref[5] += fold(d_c)
    d_r = d_out + norm_back(d_c, gain(2), r_norm, r_inv)
    dr_ref[...] = d_r
    sums_ref[1] += fold(d_r * y_norm)
    sums_ref[4] += fold(d_r)
    d_y = norm_back(d_r, gain(1), y_norm, y_inv).astype(bf16)
    dy_ref[...] = d_y
    sums_ref[3] += fold(d_y.astype(f32))
    do_ref[...] = (dot_nt(d_y, wo_ref[...]) * scale_ref[...]).astype(bf16)


def ffn(lengths, scale_row, x, z, cot, wo, w1, w2, par, table, rows=256, chunk=512, unrolled=True):
    tokens, width = x.shape
    hidden = w1.shape[1]
    by_row = lambda n: pl.BlockSpec((rows, n), lambda i: (i, 0))
    whole = lambda a: pl.BlockSpec(a.shape, lambda i: (0,) * a.ndim, pipeline_mode=pl.Buffered(1))
    sds = jax.ShapeDtypeStruct
    bf16, f32 = jnp.bfloat16, jnp.float32
    outs = [(width, bf16), (width, bf16), (hidden, bf16), (hidden, bf16), (width, bf16), (width, f32), (width, bf16)]
    return pl.pallas_call(
        functools.partial(ffn_kernel, chunk, unrolled),
        grid=(tokens // rows,),
        in_specs=[pl.BlockSpec(memory_space=pltpu.SMEM), whole(scale_row)]
        + [by_row(width)] * 3
        + [whole(a) for a in (wo, w1, w2, par, table)],
        out_specs=[by_row(n) for n, _ in outs]
        + [pl.BlockSpec((7, 8, width), lambda i: (0, 0, 0)), pl.BlockSpec((3, 8, hidden), lambda i: (0, 0, 0))],
        out_shape=[sds((tokens, n), d) for n, d in outs] + [sds((7, 8, width), f32), sds((3, 8, hidden), f32)],
        scratch_shapes=[pltpu.VMEM((rows, hidden), f32)] * 3,
        compiler_params=pltpu.CompilerParams(vmem_limit_bytes=60 << 20),
        name="ffn_both",
    )(lengths, scale_row, x, z, cot, wo, w1, w2, par, table)


head_size = 64


def head_lanes(values, second):
    lane = lax.broadcasted_iota(jnp.int32, values.shape, 1)
    keep = lane >= head_size if second else lane < head_size
    return jnp.where(keep, values, jnp.zeros_like(values))


def masked_scores(keys, queries, first, length):
    scores = dot_nt(keys, queries)
    key_pos = lax.broadcasted_iota(jnp.int32, scores.shape, 0)
    near = key_pos[first:]
    query_pos = first + lax.broadcasted_iota(jnp.int32, near.shape, 1)
    last = jnp.where((near <= query_pos) & (near < length), scores[first:], mask_fill)
    if first == 0:
        return last
    return jnp.concatenate((jnp.where(key_pos[:first] < length, scores[:first], mask_fill), last), axis=0)


def attend_unit(length, scale_ref, head, first, block, q_ref, k_ref, v_ref, z_ref, log_ref):
    rows, seen = slice(first, first + block), first + block
    scaling = jnp.bfloat16(head_size**-0.5)
    keys, values = k_ref[:seen, :], v_ref[:seen, :]
    mixed = []
    for h in range(2):
        queries = head_lanes(q_ref[rows, :], h) * scaling
        scores = masked_scores(keys, queries, first, length)
        top = jnp.max(scores, axis=0, keepdims=True)
        shifted = jnp.exp(scores - top)
        total = jnp.sum(shifted, axis=0, keepdims=True)
        log_ref[h : h + 1, rows] = top + jnp.log(total)
        attended = dot_tn(shifted.astype(jnp.bfloat16), values)
        mixed.append(attended * (scale_ref[head + h] / total).T)
    lane = lax.broadcasted_iota(jnp.int32, mixed[0].shape, 1)
    z_ref[rows, :] = jnp.where(lane < head_size, mixed[0], mixed[1]).astype(jnp.bfloat16)


def attend_kernel(block, len_ref, scale_ref, q_ref, k_ref, v_ref, z_ref, log_ref):
    for first in range(0, q_ref.shape[1], block):
        attend_unit(
            len_ref[0], scale_ref, pl.program_id(0) * 2, first, block,
            q_ref.at[0], k_ref.at[0], v_ref.at[0], z_ref, log_ref.at[0],
        )


def attend(lengths, head_scale, qkv, block=256):
    _, tokens, width = qkv.shape
    pairs = width // 128
    cols = lambda part: pl.BlockSpec((1, tokens, 128), lambda p: (part, 0, p))
    smem = pl.BlockSpec(memory_space=pltpu.SMEM)
    return pl.pallas_call(
        functools.partial(attend_kernel, min(block, tokens)),
        grid=(pairs,),
        in_specs=[smem, smem, cols(0), cols(1), cols(2)],
        out_specs=[
            pl.BlockSpec((tokens, 128), lambda p: (0, p)),
            pl.BlockSpec((1, 2, tokens), lambda p: (p, 0, 0)),
        ],
        out_shape=[
            jax.ShapeDtypeStruct((tokens, width), jnp.bfloat16),
            jax.ShapeDtypeStruct((pairs, 2, tokens), jnp.float32),
        ],
        compiler_params=pltpu.CompilerParams(vmem_limit_bytes=56 << 20),
        name="attend",
    )(lengths, head_scale, qkv, qkv, qkv)


def attend_back_unit(
    length, first, block, q_ref, k_ref, v_ref, do_ref, log_ref, dq_ref, dot_ref, dk_ref, dv_ref
):
    rows, seen = slice(first, first + block), first + block
    bf16, scaling = jnp.bfloat16, head_size**-0.5
    keys, values = k_ref[:seen, :], v_ref[:seen, :]
    mixed = []
    for h in range(2):
        queries = head_lanes(q_ref[rows, :], h) * bf16(scaling)
        grads = head_lanes(do_ref[rows, :], h)
        scores = masked_scores(keys, queries, first, length)
        weights = jnp.exp(scores - log_ref[h : h + 1, rows])
        products = weights * dot_nt(values, grads)
        total = jnp.sum(products, axis=0, keepdims=True)
        dot_ref[h : h + 1, rows] = total
        d_scores = (products - weights * total).astype(bf16)
        for ref, left, right in ((dv_ref, weights.astype(bf16), grads), (dk_ref, d_scores, queries)):
            part = dot_nn(left, right)
            if h == 0:
                ref[rows, :] = part[first:]
                if first:
                    ref[:first, :] += part[:first]
            else:
                ref[:seen, :] += part
        mixed.append(dot_tn(d_scores, keys))
    lane = lax.broadcasted_iota(jnp.int32, mixed[0].shape, 1)
    dq_ref[rows, :] = (jnp.where(lane < head_size, mixed[0], mixed[1]) * scaling).astype(bf16)


def attend_back_kernel(block, len_ref, q_ref, k_ref, v_ref, do_ref, log_ref, dqkv_ref, dot_ref, dk_ref, dv_ref):
    for first in range(0, do_ref.shape[0], block):
        attend_back_unit(
            len_ref[0], first, block, q_ref.at[0], k_ref.at[0], v_ref.at[0], do_ref, log_ref.at[0],
            dqkv_ref.at[0], dot_ref.at[0], dk_ref, dv_ref,
        )
    dqkv_ref[1] = dk_ref[...].astype(jnp.bfloat16)
    dqkv_ref[2] = dv_ref[...].astype(jnp.bfloat16)


def attend_back(lengths, qkv, d_attended, logs, block=256):
    _, tokens, width = qkv.shape
    pairs = width // 128
    cols = lambda part: pl.BlockSpec((1, tokens, 128), lambda p: (part, 0, p))
    per_pair = pl.BlockSpec((1, 2, tokens), lambda p: (p, 0, 0))
    return pl.pallas_call(
        functools.partial(attend_back_kernel, min(block, tokens)),
        grid=(pairs,),
        in_specs=[
            pl.BlockSpec(memory_space=pltpu.SMEM),
            cols(0),
            cols(1),
            cols(2),
            pl.BlockSpec((tokens, 128), lambda p: (0, p)),
            per_pair,
        ],
        out_specs=[pl.BlockSpec((3, tokens, 128), lambda p: (0, 0, p)), per_pair],
        out_shape=[
            jax.ShapeDtypeStruct((3, tokens, width), jnp.bfloat16),
            jax.ShapeDtypeStruct((pairs, 2, tokens), jnp.float32),
        ],
        scratch_shapes=[pltpu.VMEM((tokens, 128), jnp.float32)] * 2,
        compiler_params=pltpu.CompilerParams(vmem_limit_bytes=56 << 20),
        name="attend_back",
    )(lengths, qkv, qkv, qkv, d_attended, logs)


def project_kernel(x_ref, w_ref, gain_ref, bias_ref, a_ref, qkv_ref):
    width = x_ref.shape[1]
    normed, _ = norm_parts(x_ref[...].astype(jnp.float32))
    a = (normed * gain_ref[0:1, :] + bias_ref[0:1, :]).astype(jnp.bfloat16)
    a_ref[...] = a
    for part, row in ((0, 1), (1, None), (2, 2)):
        at = slice(part * width, (part + 1) * width)
        value = dot_nn(a, w_ref[:, at])
        if row is not None:
            value = value + bias_ref[row : row + 1, :]
        qkv_ref[part] = value.astype(jnp.bfloat16)


def project(x, w, gains, biases, rows=256):
    tokens, width = x.shape
    by_row = lambda n: pl.BlockSpec((rows, n), lambda i: (i, 0))
    whole = lambda a: pl.BlockSpec(a.shape, lambda i: (0,) * a.ndim, pipeline_mode=pl.Buffered(1))
    return pl.pallas_call(
        project_kernel,
        grid=(tokens // rows,),
        in_specs=[by_row(width), whole(w), whole(gains), whole(biases)],
        out_specs=[by_row(width), pl.BlockSpec((3, rows, width), lambda i: (0, i, 0))],
        out_shape=[
            jax.ShapeDtypeStruct((tokens, width), jnp.bfloat16),
            jax.ShapeDtypeStruct((3, tokens, width), jnp.bfloat16),
        ],
        compiler_params=pltpu.CompilerParams(vmem_limit_bytes=56 << 20),
        name="project",
    )(x, w, gains, biases)


def project_back_kernel(d_ref, x_ref, dr_ref, w_ref, gain_ref, dx_ref, sums_ref):
    @pl.when(pl.program_id(0) == 0)
    def _():
        sums_ref[...] = jnp.zeros_like(sums_ref)

    width = x_ref.shape[1]
    d_a = sum(dot_nt(d_ref[k], w_ref[:, k * width : (k + 1) * width]) for k in range(3))
    normed, inverse = norm_parts(x_ref[...].astype(jnp.float32))
    sums_ref[0] += fold(d_a * normed)
    sums_ref[1] += fold(d_a)
    sums_ref[2] += fold(d_ref[0].astype(jnp.float32))
    sums_ref[3] += fold(d_ref[2].astype(jnp.float32))
    back = norm_back(d_a, gain_ref[0:1, :], normed, inverse)
    dx_ref[...] = (dr_ref[...] + back).astype(jnp.bfloat16)


def project_back(d_qkv, x, d_r, w, gains, rows=256):
    tokens, width = x.shape
    by_row = pl.BlockSpec((rows, width), lambda i: (i, 0))
    whole = lambda a: pl.BlockSpec(a.shape, lambda i: (0,) * a.ndim, pipeline_mode=pl.Buffered(1))
    return pl.pallas_call(
        project_back_kernel,
        grid=(tokens // rows,),
        in_specs=[pl.BlockSpec((3, rows, width), lambda i: (0, i, 0)), by_row, by_row, whole(w), whole(gains)],
        out_specs=[by_row, pl.BlockSpec((4, 8, width), lambda i: (0, 0, 0))],
        out_shape=[
            jax.ShapeDtypeStruct((tokens, width), jnp.bfloat16),
            jax.ShapeDtypeStruct((4, 8, width), jnp.float32),
        ],
        compiler_params=pltpu.CompilerParams(vmem_limit_bytes=56 << 20),
        name="project_back",
    )(d_qkv, x, d_r, w, gains)


class Ops:
    def __init__(self, send, recv, local, place):
        self.send, self.recv, self.local, self.place = send, recv, local, place
        self.remotes = self.locals = 0
        self.now = []

    def do(self, action):
        self.now.append(action)

    def remote(self, src, dst, peer):
        k = self.remotes
        self.remotes += 1
        copy = pltpu.make_async_remote_copy(
            src_ref=src,
            dst_ref=dst,
            send_sem=self.send.at[k],
            recv_sem=self.recv.at[k],
            device_id=peer,
            device_id_type=MESH,
        )
        self.do(copy.start)
        return copy

    def copy(self, src, dst):
        copy = pltpu.make_async_copy(src, dst, self.local.at[self.locals])
        self.locals += 1
        self.do(copy.start)
        return copy


class FixedPlace(Place):
    def __init__(self, digits):
        super().__init__(digits)
        self.shifted = {}
        self.peers = {}
        for axis, n in enumerate(digits):
            for shift in range(-n, n + 1):
                self.shifted[axis, shift] = super().digit(axis, shift)
            for shift in (-1, 1):
                self.peers[axis, shift] = super().peer(axis, shift)

    def digit(self, axis, shift):
        return self.shifted[axis, shift]

    def peer(self, axis, shift):
        return self.peers[axis, shift]


def plan_ticks(ops, pieces, stride):
    queue = [(start, 0, k) for k, (start, _) in enumerate(pieces)]
    heapq.heapify(queue)
    ticks, ends = [], {}
    while queue:
        at, age, k = heapq.heappop(queue)
        ops.now = []
        alive = next(pieces[k][1], "end") != "end"
        if ops.now:
            ticks.append(ops.now)
        if alive:
            heapq.heappush(queue, (at + stride, age - 1, k))
        else:
            ends[k] = len(ticks)
    return ticks, ends


def plan_keyed(ops, pieces, stride):
    queue = [(start, 0, k) for k, (start, _) in enumerate(pieces)]
    heapq.heapify(queue)
    ticks, keys = [], []
    while queue:
        at, age, k = heapq.heappop(queue)
        ops.now = []
        if next(pieces[k][1], "end") != "end":
            heapq.heappush(queue, (at + stride, age - 1, k))
        if ops.now:
            ticks.append(ops.now)
            keys.append(at)
    return ticks, keys


class Hooks:
    def __init__(self, ticks, moments):
        self.ticks, self.moments = ticks, moments

    def run(self, step, hook):
        for at in sorted(s for s, h in self.moments if h == hook):
            numbers = self.moments[at, hook]
            if numbers:

                @pl.when(step == at)
                def _(numbers=numbers):
                    for number in numbers:
                        for action in self.ticks[number]:
                            action()


def spread_ticks(first, count, moments, weights=None):
    weights = weights or [1] * len(moments)
    table, todo, used, past = {}, list(range(first, count)), 0, 0
    for moment, weight in zip(moments, weights):
        past += weight
        upto = len(todo) * past // sum(weights)
        table[moment] = todo[used:upto]
        used = upto
    return table


def rect(rows, cols):
    return (pl.ds(*rows), pl.ds(*cols))


def gather_steps(ops, shard, full, rows, cols, order):
    place = ops.place
    held, sends, cores = set(), [], []
    core = place.peer(3, 1)

    def index(axis, slot, part):
        return slots(place, held, axis, slot, part)[:4] + rect(rows, part)

    def forward(axis, slot):
        view = full.at[index(axis, slot, cols)]
        cores.append(ops.remote(view, view, core))

    own = ops.copy(shard.at[rect(rows, cols)], full.at[index(None, None, cols)])
    first = True
    for axis in order:
        n = place.digits[axis]
        for step, directions, last in hops(n):
            started = []
            for direction in directions:
                part = column_part(*cols, direction, last)
                if part[1] == 0:
                    continue
                at = index(axis, place.digit(axis, -step * direction), part)
                src = shard.at[rect(rows, part)] if first and step == 0 else full.at[at]
                started.append((direction, ops.remote(src, full.at[at], place.peer(axis, direction))))
            yield
            for direction, copy in started:
                ops.do(copy.wait_recv)
                sends.append(copy)
                if not first and not last and n > 2:
                    forward(axis, place.digit(axis, -(step + 1) * direction))
            if not first and (last or n == 2):
                forward(axis, place.digit(axis, n // 2))
        held.add(axis)
        if first:
            ops.do(own.wait)
            forward(None, None)
            first = False
    yield
    for copy in cores:
        ops.do(copy.wait)
    for copy in sends:
        ops.do(copy.wait_send)


def add_into(target, source):
    return lambda: accumulate(target, source)


def reduce_steps_of(ops, own, sent, stage, landed, slabs, finish, cols, order):
    place, sends = ops.place, []
    if stage is not None:
        local = ops.copy(own, stage)
    copy = ops.remote(sent, landed, place.peer(3, 1))
    yield
    if stage is not None:
        ops.do(local.wait)
    ops.do(copy.wait_recv)
    sends.append(copy)
    ops.do(add_into(landed, own if stage is None else stage))
    slabs = iter(slabs)
    for left, batch in reduce_steps(place.digits, *cols, order):
        started = []
        for axis, direction, step, part, _ in batch:
            slot = place.digit(axis, (step + 1) * direction)
            src = landed.at[slots(place, left, axis, slot, part)[:3] + (slice(None), pl.ds(*part))]
            dst = next(slabs)
            copy = ops.remote(src, dst, place.peer(axis, direction))
            started.append((axis, direction * step, part, dst, copy))
        yield
        for axis, shift, part, dst, copy in started:
            ops.do(copy.wait_recv)
            sends.append(copy)
            slot = place.digit(axis, shift)
            view = slots(place, left, axis, slot, part)[:3] + (slice(None), pl.ds(*part))
            ops.do(add_into(landed.at[view], dst))
    ops.do(lambda: finish(landed[place.at[:3]].astype(jnp.float32)))
    for copy in sends:
        ops.do(copy.wait_send)
    yield


def slab_shapes(digits, rows, cols, order, dtype):
    return [
        pltpu.VMEM(lead + (rows, part[1]), dtype)
        for _, batch in reduce_steps(digits, 0, cols, order)
        for _, _, _, part, lead in batch
    ]


GATHER_ORDERS = ((0, 1, 2), (0, 2, 1), (0, 1, 2), (0, 2, 1), (1, 2, 0), (0, 2, 1), (0, 1, 2), (0, 2, 1), (2, 1, 0))
REDUCE_ORDERS = tuple(order[::-1] for order in GATHER_ORDERS)


def blocks_of(shape, rows, cols):
    rows, cols = min(rows, shape[0]), min(cols, shape[1])
    return [((r, rows), (c, cols)) for r in range(0, shape[0], rows) for c in range(0, shape[1], cols)]


def semaphores(copies, local):
    return [
        pltpu.SemaphoreType.DMA((copies,)),
        pltpu.SemaphoreType.DMA((copies,)),
        pltpu.SemaphoreType.DMA((local,)),
    ]


HEADS_WIDE = 256
QUERY_BLOCK = 256


def front_kernel(
    digits, counts,
    len_ref, scale_ref, x_ref, qkv_shard, out_shard, fc1_shard, fc2_shard, small_shard,
    a_ref, qkv_ref, z_ref, log_ref, wqkv_out, wout_ref, w1_ref, w2_ref, par_ref, wide_ref,
    wqkv_ref, small_ref, send, recv, local,
):
    step = pl.program_id(0)
    steps = counts["steps"]
    f32, bf16 = jnp.float32, jnp.bfloat16
    tokens, width = x_ref.shape
    place = FixedPlace(digits)
    ops = Ops(send, recv, local, place)
    pieces, number, start = [], 0, 0.0
    whole = lambda ref: ((0, ref.shape[0]), (0, ref.shape[1]))
    pieces.append((0.0, gather_steps(ops, small_shard, small_ref, *whole(small_shard), GATHER_ORDERS[0])))
    for s in range(steps):
        for part in range(3):
            cols = (part * width + s * HEADS_WIDE, HEADS_WIDE)
            order = GATHER_ORDERS[number % 9]
            number += 1
            pieces.append((start, gather_steps(ops, qkv_shard, wqkv_ref, (0, qkv_shard.shape[0]), cols, order)))
            start += 0.5
    for shard, full in ((out_shard, wout_ref), (fc1_shard, w1_ref), (fc2_shard, w2_ref)):
        for rows, cols in blocks_of(shard.shape, 32, 512):
            order = GATHER_ORDERS[number % 9]
            number += 1
            pieces.append((start, gather_steps(ops, shard, full, rows, cols, order)))
            start += 1.0
    ticks, ends = plan_ticks(ops, pieces, 3.0)
    ready = [max(ends[k] for k in range(4 + 3 * s)) for s in range(steps)]
    blocks = tokens // QUERY_BLOCK
    units = 2 * blocks
    table = {(s, "head"): [] for s in range(steps)}
    moments = [(s, u) for s in range(steps) for u in range(units)]
    spread = spread_ticks(ready[0], len(ticks), moments, [u % blocks + 1 for _, u in moments])
    table.update(spread)
    table[0, "head"] = list(range(ready[0]))
    for s in range(1, steps):
        late = [(m, t) for m in moments if m[0] >= s for t in table[m] if t < ready[s]]
        for moment, t in late:
            table[moment].remove(t)
            table[s, "head"].append(t)
    hooks = Hooks(ticks, table)

    @pl.when(step == 0)
    def _():
        place.greet()

    hooks.run(step, "head")

    @pl.when(step == 0)
    def _():
        total = 1
        for n in digits:
            total *= n
        for ref in (par_ref, wide_ref):
            own = ref.shape[1] // total
            for lane in range(0, ref.shape[1], 128):
                block = None
                for d in range(lane // own, max((lane + 128) // own, lane // own + 1)):
                    i3, rest = d % digits[3], d // digits[3]
                    i2, rest = rest % digits[2], rest // digits[2]
                    i1, i0 = rest % digits[1], rest // digits[1]
                    value = small_ref[i0, i1, i2, i3].astype(f32)
                    block = value if block is None else block + value
                ref[:, lane : lane + 128] = block
        for first in range(0, tokens, QUERY_BLOCK):
            rows = slice(first, first + QUERY_BLOCK)
            normed, _ = norm_parts(x_ref[rows, :].astype(f32))
            a_ref[rows, :] = (normed * par_ref[0:1, :] + par_ref[3:4, :]).astype(bf16)

    keep = pltpu.make_async_copy(wqkv_ref, wqkv_out, local.at[local.shape[0] - 1])

    @pl.when(step == steps - 1)
    def _():
        keep.start()

    at = pl.multiple_of(step * HEADS_WIDE, HEADS_WIDE)
    for part, row in ((0, 4), (1, None), (2, 5)):
        cols = pl.ds(pl.multiple_of(part * width + at, HEADS_WIDE), HEADS_WIDE)
        value = dot_nn(a_ref[...], wqkv_ref[:, :, :, :, :, cols].reshape(width, HEADS_WIDE))
        if row is not None:
            value = value + par_ref[row : row + 1, pl.ds(at, HEADS_WIDE)]
        qkv_ref[part] = value.astype(bf16)
    unit = 0
    for pair in range(HEADS_WIDE // 128):
        lanes = slice(pair * 128, pair * 128 + 128)
        for first in range(0, tokens, QUERY_BLOCK):
            attend_unit(
                len_ref[0], scale_ref, (step * (HEADS_WIDE // 128) + pair) * 2, first, QUERY_BLOCK,
                qkv_ref.at[0, :, lanes], qkv_ref.at[1, :, lanes], qkv_ref.at[2, :, lanes],
                z_ref.at[:, lanes], log_ref.at[pair],
            )
            hooks.run(step, unit)
            unit += 1

    @pl.when(step == steps - 1)
    def _():
        keep.wait()


def front(digits, lengths, head_scale, x, qkv_shard, out_shard, fc1_shard, fc2_shard, small):
    tokens, width = x.shape
    hidden = fc1_shard.shape[1]
    steps = width // HEADS_WIDE
    bf16, f32 = jnp.bfloat16, jnp.float32
    sds = jax.ShapeDtypeStruct
    anywhere = pl.BlockSpec(memory_space=pl.ANY)
    smem = pl.BlockSpec(memory_space=pltpu.SMEM)
    fixed = lambda shape: pl.BlockSpec(shape, lambda s: (0,) * len(shape), pipeline_mode=pl.Buffered(1))
    shards = (out_shard, fc1_shard, fc2_shard)
    per_step = HEADS_WIDE // 128
    return pl.pallas_call(
        functools.partial(front_kernel, digits, {"steps": steps}),
        grid=(steps,),
        in_specs=[smem, smem, fixed(x.shape)] + [anywhere] * 5,
        out_specs=[
            fixed((tokens, width)),
            pl.BlockSpec((3, tokens, HEADS_WIDE), lambda s: (0, 0, s)),
            pl.BlockSpec((tokens, HEADS_WIDE), lambda s: (0, s)),
            pl.BlockSpec((per_step, 2, tokens), lambda s: (s, 0, 0)),
            anywhere,
            anywhere,
            anywhere,
            anywhere,
            fixed((16, width)),
            fixed((16, hidden)),
        ],
        out_shape=[
            sds((tokens, width), bf16),
            sds((3, tokens, width), bf16),
            sds((tokens, width), bf16),
            sds((width // 128, 2, tokens), f32),
            sds(digits + qkv_shard.shape, bf16),
        ]
        + [sds(digits + s.shape, bf16) for s in shards]
        + [sds((16, width), f32), sds((16, hidden), f32)],
        scratch_shapes=[pltpu.VMEM(digits + qkv_shard.shape, bf16), pltpu.VMEM(digits + small.shape, bf16)]
         + semaphores(480, 64),
        compiler_params=pltpu.CompilerParams(
            collective_id=2, has_side_effects=True, vmem_limit_bytes=60 << 20
        ),
        name="front",
    )(lengths, head_scale, x, qkv_shard, *shards, small)


def back_kernel(
    digits, stages,
    len_ref, q_ref, k_ref, v_ref, do_ref, log_ref, g1_ref, g2_ref, gout_ref,
    dqkv_ref, dot_ref, s1_ref, s2_ref, sout_ref,
    dk_ref, dv_ref, *scratch,
):
    step, steps = pl.program_id(0), stages["steps"]
    place = FixedPlace(digits)
    send, recv, local = scratch[-3:]
    ops = Ops(send, recv, local, place)
    staging, rest = scratch[:4], list(scratch[4:-3])
    pieces = []
    for number, (which, rows, cols, order, many) in enumerate(stages["pieces"]):
        grad, out = ((g2_ref, s2_ref), (g1_ref, s1_ref), (gout_ref, sout_ref))[which]
        landed, slabs = rest[0], rest[1 : 1 + many]
        del rest[: 1 + many]
        all_slots = (slice(None),) * 3
        own = grad.at[all_slots + (place.at[3],) + rect(rows, cols)]
        sent = grad.at[all_slots + (place.digit(3, 1),) + rect(rows, cols)]

        def finish(value, out=out, rows=rows, cols=cols):
            out[rows[0] : rows[0] + rows[1], cols[0] : cols[0] + cols[1]] = value

        pieces.append(
            (float(number), reduce_steps_of(ops, own, sent, staging[number % 4], landed, slabs, finish, (0, cols[1]), order))
        )
    ticks, _ = plan_ticks(ops, pieces, 3.0)
    tokens = q_ref.shape[1]
    units = tokens // QUERY_BLOCK
    moments = [(s, u) for s in range(steps) for u in range(units)]
    table = {(0, "head"): [0, 1, 2, 3]}
    table.update(spread_ticks(4, len(ticks), moments, [u + 1 for _, u in moments]))
    hooks = Hooks(ticks, table)

    @pl.when(step == 0)
    def _():
        place.greet()

    hooks.run(step, "head")
    for unit in range(units):
        attend_back_unit(
            len_ref[0], unit * QUERY_BLOCK, QUERY_BLOCK, q_ref.at[0], k_ref.at[0], v_ref.at[0], do_ref, log_ref.at[0],
            dqkv_ref.at[0], dot_ref.at[0], dk_ref, dv_ref,
        )
        hooks.run(step, unit)
    dqkv_ref[1] = dk_ref[...].astype(jnp.bfloat16)
    dqkv_ref[2] = dv_ref[...].astype(jnp.bfloat16)


def back(digits, lengths, qkv, d_attended, logs, grad_fc1, grad_fc2, grad_out):
    _, tokens, width = qkv.shape
    pairs = width // 128
    bf16, f32 = jnp.bfloat16, jnp.float32
    sds = jax.ShapeDtypeStruct
    anywhere = pl.BlockSpec(memory_space=pl.ANY)
    cols = lambda part: pl.BlockSpec((1, tokens, 128), lambda p: (part, 0, p))
    per_pair = pl.BlockSpec((1, 2, tokens), lambda p: (p, 0, 0))
    fixed = lambda shape: pl.BlockSpec(shape, lambda s: (0,) * len(shape))
    grads = (grad_fc2, grad_fc1, grad_out)
    pieces, scratch, number = [], [], 0
    for which, grad in enumerate(grads):
        for rows, at in blocks_of(grad.shape[4:], 32, 512):
            order = REDUCE_ORDERS[number % 9]
            number += 1
            slabs = slab_shapes(digits, rows[1], (0, at[1])[1], order, bf16)
            pieces.append((which, rows, at, order, len(slabs)))
            scratch += [pltpu.VMEM(digits[:3] + (rows[1], at[1]), bf16)] + slabs
    stage = pltpu.VMEM(digits[:3] + (pieces[0][1][1], pieces[0][2][1]), bf16)
    outs = [g.shape[4:] for g in (grad_fc1, grad_fc2, grad_out)]
    return pl.pallas_call(
        functools.partial(back_kernel, digits, {"steps": pairs, "pieces": pieces}),
        grid=(pairs,),
        in_specs=[
            pl.BlockSpec(memory_space=pltpu.SMEM),
            cols(0),
            cols(1),
            cols(2),
            pl.BlockSpec((tokens, 128), lambda p: (0, p)),
            per_pair,
        ]
        + [anywhere] * 3,
        out_specs=[pl.BlockSpec((3, tokens, 128), lambda p: (0, 0, p)), per_pair] + [fixed(s) for s in outs],
        out_shape=[sds((3, tokens, width), bf16), sds((pairs, 2, tokens), f32)] + [sds(s, f32) for s in outs],
        scratch_shapes=[pltpu.VMEM((tokens, 128), f32)] * 2
        + [stage] * 4
        + scratch
        + semaphores(len(scratch), len(pieces)),
        compiler_params=pltpu.CompilerParams(
            collective_id=3, has_side_effects=True, vmem_limit_bytes=60 << 20
        ),
        name="back",
    )(lengths, qkv, qkv, qkv, d_attended, logs, grad_fc1, grad_fc2, grad_out)


def last_kernel(
    digits, stages,
    a_ref, d_ref, wq_ref, wk_ref, wv_ref, x_ref, dr_ref, par_ref, sums_ref, wide_ref, dot_ref,
    dx_ref, sqkv_ref, ssmall_ref,
    da_ref, made_ref, rows_ref, block_ref, *scratch,
):
    step, steps = pl.program_id(0), stages["steps"]
    f32, bf16 = jnp.float32, jnp.bfloat16
    place = FixedPlace(digits)
    send, recv, local = scratch[-3:]
    ops = Ops(send, recv, local, place)
    rest = list(scratch[:-3])
    tokens, width = x_ref.shape
    pieces = []
    all_slots = (slice(None),) * 3
    for start, cols, order, many in stages["pieces"]:
        landed, slabs = rest[0], rest[1 : 1 + many]
        del rest[: 1 + many]
        source, out = (block_ref, ssmall_ref) if cols is None else (made_ref, sqkv_ref)
        cols = (0, 128) if cols is None else cols
        view = (slice(None), pl.ds(*cols))
        own = source.at[all_slots + (place.at[3],) + view]
        sent = source.at[all_slots + (place.digit(3, 1),) + view]

        def finish(value, out=out, cols=cols):
            out[:, cols[0] : cols[0] + cols[1]] = value

        pieces.append((start, reduce_steps_of(ops, own, sent, None, landed, slabs, finish, (0, cols[1]), order)))
    blocks = tokens // QUERY_BLOCK
    ticks, keys = plan_keyed(ops, pieces, 2.0)
    moments = [(s, name) for s in range(steps) for name in ("made", "used")]
    moments += [(steps - 1, b) for b in range(blocks)]
    table = {(steps - 1, "end"): []}
    table.update({moment: [] for moment in moments})
    for t, key in enumerate(keys):
        moment = moments[int(key)] if key < len(moments) else (steps - 1, "end")
        table[moment].append(t)
    hooks = Hooks(ticks, table)

    @pl.when(step == 0)
    def _():
        place.greet()
        da_ref[...] = jnp.zeros_like(da_ref)
        rows_ref[...] = jnp.zeros_like(rows_ref)

    at = pl.multiple_of(step * HEADS_WIDE, HEADS_WIDE)
    for part in range(3):
        made = dot_tn(a_ref[...], d_ref[part]).astype(bf16)
        cols = pl.ds(pl.multiple_of(part * width + at, HEADS_WIDE), HEADS_WIDE)
        made_ref[:, :, :, :, :, cols] = made.reshape(made_ref.shape[:5] + (HEADS_WIDE,))
    hooks.run(step, "made")
    for part, row in ((0, 4), (2, 5)):
        rows_ref[row : row + 1, pl.ds(at, HEADS_WIDE)] = jnp.sum(d_ref[part].astype(f32), axis=0, keepdims=True)
    for first in range(0, tokens, QUERY_BLOCK):
        rows = slice(first, first + QUERY_BLOCK)
        total = da_ref[rows, :]
        for part, w_ref in enumerate((wq_ref, wk_ref, wv_ref)):
            total = total + dot_nt(d_ref[part, rows, :], w_ref[...])
        da_ref[rows, :] = total
    hooks.run(step, "used")
    end = step == steps - 1
    for b in range(blocks):

        @pl.when(end)
        def _(b=b):
            rows = slice(b * QUERY_BLOCK, (b + 1) * QUERY_BLOCK)
            normed, inverse = norm_parts(x_ref[rows, :].astype(f32))
            d_a = da_ref[rows, :]
            rows_ref[0:1, :] += jnp.sum(d_a * normed, axis=0, keepdims=True)
            rows_ref[3:4, :] += jnp.sum(d_a, axis=0, keepdims=True)
            dx_ref[rows, :] = (dr_ref[rows, :] + norm_back(d_a, par_ref[0:1, :], normed, inverse)).astype(bf16)

        hooks.run(step, b)

    @pl.when(end)
    def _():
        for row, k in ((1, 1), (2, 2), (6, 3), (7, 4), (8, 5), (9, 6)):
            rows_ref[row : row + 1, :] = jnp.sum(sums_ref[k], axis=0, keepdims=True)
        wide = [jnp.sum(wide_ref[k], axis=0, keepdims=True) for k in range(3)]
        dots = [sum(dot_ref[p, :, lane : lane + 128] for lane in range(0, tokens, 128)) for p in range(dot_ref.shape[0])]
        total = digits[0] * digits[1] * digits[2] * digits[3]
        own, own_wide = width // total, wide_ref.shape[2] // total
        for d in range(total):
            i3, left = d % digits[3], d // digits[3]
            i2, left = left % digits[2], left // digits[2]
            i1, i0 = left % digits[1], left // digits[1]
            lane, lane_wide = d * own // 128 * 128, d * own_wide // 128 * 128
            block_ref[i0, i1, i2, i3, 0:16, :] = rows_ref[:, lane : lane + 128]
            for k in range(3):
                block_ref[i0, i1, i2, i3, 10 + k : 11 + k, :] = wide[k][:, lane_wide : lane_wide + 128]
            for p, value in enumerate(dots):
                block_ref[i0, i1, i2, i3, 16 + 2 * p : 18 + 2 * p, :] = value

    hooks.run(step, "end")


def last(digits, a, d_qkv, w_qkv, x, d_r, par, sums, wide, dots):
    tokens, width = x.shape
    steps = width // HEADS_WIDE
    bf16, f32 = jnp.bfloat16, jnp.float32
    sds = jax.ShapeDtypeStruct
    fixed = lambda shape: pl.BlockSpec(shape, lambda s: (0,) * len(shape), pipeline_mode=pl.Buffered(1))
    rows = width // (digits[0] * digits[1] * digits[2] * digits[3])
    small_rows = 16 + 2 * dots.shape[0]
    small_at = 2.0 * steps + tokens // QUERY_BLOCK
    pieces, scratch, number = [], [], 0
    for s in range(steps):
        for part in range(3):
            cols = (part * width + s * HEADS_WIDE, HEADS_WIDE)
            order = REDUCE_ORDERS[number % 9]
            number += 1
            slabs = slab_shapes(digits, rows, cols[1], order, bf16)
            pieces.append((2.0 * s, cols, order, len(slabs)))
            scratch += [pltpu.VMEM(digits[:3] + (rows, cols[1]), bf16)] + slabs
    slabs = slab_shapes(digits, small_rows, 128, REDUCE_ORDERS[0], f32)
    pieces.append((small_at, None, REDUCE_ORDERS[0], len(slabs)))
    scratch += [pltpu.VMEM(digits[:3] + (small_rows, 128), f32)] + slabs
    weight = lambda part: pl.BlockSpec((width, HEADS_WIDE), lambda s: (0, part * steps + s))
    return pl.pallas_call(
        functools.partial(last_kernel, digits, {"steps": steps, "pieces": pieces, "small_at": small_at}),
        grid=(steps,),
        in_specs=[fixed(a.shape), pl.BlockSpec((3, tokens, HEADS_WIDE), lambda s: (0, 0, s))]
        + [weight(part) for part in range(3)]
        + [fixed(v.shape) for v in (x, d_r, par, sums, wide, dots)],
        out_specs=[fixed((tokens, width)), fixed((rows, 3 * width)), fixed((small_rows, 128))],
        out_shape=[sds((tokens, width), bf16), sds((rows, 3 * width), f32), sds((small_rows, 128), f32)],
        scratch_shapes=[
            pltpu.VMEM((tokens, width), f32),
            pltpu.VMEM(digits + (rows, 3 * width), bf16),
            pltpu.VMEM((16, width), f32),
            pltpu.VMEM(digits + (small_rows, 128), f32),
        ]
        + scratch
        + semaphores(len(scratch), 1),
        compiler_params=pltpu.CompilerParams(
            collective_id=4, has_side_effects=True, vmem_limit_bytes=60 << 20
        ),
        name="last",
    )(a, d_qkv, w_qkv, w_qkv, w_qkv, x, d_r, par, sums, wide, dots)


def plain_gather(digits, weights, small_parts):
    small = jnp.concatenate([to_bf16(v).reshape(-1) for v in small_parts])
    small = jnp.pad(small, (0, 2048 - small.shape[0])).reshape(16, 128)
    shards_in = [to_bf16(w).reshape(tiled_rows(*w.shape)) for w in weights] + [small]
    gathered = gather_all(digits, shards_in)
    fulls = [g.reshape((-1, w.shape[1])) for g, w in zip(gathered, weights)]
    smalls, parts, used = gathered[4].reshape(-1, 2048), [], 0
    for v in small_parts:
        block = smalls[:, used : used + v.size].reshape((-1,) + (v.shape if v.ndim == 2 else (1,) + v.shape))
        parts.append(block.transpose(1, 0, 2).reshape(block.shape[1], -1).astype(jnp.float32))
        used += v.size
    par = jnp.pad(jnp.concatenate(parts[:2]), ((0, 6), (0, 0)))
    table = jnp.pad(jnp.concatenate(parts[2:]), ((10, 3), (0, 0)))
    return fulls, par, table


def plain_reduce(digits, weights, grads, small_parts, small_grads):
    total = digits[0] * digits[1] * digits[2] * digits[3]
    block = [v.reshape(v.shape[0], total, -1).transpose(1, 0, 2).reshape(total, -1) for v in small_grads[:-1]]
    block.append(jnp.broadcast_to(small_grads[-1][None], (total, small_grads[-1].shape[0])))
    block = jnp.concatenate(block, axis=1)
    block = jnp.pad(block, ((0, 0), (0, 1024 - block.shape[1]))).reshape(digits + (8, 128))
    blocks = [to_bf16(g).reshape(digits + tiled_rows(*w.shape)) for g, w in zip(grads, weights)]
    summed = reduce_all(digits, blocks + [block])
    flat, used, owned = summed[4].reshape(-1), 0, []
    for v in small_parts:
        owned.append(flat[used : used + v.size].reshape(v.shape))
        used += v.size
    return [g.reshape(w.shape) for g, w in zip(summed[:4], weights)] + owned


def packed_small(digits, norm_gain, norm_bias, mid_gain, ff_bias):
    total = digits[0] * digits[1] * digits[2] * digits[3]
    me = lax.axis_index("dp") * (digits[2] * digits[3]) + lax.axis_index("fsdp")
    narrow = to_bf16(jnp.concatenate((norm_gain, norm_bias)))
    wide = to_bf16(jnp.concatenate((mid_gain[None], ff_bias)))

    def placed(v):
        repeated = jnp.tile(v, (1, 128 // v.shape[1]))
        lane = jnp.arange(128, dtype=jnp.int32) // v.shape[1]
        return jnp.where(lane == me % (128 // v.shape[1]), repeated, jnp.zeros_like(repeated))

    return jnp.pad(jnp.concatenate((placed(narrow), placed(wide))), ((0, 3), (0, 0)))


def shards(
    digits, tokens, lengths, cotangent, w_qkv, w_out, w_fc1, w_fc2, norm_gain, norm_bias, mid_gain, ff_bias, head_scale
):
    weights = (w_qkv, w_out, w_fc1, w_fc2)
    small_parts = (norm_gain, norm_bias, mid_gain, ff_bias)
    heads = head_scale.shape[0]
    total = digits[0] * digits[1] * digits[2] * digits[3]
    scale_row = jnp.repeat(head_scale, tokens.shape[1] // heads)[None]
    tiled = w_qkv.shape[0] % 16 == 0
    if tiled:
        small = packed_small(digits, *small_parts)
        normed_in, qkv, mixed, logs, full_qkv, full_out, full_fc1, full_fc2, par, table = front(
            digits, lengths, head_scale, tokens, *[to_bf16(w) for w in weights], small
        )
        full_qkv, full_out, full_fc1, full_fc2 = (
            g.reshape((-1, g.shape[-1])) for g in (full_qkv, full_out, full_fc1, full_fc2)
        )
    else:
        (full_qkv, full_out, full_fc1, full_fc2), par, table = plain_gather(digits, weights, small_parts)
        normed_in, qkv = project(tokens, full_qkv, par[0:3], par[3:10])
        mixed, logs = attend(lengths, head_scale, qkv)
    result, normed_ff, normed_mid, grad_pre, grad_projection, grad_residual, grad_attended, sums, wide = ffn(
        lengths, scale_row, tokens, mixed, cotangent, full_out, full_fc1, full_fc2, par, table
    )
    positions = jnp.arange(tokens.shape[0], dtype=jnp.int32)[:, None]
    grad_branch = jnp.where(positions < lengths, cotangent, jnp.zeros_like(cotangent))
    grad_fc2 = to_bf16(dot_tn(normed_mid, grad_branch))
    grad_fc1 = to_bf16(dot_tn(normed_ff, grad_pre))
    grad_out_w = to_bf16(dot_tn(mixed, grad_projection))
    if tiled:
        grads = [g.reshape(digits + w.shape) for g, w in ((grad_fc1, w_fc1), (grad_fc2, w_fc2), (grad_out_w, w_out))]
        d_qkv, dots, sum_fc1, sum_fc2, sum_out = back(digits, lengths, qkv, grad_attended, logs, *grads)
        grad_tokens, sum_qkv, sum_small = last(
            digits, normed_in, d_qkv, full_qkv, tokens, grad_residual, par, sums, wide, dots
        )
        me = lax.axis_index("dp") * (digits[2] * digits[3]) + lax.axis_index("fsdp")
        own, own_wide = norm_gain.shape[1], mid_gain.shape[0]
        narrow = lax.dynamic_slice(sum_small, (0, me * own % 128), (10, own))
        broad = lax.dynamic_slice(sum_small, (10, me * own_wide % 128), (3, own_wide))
        scales = sum_small[16:].sum(1) / head_scale
        summed = (sum_qkv, sum_out, sum_fc1, sum_fc2, narrow[:3], narrow[3:], broad[0], broad[1:], scales)
    else:
        d_qkv, dots = attend_back(lengths, qkv, grad_attended, logs)
        grad_tokens, first_sums = project_back(d_qkv, tokens, grad_residual, full_qkv, par[0:3])
        grad_qkv = jnp.concatenate([dot_tn(normed_in, d_qkv[k]) for k in range(3)], axis=1)
        sums, wide, first_sums = sums.sum(1), wide.sum(1), first_sums.sum(1)
        small_grads = (
            jnp.concatenate((first_sums[0:1], sums[1:3])),
            jnp.concatenate((first_sums[1:4], sums[3:7])),
            wide[0:1],
            wide[1:3],
            dots.sum(-1).reshape(heads) / head_scale,
        )
        summed = plain_reduce(
            digits, weights, (grad_qkv, grad_out_w, grad_fc1, grad_fc2), small_parts + (head_scale,), small_grads
        )
    return (result, grad_tokens) + tuple(summed)


def solution(mesh):
    placed = (
        P(("dp", "fsdp"), None),
        P(("dp", "fsdp")),
        P(("dp", "fsdp"), None),
        P(("dp", "fsdp"), None),
        P(("dp", "fsdp"), None),
        P(("dp", "fsdp"), None),
        P(("dp", "fsdp"), None),
        P(None, ("dp", "fsdp")),
        P(None, ("dp", "fsdp")),
        P(("dp", "fsdp")),
        P(None, ("dp", "fsdp")),
        P(),
    )
    return jax.shard_map(
        functools.partial(shards, digits_of(mesh)),
        mesh=mesh,
        in_specs=placed,
        out_specs=(
            P(("dp", "fsdp"), None),
            P(("dp", "fsdp"), None),
            P(("dp", "fsdp"), None),
            P(("dp", "fsdp"), None),
            P(("dp", "fsdp"), None),
            P(("dp", "fsdp"), None),
            P(None, ("dp", "fsdp")),
            P(None, ("dp", "fsdp")),
            P(("dp", "fsdp")),
            P(None, ("dp", "fsdp")),
            P(),
        ),
        check_vma=False,
    )
```

```python
import functools
import heapq

import jax
import jax.numpy as jnp
from jax import lax
from jax.experimental import pallas as pl
from jax.experimental.pallas import tpu as pltpu
from jax.sharding import PartitionSpec as P

epsilon = 1e-05
mask_fill = -1e30
MESH = pl.DeviceIdType.MESH
ORDERS = ((1, 2, 0), (2, 1, 0), (0, 1, 2), (0, 2, 1))


def digits_of(mesh):
    dp, fsdp = mesh.shape["dp"], mesh.shape["fsdp"]
    minor = 2 if dp <= 8 else 8
    return (dp // minor, minor, fsdp // 2, 2)


class Place:
    def __init__(self, digits):
        self.digits = digits
        dp, fs = lax.axis_index("dp"), lax.axis_index("fsdp")
        self.at = (dp // digits[1], dp % digits[1], fs // digits[3], fs % digits[3])

    def digit(self, axis, shift):
        n = self.digits[axis]
        return (self.at[axis] + shift + n) % n

    def peer(self, axis, shift):
        at = list(self.at)
        at[axis] = self.digit(axis, shift)
        return (at[0] * self.digits[1] + at[1], at[2] * self.digits[3] + at[3])

    def greet(self):
        barrier = pltpu.get_barrier_semaphore()
        peers = []
        for axis, n in enumerate(self.digits):
            if n > 1:
                peers.append(self.peer(axis, 1))
            if n > 2:
                peers.append(self.peer(axis, -1))
        for peer in peers:
            pl.semaphore_signal(barrier, inc=1, device_id=peer, device_id_type=MESH)
        pl.semaphore_wait(barrier, len(peers))


class Sems:
    def __init__(self, send, recv, local):
        self.send, self.recv, self.local = send, recv, local
        self.remotes = self.locals = 0

    def remote(self, src, dst, peer):
        copy = pltpu.make_async_remote_copy(
            src_ref=src,
            dst_ref=dst,
            send_sem=self.send.at[self.remotes],
            recv_sem=self.recv.at[self.remotes],
            device_id=peer,
            device_id_type=MESH,
        )
        self.remotes += 1
        copy.start()
        return copy

    def copy(self, src, dst):
        copy = pltpu.make_async_copy(src, dst, self.local.at[self.locals])
        self.locals += 1
        copy.start()
        return copy


def hops(n):
    if n == 1:
        return []
    if n == 2:
        return [(0, (1,), False)]
    return [(s, (1, -1), s == n // 2 - 1) for s in range(n // 2)]


def column_part(start, size, direction, halved):
    if not halved:
        return start, size
    first = size // 256 * 128
    if first == 0:
        return (start, size) if direction > 0 else (start, 0)
    return (start, first) if direction > 0 else (start + first, size - first)


def slots(place, view, axis, slot, part):
    index = []
    for other, n in enumerate(place.digits):
        if other == axis:
            index.append(slot)
        elif other in view:
            index.append(pl.ds(0, n))
        else:
            index.append(place.at[other])
    return tuple(index) + (slice(None), pl.ds(*part))


def gather_piece(place, sems, shard, full, start, size, order):
    held, sends, cores = set(), [], []
    own = sems.copy(
        shard.at[:, pl.ds(start, size)], full.at[slots(place, (), None, None, (start, size))]
    )
    core = place.peer(3, 1)

    def forward(axis, slot, part):
        view = full.at[slots(place, held, axis, slot, part)]
        cores.append(sems.remote(view, view, core))

    first = True
    for axis in order:
        n = place.digits[axis]
        for step, directions, last in hops(n):
            started = []
            for direction in directions:
                part = column_part(start, size, direction, last)
                if part[1] == 0:
                    continue
                index = slots(place, held, axis, place.digit(axis, -step * direction), part)
                src = shard.at[:, pl.ds(*part)] if first and step == 0 else full.at[index]
                started.append(
                    (direction, sems.remote(src, full.at[index], place.peer(axis, direction)))
                )
            yield
            for direction, copy in started:
                copy.wait_recv()
                sends.append(copy)
                if not first and not last and n > 2:
                    forward(axis, place.digit(axis, -(step + 1) * direction), (start, size))
            if not first and (last or n == 2):
                forward(axis, place.digit(axis, n // 2), (start, size))
        if n > 1:
            held.add(axis)
            if first:
                own.wait()
                forward(None, None, (start, size))
                first = False
    if first:
        own.wait()
        forward(None, None, (start, size))
    yield
    for copy in cores:
        copy.wait()
    for copy in sends:
        copy.wait_send()


def accumulate(target, source, result=None):
    lead, dims = target.shape[:-2], target.shape
    count = 1
    for n in lead:
        count *= n

    def index_of(flat):
        index = []
        for n in reversed(lead):
            index.append(flat % n)
            flat = flat // n
        return tuple(reversed(index)) + (slice(None), slice(None))

    def body(flat, carry):
        index = index_of(flat)
        total = target[index].astype(jnp.float32) + source[index].astype(jnp.float32)
        target[index] = total.astype(target.dtype)
        return carry

    if lead:
        lax.fori_loop(0, count, body, 0)
    else:
        body(0, 0)


def reduce_steps(digits, start, size, order):
    left, plan = [0, 1, 2], []
    for axis in order:
        n = digits[axis]
        left.remove(axis)
        lead = tuple(digits[a] for a in left)
        for step, directions, last in reversed(hops(n)):
            batch = []
            for direction in directions:
                part = column_part(start, size, direction, last)
                if part[1] > 0:
                    batch.append((axis, direction, step, part, lead))
            plan.append((tuple(left), batch))
    return plan


def reduce_piece(place, sems, grad, acc, landed, slabs, out, start, size, order):
    sends = []
    lead = (slice(None),) * 3
    whole = (slice(None), pl.ds(start, size))
    mine = acc.at[lead + whole]
    other = landed.at[lead + whole]
    own = sems.copy(grad.at[lead + (place.at[3],) + whole], mine)
    sent = sems.remote(grad.at[lead + (place.digit(3, 1),) + whole], other, place.peer(3, 1))
    yield
    own.wait()
    sent.wait_recv()
    sends.append(sent)
    accumulate(mine, other)
    slabs = iter(slabs)
    for left, batch in reduce_steps(place.digits, start, size, order):
        started = []
        for axis, direction, step, part, _ in batch:
            slot = place.digit(axis, (step + 1) * direction)
            src = acc.at[slots(place, left, axis, slot, part)[:3] + (slice(None), pl.ds(*part))]
            dst = next(slabs)
            sent = sems.remote(src, dst, place.peer(axis, direction))
            started.append((axis, direction * step, part, dst, sent))
        yield
        for axis, shift, part, dst, sent in started:
            sent.wait_recv()
            sends.append(sent)
            slot = place.digit(axis, shift)
            view = slots(place, left, axis, slot, part)[:3] + (slice(None), pl.ds(*part))
            accumulate(acc.at[view], dst)
    out[:, pl.ds(start, size)] = acc[place.at[:3] + whole].astype(jnp.float32)
    for sent in sends:
        sent.wait_send()
    yield


def pieces_of(cols, wanted=4):
    tiles = cols // 128
    count = wanted
    while tiles % count:
        count -= 1
    size = tiles // count * 128
    return [(k * size, size) for k in range(count)]


def run_all(generators):
    live = list(generators)
    while live:
        still = []
        for generator in live:
            try:
                next(generator)
                still.append(generator)
            except StopIteration:
                pass
        live = still


def gather_kernel(digits, count, *refs):
    shards, fulls = refs[:count], refs[count : 2 * count]
    send, recv, local = refs[2 * count :]
    place = Place(digits)
    sems = Sems(send, recv, local)
    place.greet()
    run_all(
        gather_piece(place, sems, shard, full, start, size, ORDERS[k % 4])
        for shard, full in zip(shards, fulls)
        for k, (start, size) in enumerate(pieces_of(shard.shape[1]))
    )


def gather_all(digits, shards):
    count = len(shards)
    copies = 16 * 4 * count * max(1, max(digits) // 4)
    whole = [jax.ShapeDtypeStruct(digits + s.shape, s.dtype) for s in shards]
    return pl.pallas_call(
        functools.partial(gather_kernel, digits, count),
        out_shape=whole,
        in_specs=[pl.BlockSpec(memory_space=pl.ANY)] * count,
        out_specs=[pl.BlockSpec(memory_space=pl.ANY)] * count,
        scratch_shapes=[
            pltpu.SemaphoreType.DMA((copies,)),
            pltpu.SemaphoreType.DMA((copies,)),
            pltpu.SemaphoreType.DMA((4 * count,)),
        ],
        compiler_params=pltpu.CompilerParams(collective_id=0, has_side_effects=True),
        name="gather_all",
    )(*shards)


def reduce_plan(digits, grads):
    plan = []
    for g, grad in enumerate(grads):
        for k, (start, size) in enumerate(pieces_of(grad.shape[-1])):
            plan.append((g, start, size, ORDERS[k % 4]))
    return plan


def reduce_kernel(digits, plan, slab_counts, count, *refs):
    grads, outs = refs[:count], refs[count : 2 * count]
    accs, landed = refs[2 * count : 3 * count], refs[3 * count : 4 * count]
    slabs = refs[4 * count : -3]
    send, recv, local = refs[-3:]
    place = Place(digits)
    sems = Sems(send, recv, local)
    place.greet()
    generators, used = [], 0
    for (g, start, size, order), many in zip(plan, slab_counts):
        own = slabs[used : used + many]
        used += many
        generators.append(
            reduce_piece(place, sems, grads[g], accs[g], landed[g], own, outs[g], start, size, order)
        )
    run_all(generators)


def reduce_all(digits, grads):
    count = len(grads)
    plan = reduce_plan(digits, grads)
    slabs, slab_counts = [], []
    for g, start, size, order in plan:
        shapes = [
            pltpu.VMEM(lead + (grads[g].shape[-2], part[1]), grads[g].dtype)
            for _, batch in reduce_steps(digits, start, size, order)
            for _, _, _, part, lead in batch
        ]
        slabs += shapes
        slab_counts.append(len(shapes))
    blocks = [pltpu.VMEM(digits[:3] + g.shape[-2:], g.dtype) for g in grads]
    copies = len(slabs) + len(plan)
    return pl.pallas_call(
        functools.partial(reduce_kernel, digits, plan, slab_counts, count),
        out_shape=[jax.ShapeDtypeStruct(g.shape[-2:], jnp.float32) for g in grads],
        in_specs=[pl.BlockSpec(memory_space=pl.ANY)] * count,
        out_specs=[pl.BlockSpec(memory_space=pltpu.VMEM)] * count,
        scratch_shapes=blocks
        + blocks
        + slabs
        + [
            pltpu.SemaphoreType.DMA((copies,)),
            pltpu.SemaphoreType.DMA((copies,)),
            pltpu.SemaphoreType.DMA((len(plan),)),
        ],
        compiler_params=pltpu.CompilerParams(
            collective_id=1, has_side_effects=True, vmem_limit_bytes=58 << 20
        ),
        name="reduce_all",
    )(*grads)


def tiled_rows(rows, cols):
    return (rows, cols) if rows % 16 == 0 else (16, rows * cols // 16)


def to_bf16(values):
    return values.astype(jnp.bfloat16)


def dot_nn(a, b):
    return lax.dot_general(a, b, (((1,), (0,)), ((), ())), preferred_element_type=jnp.float32)


def dot_nt(a, b):
    return lax.dot_general(a, b, (((1,), (1,)), ((), ())), preferred_element_type=jnp.float32)


def dot_tn(a, b):
    return lax.dot_general(a, b, (((0,), (0,)), ((), ())), preferred_element_type=jnp.float32)


def row_mean(v):
    return jnp.mean(v, axis=-1, keepdims=True)


def norm_parts(v):
    centered = v - row_mean(v)
    inverse = lax.rsqrt(row_mean(centered * centered) + epsilon)
    return centered * inverse, inverse


def norm_back(grad, gain, normed, inverse):
    scaled = grad * gain
    return (scaled - row_mean(scaled) - normed * row_mean(scaled * normed)) * inverse


def fold(v):
    return v.reshape(v.shape[0] // 8, 8, v.shape[1]).sum(0)


def ffn_kernel(
    chunk, unrolled,
    len_ref, x_ref, z_ref, cot_ref, wo_ref, w1_ref, w2_ref, par_ref, table_ref,
    out_ref, c_ref, m_ref, df_ref, dy_ref, dr_ref, do_ref, sums_ref, wide_ref,
    act_ref, slope_ref, dm_ref,
):
    step = pl.program_id(0)
    rows, width = x_ref.shape
    hidden = w1_ref.shape[1]
    f32, bf16 = jnp.float32, jnp.bfloat16

    @pl.when(step == 0)
    def _():
        sums_ref[...] = jnp.zeros_like(sums_ref)
        wide_ref[...] = jnp.zeros_like(wide_ref)

    def each(body, carry):
        if unrolled:
            for j in range(hidden // chunk):
                carry = body(slice(j * chunk, (j + 1) * chunk), carry)
            return carry
        return lax.fori_loop(
            0, hidden // chunk, lambda j, c: body(pl.ds(pl.multiple_of(j * chunk, chunk), chunk), c), carry
        )

    gain = lambda k: par_ref[k : k + 1, :]
    bias = lambda k: par_ref[3 + k : 4 + k, :]
    y_norm, y_inv = norm_parts(dot_nn(z_ref[...], wo_ref[...]) + bias(3))
    residual = x_ref[...].astype(f32) + (y_norm * gain(1) + bias(4))
    r_norm, r_inv = norm_parts(residual)
    normed = (r_norm * gain(2) + bias(5)).astype(bf16)
    c_ref[...] = normed

    def expand(at, total):
        pre = dot_nn(normed, w1_ref[:, at]) + table_ref[11:12, at]
        cdf = 0.5 * (1.0 + lax.erf(pre * (0.5**0.5)))
        pdf = jnp.exp(pre * pre * -0.5) * 0.3989422804014327
        act = pre * cdf
        act_ref[:, at] = act
        slope_ref[:, at] = cdf + pre * pdf
        return total + jnp.sum(act, axis=-1, keepdims=True)

    zero = jnp.zeros((rows, 1), f32)
    average = each(expand, zero) / hidden

    def spread(at, total):
        centered = act_ref[:, at] - average
        return total + jnp.sum(centered * centered, axis=-1, keepdims=True)

    m_inv = lax.rsqrt(each(spread, zero) / hidden + epsilon)

    def contract(at, total):
        n = (act_ref[:, at] - average) * m_inv
        act_ref[:, at] = n
        m = (n * table_ref[10:11, at] + table_ref[12:13, at]).astype(bf16)
        m_ref[:, at] = m
        return total + dot_nn(m, w2_ref[at, :])

    branch = each(contract, jnp.zeros((rows, width), f32))
    out_ref[...] = (residual + (branch + bias(6))).astype(bf16)

    position = step * rows + lax.broadcasted_iota(jnp.int32, (rows, 1), 0)
    d_out = jnp.where(position < len_ref[0], cot_ref[...].astype(f32), 0.0)
    d_w = d_out.astype(bf16)
    sums_ref[6] += fold(d_out)

    def back_mid(at, totals):
        dm = dot_nt(d_w, w2_ref[at, :])
        n = act_ref[:, at]
        dn = dm * n
        wide_ref[0, :, at] += fold(dn)
        wide_ref[2, :, at] += fold(dm)
        g = table_ref[10:11, at]
        dm_ref[:, at] = dm
        return (
            totals[0] + jnp.sum(dm * g, axis=-1, keepdims=True),
            totals[1] + jnp.sum(dn * g, axis=-1, keepdims=True),
        )

    first, second = each(back_mid, (zero, zero))
    first, second = first / hidden, second / hidden

    def back_act(at, total):
        du = (dm_ref[:, at] * table_ref[10:11, at] - first - act_ref[:, at] * second) * m_inv
        df = (du * slope_ref[:, at]).astype(bf16)
        df_ref[:, at] = df
        wide_ref[1, :, at] += fold(df.astype(f32))
        return total + dot_nt(df, w1_ref[:, at])

    d_c = each(back_act, jnp.zeros((rows, width), f32))
    sums_ref[2] += fold(d_c * r_norm)
    sums_ref[5] += fold(d_c)
    d_r = d_out + norm_back(d_c, gain(2), r_norm, r_inv)
    dr_ref[...] = d_r
    sums_ref[1] += fold(d_r * y_norm)
    sums_ref[4] += fold(d_r)
    d_y = norm_back(d_r, gain(1), y_norm, y_inv).astype(bf16)
    dy_ref[...] = d_y
    sums_ref[3] += fold(d_y.astype(f32))
    do_ref[...] = (dot_nt(d_y, wo_ref[...]) * par_ref[SCALE_ROW : SCALE_ROW + 1, :]).astype(bf16)


def ffn(lengths, x, z, cot, wo, w1, w2, par, table, rows=256, chunk=512, unrolled=True):
    tokens, width = x.shape
    hidden = w1.shape[1]
    by_row = lambda n: pl.BlockSpec((rows, n), lambda i: (i, 0))
    whole = lambda a: pl.BlockSpec(a.shape, lambda i: (0,) * a.ndim, pipeline_mode=pl.Buffered(1))
    sds = jax.ShapeDtypeStruct
    bf16, f32 = jnp.bfloat16, jnp.float32
    outs = [(width, bf16), (width, bf16), (hidden, bf16), (hidden, bf16), (width, bf16), (width, f32), (width, bf16)]
    return pl.pallas_call(
        functools.partial(ffn_kernel, chunk, unrolled),
        grid=(tokens // rows,),
        in_specs=[pl.BlockSpec(memory_space=pltpu.SMEM)]
        + [by_row(width)] * 3
        + [whole(a) for a in (wo, w1, w2, par, table)],
        out_specs=[by_row(n) for n, _ in outs]
        + [pl.BlockSpec((7, 8, width), lambda i: (0, 0, 0)), pl.BlockSpec((3, 8, hidden), lambda i: (0, 0, 0))],
        out_shape=[sds((tokens, n), d) for n, d in outs] + [sds((7, 8, width), f32), sds((3, 8, hidden), f32)],
        scratch_shapes=[pltpu.VMEM((rows, hidden), f32)] * 3,
        compiler_params=pltpu.CompilerParams(vmem_limit_bytes=60 << 20),
        name="ffn_both",
    )(lengths, x, z, cot, wo, w1, w2, par, table)


head_size = 64


def head_lanes(values, second):
    lane = lax.broadcasted_iota(jnp.int32, values.shape, 1)
    keep = lane >= head_size if second else lane < head_size
    return jnp.where(keep, values, jnp.zeros_like(values))


def masked_scores(keys, queries, first, length):
    scores = dot_nt(keys, queries)
    key_pos = lax.broadcasted_iota(jnp.int32, scores.shape, 0)
    near = key_pos[first:]
    query_pos = first + lax.broadcasted_iota(jnp.int32, near.shape, 1)
    last = jnp.where((near <= query_pos) & (near < length), scores[first:], mask_fill)
    if first == 0:
        return last
    return jnp.concatenate((jnp.where(key_pos[:first] < length, scores[:first], mask_fill), last), axis=0)


def attend_unit(length, scale_ref, head, first, block, q_ref, k_ref, v_ref, z_ref, log_ref):
    rows, seen = slice(first, first + block), first + block
    scaling = jnp.bfloat16(head_size**-0.5)
    keys, values = k_ref[:seen, :], v_ref[:seen, :]
    mixed = []
    for h in range(2):
        queries = head_lanes(q_ref[rows, :], h) * scaling
        scores = masked_scores(keys, queries, first, length)
        top = jnp.max(scores, axis=0, keepdims=True)
        shifted = jnp.exp(scores - top)
        total = jnp.sum(shifted, axis=0, keepdims=True)
        log_ref[h : h + 1, rows] = top + jnp.log(total)
        attended = dot_tn(shifted.astype(jnp.bfloat16), values)
        mixed.append(attended * (scale_ref[head + h] / total).T)
    lane = lax.broadcasted_iota(jnp.int32, mixed[0].shape, 1)
    z_ref[rows, :] = jnp.where(lane < head_size, mixed[0], mixed[1]).astype(jnp.bfloat16)


def attend_kernel(block, len_ref, scale_ref, q_ref, k_ref, v_ref, z_ref, log_ref):
    for first in range(0, q_ref.shape[1], block):
        attend_unit(
            len_ref[0], scale_ref, pl.program_id(0) * 2, first, block,
            q_ref.at[0], k_ref.at[0], v_ref.at[0], z_ref, log_ref.at[0],
        )


def attend(lengths, head_scale, qkv, block=256):
    _, tokens, width = qkv.shape
    pairs = width // 128
    cols = lambda part: pl.BlockSpec((1, tokens, 128), lambda p: (part, 0, p))
    smem = pl.BlockSpec(memory_space=pltpu.SMEM)
    return pl.pallas_call(
        functools.partial(attend_kernel, min(block, tokens)),
        grid=(pairs,),
        in_specs=[smem, smem, cols(0), cols(1), cols(2)],
        out_specs=[
            pl.BlockSpec((tokens, 128), lambda p: (0, p)),
            pl.BlockSpec((1, 2, tokens), lambda p: (p, 0, 0)),
        ],
        out_shape=[
            jax.ShapeDtypeStruct((tokens, width), jnp.bfloat16),
            jax.ShapeDtypeStruct((pairs, 2, tokens), jnp.float32),
        ],
        compiler_params=pltpu.CompilerParams(vmem_limit_bytes=56 << 20),
        name="attend",
    )(lengths, head_scale, qkv, qkv, qkv)


def attend_back_unit(
    length, first, block, q_ref, k_ref, v_ref, do_ref, log_ref, dq_ref, dot_ref, dk_ref, dv_ref
):
    rows, seen = slice(first, first + block), first + block
    bf16, scaling = jnp.bfloat16, head_size**-0.5
    keys, values = k_ref[:seen, :], v_ref[:seen, :]
    mixed = []
    for h in range(2):
        queries = head_lanes(q_ref[rows, :], h) * bf16(scaling)
        grads = head_lanes(do_ref[rows, :], h)
        scores = masked_scores(keys, queries, first, length)
        weights = jnp.exp(scores - log_ref[h : h + 1, rows])
        products = weights * dot_nt(values, grads)
        total = jnp.sum(products, axis=0, keepdims=True)
        dot_ref[h : h + 1, rows] = total
        d_scores = (products - weights * total).astype(bf16)
        for ref, left, right in ((dv_ref, weights.astype(bf16), grads), (dk_ref, d_scores, queries)):
            part = dot_nn(left, right)
            if h == 0:
                ref[rows, :] = part[first:]
                if first:
                    ref[:first, :] += part[:first]
            else:
                ref[:seen, :] += part
        mixed.append(dot_tn(d_scores, keys))
    lane = lax.broadcasted_iota(jnp.int32, mixed[0].shape, 1)
    dq_ref[rows, :] = (jnp.where(lane < head_size, mixed[0], mixed[1]) * scaling).astype(bf16)


def attend_back_kernel(block, len_ref, q_ref, k_ref, v_ref, do_ref, log_ref, dqkv_ref, dot_ref, dk_ref, dv_ref):
    for first in range(0, do_ref.shape[0], block):
        attend_back_unit(
            len_ref[0], first, block, q_ref.at[0], k_ref.at[0], v_ref.at[0], do_ref, log_ref.at[0],
            dqkv_ref.at[0], dot_ref.at[0], dk_ref, dv_ref,
        )
    dqkv_ref[1] = dk_ref[...].astype(jnp.bfloat16)
    dqkv_ref[2] = dv_ref[...].astype(jnp.bfloat16)


def attend_back(lengths, qkv, d_attended, logs, block=256):
    _, tokens, width = qkv.shape
    pairs = width // 128
    cols = lambda part: pl.BlockSpec((1, tokens, 128), lambda p: (part, 0, p))
    per_pair = pl.BlockSpec((1, 2, tokens), lambda p: (p, 0, 0))
    return pl.pallas_call(
        functools.partial(attend_back_kernel, min(block, tokens)),
        grid=(pairs,),
        in_specs=[
            pl.BlockSpec(memory_space=pltpu.SMEM),
            cols(0),
            cols(1),
            cols(2),
            pl.BlockSpec((tokens, 128), lambda p: (0, p)),
            per_pair,
        ],
        out_specs=[pl.BlockSpec((3, tokens, 128), lambda p: (0, 0, p)), per_pair],
        out_shape=[
            jax.ShapeDtypeStruct((3, tokens, width), jnp.bfloat16),
            jax.ShapeDtypeStruct((pairs, 2, tokens), jnp.float32),
        ],
        scratch_shapes=[pltpu.VMEM((tokens, 128), jnp.float32)] * 2,
        compiler_params=pltpu.CompilerParams(vmem_limit_bytes=56 << 20),
        name="attend_back",
    )(lengths, qkv, qkv, qkv, d_attended, logs)


def project_kernel(x_ref, w_ref, gain_ref, bias_ref, a_ref, qkv_ref):
    width = x_ref.shape[1]
    normed, _ = norm_parts(x_ref[...].astype(jnp.float32))
    a = (normed * gain_ref[0:1, :] + bias_ref[0:1, :]).astype(jnp.bfloat16)
    a_ref[...] = a
    for part, row in ((0, 1), (1, None), (2, 2)):
        at = slice(part * width, (part + 1) * width)
        value = dot_nn(a, w_ref[:, at])
        if row is not None:
            value = value + bias_ref[row : row + 1, :]
        qkv_ref[part] = value.astype(jnp.bfloat16)


def project(x, w, gains, biases, rows=256):
    tokens, width = x.shape
    by_row = lambda n: pl.BlockSpec((rows, n), lambda i: (i, 0))
    whole = lambda a: pl.BlockSpec(a.shape, lambda i: (0,) * a.ndim, pipeline_mode=pl.Buffered(1))
    return pl.pallas_call(
        project_kernel,
        grid=(tokens // rows,),
        in_specs=[by_row(width), whole(w), whole(gains), whole(biases)],
        out_specs=[by_row(width), pl.BlockSpec((3, rows, width), lambda i: (0, i, 0))],
        out_shape=[
            jax.ShapeDtypeStruct((tokens, width), jnp.bfloat16),
            jax.ShapeDtypeStruct((3, tokens, width), jnp.bfloat16),
        ],
        compiler_params=pltpu.CompilerParams(vmem_limit_bytes=56 << 20),
        name="project",
    )(x, w, gains, biases)


def project_back_kernel(d_ref, x_ref, dr_ref, w_ref, gain_ref, dx_ref, sums_ref):
    @pl.when(pl.program_id(0) == 0)
    def _():
        sums_ref[...] = jnp.zeros_like(sums_ref)

    width = x_ref.shape[1]
    d_a = sum(dot_nt(d_ref[k], w_ref[:, k * width : (k + 1) * width]) for k in range(3))
    normed, inverse = norm_parts(x_ref[...].astype(jnp.float32))
    sums_ref[0] += fold(d_a * normed)
    sums_ref[1] += fold(d_a)
    sums_ref[2] += fold(d_ref[0].astype(jnp.float32))
    sums_ref[3] += fold(d_ref[2].astype(jnp.float32))
    back = norm_back(d_a, gain_ref[0:1, :], normed, inverse)
    dx_ref[...] = (dr_ref[...] + back).astype(jnp.bfloat16)


def project_back(d_qkv, x, d_r, w, gains, rows=256):
    tokens, width = x.shape
    by_row = pl.BlockSpec((rows, width), lambda i: (i, 0))
    whole = lambda a: pl.BlockSpec(a.shape, lambda i: (0,) * a.ndim, pipeline_mode=pl.Buffered(1))
    return pl.pallas_call(
        project_back_kernel,
        grid=(tokens // rows,),
        in_specs=[pl.BlockSpec((3, rows, width), lambda i: (0, i, 0)), by_row, by_row, whole(w), whole(gains)],
        out_specs=[by_row, pl.BlockSpec((4, 8, width), lambda i: (0, 0, 0))],
        out_shape=[
            jax.ShapeDtypeStruct((tokens, width), jnp.bfloat16),
            jax.ShapeDtypeStruct((4, 8, width), jnp.float32),
        ],
        compiler_params=pltpu.CompilerParams(vmem_limit_bytes=56 << 20),
        name="project_back",
    )(d_qkv, x, d_r, w, gains)


class Ops:
    def __init__(self, send, recv, local, place):
        self.send, self.recv, self.local, self.place = send, recv, local, place
        self.remotes = self.locals = 0
        self.now = []

    def do(self, action):
        self.now.append(action)

    def remote(self, src, dst, peer):
        k = self.remotes
        self.remotes += 1
        copy = pltpu.make_async_remote_copy(
            src_ref=src,
            dst_ref=dst,
            send_sem=self.send.at[k],
            recv_sem=self.recv.at[k],
            device_id=peer,
            device_id_type=MESH,
        )
        self.do(copy.start)
        return copy

    def copy(self, src, dst):
        copy = pltpu.make_async_copy(src, dst, self.local.at[self.locals])
        self.locals += 1
        self.do(copy.start)
        return copy


class FixedPlace(Place):
    def __init__(self, digits):
        super().__init__(digits)
        self.shifted = {}
        self.peers = {}
        for axis, n in enumerate(digits):
            for shift in range(-n, n + 1):
                self.shifted[axis, shift] = super().digit(axis, shift)
            for shift in (-1, 1):
                self.peers[axis, shift] = super().peer(axis, shift)

    def device(self, shifts):
        at = [self.shifted[axis, shift] for axis, shift in enumerate(shifts)]
        return (at[0] * self.digits[1] + at[1], at[2] * self.digits[3] + at[3])

    def greet_group(self, group):
        barrier = pltpu.get_barrier_semaphore()
        for shifts in group:
            pl.semaphore_signal(barrier, inc=1, device_id=self.device(shifts), device_id_type=MESH)
        pl.semaphore_wait(barrier, len(group))

    def digit(self, axis, shift):
        return self.shifted[axis, shift]

    def peer(self, axis, shift):
        return self.peers[axis, shift]


def plan_ticks(ops, pieces, stride):
    queue = [(start, 0, k) for k, (start, _) in enumerate(pieces)]
    heapq.heapify(queue)
    ticks, ends = [], {}
    while queue:
        at, age, k = heapq.heappop(queue)
        ops.now = []
        alive = next(pieces[k][1], "end") != "end"
        if ops.now:
            ticks.append(ops.now)
        if alive:
            heapq.heappush(queue, (at + stride, age - 1, k))
        else:
            ends[k] = len(ticks)
    return ticks, ends


def schedule(ops, pieces, stride, moments, times, scale):
    queue = [(start, 0, k) for k, (start, _, _) in enumerate(pieces)]
    floor = [earliest for _, earliest, _ in pieces]
    heapq.heapify(queue)
    parts = []
    while queue:
        at, age, k = heapq.heappop(queue)
        ops.now = []
        if next(pieces[k][2], "end") != "end":
            heapq.heappush(queue, (at + stride, age - 1, k))
        where = next((m for m, time in enumerate(times) if time >= at * scale), len(times) - 1)
        floor[k] = max(floor[k], where)
        parts.append((floor[k], at, len(parts), ops.now))
    parts.sort(key=lambda part: part[:3])
    ticks = [actions for _, _, _, actions in parts]
    table = {moment: [] for moment in moments}
    for number, (where, _, _, _) in enumerate(parts):
        table[moments[where]].append(number)
    return Hooks(ticks, table)


class Hooks:
    def __init__(self, ticks, moments):
        self.ticks, self.moments = ticks, moments

    def run(self, step, hook):
        for at in sorted(s for s, h in self.moments if h == hook):
            numbers = self.moments[at, hook]
            if numbers:

                @pl.when(step == at)
                def _(numbers=numbers):
                    for number in numbers:
                        for action in self.ticks[number]:
                            action()


def spread_ticks(first, count, moments, weights=None):
    weights = weights or [1] * len(moments)
    table, todo, used, past = {}, list(range(first, count)), 0, 0
    for moment, weight in zip(moments, weights):
        past += weight
        upto = len(todo) * past // sum(weights)
        table[moment] = todo[used:upto]
        used = upto
    return table


def rect(rows, cols):
    return (pl.ds(*rows), pl.ds(*cols))


def ways(n, turn):
    if n == 1:
        return []
    return [(s, (turn,) if n == 2 or s == n // 2 - 1 else (1, -1)) for s in range(n // 2)]


def copies_of(digits):
    return 1 + sum(len(directions) for n in digits[:3] for _, directions in ways(n, 1))


def gather_steps(ops, shard, full, rows, cols, order, turn):
    place = ops.place
    held, sends = set(), []

    def index(axis, slot):
        return slots(place, held, axis, slot, cols)[:4] + rect(rows, cols)

    own = ops.copy(shard.at[rect(rows, cols)], full.at[index(None, None)])
    first = True
    for axis in order:
        n = place.digits[axis]
        for step, directions in ways(n, turn):
            started = []
            for direction in directions:
                at = index(axis, place.digit(axis, -step * direction))
                src = shard.at[rect(rows, cols)] if first and step == 0 else full.at[at]
                started.append(ops.remote(src, full.at[at], place.peer(axis, direction)))
            yield
            for copy in started:
                ops.do(copy.wait_recv)
            sends += started
        held.add(axis)
        if first:
            ops.do(own.wait)
            first = False
    view = full.at[index(None, None)]
    copy = ops.remote(view, view, place.peer(3, 1))
    yield
    ops.do(copy.wait_recv)
    for copy in sends + [copy]:
        ops.do(copy.wait_send)


def add_into(target, source):
    return lambda: accumulate(target, source)


def staged_sums(digits, order, turn):
    left, plan = [0, 1, 2], []
    for axis in order:
        left.remove(axis)
        lead = tuple(digits[a] for a in left)
        for step, directions in reversed(ways(digits[axis], turn)):
            plan.append((tuple(left), [(axis, direction, step) for direction in directions], lead))
    return plan


def reduce_steps_of(ops, own, sent, stage, landed, slabs, finish, order, turn):
    place, sends = ops.place, []
    if stage is not None:
        local = ops.copy(own, stage)
    copy = ops.remote(sent, landed, place.peer(3, 1))
    yield
    if stage is not None:
        ops.do(local.wait)
    ops.do(copy.wait_recv)
    sends.append(copy)
    ops.do(add_into(landed, own if stage is None else stage))
    slabs = iter(slabs)
    every = (slice(None), slice(None))
    for left, batch, _ in staged_sums(place.digits, order, turn):
        started = []
        for axis, direction, step in batch:
            slot = place.digit(axis, (step + 1) * direction)
            src = landed.at[slots(place, left, axis, slot, (0, 0))[:3] + every]
            dst = next(slabs)
            copy = ops.remote(src, dst, place.peer(axis, direction))
            started.append((axis, direction * step, dst, copy))
        yield
        for axis, shift, dst, copy in started:
            ops.do(copy.wait_recv)
            sends.append(copy)
            view = slots(place, left, axis, place.digit(axis, shift), (0, 0))[:3] + every
            ops.do(add_into(landed.at[view], dst))
    ops.do(lambda: finish(landed[place.at[:3]].astype(jnp.float32)))
    for copy in sends:
        ops.do(copy.wait_send)
    yield


def slab_shapes(digits, rows, cols, order, turn, dtype):
    return [
        pltpu.VMEM(lead + (rows, cols), dtype) for _, batch, lead in staged_sums(digits, order, turn) for _ in batch
    ]


GATHER_ORDERS = ((0, 1, 2), (0, 2, 1), (0, 1, 2), (0, 2, 1), (1, 2, 0), (0, 2, 1), (0, 1, 2), (0, 2, 1), (2, 1, 0))
X, Y, Z, W = (1, 2, 0), (2, 1, 0), (0, 1, 2), (0, 2, 1)
REDUCE_ORDERS = (W, X, (2, 0, 1), W, X, (1, 0, 2), Y, Z, (1, 0, 2), Y, X, X, Y, Z, X, Y)
LAST_ORDERS = (W, X, Z, Y, Z, (1, 0, 2), (2, 0, 1), Y, X, W, Y, Y, X, X)


def blocks_of(shape, rows, cols):
    rows, cols = min(rows, shape[0]), min(cols, shape[1])
    return [((r, rows), (c, cols)) for r in range(0, shape[0], rows) for c in range(0, shape[1], cols)]


def semaphores(copies, local):
    return [
        pltpu.SemaphoreType.DMA((copies,)),
        pltpu.SemaphoreType.DMA((copies,)),
        pltpu.SemaphoreType.DMA((local,)),
    ]


HEADS_WIDE = 256
QUERY_BLOCK = 256
SCALE_ROW = 13


def front_kernel(
    digits, counts,
    len_ref, scale_ref, x_ref, w_qkv, w_out, w_fc1, w_fc2, gain_ref, bias_ref, mid_ref, ffb_ref,
    a_ref, qkv_ref, z_ref, log_ref, wqkv_out, wout_ref, w1_ref, w2_ref, par_ref, wide_ref,
    wqkv_ref, small_ref, qkv_shard, out_shard, fc1_shard, fc2_shard, small_shard, mine_ref, send, recv, local,
):
    step = pl.program_id(0)
    steps = counts["steps"]
    f32, bf16 = jnp.float32, jnp.bfloat16
    tokens, width = x_ref.shape
    place = FixedPlace(digits)
    ops = Ops(send, recv, local, place)
    pieces, number, start = [], 0, 0.0
    whole = lambda ref: ((0, ref.shape[0]), (0, ref.shape[1]))
    pieces.append((0.0, gather_steps(ops, small_shard, small_ref, *whole(small_shard), GATHER_ORDERS[0], 1)))
    for s in range(steps):
        for part in range(3):
            cols = (part * width + s * HEADS_WIDE, HEADS_WIDE)
            order, turn = GATHER_ORDERS[number % 9], 1 - number % 2 * 2
            number += 1
            pieces.append((start, gather_steps(ops, qkv_shard, wqkv_ref, (0, qkv_shard.shape[0]), cols, order, turn)))
            start += 0.5
    for shard, full in ((out_shard, wout_ref), (fc1_shard, w1_ref), (fc2_shard, w2_ref)):
        for rows, cols in blocks_of(shard.shape, 32, 512):
            order, turn = GATHER_ORDERS[number % 9], 1 - number % 2 * 2
            number += 1
            pieces.append((start, gather_steps(ops, shard, full, rows, cols, order, turn)))
            start += 1.0
    ticks, ends = plan_ticks(ops, pieces, 4.0)
    ready = [max(ends[k] for k in range(4 + 3 * s)) for s in range(steps)]
    blocks = tokens // QUERY_BLOCK
    units = 2 * blocks
    table = {(s, "head"): [] for s in range(steps)}
    moments = [(s, u) for s in range(steps) for u in range(units)]
    spread = spread_ticks(ready[0], len(ticks), moments, [u % blocks + 1 for _, u in moments])
    table.update(spread)
    table[0, "head"] = list(range(ready[0]))
    for s in range(1, steps):
        late = [(m, t) for m in moments if m[0] >= s for t in table[m] if t < ready[s]]
        for moment, t in late:
            table[moment].remove(t)
            table[s, "head"].append(t)
    hooks = Hooks(ticks, table)

    total = digits[0] * digits[1] * digits[2] * digits[3]

    @pl.when(step == 0)
    def _():
        for shard, w in ((qkv_shard, w_qkv), (out_shard, w_out), (fc1_shard, w_fc1), (fc2_shard, w_fc2)):
            shard[...] = w[...].astype(bf16)
        me = ((place.at[0] * digits[1] + place.at[1]) * digits[2] + place.at[2]) * digits[3] + place.at[3]
        mine_ref[...] = jnp.zeros_like(mine_ref)
        for k, (row, ref) in enumerate(((0, gain_ref), (3, bias_ref), (10, mid_ref), (11, ffb_ref))):
            mine_ref[k // 2, row : row + ref.shape[0], 0 : ref.shape[1]] = ref[...]
        narrow = pltpu.roll(mine_ref[0], me * gain_ref.shape[1] % 128, 1)
        wide = pltpu.roll(mine_ref[1], me * mid_ref.shape[1] % 128, 1)
        small_shard[...] = (narrow + wide).astype(bf16)
        place.greet()

    hooks.run(step, "head")

    @pl.when(step == 0)
    def _():
        for ref in (par_ref, wide_ref):
            own = ref.shape[1] // total
            for lane in range(0, ref.shape[1], 128):
                block = None
                for d in range(lane // own, max((lane + 128) // own, lane // own + 1)):
                    i3, rest = d % digits[3], d // digits[3]
                    i2, rest = rest % digits[2], rest // digits[2]
                    i1, i0 = rest % digits[1], rest // digits[1]
                    value = small_ref[i0, i1, i2, i3].astype(f32)
                    block = value if block is None else block + value
                ref[:, lane : lane + 128] = block
        lane = lax.broadcasted_iota(jnp.int32, (1, 128), 1)
        for pair in range(width // 128):
            scales = jnp.where(lane < head_size, scale_ref[2 * pair], scale_ref[2 * pair + 1])
            par_ref[SCALE_ROW : SCALE_ROW + 1, pair * 128 : pair * 128 + 128] = scales
        for first in range(0, tokens, QUERY_BLOCK):
            rows = slice(first, first + QUERY_BLOCK)
            normed, _ = norm_parts(x_ref[rows, :].astype(f32))
            a_ref[rows, :] = (normed * par_ref[0:1, :] + par_ref[3:4, :]).astype(bf16)

    keep = pltpu.make_async_copy(wqkv_ref, wqkv_out, local.at[local.shape[0] - 1])

    @pl.when(step == steps - 1)
    def _():
        keep.start()

    at = pl.multiple_of(step * HEADS_WIDE, HEADS_WIDE)
    for part, row in ((0, 4), (1, None), (2, 5)):
        cols = pl.ds(pl.multiple_of(part * width + at, HEADS_WIDE), HEADS_WIDE)
        value = dot_nn(a_ref[...], wqkv_ref[:, :, :, :, :, cols].reshape(width, HEADS_WIDE))
        if row is not None:
            value = value + par_ref[row : row + 1, pl.ds(at, HEADS_WIDE)]
        qkv_ref[part] = value.astype(bf16)
    unit = 0
    for pair in range(HEADS_WIDE // 128):
        lanes = slice(pair * 128, pair * 128 + 128)
        for first in range(0, tokens, QUERY_BLOCK):
            attend_unit(
                len_ref[0], scale_ref, (step * (HEADS_WIDE // 128) + pair) * 2, first, QUERY_BLOCK,
                qkv_ref.at[0, :, lanes], qkv_ref.at[1, :, lanes], qkv_ref.at[2, :, lanes],
                z_ref.at[:, lanes], log_ref.at[pair],
            )
            hooks.run(step, unit)
            unit += 1

    @pl.when(step == steps - 1)
    def _():
        keep.wait()


def front(digits, lengths, head_scale, x, weights, small_parts):
    tokens, width = x.shape
    hidden = weights[2].shape[1]
    steps = width // HEADS_WIDE
    bf16, f32 = jnp.bfloat16, jnp.float32
    sds = jax.ShapeDtypeStruct
    anywhere = pl.BlockSpec(memory_space=pl.ANY)
    smem = pl.BlockSpec(memory_space=pltpu.SMEM)
    fixed = lambda shape: pl.BlockSpec(shape, lambda s: (0,) * len(shape), pipeline_mode=pl.Buffered(1))
    per_step = HEADS_WIDE // 128
    pieces = 1 + 3 * steps + sum(len(blocks_of(w.shape, 32, 512)) for w in weights[1:])
    return pl.pallas_call(
        functools.partial(front_kernel, digits, {"steps": steps}),
        grid=(steps,),
        in_specs=[smem, smem] + [fixed(v.shape) for v in (x, *weights, *small_parts)],
        out_specs=[
            fixed((tokens, width)),
            pl.BlockSpec((3, tokens, HEADS_WIDE), lambda s: (0, 0, s)),
            pl.BlockSpec((tokens, HEADS_WIDE), lambda s: (0, s)),
            pl.BlockSpec((per_step, 2, tokens), lambda s: (s, 0, 0)),
            anywhere,
            anywhere,
            anywhere,
            anywhere,
            fixed((16, width)),
            fixed((16, hidden)),
        ],
        out_shape=[
            sds((tokens, width), bf16),
            sds((3, tokens, width), bf16),
            sds((tokens, width), bf16),
            sds((width // 128, 2, tokens), f32),
        ]
        + [sds(digits + w.shape, bf16) for w in weights]
        + [sds((16, width), f32), sds((16, hidden), f32)],
        scratch_shapes=[pltpu.VMEM(digits + weights[0].shape, bf16), pltpu.VMEM(digits + (16, 128), bf16)]
        + [pltpu.VMEM(w.shape, bf16) for w in weights]
        + [pltpu.VMEM((16, 128), bf16), pltpu.VMEM((2, 16, 128), f32)]
        + semaphores(pieces * copies_of(digits), pieces + 1),
        compiler_params=pltpu.CompilerParams(
            collective_id=2, has_side_effects=True, vmem_limit_bytes=60 << 20
        ),
        name="front",
    )(lengths, head_scale, x, *weights, *small_parts)


def back_kernel(
    digits, stages,
    len_ref, q_ref, k_ref, v_ref, do_ref, log_ref, c_ref, df_ref, z_ref, dy_ref, g2_ref,
    dqkv_ref, dot_ref, gout_ref, s1_ref, s2_ref,
    dk_ref, dv_ref, made_ref, *scratch,
):
    step, steps = pl.program_id(0), stages["steps"]
    half = steps // 2
    bf16 = jnp.bfloat16
    place = FixedPlace(digits)
    send, recv, local = scratch[-3:]
    ops = Ops(send, recv, local, place)
    staging, rest = scratch[:4], list(scratch[4:-3])
    tokens = q_ref.shape[1]
    units = tokens // QUERY_BLOCK
    moments, times, now = [(0, "head")], [0.0], 0.0
    for s in range(steps):
        if s < half:
            now += 2.7
            moments.append((s, "made"))
            times.append(now)
        else:
            now += 1.3
        for u in range(units):
            now += 0.52 * (u + 1)
            moments.append((s, u))
            times.append(now)
    pieces, staged = [], 0
    all_slots = (slice(None),) * 3
    for start, which, rows, cols, order, turn, many in stages["pieces"]:
        grad, out = ((g2_ref, s2_ref), (made_ref, s1_ref))[which]
        landed, slabs = rest[0], rest[1 : 1 + many]
        del rest[: 1 + many]
        own = grad.at[all_slots + (place.at[3],) + rect(rows, cols)]
        sent = grad.at[all_slots + (place.digit(3, 1),) + rect(rows, cols)]
        stage, earliest = None, 0
        if which == 0:
            stage = staging[staged % 4]
            staged += 1
        else:
            earliest = moments.index((cols[0] // (made_ref.shape[-1] // half), "made"))

        def finish(value, out=out, rows=rows, cols=cols):
            out[rows[0] : rows[0] + rows[1], cols[0] : cols[0] + cols[1]] = value

        pieces.append(
            (start, earliest, reduce_steps_of(ops, own, sent, stage, landed, slabs, finish, order, turn))
        )
    stride = stages["stride"]
    span = max(start for start, _, _ in pieces) + 5 * stride
    hooks = schedule(ops, pieces, stride, moments, times, now / span)

    @pl.when(step == 0)
    def _():
        place.greet()

    hooks.run(step, "head")

    @pl.when(step < half)
    def _():
        wide = df_ref.shape[1]
        made = dot_tn(c_ref[...], df_ref[...]).astype(bf16)
        cols = pl.ds(pl.multiple_of(step * wide, wide), wide)
        made_ref[:, :, :, :, :, cols] = made.reshape(made_ref.shape[:5] + (wide,))

    hooks.run(step, "made")

    @pl.when(step >= half)
    def _():
        gout_ref[...] = dot_tn(z_ref[...], dy_ref[...]).astype(bf16)

    for unit in range(units):
        attend_back_unit(
            len_ref[0], unit * QUERY_BLOCK, QUERY_BLOCK, q_ref.at[0], k_ref.at[0], v_ref.at[0], do_ref, log_ref.at[0],
            dqkv_ref.at[0], dot_ref.at[0], dk_ref, dv_ref,
        )
        if unit == units - 1:
            dqkv_ref[1] = dk_ref[...].astype(bf16)
            dqkv_ref[2] = dv_ref[...].astype(bf16)
        hooks.run(step, unit)


def back(digits, lengths, qkv, d_attended, logs, c, d_f, z, d_y, grad_fc2):
    _, tokens, width = qkv.shape
    hidden = d_f.shape[1]
    pairs = width // 128
    half = pairs // 2
    bf16, f32 = jnp.bfloat16, jnp.float32
    sds = jax.ShapeDtypeStruct
    anywhere = pl.BlockSpec(memory_space=pl.ANY)
    cols = lambda part: pl.BlockSpec((1, tokens, 128), lambda p: (part, 0, p))
    per_pair = pl.BlockSpec((1, 2, tokens), lambda p: (p, 0, 0))
    fixed = lambda shape: pl.BlockSpec(shape, lambda s: (0,) * len(shape), pipeline_mode=pl.Buffered(1))
    early = pl.BlockSpec((tokens, hidden // half), lambda p: (0, jnp.minimum(p, half - 1)))
    late = pl.BlockSpec((tokens, width // half), lambda p: (0, jnp.maximum(p - half, 0)))
    total = digits[0] * digits[1] * digits[2] * digits[3]
    shapes = (grad_fc2.shape[4:], (width // total, hidden))
    listed = [[(which, *piece) for piece in blocks_of(shape, 32, 512)] for which, shape in enumerate(shapes)]
    mixed = []
    while any(listed):
        for some in listed:
            mixed += some[:2]
            del some[:2]
    pieces, scratch = [], []
    for number, (which, rows, at) in enumerate(mixed):
        order, turn = REDUCE_ORDERS[number % len(REDUCE_ORDERS)], 1 - number % 2 * 2
        slabs = slab_shapes(digits, rows[1], at[1], order, turn, bf16)
        pieces.append((float(number), which, rows, at, order, turn, len(slabs)))
        scratch += [pltpu.VMEM(digits[:3] + (rows[1], at[1]), bf16)] + slabs
    stage = pltpu.VMEM(digits[:3] + (mixed[0][1][1], mixed[0][2][1]), bf16)
    return pl.pallas_call(
        functools.partial(back_kernel, digits, {"steps": pairs, "pieces": pieces, "stride": 4.0}),
        grid=(pairs,),
        in_specs=[
            pl.BlockSpec(memory_space=pltpu.SMEM),
            cols(0),
            cols(1),
            cols(2),
            pl.BlockSpec((tokens, 128), lambda p: (0, p)),
            per_pair,
            fixed(c.shape),
            early,
            fixed(z.shape),
            late,
            anywhere,
        ],
        out_specs=[
            pl.BlockSpec((3, tokens, 128), lambda p: (0, 0, p)),
            per_pair,
            pl.BlockSpec((width, width // half), lambda p: (0, jnp.maximum(p - half, 0))),
            fixed(shapes[1]),
            fixed(shapes[0]),
        ],
        out_shape=[
            sds((3, tokens, width), bf16),
            sds((pairs, 2, tokens), f32),
            sds((width, width), bf16),
            sds(shapes[1], f32),
            sds(shapes[0], f32),
        ],
        scratch_shapes=[pltpu.VMEM((tokens, 128), f32)] * 2
        + [pltpu.VMEM(digits + shapes[1], bf16)]
        + [stage] * 4
        + scratch
        + semaphores(len(scratch), len(pieces)),
        compiler_params=pltpu.CompilerParams(
            collective_id=3, has_side_effects=True, vmem_limit_bytes=60 << 20
        ),
        name="back",
    )(lengths, qkv, qkv, qkv, d_attended, logs, c, d_f, z, d_y, grad_fc2)


def sum_direct(ops, block, first, second, result):
    place = ops.place
    digits = place.digits
    plane = [(0, a, b, c) for a in range(digits[1]) for b in range(digits[2]) for c in range(digits[3])][1:]
    copies = []
    for k, shifts in enumerate(plane):
        to = [place.digit(axis, shift) for axis, shift in enumerate(shifts)]
        src = block.at[:, to[1], to[2], to[3]]
        copies.append(ops.remote(src, first.at[k], place.device(shifts)))
    yield
    for copy in copies:
        ops.do(copy.wait_recv)

    def add_plane():
        total = block[:, place.at[1], place.at[2], place.at[3]]
        for k in range(len(plane)):
            total = total + first[k]
        result[...] = total

    ops.do(add_plane)
    others = []
    for shift in range(1, digits[0]):
        src = result.at[place.digit(0, shift)]
        others.append(ops.remote(src, second.at[shift - 1], place.device((shift, 0, 0, 0))))
    yield
    for copy in others:
        ops.do(copy.wait_recv)
    for copy in copies + others:
        ops.do(copy.wait_send)
    yield


def direct_group(digits):
    plane = [(0, a, b, c) for a in range(digits[1]) for b in range(digits[2]) for c in range(digits[3])][1:]
    return plane + [(shift, 0, 0, 0) for shift in range(1, digits[0])]


def last_kernel(
    digits, stages,
    a_ref, d_ref, wq_ref, wk_ref, wv_ref, x_ref, dr_ref, par_ref, sums_ref, wide_ref, dot_ref, scale_ref, gout_ref,
    dx_ref, sqkv_ref, sout_ref, gain_ref, bias_ref, mid_ref, ffb_ref, dscale_ref,
    da_ref, made_ref, rows_ref, block_ref, late_ref, first_ref, second_ref, plane_ref, found_ref, stage_ref, *scratch,
):
    step, steps = pl.program_id(0), stages["steps"]
    half = steps // 2
    f32, bf16 = jnp.float32, jnp.bfloat16
    place = FixedPlace(digits)
    send, recv, local = scratch[-3:]
    ops = Ops(send, recv, local, place)
    rest = list(scratch[:-3])
    tokens, width = x_ref.shape
    blocks = tokens // QUERY_BLOCK
    moments, times, now = [(0, "head")], [0.0], 0.0
    for s in range(half):
        now += 3.0
        moments.append((s, "made"))
        times.append(now)
    for s in range(half, steps):
        for b in range(blocks):
            now += 0.85
            moments.append((s, b))
            times.append(now)
    for b in range(blocks):
        now += 1.0
        moments.append((steps - 1, "norm%d" % b))
        times.append(now)
    moments.append((steps - 1, "end"))
    times.append(1e9)
    pieces = []
    all_slots = (slice(None),) * 3
    sources = {"small": block_ref, "qkv": made_ref, "out": gout_ref}
    for start, name, cols, order, turn, many in stages["pieces"]:
        landed, slabs = rest[0], rest[1 : 1 + many]
        del rest[: 1 + many]
        source = sources[name]
        view = (slice(None), pl.ds(*cols))
        own = source.at[all_slots + (place.at[3],) + view]
        sent = source.at[all_slots + (place.digit(3, 1),) + view]
        stage, earliest = None, 0
        if name == "out":
            stage = stage_ref.at[cols[0] // cols[1]]
        if name == "qkv":
            earliest = moments.index((cols[0] % width // HEADS_WIDE, "made"))
        out = {"small": found_ref, "qkv": sqkv_ref, "out": sout_ref}[name]

        def finish(value, out=out, cols=cols):
            out[:, cols[0] : cols[0] + cols[1]] = value

        pieces.append(
            (start, earliest, reduce_steps_of(ops, own, sent, stage, landed, slabs, finish, order, turn))
        )
    stride = stages["stride"]
    span = max(start for start, _, _ in pieces) + 5 * stride
    late_key = max(start for start, _, _ in pieces) + stride
    pieces.append((late_key, len(moments) - 1, sum_direct(ops, late_ref, first_ref, second_ref, plane_ref)))
    hooks = schedule(ops, pieces, stride, moments, times, now / span)

    @pl.when(step == 0)
    def _():
        place.greet_group(direct_group(digits))
        da_ref[...] = jnp.zeros_like(da_ref)
        rows_ref[...] = jnp.zeros_like(rows_ref)
        for row, k in ((1, 1), (2, 2), (6, 3), (7, 4), (8, 5), (9, 6)):
            rows_ref[row : row + 1, :] = jnp.sum(sums_ref[k], axis=0, keepdims=True)
        wide = [jnp.sum(wide_ref[k], axis=0, keepdims=True) for k in range(3)]
        dots = [sum(dot_ref[p, :, lane : lane + 128] for lane in range(0, tokens, 128)) for p in range(dot_ref.shape[0])]
        for d, slot, lane, lane_wide in small_slots(digits, width, wide_ref.shape[2]):
            block_ref[slot + (slice(0, 16),)] = rows_ref[:, lane : lane + 128]
            for k in range(3):
                block_ref[slot + (slice(10 + k, 11 + k),)] = wide[k][:, lane_wide : lane_wide + 128]
            for p, value in enumerate(dots):
                block_ref[slot + (slice(16 + 2 * p, 18 + 2 * p),)] = value

    hooks.run(step, "head")

    @pl.when(step < half)
    def _():
        at = pl.multiple_of(step * HEADS_WIDE, HEADS_WIDE)
        for part in range(3):
            made = dot_tn(a_ref[...], d_ref[part]).astype(bf16)
            cols = pl.ds(pl.multiple_of(part * width + at, HEADS_WIDE), HEADS_WIDE)
            made_ref[:, :, :, :, :, cols] = made.reshape(made_ref.shape[:5] + (HEADS_WIDE,))
        for part, row in ((0, 4), (2, 5)):
            rows_ref[row : row + 1, pl.ds(at, HEADS_WIDE)] = jnp.sum(d_ref[part].astype(f32), axis=0, keepdims=True)

    hooks.run(step, "made")
    end = step == steps - 1
    for b in range(blocks):

        @pl.when(step >= half)
        def _(b=b):
            rows = slice(b * QUERY_BLOCK, (b + 1) * QUERY_BLOCK)
            total = da_ref[rows, :]
            for part, w_ref in enumerate((wq_ref, wk_ref, wv_ref)):
                total = total + dot_nt(d_ref[part, rows, :], w_ref[...])
            da_ref[rows, :] = total

        hooks.run(step, b)
    for b in range(blocks):

        @pl.when(end)
        def _(b=b):
            rows = slice(b * QUERY_BLOCK, (b + 1) * QUERY_BLOCK)
            normed, inverse = norm_parts(x_ref[rows, :].astype(f32))
            d_a = da_ref[rows, :]
            rows_ref[0:1, :] += jnp.sum(d_a * normed, axis=0, keepdims=True)
            rows_ref[3:4, :] += jnp.sum(d_a, axis=0, keepdims=True)
            dx_ref[rows, :] = (dr_ref[rows, :] + norm_back(d_a, par_ref[0:1, :], normed, inverse)).astype(bf16)

        hooks.run(step, "norm%d" % b)

    @pl.when(end)
    def _():
        for d, slot, lane, _ in small_slots(digits, width, wide_ref.shape[2]):
            late_ref[slot] = rows_ref[0:8, lane : lane + 128]

    hooks.run(step, "end")

    @pl.when(end)
    def _():
        late = plane_ref[place.at[0]]
        for k in range(digits[0] - 1):
            late = late + second_ref[k]
        me = ((place.at[0] * digits[1] + place.at[1]) * digits[2] + place.at[2]) * digits[3] + place.at[3]
        row = lax.broadcasted_iota(jnp.int32, (8, 128), 0)
        swapped = (row == 0) | ((row >= 3) & (row <= 5))
        found_ref[0:8, :] = jnp.where(swapped, late, found_ref[0:8, :])
        own, own_wide = gain_ref.shape[1], mid_ref.shape[1]
        narrow = pltpu.roll(found_ref[0:16, :], (128 - me * own % 128) % 128, 1)
        broad = pltpu.roll(found_ref[0:16, :], (128 - me * own_wide % 128) % 128, 1)
        gain_ref[...] = narrow[0:3, 0:own]
        bias_ref[...] = narrow[3:10, 0:own]
        mid_ref[...] = broad[10:11, 0:own_wide]
        ffb_ref[...] = broad[11:13, 0:own_wide]
        heads = dscale_ref.shape[1]
        dscale_ref[...] = jnp.sum(found_ref[16 : 16 + heads, :].T, axis=0, keepdims=True) / scale_ref[...]


def small_slots(digits, width, hidden):
    total = digits[0] * digits[1] * digits[2] * digits[3]
    listed = []
    for d in range(total):
        i3, left = d % digits[3], d // digits[3]
        i2, left = left % digits[2], left // digits[2]
        slot = (left // digits[1], left % digits[1], i2, i3)
        listed.append((d, slot, d * (width // total) // 128 * 128, d * (hidden // total) // 128 * 128))
    return listed


def last(digits, a, d_qkv, w_qkv, x, d_r, par, sums, wide, dots, head_scale, grad_out):
    tokens, width = x.shape
    hidden = wide.shape[2]
    half = width // HEADS_WIDE
    bf16, f32 = jnp.bfloat16, jnp.float32
    sds = jax.ShapeDtypeStruct
    fixed = lambda shape: pl.BlockSpec(shape, lambda s: (0,) * len(shape), pipeline_mode=pl.Buffered(1))
    total = digits[0] * digits[1] * digits[2] * digits[3]
    rows = width // total
    small_rows = 16 + 2 * dots.shape[0]
    pieces, scratch = [], []

    def add(start, name, height, cols, order, kind):
        turn = 1 - len(pieces) % 2 * 2
        slabs = slab_shapes(digits, height, cols[1], order, turn, kind)
        pieces.append((start, name, cols, order, turn, len(slabs)))
        scratch.extend([pltpu.VMEM(digits[:3] + (height, cols[1]), kind)] + slabs)

    for k in range(2):
        add(0.5 * k, "out", rows, (k * (width // 2), width // 2), LAST_ORDERS[k], bf16)
    add(1.0, "small", small_rows, (0, 128), X, f32)
    number = 2
    for s in range(half):
        for part in range(3):
            cols = (part * width + s * HEADS_WIDE, HEADS_WIDE)
            add(0.5 * number + 0.5, "qkv", rows, cols, LAST_ORDERS[number % len(LAST_ORDERS)], bf16)
            number += 1
    weight = lambda part: pl.BlockSpec((width, HEADS_WIDE), lambda s: (0, part * half + jnp.maximum(s - half, 0)))
    smalls = [(3, rows), (7, rows), (1, hidden // total), (2, hidden // total), (1, head_scale.shape[1])]
    plane = digits[1] * digits[2] * digits[3]
    return pl.pallas_call(
        functools.partial(last_kernel, digits, {"steps": 2 * half, "pieces": pieces, "stride": 3.0}),
        grid=(2 * half,),
        in_specs=[fixed(a.shape), pl.BlockSpec((3, tokens, HEADS_WIDE), lambda s: (0, 0, s % half))]
        + [weight(part) for part in range(3)]
        + [fixed(v.shape) for v in (x, d_r, par, sums, wide, dots, head_scale)]
        + [pl.BlockSpec(memory_space=pl.ANY)],
        out_specs=[fixed(s) for s in [(tokens, width), (rows, 3 * width), (rows, width)] + smalls],
        out_shape=[sds((tokens, width), bf16), sds((rows, 3 * width), f32), sds((rows, width), f32)]
        + [sds(s, f32) for s in smalls],
        scratch_shapes=[
            pltpu.VMEM((tokens, width), f32),
            pltpu.VMEM(digits + (rows, 3 * width), bf16),
            pltpu.VMEM((16, width), f32),
            pltpu.VMEM(digits + (small_rows, 128), f32),
            pltpu.VMEM(digits + (8, 128), f32),
            pltpu.VMEM((plane - 1, digits[0], 8, 128), f32),
            pltpu.VMEM((digits[0] - 1, 8, 128), f32),
            pltpu.VMEM((digits[0], 8, 128), f32),
            pltpu.VMEM((small_rows, 128), f32),
            pltpu.VMEM((2,) + digits[:3] + (rows, width // 2), bf16),
        ]
        + scratch
        + semaphores(len(scratch) + plane + digits[0], 2),
        compiler_params=pltpu.CompilerParams(
            collective_id=4, has_side_effects=True, vmem_limit_bytes=60 << 20
        ),
        name="last",
    )(a, d_qkv, w_qkv, w_qkv, w_qkv, x, d_r, par, sums, wide, dots, head_scale, grad_out)


def plain_gather(digits, weights, small_parts):
    small = jnp.concatenate([to_bf16(v).reshape(-1) for v in small_parts])
    small = jnp.pad(small, (0, 2048 - small.shape[0])).reshape(16, 128)
    shards_in = [to_bf16(w).reshape(tiled_rows(*w.shape)) for w in weights] + [small]
    gathered = gather_all(digits, shards_in)
    fulls = [g.reshape((-1, w.shape[1])) for g, w in zip(gathered, weights)]
    smalls, parts, used = gathered[4].reshape(-1, 2048), [], 0
    for v in small_parts:
        block = smalls[:, used : used + v.size].reshape((-1,) + (v.shape if v.ndim == 2 else (1,) + v.shape))
        parts.append(block.transpose(1, 0, 2).reshape(block.shape[1], -1).astype(jnp.float32))
        used += v.size
    par = jnp.pad(jnp.concatenate(parts[:2]), ((0, 6), (0, 0)))
    table = jnp.pad(jnp.concatenate(parts[2:]), ((10, 3), (0, 0)))
    return fulls, par, table


def plain_reduce(digits, weights, grads, small_parts, small_grads):
    total = digits[0] * digits[1] * digits[2] * digits[3]
    block = [v.reshape(v.shape[0], total, -1).transpose(1, 0, 2).reshape(total, -1) for v in small_grads[:-1]]
    block.append(jnp.broadcast_to(small_grads[-1][None], (total, small_grads[-1].shape[0])))
    block = jnp.concatenate(block, axis=1)
    block = jnp.pad(block, ((0, 0), (0, 1024 - block.shape[1]))).reshape(digits + (8, 128))
    blocks = [to_bf16(g).reshape(digits + tiled_rows(*w.shape)) for g, w in zip(grads, weights)]
    summed = reduce_all(digits, blocks + [block])
    flat, used, owned = summed[4].reshape(-1), 0, []
    for v in small_parts:
        owned.append(flat[used : used + v.size].reshape(v.shape))
        used += v.size
    return [g.reshape(w.shape) for g, w in zip(summed[:4], weights)] + owned


def shards(
    digits, tokens, lengths, cotangent, w_qkv, w_out, w_fc1, w_fc2, norm_gain, norm_bias, mid_gain, ff_bias, head_scale
):
    weights = (w_qkv, w_out, w_fc1, w_fc2)
    small_parts = (norm_gain, norm_bias, mid_gain, ff_bias)
    heads = head_scale.shape[0]
    total = digits[0] * digits[1] * digits[2] * digits[3]
    tiled = w_qkv.shape[0] % 16 == 0
    if tiled:
        normed_in, qkv, mixed, logs, full_qkv, full_out, full_fc1, full_fc2, par, table = front(
            digits, lengths, head_scale, tokens, weights, (norm_gain, norm_bias, mid_gain[None], ff_bias)
        )
        full_qkv, full_out, full_fc1, full_fc2 = (
            g.reshape((-1, g.shape[-1])) for g in (full_qkv, full_out, full_fc1, full_fc2)
        )
    else:
        (full_qkv, full_out, full_fc1, full_fc2), par, table = plain_gather(digits, weights, small_parts)
        scale_row = jnp.repeat(head_scale, tokens.shape[1] // heads)[None]
        par = jnp.concatenate((par[:SCALE_ROW], scale_row, par[SCALE_ROW + 1 :]))
        normed_in, qkv = project(tokens, full_qkv, par[0:3], par[3:10])
        mixed, logs = attend(lengths, head_scale, qkv)
    result, normed_ff, normed_mid, grad_pre, grad_projection, grad_residual, grad_attended, sums, wide = ffn(
        lengths, tokens, mixed, cotangent, full_out, full_fc1, full_fc2, par, table
    )
    positions = jnp.arange(tokens.shape[0], dtype=jnp.int32)[:, None]
    grad_branch = jnp.where(positions < lengths, cotangent, jnp.zeros_like(cotangent))
    grad_fc2 = to_bf16(dot_tn(normed_mid, grad_branch))
    if tiled:
        d_qkv, dots, grad_out_w, sum_fc1, sum_fc2 = back(
            digits, lengths, qkv, grad_attended, logs, normed_ff, grad_pre, mixed, grad_projection,
            grad_fc2.reshape(digits + w_fc2.shape),
        )
        grad_tokens, sum_qkv, sum_out, d_gain, d_bias, d_mid, d_ffb, d_scale = last(
            digits, normed_in, d_qkv, full_qkv, tokens, grad_residual, par, sums, wide, dots, head_scale[None],
            grad_out_w.reshape(digits + w_out.shape),
        )
        summed = (sum_qkv, sum_out, sum_fc1, sum_fc2, d_gain, d_bias, d_mid[0], d_ffb, d_scale[0])
    else:
        grad_fc1 = to_bf16(dot_tn(normed_ff, grad_pre))
        grad_out_w = to_bf16(dot_tn(mixed, grad_projection))
        d_qkv, dots = attend_back(lengths, qkv, grad_attended, logs)
        grad_tokens, first_sums = project_back(d_qkv, tokens, grad_residual, full_qkv, par[0:3])
        grad_qkv = jnp.concatenate([dot_tn(normed_in, d_qkv[k]) for k in range(3)], axis=1)
        sums, wide, first_sums = sums.sum(1), wide.sum(1), first_sums.sum(1)
        small_grads = (
            jnp.concatenate((first_sums[0:1], sums[1:3])),
            jnp.concatenate((first_sums[1:4], sums[3:7])),
            wide[0:1],
            wide[1:3],
            dots.sum(-1).reshape(heads) / head_scale,
        )
        summed = plain_reduce(
            digits, weights, (grad_qkv, grad_out_w, grad_fc1, grad_fc2), small_parts + (head_scale,), small_grads
        )
    return (result, grad_tokens) + tuple(summed)


def solution(mesh):
    placed = (
        P(("dp", "fsdp"), None),
        P(("dp", "fsdp")),
        P(("dp", "fsdp"), None),
        P(("dp", "fsdp"), None),
        P(("dp", "fsdp"), None),
        P(("dp", "fsdp"), None),
        P(("dp", "fsdp"), None),
        P(None, ("dp", "fsdp")),
        P(None, ("dp", "fsdp")),
        P(("dp", "fsdp")),
        P(None, ("dp", "fsdp")),
        P(),
    )
    return jax.shard_map(
        functools.partial(shards, digits_of(mesh)),
        mesh=mesh,
        in_specs=placed,
        out_specs=(
            P(("dp", "fsdp"), None),
            P(("dp", "fsdp"), None),
            P(("dp", "fsdp"), None),
            P(("dp", "fsdp"), None),
            P(("dp", "fsdp"), None),
            P(("dp", "fsdp"), None),
            P(None, ("dp", "fsdp")),
            P(None, ("dp", "fsdp")),
            P(("dp", "fsdp")),
            P(None, ("dp", "fsdp")),
            P(),
        ),
        check_vma=False,
    )
```

```python
import functools
import heapq

import jax
import jax.numpy as jnp
from jax import lax
from jax.experimental import pallas as pl
from jax.experimental.pallas import tpu as pltpu
from jax.sharding import PartitionSpec as P

epsilon = 1e-05
mask_fill = -1e30
MESH = pl.DeviceIdType.MESH
ORDERS = ((1, 2, 0), (2, 1, 0), (0, 1, 2), (0, 2, 1))


def digits_of(mesh):
    dp, fsdp = mesh.shape["dp"], mesh.shape["fsdp"]
    minor = 2 if dp <= 8 else 8
    return (dp // minor, minor, fsdp // 2, 2)


class Place:
    def __init__(self, digits):
        self.digits = digits
        dp, fs = lax.axis_index("dp"), lax.axis_index("fsdp")
        self.at = (dp // digits[1], dp % digits[1], fs // digits[3], fs % digits[3])

    def digit(self, axis, shift):
        n = self.digits[axis]
        return (self.at[axis] + shift + n) % n

    def peer(self, axis, shift):
        at = list(self.at)
        at[axis] = self.digit(axis, shift)
        return (at[0] * self.digits[1] + at[1], at[2] * self.digits[3] + at[3])

    def greet(self):
        barrier = pltpu.get_barrier_semaphore()
        peers = []
        for axis, n in enumerate(self.digits):
            if n > 1:
                peers.append(self.peer(axis, 1))
            if n > 2:
                peers.append(self.peer(axis, -1))
        for peer in peers:
            pl.semaphore_signal(barrier, inc=1, device_id=peer, device_id_type=MESH)
        pl.semaphore_wait(barrier, len(peers))


class Sems:
    def __init__(self, send, recv, local):
        self.send, self.recv, self.local = send, recv, local
        self.remotes = self.locals = 0

    def remote(self, src, dst, peer):
        copy = pltpu.make_async_remote_copy(
            src_ref=src,
            dst_ref=dst,
            send_sem=self.send.at[self.remotes],
            recv_sem=self.recv.at[self.remotes],
            device_id=peer,
            device_id_type=MESH,
        )
        self.remotes += 1
        copy.start()
        return copy

    def copy(self, src, dst):
        copy = pltpu.make_async_copy(src, dst, self.local.at[self.locals])
        self.locals += 1
        copy.start()
        return copy


def hops(n):
    if n == 1:
        return []
    if n == 2:
        return [(0, (1,), False)]
    return [(s, (1, -1), s == n // 2 - 1) for s in range(n // 2)]


def column_part(start, size, direction, halved):
    if not halved:
        return start, size
    first = size // 256 * 128
    if first == 0:
        return (start, size) if direction > 0 else (start, 0)
    return (start, first) if direction > 0 else (start + first, size - first)


def slots(place, view, axis, slot, part):
    index = []
    for other, n in enumerate(place.digits):
        if other == axis:
            index.append(slot)
        elif other in view:
            index.append(pl.ds(0, n))
        else:
            index.append(place.at[other])
    return tuple(index) + (slice(None), pl.ds(*part))


def gather_piece(place, sems, shard, full, start, size, order):
    held, sends, cores = set(), [], []
    own = sems.copy(
        shard.at[:, pl.ds(start, size)], full.at[slots(place, (), None, None, (start, size))]
    )
    core = place.peer(3, 1)

    def forward(axis, slot, part):
        view = full.at[slots(place, held, axis, slot, part)]
        cores.append(sems.remote(view, view, core))

    first = True
    for axis in order:
        n = place.digits[axis]
        for step, directions, last in hops(n):
            started = []
            for direction in directions:
                part = column_part(start, size, direction, last)
                if part[1] == 0:
                    continue
                index = slots(place, held, axis, place.digit(axis, -step * direction), part)
                src = shard.at[:, pl.ds(*part)] if first and step == 0 else full.at[index]
                started.append(
                    (direction, sems.remote(src, full.at[index], place.peer(axis, direction)))
                )
            yield
            for direction, copy in started:
                copy.wait_recv()
                sends.append(copy)
                if not first and not last and n > 2:
                    forward(axis, place.digit(axis, -(step + 1) * direction), (start, size))
            if not first and (last or n == 2):
                forward(axis, place.digit(axis, n // 2), (start, size))
        if n > 1:
            held.add(axis)
            if first:
                own.wait()
                forward(None, None, (start, size))
                first = False
    if first:
        own.wait()
        forward(None, None, (start, size))
    yield
    for copy in cores:
        copy.wait()
    for copy in sends:
        copy.wait_send()


def accumulate(target, source, result=None):
    lead, dims = target.shape[:-2], target.shape
    count = 1
    for n in lead:
        count *= n

    def index_of(flat):
        index = []
        for n in reversed(lead):
            index.append(flat % n)
            flat = flat // n
        return tuple(reversed(index)) + (slice(None), slice(None))

    def body(flat, carry):
        index = index_of(flat)
        total = target[index].astype(jnp.float32) + source[index].astype(jnp.float32)
        target[index] = total.astype(target.dtype)
        return carry

    if lead:
        lax.fori_loop(0, count, body, 0)
    else:
        body(0, 0)


def reduce_steps(digits, start, size, order):
    left, plan = [0, 1, 2], []
    for axis in order:
        n = digits[axis]
        left.remove(axis)
        lead = tuple(digits[a] for a in left)
        for step, directions, last in reversed(hops(n)):
            batch = []
            for direction in directions:
                part = column_part(start, size, direction, last)
                if part[1] > 0:
                    batch.append((axis, direction, step, part, lead))
            plan.append((tuple(left), batch))
    return plan


def reduce_piece(place, sems, grad, acc, landed, slabs, out, start, size, order):
    sends = []
    lead = (slice(None),) * 3
    whole = (slice(None), pl.ds(start, size))
    mine = acc.at[lead + whole]
    other = landed.at[lead + whole]
    own = sems.copy(grad.at[lead + (place.at[3],) + whole], mine)
    sent = sems.remote(grad.at[lead + (place.digit(3, 1),) + whole], other, place.peer(3, 1))
    yield
    own.wait()
    sent.wait_recv()
    sends.append(sent)
    accumulate(mine, other)
    slabs = iter(slabs)
    for left, batch in reduce_steps(place.digits, start, size, order):
        started = []
        for axis, direction, step, part, _ in batch:
            slot = place.digit(axis, (step + 1) * direction)
            src = acc.at[slots(place, left, axis, slot, part)[:3] + (slice(None), pl.ds(*part))]
            dst = next(slabs)
            sent = sems.remote(src, dst, place.peer(axis, direction))
            started.append((axis, direction * step, part, dst, sent))
        yield
        for axis, shift, part, dst, sent in started:
            sent.wait_recv()
            sends.append(sent)
            slot = place.digit(axis, shift)
            view = slots(place, left, axis, slot, part)[:3] + (slice(None), pl.ds(*part))
            accumulate(acc.at[view], dst)
    out[:, pl.ds(start, size)] = acc[place.at[:3] + whole].astype(jnp.float32)
    for sent in sends:
        sent.wait_send()
    yield


def pieces_of(cols, wanted=4):
    tiles = cols // 128
    count = wanted
    while tiles % count:
        count -= 1
    size = tiles // count * 128
    return [(k * size, size) for k in range(count)]


def run_all(generators):
    live = list(generators)
    while live:
        still = []
        for generator in live:
            try:
                next(generator)
                still.append(generator)
            except StopIteration:
                pass
        live = still


def gather_kernel(digits, count, *refs):
    shards, fulls = refs[:count], refs[count : 2 * count]
    send, recv, local = refs[2 * count :]
    place = Place(digits)
    sems = Sems(send, recv, local)
    place.greet()
    run_all(
        gather_piece(place, sems, shard, full, start, size, ORDERS[k % 4])
        for shard, full in zip(shards, fulls)
        for k, (start, size) in enumerate(pieces_of(shard.shape[1]))
    )


def gather_all(digits, shards):
    count = len(shards)
    copies = 16 * 4 * count * max(1, max(digits) // 4)
    whole = [jax.ShapeDtypeStruct(digits + s.shape, s.dtype) for s in shards]
    return pl.pallas_call(
        functools.partial(gather_kernel, digits, count),
        out_shape=whole,
        in_specs=[pl.BlockSpec(memory_space=pl.ANY)] * count,
        out_specs=[pl.BlockSpec(memory_space=pl.ANY)] * count,
        scratch_shapes=[
            pltpu.SemaphoreType.DMA((copies,)),
            pltpu.SemaphoreType.DMA((copies,)),
            pltpu.SemaphoreType.DMA((4 * count,)),
        ],
        compiler_params=pltpu.CompilerParams(collective_id=0, has_side_effects=True),
        name="gather_all",
    )(*shards)


def reduce_plan(digits, grads):
    plan = []
    for g, grad in enumerate(grads):
        for k, (start, size) in enumerate(pieces_of(grad.shape[-1])):
            plan.append((g, start, size, ORDERS[k % 4]))
    return plan


def reduce_kernel(digits, plan, slab_counts, count, *refs):
    grads, outs = refs[:count], refs[count : 2 * count]
    accs, landed = refs[2 * count : 3 * count], refs[3 * count : 4 * count]
    slabs = refs[4 * count : -3]
    send, recv, local = refs[-3:]
    place = Place(digits)
    sems = Sems(send, recv, local)
    place.greet()
    generators, used = [], 0
    for (g, start, size, order), many in zip(plan, slab_counts):
        own = slabs[used : used + many]
        used += many
        generators.append(
            reduce_piece(place, sems, grads[g], accs[g], landed[g], own, outs[g], start, size, order)
        )
    run_all(generators)


def reduce_all(digits, grads):
    count = len(grads)
    plan = reduce_plan(digits, grads)
    slabs, slab_counts = [], []
    for g, start, size, order in plan:
        shapes = [
            pltpu.VMEM(lead + (grads[g].shape[-2], part[1]), grads[g].dtype)
            for _, batch in reduce_steps(digits, start, size, order)
            for _, _, _, part, lead in batch
        ]
        slabs += shapes
        slab_counts.append(len(shapes))
    blocks = [pltpu.VMEM(digits[:3] + g.shape[-2:], g.dtype) for g in grads]
    copies = len(slabs) + len(plan)
    return pl.pallas_call(
        functools.partial(reduce_kernel, digits, plan, slab_counts, count),
        out_shape=[jax.ShapeDtypeStruct(g.shape[-2:], jnp.float32) for g in grads],
        in_specs=[pl.BlockSpec(memory_space=pl.ANY)] * count,
        out_specs=[pl.BlockSpec(memory_space=pltpu.VMEM)] * count,
        scratch_shapes=blocks
        + blocks
        + slabs
        + [
            pltpu.SemaphoreType.DMA((copies,)),
            pltpu.SemaphoreType.DMA((copies,)),
            pltpu.SemaphoreType.DMA((len(plan),)),
        ],
        compiler_params=pltpu.CompilerParams(
            collective_id=1, has_side_effects=True, vmem_limit_bytes=58 << 20
        ),
        name="reduce_all",
    )(*grads)


def tiled_rows(rows, cols):
    return (rows, cols) if rows % 16 == 0 else (16, rows * cols // 16)


def to_bf16(values):
    return values.astype(jnp.bfloat16)


def dot_nn(a, b):
    return lax.dot_general(a, b, (((1,), (0,)), ((), ())), preferred_element_type=jnp.float32)


def dot_nt(a, b):
    return lax.dot_general(a, b, (((1,), (1,)), ((), ())), preferred_element_type=jnp.float32)


def dot_tn(a, b):
    return lax.dot_general(a, b, (((0,), (0,)), ((), ())), preferred_element_type=jnp.float32)


def row_mean(v):
    return jnp.mean(v, axis=-1, keepdims=True)


def norm_parts(v):
    centered = v - row_mean(v)
    inverse = lax.rsqrt(row_mean(centered * centered) + epsilon)
    return centered * inverse, inverse


def norm_back(grad, gain, normed, inverse):
    scaled = grad * gain
    return (scaled - row_mean(scaled) - normed * row_mean(scaled * normed)) * inverse


def fold(v):
    return v.reshape(v.shape[0] // 8, 8, v.shape[1]).sum(0)


def normal_parts(v):
    return 0.5 * (1.0 + lax.erf(v * 0.5**0.5)), jnp.exp(v * v * -0.5) * 0.3989422804014327


def ffn_kernel(
    chunk,
    len_ref, x_ref, z_ref, cot_ref, wo_hbm, w1_hbm, w2_hbm, par_ref, table_ref,
    out_ref, c_ref, m_ref, df_ref, dy_ref, dr_ref, do_ref, sums_ref, wide_ref,
    act_ref, slope_ref, wo_ref, w1_ref, w2_ref, fixed_ref, sems,
):
    step = pl.program_id(0)
    rows, width = x_ref.shape
    hidden = w1_ref.shape[1]
    f32, bf16 = jnp.float32, jnp.bfloat16
    chunks = [slice(j, j + chunk) for j in range(0, hidden, chunk)]
    loads = [pltpu.make_async_copy(wo_hbm, wo_ref, sems.at[0]), pltpu.make_async_copy(w2_hbm, w2_ref, sems.at[1])]
    for k, at in enumerate(chunks):
        loads.append(pltpu.make_async_copy(w1_hbm.at[:, at], w1_ref.at[:, at], sems.at[2 + k]))

    def arrived(k):
        @pl.when(step == 0)
        def _():
            loads[k].wait()

    @pl.when(step == 0)
    def _():
        for k in [0, *range(2, len(loads)), 1]:
            loads[k].start()
        sums_ref[...] = jnp.zeros_like(sums_ref)
        wide_ref[...] = jnp.zeros_like(wide_ref)

    gain = lambda k: par_ref[k : k + 1, :]
    bias = lambda k: par_ref[3 + k : 4 + k, :]
    arrived(0)
    y_norm, y_inv = norm_parts(dot_nn(z_ref[...], wo_ref[...]) + bias(3))
    residual = x_ref[...].astype(f32) + (y_norm * gain(1) + bias(4))
    r_norm, r_inv = norm_parts(residual)
    normed = (r_norm * gain(2) + bias(5)).astype(bf16)
    c_ref[...] = normed

    @pl.when(step == 0)
    def _():
        for k in range(2, len(loads)):
            loads[k].wait()

    total = jnp.zeros((rows, 1), f32)
    ahead = dot_nn(normed, w1_ref[:, chunks[0]])
    for k, at in enumerate(chunks):
        pre = ahead + table_ref[11:12, at]
        if k + 1 < len(chunks):
            ahead = dot_nn(normed, w1_ref[:, chunks[k + 1]])
        cdf, pdf = normal_parts(pre)
        act = pre * cdf
        act_ref[:, at] = act
        slope_ref[:, at] = cdf + pre * pdf
        total = total + jnp.sum(act, axis=-1, keepdims=True)
    average = total / hidden
    total = jnp.zeros((rows, 1), f32)
    for at in chunks:
        centered = act_ref[:, at] - average
        total = total + jnp.sum(centered * centered, axis=-1, keepdims=True)
    m_inv = lax.rsqrt(total / hidden + epsilon)

    @pl.when(step == 0)
    def _():
        loads[1].wait()
        fixed_ref[...] = dot_nn(table_ref[8:16, :].astype(bf16), w2_ref[...])

    branch = jnp.zeros((rows, width), f32)
    for k in range(len(chunks) + 1):
        if k < len(chunks):
            at = chunks[k]
            n = (act_ref[:, at] - average) * m_inv
            act_ref[:, at] = n
            m_ref[:, at] = (n * table_ref[10:11, at] + table_ref[12:13, at]).astype(bf16)
        if k > 0:
            branch = branch + dot_nn(m_ref[:, chunks[k - 1]], w2_ref[chunks[k - 1], :])
    out_ref[...] = (residual + (branch + bias(6))).astype(bf16)

    position = step * rows + lax.broadcasted_iota(jnp.int32, (rows, 1), 0)
    d_out = jnp.where(position < len_ref[0], cot_ref[...].astype(f32), 0.0)
    d_w = d_out.astype(bf16)
    sums_ref[6] += fold(d_out)
    first = jnp.sum(d_out * fixed_ref[2:3, :], axis=-1, keepdims=True) / hidden
    second = jnp.sum(d_out * (branch - fixed_ref[4:5, :]), axis=-1, keepdims=True) / hidden
    d_c = jnp.zeros((rows, width), f32)
    ahead = dot_nt(d_w, w2_ref[chunks[0], :])
    for k in range(len(chunks) + 1):
        dm = ahead
        if k + 1 < len(chunks):
            ahead = dot_nt(d_w, w2_ref[chunks[k + 1], :])
        if k > 0:
            d_c = d_c + dot_nt(df_ref[:, chunks[k - 1]], w1_ref[:, chunks[k - 1]])
        if k < len(chunks):
            at = chunks[k]
            n = act_ref[:, at]
            wide_ref[0, :, at] += fold(dm * n)
            wide_ref[2, :, at] += fold(dm)
            du = (dm * table_ref[10:11, at] - first - n * second) * m_inv
            df = (du * slope_ref[:, at]).astype(bf16)
            df_ref[:, at] = df
            wide_ref[1, :, at] += fold(df.astype(f32))
    sums_ref[2] += fold(d_c * r_norm)
    sums_ref[5] += fold(d_c)
    d_r = d_out + norm_back(d_c, gain(2), r_norm, r_inv)
    dr_ref[...] = d_r
    sums_ref[1] += fold(d_r * y_norm)
    sums_ref[4] += fold(d_r)
    d_y = norm_back(d_r, gain(1), y_norm, y_inv).astype(bf16)
    dy_ref[...] = d_y
    sums_ref[3] += fold(d_y.astype(f32))
    do_ref[...] = (dot_nt(d_y, wo_ref[...]) * par_ref[SCALE_ROW : SCALE_ROW + 1, :]).astype(bf16)


def ffn(lengths, x, z, cot, wo, w1, w2, par, table, rows=256, chunk=512):
    tokens, width = x.shape
    hidden = w1.shape[1]
    by_row = lambda n: pl.BlockSpec((rows, n), lambda i: (i, 0))
    whole = lambda a: pl.BlockSpec(a.shape, lambda i: (0,) * a.ndim, pipeline_mode=pl.Buffered(1))
    anywhere = pl.BlockSpec(memory_space=pl.ANY)
    sds = jax.ShapeDtypeStruct
    bf16, f32 = jnp.bfloat16, jnp.float32
    outs = [(width, bf16), (width, bf16), (hidden, bf16), (hidden, bf16), (width, bf16), (width, f32), (width, bf16)]
    return pl.pallas_call(
        functools.partial(ffn_kernel, chunk),
        grid=(tokens // rows,),
        in_specs=[pl.BlockSpec(memory_space=pltpu.SMEM)]
        + [by_row(width)] * 3
        + [anywhere] * 3
        + [whole(par), whole(table)],
        out_specs=[by_row(n) for n, _ in outs]
        + [pl.BlockSpec((7, 8, width), lambda i: (0, 0, 0)), pl.BlockSpec((3, 8, hidden), lambda i: (0, 0, 0))],
        out_shape=[sds((tokens, n), d) for n, d in outs] + [sds((7, 8, width), f32), sds((3, 8, hidden), f32)],
        scratch_shapes=[pltpu.VMEM((rows, hidden), f32)] * 2
        + [pltpu.VMEM(w.shape, bf16) for w in (wo, w1, w2)]
        + [pltpu.VMEM((8, width), f32), pltpu.SemaphoreType.DMA((2 + hidden // chunk,))],
        compiler_params=pltpu.CompilerParams(vmem_limit_bytes=60 << 20),
        name="ffn_both",
    )(lengths, x, z, cot, wo, w1, w2, par, table)


head_size = 64


def head_lanes(values, second):
    lane = lax.broadcasted_iota(jnp.int32, values.shape, 1)
    keep = lane >= head_size if second else lane < head_size
    return jnp.where(keep, values, jnp.zeros_like(values))


def masked_scores(keys, queries, first, length):
    scores = dot_nt(keys, queries)
    key_pos = lax.broadcasted_iota(jnp.int32, scores.shape, 0)
    near = key_pos[first:]
    query_pos = first + lax.broadcasted_iota(jnp.int32, near.shape, 1)
    last = jnp.where((near <= query_pos) & (near < length), scores[first:], mask_fill)
    if first == 0:
        return last
    return jnp.concatenate((jnp.where(key_pos[:first] < length, scores[:first], mask_fill), last), axis=0)


def attend_unit(length, scale_ref, head, first, block, q_ref, k_ref, v_ref, z_ref, log_ref):
    rows, seen = slice(first, first + block), first + block
    scaling = jnp.bfloat16(head_size**-0.5)
    keys, values = k_ref[:seen, :], v_ref[:seen, :]
    mixed = []
    for h in range(2):
        queries = head_lanes(q_ref[rows, :], h) * scaling
        scores = masked_scores(keys, queries, first, length)
        top = jnp.max(scores, axis=0, keepdims=True)
        shifted = jnp.exp(scores - top)
        total = jnp.sum(shifted, axis=0, keepdims=True)
        log_ref[h : h + 1, rows] = top + jnp.log(total)
        attended = dot_tn(shifted.astype(jnp.bfloat16), values)
        mixed.append(attended * (scale_ref[head + h] / total).T)
    lane = lax.broadcasted_iota(jnp.int32, mixed[0].shape, 1)
    z_ref[rows, :] = jnp.where(lane < head_size, mixed[0], mixed[1]).astype(jnp.bfloat16)


def attend_kernel(block, len_ref, scale_ref, q_ref, k_ref, v_ref, z_ref, log_ref):
    for first in range(0, q_ref.shape[1], block):
        attend_unit(
            len_ref[0], scale_ref, pl.program_id(0) * 2, first, block,
            q_ref.at[0], k_ref.at[0], v_ref.at[0], z_ref, log_ref.at[0],
        )


def attend(lengths, head_scale, qkv, block=256):
    _, tokens, width = qkv.shape
    pairs = width // 128
    cols = lambda part: pl.BlockSpec((1, tokens, 128), lambda p: (part, 0, p))
    smem = pl.BlockSpec(memory_space=pltpu.SMEM)
    return pl.pallas_call(
        functools.partial(attend_kernel, min(block, tokens)),
        grid=(pairs,),
        in_specs=[smem, smem, cols(0), cols(1), cols(2)],
        out_specs=[
            pl.BlockSpec((tokens, 128), lambda p: (0, p)),
            pl.BlockSpec((1, 2, tokens), lambda p: (p, 0, 0)),
        ],
        out_shape=[
            jax.ShapeDtypeStruct((tokens, width), jnp.bfloat16),
            jax.ShapeDtypeStruct((pairs, 2, tokens), jnp.float32),
        ],
        compiler_params=pltpu.CompilerParams(vmem_limit_bytes=56 << 20),
        name="attend",
    )(lengths, head_scale, qkv, qkv, qkv)


def attend_back_unit(
    length, first, block, q_ref, k_ref, v_ref, do_ref, log_ref, dq_ref, dot_ref, dk_ref, dv_ref
):
    rows, seen = slice(first, first + block), first + block
    bf16, scaling = jnp.bfloat16, head_size**-0.5
    keys, values = k_ref[:seen, :], v_ref[:seen, :]
    mixed = []
    for h in range(2):
        queries = head_lanes(q_ref[rows, :], h) * bf16(scaling)
        grads = head_lanes(do_ref[rows, :], h)
        scores = masked_scores(keys, queries, first, length)
        weights = jnp.exp(scores - log_ref[h : h + 1, rows])
        products = weights * dot_nt(values, grads)
        total = jnp.sum(products, axis=0, keepdims=True)
        dot_ref[h : h + 1, rows] = total
        d_scores = (products - weights * total).astype(bf16)
        for ref, left, right in ((dv_ref, weights.astype(bf16), grads), (dk_ref, d_scores, queries)):
            part = dot_nn(left, right)
            if h == 0:
                ref[rows, :] = part[first:]
                if first:
                    ref[:first, :] += part[:first]
            else:
                ref[:seen, :] += part
        mixed.append(dot_tn(d_scores, keys))
    lane = lax.broadcasted_iota(jnp.int32, mixed[0].shape, 1)
    dq_ref[rows, :] = (jnp.where(lane < head_size, mixed[0], mixed[1]) * scaling).astype(bf16)


def attend_back_kernel(block, len_ref, q_ref, k_ref, v_ref, do_ref, log_ref, dqkv_ref, dot_ref, dk_ref, dv_ref):
    for first in range(0, do_ref.shape[0], block):
        attend_back_unit(
            len_ref[0], first, block, q_ref.at[0], k_ref.at[0], v_ref.at[0], do_ref, log_ref.at[0],
            dqkv_ref.at[0], dot_ref.at[0], dk_ref, dv_ref,
        )
    dqkv_ref[1] = dk_ref[...].astype(jnp.bfloat16)
    dqkv_ref[2] = dv_ref[...].astype(jnp.bfloat16)


def attend_back(lengths, qkv, d_attended, logs, block=256):
    _, tokens, width = qkv.shape
    pairs = width // 128
    cols = lambda part: pl.BlockSpec((1, tokens, 128), lambda p: (part, 0, p))
    per_pair = pl.BlockSpec((1, 2, tokens), lambda p: (p, 0, 0))
    return pl.pallas_call(
        functools.partial(attend_back_kernel, min(block, tokens)),
        grid=(pairs,),
        in_specs=[
            pl.BlockSpec(memory_space=pltpu.SMEM),
            cols(0),
            cols(1),
            cols(2),
            pl.BlockSpec((tokens, 128), lambda p: (0, p)),
            per_pair,
        ],
        out_specs=[pl.BlockSpec((3, tokens, 128), lambda p: (0, 0, p)), per_pair],
        out_shape=[
            jax.ShapeDtypeStruct((3, tokens, width), jnp.bfloat16),
            jax.ShapeDtypeStruct((pairs, 2, tokens), jnp.float32),
        ],
        scratch_shapes=[pltpu.VMEM((tokens, 128), jnp.float32)] * 2,
        compiler_params=pltpu.CompilerParams(vmem_limit_bytes=56 << 20),
        name="attend_back",
    )(lengths, qkv, qkv, qkv, d_attended, logs)


def project_kernel(x_ref, w_ref, gain_ref, bias_ref, a_ref, qkv_ref):
    width = x_ref.shape[1]
    normed, _ = norm_parts(x_ref[...].astype(jnp.float32))
    a = (normed * gain_ref[0:1, :] + bias_ref[0:1, :]).astype(jnp.bfloat16)
    a_ref[...] = a
    for part, row in ((0, 1), (1, None), (2, 2)):
        at = slice(part * width, (part + 1) * width)
        value = dot_nn(a, w_ref[:, at])
        if row is not None:
            value = value + bias_ref[row : row + 1, :]
        qkv_ref[part] = value.astype(jnp.bfloat16)


def project(x, w, gains, biases, rows=256):
    tokens, width = x.shape
    by_row = lambda n: pl.BlockSpec((rows, n), lambda i: (i, 0))
    whole = lambda a: pl.BlockSpec(a.shape, lambda i: (0,) * a.ndim, pipeline_mode=pl.Buffered(1))
    return pl.pallas_call(
        project_kernel,
        grid=(tokens // rows,),
        in_specs=[by_row(width), whole(w), whole(gains), whole(biases)],
        out_specs=[by_row(width), pl.BlockSpec((3, rows, width), lambda i: (0, i, 0))],
        out_shape=[
            jax.ShapeDtypeStruct((tokens, width), jnp.bfloat16),
            jax.ShapeDtypeStruct((3, tokens, width), jnp.bfloat16),
        ],
        compiler_params=pltpu.CompilerParams(vmem_limit_bytes=56 << 20),
        name="project",
    )(x, w, gains, biases)


def project_back_kernel(d_ref, x_ref, dr_ref, w_ref, gain_ref, dx_ref, sums_ref):
    @pl.when(pl.program_id(0) == 0)
    def _():
        sums_ref[...] = jnp.zeros_like(sums_ref)

    width = x_ref.shape[1]
    d_a = sum(dot_nt(d_ref[k], w_ref[:, k * width : (k + 1) * width]) for k in range(3))
    normed, inverse = norm_parts(x_ref[...].astype(jnp.float32))
    sums_ref[0] += fold(d_a * normed)
    sums_ref[1] += fold(d_a)
    sums_ref[2] += fold(d_ref[0].astype(jnp.float32))
    sums_ref[3] += fold(d_ref[2].astype(jnp.float32))
    back = norm_back(d_a, gain_ref[0:1, :], normed, inverse)
    dx_ref[...] = (dr_ref[...] + back).astype(jnp.bfloat16)


def project_back(d_qkv, x, d_r, w, gains, rows=256):
    tokens, width = x.shape
    by_row = pl.BlockSpec((rows, width), lambda i: (i, 0))
    whole = lambda a: pl.BlockSpec(a.shape, lambda i: (0,) * a.ndim, pipeline_mode=pl.Buffered(1))
    return pl.pallas_call(
        project_back_kernel,
        grid=(tokens // rows,),
        in_specs=[pl.BlockSpec((3, rows, width), lambda i: (0, i, 0)), by_row, by_row, whole(w), whole(gains)],
        out_specs=[by_row, pl.BlockSpec((4, 8, width), lambda i: (0, 0, 0))],
        out_shape=[
            jax.ShapeDtypeStruct((tokens, width), jnp.bfloat16),
            jax.ShapeDtypeStruct((4, 8, width), jnp.float32),
        ],
        compiler_params=pltpu.CompilerParams(vmem_limit_bytes=56 << 20),
        name="project_back",
    )(d_qkv, x, d_r, w, gains)


class Ops:
    def __init__(self, send, recv, local, place):
        self.send, self.recv, self.local, self.place = send, recv, local, place
        self.remotes = self.locals = 0
        self.now = []

    def do(self, action):
        self.now.append(action)

    def remote(self, src, dst, peer):
        k = self.remotes
        self.remotes += 1
        copy = pltpu.make_async_remote_copy(
            src_ref=src,
            dst_ref=dst,
            send_sem=self.send.at[k],
            recv_sem=self.recv.at[k],
            device_id=peer,
            device_id_type=MESH,
        )
        self.do(copy.start)
        return copy

    def copy(self, src, dst):
        copy = pltpu.make_async_copy(src, dst, self.local.at[self.locals])
        self.locals += 1
        self.do(copy.start)
        return copy


class FixedPlace(Place):
    def __init__(self, digits):
        super().__init__(digits)
        self.shifted = {}
        self.peers = {}
        for axis, n in enumerate(digits):
            for shift in range(-n, n + 1):
                self.shifted[axis, shift] = super().digit(axis, shift)
            for shift in (-1, 1):
                self.peers[axis, shift] = super().peer(axis, shift)

    def device(self, shifts):
        at = [self.shifted[axis, shift] for axis, shift in enumerate(shifts)]
        return (at[0] * self.digits[1] + at[1], at[2] * self.digits[3] + at[3])

    def greet_group(self, group):
        barrier = pltpu.get_barrier_semaphore()
        for shifts in group:
            pl.semaphore_signal(barrier, inc=1, device_id=self.device(shifts), device_id_type=MESH)
        pl.semaphore_wait(barrier, len(group))

    def digit(self, axis, shift):
        return self.shifted[axis, shift]

    def peer(self, axis, shift):
        return self.peers[axis, shift]


def plan_ticks(ops, pieces, stride):
    queue = [(start, 0, k) for k, (start, _) in enumerate(pieces)]
    heapq.heapify(queue)
    ticks, ends = [], {}
    while queue:
        at, age, k = heapq.heappop(queue)
        ops.now = []
        alive = next(pieces[k][1], "end") != "end"
        if ops.now:
            ticks.append(ops.now)
        if alive:
            heapq.heappush(queue, (at + stride, age - 1, k))
        else:
            ends[k] = len(ticks)
    return ticks, ends


def schedule(ops, pieces, stride, moments, times, scale):
    queue = [(start, 0, k) for k, (start, _, _) in enumerate(pieces)]
    floor = [earliest for _, earliest, _ in pieces]
    heapq.heapify(queue)
    parts = []
    while queue:
        at, age, k = heapq.heappop(queue)
        ops.now = []
        if next(pieces[k][2], "end") != "end":
            heapq.heappush(queue, (at + stride, age - 1, k))
        where = next((m for m, time in enumerate(times) if time >= at * scale), len(times) - 1)
        floor[k] = max(floor[k], where)
        parts.append((floor[k], at, len(parts), ops.now))
    parts.sort(key=lambda part: part[:3])
    ticks = [actions for _, _, _, actions in parts]
    table = {moment: [] for moment in moments}
    for number, (where, _, _, _) in enumerate(parts):
        table[moments[where]].append(number)
    return Hooks(ticks, table)


class Hooks:
    def __init__(self, ticks, moments):
        self.ticks, self.moments = ticks, moments

    def run(self, step, hook):
        for at in sorted(s for s, h in self.moments if h == hook):
            numbers = self.moments[at, hook]
            if numbers:

                @pl.when(step == at)
                def _(numbers=numbers):
                    for number in numbers:
                        for action in self.ticks[number]:
                            action()


def spread_ticks(first, count, moments, weights=None):
    weights = weights or [1] * len(moments)
    table, todo, used, past = {}, list(range(first, count)), 0, 0
    for moment, weight in zip(moments, weights):
        past += weight
        upto = len(todo) * past // sum(weights)
        table[moment] = todo[used:upto]
        used = upto
    return table


def rect(rows, cols):
    return (pl.ds(*rows), pl.ds(*cols))


def ways(n, turn):
    if n == 1:
        return []
    return [(s, (turn,) if n == 2 or s == n // 2 - 1 else (1, -1)) for s in range(n // 2)]


def copies_of(digits):
    return 1 + sum(len(directions) for n in digits[:3] for _, directions in ways(n, 1))


def gather_steps(ops, shard, full, rows, cols, order, turn):
    place = ops.place
    held, sends = set(), []

    def index(axis, slot):
        return slots(place, held, axis, slot, cols)[:4] + rect(rows, cols)

    own = ops.copy(shard.at[rect(rows, cols)], full.at[index(None, None)])
    first = True
    for axis in order:
        n = place.digits[axis]
        for step, directions in ways(n, turn):
            started = []
            for direction in directions:
                at = index(axis, place.digit(axis, -step * direction))
                src = shard.at[rect(rows, cols)] if first and step == 0 else full.at[at]
                started.append(ops.remote(src, full.at[at], place.peer(axis, direction)))
            yield
            for copy in started:
                ops.do(copy.wait_recv)
            sends += started
        held.add(axis)
        if first:
            ops.do(own.wait)
            first = False
    view = full.at[index(None, None)]
    copy = ops.remote(view, view, place.peer(3, 1))
    yield
    ops.do(copy.wait_recv)
    for copy in sends + [copy]:
        ops.do(copy.wait_send)


def add_into(target, source):
    return lambda: accumulate(target, source)


def staged_sums(digits, order, turn):
    left, plan = [0, 1, 2], []
    for axis in order:
        left.remove(axis)
        lead = tuple(digits[a] for a in left)
        for step, directions in reversed(ways(digits[axis], turn)):
            plan.append((tuple(left), [(axis, direction, step) for direction in directions], lead))
    return plan


def reduce_steps_of(ops, own, sent, stage, landed, slabs, finish, order, turn):
    place, sends = ops.place, []
    if stage is not None:
        local = ops.copy(own, stage)
    copy = ops.remote(sent, landed, place.peer(3, 1))
    yield
    if stage is not None:
        ops.do(local.wait)
    ops.do(copy.wait_recv)
    sends.append(copy)
    ops.do(add_into(landed, own if stage is None else stage))
    slabs = iter(slabs)
    every = (slice(None), slice(None))
    for left, batch, _ in staged_sums(place.digits, order, turn):
        started = []
        for axis, direction, step in batch:
            slot = place.digit(axis, (step + 1) * direction)
            src = landed.at[slots(place, left, axis, slot, (0, 0))[:3] + every]
            dst = next(slabs)
            copy = ops.remote(src, dst, place.peer(axis, direction))
            started.append((axis, direction * step, dst, copy))
        yield
        for axis, shift, dst, copy in started:
            ops.do(copy.wait_recv)
            sends.append(copy)
            view = slots(place, left, axis, place.digit(axis, shift), (0, 0))[:3] + every
            ops.do(add_into(landed.at[view], dst))
    ops.do(lambda: finish(landed[place.at[:3]].astype(jnp.float32)))
    for copy in sends:
        ops.do(copy.wait_send)
    yield


def slab_shapes(digits, rows, cols, order, turn, dtype):
    return [
        pltpu.VMEM(lead + (rows, cols), dtype) for _, batch, lead in staged_sums(digits, order, turn) for _ in batch
    ]


GATHER_ORDERS = ((0, 1, 2), (0, 2, 1), (0, 1, 2), (0, 2, 1), (1, 2, 0), (0, 2, 1), (0, 1, 2), (0, 2, 1), (2, 1, 0))
X, Y, Z, W = (1, 2, 0), (2, 1, 0), (0, 1, 2), (0, 2, 1)
REDUCE_ORDERS = (W, X, (2, 0, 1), W, X, (1, 0, 2), Y, Z, (1, 0, 2), Y, X, X, Y, Z, X, Y)
LAST_ROUNDS = 2.5
OUT_PACE = 0.0
BACK_HOOKS = (1, 2, 3)
LAST_HOOKS = (0, 1, 2, 3)
LAST_ORDERS = (W, X, Z, Y, Z, (1, 0, 2), (2, 0, 1), Y, X, W, Y, Y, X, X)


def blocks_of(shape, rows, cols):
    rows, cols = min(rows, shape[0]), min(cols, shape[1])
    return [((r, rows), (c, cols)) for r in range(0, shape[0], rows) for c in range(0, shape[1], cols)]


def semaphores(copies, local):
    return [
        pltpu.SemaphoreType.DMA((copies,)),
        pltpu.SemaphoreType.DMA((copies,)),
        pltpu.SemaphoreType.DMA((local,)),
    ]


HEADS_WIDE = 256
QUERY_BLOCK = 256
SCALE_ROW = 13


def front_kernel(
    digits, counts,
    len_ref, scale_ref, x_ref, w_qkv, w_out, w_fc1, w_fc2, gain_ref, bias_ref, mid_ref, ffb_ref,
    a_ref, qkv_ref, z_ref, log_ref, wqkv_out, wout_ref, w1_ref, w2_ref, par_ref, wide_ref,
    wqkv_ref, small_ref, qkv_shard, out_shard, fc1_shard, fc2_shard, small_shard, mine_ref, send, recv, local,
):
    step = pl.program_id(0)
    steps = counts["steps"]
    f32, bf16 = jnp.float32, jnp.bfloat16
    tokens, width = x_ref.shape
    place = FixedPlace(digits)
    ops = Ops(send, recv, local, place)
    pieces, number, start = [], 0, 0.0
    whole = lambda ref: ((0, ref.shape[0]), (0, ref.shape[1]))
    pieces.append((0.0, gather_steps(ops, small_shard, small_ref, *whole(small_shard), GATHER_ORDERS[0], 1)))
    for s in range(steps):
        for part in range(3):
            cols = (part * width + s * HEADS_WIDE, HEADS_WIDE)
            order, turn = GATHER_ORDERS[number % 9], 1 - number % 2 * 2
            number += 1
            pieces.append((start, gather_steps(ops, qkv_shard, wqkv_ref, (0, qkv_shard.shape[0]), cols, order, turn)))
            start += 0.5
    for shard, full in ((out_shard, wout_ref), (fc1_shard, w1_ref), (fc2_shard, w2_ref)):
        for rows, cols in blocks_of(shard.shape, 32, 512):
            order, turn = GATHER_ORDERS[number % 9], 1 - number % 2 * 2
            number += 1
            pieces.append((start, gather_steps(ops, shard, full, rows, cols, order, turn)))
            start += 1.0
    ticks, ends = plan_ticks(ops, pieces, 3.0)
    ready = [max(ends[k] for k in range(4 + 3 * s)) for s in range(steps)]
    blocks = tokens // QUERY_BLOCK
    units = 2 * blocks
    table = {(s, "head"): [] for s in range(steps)}
    moments = [(s, u) for s in range(steps) for u in range(units)]
    spread = spread_ticks(ready[0], len(ticks), moments, [u % blocks + 1 for _, u in moments])
    table.update(spread)
    table[0, "head"] = list(range(ready[0]))
    for s in range(1, steps):
        late = [(m, t) for m in moments if m[0] >= s for t in table[m] if t < ready[s]]
        for moment, t in late:
            table[moment].remove(t)
            table[s, "head"].append(t)
    hooks = Hooks(ticks, table)

    total = digits[0] * digits[1] * digits[2] * digits[3]

    @pl.when(step == 0)
    def _():
        for shard, w in ((qkv_shard, w_qkv), (out_shard, w_out), (fc1_shard, w_fc1), (fc2_shard, w_fc2)):
            shard[...] = w[...].astype(bf16)
        me = ((place.at[0] * digits[1] + place.at[1]) * digits[2] + place.at[2]) * digits[3] + place.at[3]
        mine_ref[...] = jnp.zeros_like(mine_ref)
        for k, (row, ref) in enumerate(((0, gain_ref), (3, bias_ref), (10, mid_ref), (11, ffb_ref))):
            mine_ref[k // 2, row : row + ref.shape[0], 0 : ref.shape[1]] = ref[...]
        narrow = pltpu.roll(mine_ref[0], me * gain_ref.shape[1] % 128, 1)
        wide = pltpu.roll(mine_ref[1], me * mid_ref.shape[1] % 128, 1)
        small_shard[...] = (narrow + wide).astype(bf16)
        place.greet()

    hooks.run(step, "head")

    @pl.when(step == 0)
    def _():
        for ref in (par_ref, wide_ref):
            own = ref.shape[1] // total
            for lane in range(0, ref.shape[1], 128):
                block = None
                for d in range(lane // own, max((lane + 128) // own, lane // own + 1)):
                    i3, rest = d % digits[3], d // digits[3]
                    i2, rest = rest % digits[2], rest // digits[2]
                    i1, i0 = rest % digits[1], rest // digits[1]
                    value = small_ref[i0, i1, i2, i3].astype(f32)
                    block = value if block is None else block + value
                ref[:, lane : lane + 128] = block
        lane = lax.broadcasted_iota(jnp.int32, (1, 128), 1)
        for pair in range(width // 128):
            scales = jnp.where(lane < head_size, scale_ref[2 * pair], scale_ref[2 * pair + 1])
            par_ref[SCALE_ROW : SCALE_ROW + 1, pair * 128 : pair * 128 + 128] = scales
        for first in range(0, tokens, QUERY_BLOCK):
            rows = slice(first, first + QUERY_BLOCK)
            normed, _ = norm_parts(x_ref[rows, :].astype(f32))
            a_ref[rows, :] = (normed * par_ref[0:1, :] + par_ref[3:4, :]).astype(bf16)

    keep = pltpu.make_async_copy(wqkv_ref, wqkv_out, local.at[local.shape[0] - 1])

    @pl.when(step == steps - 1)
    def _():
        keep.start()

    at = pl.multiple_of(step * HEADS_WIDE, HEADS_WIDE)
    for part, row in ((0, 4), (1, None), (2, 5)):
        cols = pl.ds(pl.multiple_of(part * width + at, HEADS_WIDE), HEADS_WIDE)
        value = dot_nn(a_ref[...], wqkv_ref[:, :, :, :, :, cols].reshape(width, HEADS_WIDE))
        if row is not None:
            value = value + par_ref[row : row + 1, pl.ds(at, HEADS_WIDE)]
        qkv_ref[part] = value.astype(bf16)
    unit = 0
    for pair in range(HEADS_WIDE // 128):
        lanes = slice(pair * 128, pair * 128 + 128)
        for first in range(0, tokens, QUERY_BLOCK):
            attend_unit(
                len_ref[0], scale_ref, (step * (HEADS_WIDE // 128) + pair) * 2, first, QUERY_BLOCK,
                qkv_ref.at[0, :, lanes], qkv_ref.at[1, :, lanes], qkv_ref.at[2, :, lanes],
                z_ref.at[:, lanes], log_ref.at[pair],
            )
            hooks.run(step, unit)
            unit += 1

    @pl.when(step == steps - 1)
    def _():
        keep.wait()


def front(digits, lengths, head_scale, x, weights, small_parts):
    tokens, width = x.shape
    hidden = weights[2].shape[1]
    steps = width // HEADS_WIDE
    bf16, f32 = jnp.bfloat16, jnp.float32
    sds = jax.ShapeDtypeStruct
    anywhere = pl.BlockSpec(memory_space=pl.ANY)
    smem = pl.BlockSpec(memory_space=pltpu.SMEM)
    fixed = lambda shape: pl.BlockSpec(shape, lambda s: (0,) * len(shape), pipeline_mode=pl.Buffered(1))
    per_step = HEADS_WIDE // 128
    pieces = 1 + 3 * steps + sum(len(blocks_of(w.shape, 32, 512)) for w in weights[1:])
    return pl.pallas_call(
        functools.partial(front_kernel, digits, {"steps": steps}),
        grid=(steps,),
        in_specs=[smem, smem] + [fixed(v.shape) for v in (x, *weights, *small_parts)],
        out_specs=[
            fixed((tokens, width)),
            pl.BlockSpec((3, tokens, HEADS_WIDE), lambda s: (0, 0, s)),
            pl.BlockSpec((tokens, HEADS_WIDE), lambda s: (0, s)),
            pl.BlockSpec((per_step, 2, tokens), lambda s: (s, 0, 0)),
            anywhere,
            anywhere,
            anywhere,
            anywhere,
            fixed((16, width)),
            fixed((16, hidden)),
        ],
        out_shape=[
            sds((tokens, width), bf16),
            sds((3, tokens, width), bf16),
            sds((tokens, width), bf16),
            sds((width // 128, 2, tokens), f32),
        ]
        + [sds(digits + w.shape, bf16) for w in weights]
        + [sds((16, width), f32), sds((16, hidden), f32)],
        scratch_shapes=[pltpu.VMEM(digits + weights[0].shape, bf16), pltpu.VMEM(digits + (16, 128), bf16)]
        + [pltpu.VMEM(w.shape, bf16) for w in weights]
        + [pltpu.VMEM((16, 128), bf16), pltpu.VMEM((2, 16, 128), f32)]
        + semaphores(pieces * copies_of(digits), pieces + 1),
        compiler_params=pltpu.CompilerParams(
            collective_id=2, has_side_effects=True, vmem_limit_bytes=60 << 20
        ),
        name="front",
    )(lengths, head_scale, x, *weights, *small_parts)


def back_kernel(
    digits, stages,
    len_ref, q_ref, k_ref, v_ref, do_ref, log_ref, c_ref, df_ref, z_ref, dy_ref, g2_ref,
    dqkv_ref, dot_ref, gout_ref, s1_ref, s2_ref,
    dk_ref, dv_ref, made_ref, *scratch,
):
    step, steps = pl.program_id(0), stages["steps"]
    half = steps // 2
    bf16 = jnp.bfloat16
    place = FixedPlace(digits)
    send, recv, local = scratch[-3:]
    ops = Ops(send, recv, local, place)
    staging, rest = scratch[:4], list(scratch[4:-3])
    tokens = q_ref.shape[1]
    units = tokens // QUERY_BLOCK
    moments, times, now = [(0, "head")], [0.0], 0.0
    for s in range(steps):
        if s < half:
            now += 2.7
            moments.append((s, "made"))
            times.append(now)
        else:
            now += 1.3
        for u in range(units):
            now += 0.52 * (u + 1)
            if u in BACK_HOOKS:
                moments.append((s, u))
                times.append(now)
    pieces, staged = [], 0
    all_slots = (slice(None),) * 3
    for start, which, rows, cols, order, turn, many in stages["pieces"]:
        grad, out = ((g2_ref, s2_ref), (made_ref, s1_ref))[which]
        landed, slabs = rest[0], rest[1 : 1 + many]
        del rest[: 1 + many]
        own = grad.at[all_slots + (place.at[3],) + rect(rows, cols)]
        sent = grad.at[all_slots + (place.digit(3, 1),) + rect(rows, cols)]
        stage, earliest = None, 0
        if which == 0:
            stage = staging[staged % 4]
            staged += 1
        else:
            earliest = moments.index((cols[0] // (made_ref.shape[-1] // half), "made"))

        def finish(value, out=out, rows=rows, cols=cols):
            out[rows[0] : rows[0] + rows[1], cols[0] : cols[0] + cols[1]] = value

        pieces.append(
            (start, earliest, reduce_steps_of(ops, own, sent, stage, landed, slabs, finish, order, turn))
        )
    stride = stages["stride"]
    span = max(start for start, _, _ in pieces) + 5 * stride
    hooks = schedule(ops, pieces, stride, moments, times, now / span)

    @pl.when(step == 0)
    def _():
        place.greet()

    hooks.run(step, "head")

    @pl.when(step < half)
    def _():
        wide = df_ref.shape[1]
        made = dot_tn(c_ref[...], df_ref[...]).astype(bf16)
        cols = pl.ds(pl.multiple_of(step * wide, wide), wide)
        made_ref[:, :, :, :, :, cols] = made.reshape(made_ref.shape[:5] + (wide,))

    hooks.run(step, "made")

    @pl.when(step >= half)
    def _():
        gout_ref[...] = dot_tn(z_ref[...], dy_ref[...]).astype(bf16)

    for unit in range(units):
        attend_back_unit(
            len_ref[0], unit * QUERY_BLOCK, QUERY_BLOCK, q_ref.at[0], k_ref.at[0], v_ref.at[0], do_ref, log_ref.at[0],
            dqkv_ref.at[0], dot_ref.at[0], dk_ref, dv_ref,
        )
        if unit == units - 1:
            dqkv_ref[1] = dk_ref[...].astype(bf16)
            dqkv_ref[2] = dv_ref[...].astype(bf16)
        hooks.run(step, unit)


def back(digits, lengths, qkv, d_attended, logs, c, d_f, z, d_y, grad_fc2):
    _, tokens, width = qkv.shape
    hidden = d_f.shape[1]
    pairs = width // 128
    half = pairs // 2
    bf16, f32 = jnp.bfloat16, jnp.float32
    sds = jax.ShapeDtypeStruct
    anywhere = pl.BlockSpec(memory_space=pl.ANY)
    cols = lambda part: pl.BlockSpec((1, tokens, 128), lambda p: (part, 0, p))
    per_pair = pl.BlockSpec((1, 2, tokens), lambda p: (p, 0, 0))
    fixed = lambda shape: pl.BlockSpec(shape, lambda s: (0,) * len(shape), pipeline_mode=pl.Buffered(1))
    early = pl.BlockSpec((tokens, hidden // half), lambda p: (0, jnp.minimum(p, half - 1)))
    late = pl.BlockSpec((tokens, width // half), lambda p: (0, jnp.maximum(p - half, 0)))
    total = digits[0] * digits[1] * digits[2] * digits[3]
    shapes = (grad_fc2.shape[4:], (width // total, hidden))
    listed = [[(which, *piece) for piece in blocks_of(shape, 32, 512)] for which, shape in enumerate(shapes)]
    mixed = []
    while any(listed):
        for some in listed:
            mixed += some[:2]
            del some[:2]
    pieces, scratch = [], []
    for number, (which, rows, at) in enumerate(mixed):
        order, turn = REDUCE_ORDERS[number % len(REDUCE_ORDERS)], 1 - number % 2 * 2
        slabs = slab_shapes(digits, rows[1], at[1], order, turn, bf16)
        pieces.append((float(number), which, rows, at, order, turn, len(slabs)))
        scratch += [pltpu.VMEM(digits[:3] + (rows[1], at[1]), bf16)] + slabs
    stage = pltpu.VMEM(digits[:3] + (mixed[0][1][1], mixed[0][2][1]), bf16)
    return pl.pallas_call(
        functools.partial(back_kernel, digits, {"steps": pairs, "pieces": pieces, "stride": 4.0}),
        grid=(pairs,),
        in_specs=[
            pl.BlockSpec(memory_space=pltpu.SMEM),
            cols(0),
            cols(1),
            cols(2),
            pl.BlockSpec((tokens, 128), lambda p: (0, p)),
            per_pair,
            fixed(c.shape),
            early,
            fixed(z.shape),
            late,
            anywhere,
        ],
        out_specs=[
            pl.BlockSpec((3, tokens, 128), lambda p: (0, 0, p)),
            per_pair,
            pl.BlockSpec((width, width // half), lambda p: (0, jnp.maximum(p - half, 0))),
            fixed(shapes[1]),
            fixed(shapes[0]),
        ],
        out_shape=[
            sds((3, tokens, width), bf16),
            sds((pairs, 2, tokens), f32),
            sds((width, width), bf16),
            sds(shapes[1], f32),
            sds(shapes[0], f32),
        ],
        scratch_shapes=[pltpu.VMEM((tokens, 128), f32)] * 2
        + [pltpu.VMEM(digits + shapes[1], bf16)]
        + [stage] * 4
        + scratch
        + semaphores(len(scratch), len(pieces)),
        compiler_params=pltpu.CompilerParams(
            collective_id=3, has_side_effects=True, vmem_limit_bytes=60 << 20
        ),
        name="back",
    )(lengths, qkv, qkv, qkv, d_attended, logs, c, d_f, z, d_y, grad_fc2)


def sum_direct(ops, block, first, second, result):
    place = ops.place
    digits = place.digits
    plane = [(0, a, b, c) for a in range(digits[1]) for b in range(digits[2]) for c in range(digits[3])][1:]
    copies = []
    for k, shifts in enumerate(plane):
        to = [place.digit(axis, shift) for axis, shift in enumerate(shifts)]
        src = block.at[:, to[1], to[2], to[3]]
        copies.append(ops.remote(src, first.at[k], place.device(shifts)))
    yield
    for copy in copies:
        ops.do(copy.wait_recv)

    def add_plane():
        total = block[:, place.at[1], place.at[2], place.at[3]]
        for k in range(len(plane)):
            total = total + first[k]
        result[...] = total

    ops.do(add_plane)
    others = []
    for shift in range(1, digits[0]):
        src = result.at[place.digit(0, shift)]
        others.append(ops.remote(src, second.at[shift - 1], place.device((shift, 0, 0, 0))))
    yield
    for copy in others:
        ops.do(copy.wait_recv)
    for copy in copies + others:
        ops.do(copy.wait_send)
    yield


def direct_group(digits):
    plane = [(0, a, b, c) for a in range(digits[1]) for b in range(digits[2]) for c in range(digits[3])][1:]
    return plane + [(shift, 0, 0, 0) for shift in range(1, digits[0])]


def last_kernel(
    digits, stages,
    a_ref, d_ref, wq_ref, wk_ref, wv_ref, x_ref, dr_ref, par_ref, sums_ref, wide_ref, dot_ref, scale_ref, gout_ref,
    dx_ref, sqkv_ref, sout_ref, gain_ref, bias_ref, mid_ref, ffb_ref, dscale_ref,
    da_ref, made_ref, rows_ref, block_ref, late_ref, first_ref, second_ref, plane_ref, found_ref, stage_ref, *scratch,
):
    step, steps = pl.program_id(0), stages["steps"]
    half = steps // 2
    f32, bf16 = jnp.float32, jnp.bfloat16
    place = FixedPlace(digits)
    send, recv, local = scratch[-3:]
    ops = Ops(send, recv, local, place)
    rest = list(scratch[:-3])
    tokens, width = x_ref.shape
    blocks = tokens // QUERY_BLOCK
    moments, times, now = [(0, "head"), (0, "block")], [0.0, 0.01], 0.0
    for s in range(half):
        now += 3.0
        moments.append((s, "made"))
        times.append(now)
    for s in range(half, steps):
        for b in range(blocks):
            now += 0.85
            if b in LAST_HOOKS:
                moments.append((s, b))
                times.append(now)
    for b in range(blocks):
        now += 1.0
        moments.append((steps - 1, "norm%d" % b))
        times.append(now)
    moments.append((steps - 1, "end"))
    times.append(1e9)
    pieces = []
    all_slots = (slice(None),) * 3
    sources = {"small": block_ref, "qkv": made_ref, "out": gout_ref}
    for start, name, cols, order, turn, many in stages["pieces"]:
        landed, slabs = rest[0], rest[1 : 1 + many]
        del rest[: 1 + many]
        source = sources[name]
        view = (slice(None), pl.ds(*cols))
        own = source.at[all_slots + (place.at[3],) + view]
        sent = source.at[all_slots + (place.digit(3, 1),) + view]
        stage, earliest = None, int(name == "small")
        if name == "out":
            stage = stage_ref.at[cols[0] // cols[1]]
        if name == "qkv":
            earliest = moments.index((cols[0] % width // HEADS_WIDE, "made"))
        out = {"small": found_ref, "qkv": sqkv_ref, "out": sout_ref}[name]

        def finish(value, out=out, cols=cols):
            out[:, cols[0] : cols[0] + cols[1]] = value

        pieces.append(
            (start, earliest, reduce_steps_of(ops, own, sent, stage, landed, slabs, finish, order, turn))
        )
    stride = stages["stride"]
    span = max(start for start, _, _ in pieces) + LAST_ROUNDS * stride
    late_key = span + 0.01
    pieces.append((late_key, len(moments) - 1, sum_direct(ops, late_ref, first_ref, second_ref, plane_ref)))
    hooks = schedule(ops, pieces, stride, moments, times, now / span)

    @pl.when(step == 0)
    def _():
        place.greet_group(direct_group(digits))
        da_ref[...] = jnp.zeros_like(da_ref)
        rows_ref[...] = jnp.zeros_like(rows_ref)

    hooks.run(step, "head")

    @pl.when(step == 0)
    def _():
        for row, k in ((1, 1), (2, 2), (6, 3), (7, 4), (8, 5), (9, 6)):
            rows_ref[row : row + 1, :] = jnp.sum(sums_ref[k], axis=0, keepdims=True)
        wide = [jnp.sum(wide_ref[k], axis=0, keepdims=True) for k in range(3)]
        dots = [sum(dot_ref[p, :, lane : lane + 128] for lane in range(0, tokens, 128)) for p in range(dot_ref.shape[0])]
        for d, slot, lane, lane_wide in small_slots(digits, width, wide_ref.shape[2]):
            block_ref[slot + (slice(0, 16),)] = rows_ref[:, lane : lane + 128]
            for k in range(3):
                block_ref[slot + (slice(10 + k, 11 + k),)] = wide[k][:, lane_wide : lane_wide + 128]
            for p, value in enumerate(dots):
                block_ref[slot + (slice(16 + 2 * p, 18 + 2 * p),)] = value

    hooks.run(step, "block")

    @pl.when(step < half)
    def _():
        at = pl.multiple_of(step * HEADS_WIDE, HEADS_WIDE)
        for part in range(3):
            made = dot_tn(a_ref[...], d_ref[part]).astype(bf16)
            cols = pl.ds(pl.multiple_of(part * width + at, HEADS_WIDE), HEADS_WIDE)
            made_ref[:, :, :, :, :, cols] = made.reshape(made_ref.shape[:5] + (HEADS_WIDE,))
        for part, row in ((0, 4), (2, 5)):
            rows_ref[row : row + 1, pl.ds(at, HEADS_WIDE)] = jnp.sum(d_ref[part].astype(f32), axis=0, keepdims=True)

    hooks.run(step, "made")
    end = step == steps - 1
    for b in range(blocks):

        @pl.when(step >= half)
        def _(b=b):
            rows = slice(b * QUERY_BLOCK, (b + 1) * QUERY_BLOCK)
            total = da_ref[rows, :]
            for part, w_ref in enumerate((wq_ref, wk_ref, wv_ref)):
                total = total + dot_nt(d_ref[part, rows, :], w_ref[...])
            da_ref[rows, :] = total

        hooks.run(step, b)
    for b in range(blocks):

        @pl.when(end)
        def _(b=b):
            rows = slice(b * QUERY_BLOCK, (b + 1) * QUERY_BLOCK)
            normed, inverse = norm_parts(x_ref[rows, :].astype(f32))
            d_a = da_ref[rows, :]
            rows_ref[0:1, :] += jnp.sum(d_a * normed, axis=0, keepdims=True)
            rows_ref[3:4, :] += jnp.sum(d_a, axis=0, keepdims=True)
            dx_ref[rows, :] = (dr_ref[rows, :] + norm_back(d_a, par_ref[0:1, :], normed, inverse)).astype(bf16)

        hooks.run(step, "norm%d" % b)

    @pl.when(end)
    def _():
        for d, slot, lane, _ in small_slots(digits, width, wide_ref.shape[2]):
            late_ref[slot] = rows_ref[0:8, lane : lane + 128]

    hooks.run(step, "end")

    @pl.when(end)
    def _():
        late = plane_ref[place.at[0]]
        for k in range(digits[0] - 1):
            late = late + second_ref[k]
        me = ((place.at[0] * digits[1] + place.at[1]) * digits[2] + place.at[2]) * digits[3] + place.at[3]
        row = lax.broadcasted_iota(jnp.int32, (8, 128), 0)
        swapped = (row == 0) | ((row >= 3) & (row <= 5))
        found_ref[0:8, :] = jnp.where(swapped, late, found_ref[0:8, :])
        own, own_wide = gain_ref.shape[1], mid_ref.shape[1]
        narrow = pltpu.roll(found_ref[0:16, :], (128 - me * own % 128) % 128, 1)
        broad = pltpu.roll(found_ref[0:16, :], (128 - me * own_wide % 128) % 128, 1)
        gain_ref[...] = narrow[0:3, 0:own]
        bias_ref[...] = narrow[3:10, 0:own]
        mid_ref[...] = broad[10:11, 0:own_wide]
        ffb_ref[...] = broad[11:13, 0:own_wide]
        heads = dscale_ref.shape[1]
        dscale_ref[...] = jnp.sum(found_ref[16 : 16 + heads, :].T, axis=0, keepdims=True) / scale_ref[...]


def small_slots(digits, width, hidden):
    total = digits[0] * digits[1] * digits[2] * digits[3]
    listed = []
    for d in range(total):
        i3, left = d % digits[3], d // digits[3]
        i2, left = left % digits[2], left // digits[2]
        slot = (left // digits[1], left % digits[1], i2, i3)
        listed.append((d, slot, d * (width // total) // 128 * 128, d * (hidden // total) // 128 * 128))
    return listed


def last(digits, a, d_qkv, w_qkv, x, d_r, par, sums, wide, dots, head_scale, grad_out):
    tokens, width = x.shape
    hidden = wide.shape[2]
    half = width // HEADS_WIDE
    bf16, f32 = jnp.bfloat16, jnp.float32
    sds = jax.ShapeDtypeStruct
    fixed = lambda shape: pl.BlockSpec(shape, lambda s: (0,) * len(shape), pipeline_mode=pl.Buffered(1))
    total = digits[0] * digits[1] * digits[2] * digits[3]
    rows = width // total
    small_rows = 16 + 2 * dots.shape[0]
    pieces, scratch = [], []

    def add(start, name, height, cols, order, kind):
        turn = 1 - len(pieces) % 2 * 2
        slabs = slab_shapes(digits, height, cols[1], order, turn, kind)
        pieces.append((start, name, cols, order, turn, len(slabs)))
        scratch.extend([pltpu.VMEM(digits[:3] + (height, cols[1]), kind)] + slabs)

    for k in range(2):
        add(OUT_PACE * k, "out", rows, (k * (width // 2), width // 2), LAST_ORDERS[k], bf16)
    add(1.0, "small", small_rows, (0, 128), X, f32)
    number = 2
    for s in range(half):
        for part in range(3):
            cols = (part * width + s * HEADS_WIDE, HEADS_WIDE)
            add(0.5 * number + 0.5, "qkv", rows, cols, LAST_ORDERS[number % len(LAST_ORDERS)], bf16)
            number += 1
    weight = lambda part: pl.BlockSpec((width, HEADS_WIDE), lambda s: (0, part * half + jnp.maximum(s - half, 0)))
    smalls = [(3, rows), (7, rows), (1, hidden // total), (2, hidden // total), (1, head_scale.shape[1])]
    plane = digits[1] * digits[2] * digits[3]
    return pl.pallas_call(
        functools.partial(last_kernel, digits, {"steps": 2 * half, "pieces": pieces, "stride": 3.0}),
        grid=(2 * half,),
        in_specs=[fixed(a.shape), pl.BlockSpec((3, tokens, HEADS_WIDE), lambda s: (0, 0, s % half))]
        + [weight(part) for part in range(3)]
        + [fixed(v.shape) for v in (x, d_r, par, sums, wide, dots, head_scale)]
        + [pl.BlockSpec(memory_space=pl.ANY)],
        out_specs=[fixed(s) for s in [(tokens, width), (rows, 3 * width), (rows, width)] + smalls],
        out_shape=[sds((tokens, width), bf16), sds((rows, 3 * width), f32), sds((rows, width), f32)]
        + [sds(s, f32) for s in smalls],
        scratch_shapes=[
            pltpu.VMEM((tokens, width), f32),
            pltpu.VMEM(digits + (rows, 3 * width), bf16),
            pltpu.VMEM((16, width), f32),
            pltpu.VMEM(digits + (small_rows, 128), f32),
            pltpu.VMEM(digits + (8, 128), f32),
            pltpu.VMEM((plane - 1, digits[0], 8, 128), f32),
            pltpu.VMEM((digits[0] - 1, 8, 128), f32),
            pltpu.VMEM((digits[0], 8, 128), f32),
            pltpu.VMEM((small_rows, 128), f32),
            pltpu.VMEM((2,) + digits[:3] + (rows, width // 2), bf16),
        ]
        + scratch
        + semaphores(len(scratch) + plane + digits[0], 2),
        compiler_params=pltpu.CompilerParams(
            collective_id=4, has_side_effects=True, vmem_limit_bytes=60 << 20
        ),
        name="last",
    )(a, d_qkv, w_qkv, w_qkv, w_qkv, x, d_r, par, sums, wide, dots, head_scale, grad_out)


def settle_kernel(count, *refs):
    for k in range(count):
        refs[count + k][...] = refs[k][...]


def settle(arrays, steps=4):
    def block(shape):
        if shape[0] % (8 * steps) == 0:
            return pl.BlockSpec((shape[0] // steps, shape[1]), lambda s: (s, 0))
        return pl.BlockSpec(shape, lambda s: (0, 0))

    blocks = [block(a.shape) for a in arrays]
    return pl.pallas_call(
        functools.partial(settle_kernel, len(arrays)),
        grid=(steps,),
        in_specs=blocks,
        out_specs=blocks,
        out_shape=[jax.ShapeDtypeStruct(a.shape, a.dtype) for a in arrays],
        compiler_params=pltpu.CompilerParams(vmem_limit_bytes=40 << 20),
        name="settle",
    )(*arrays)


def plain_gather(digits, weights, small_parts):
    small = jnp.concatenate([to_bf16(v).reshape(-1) for v in small_parts])
    small = jnp.pad(small, (0, 2048 - small.shape[0])).reshape(16, 128)
    shards_in = [to_bf16(w).reshape(tiled_rows(*w.shape)) for w in weights] + [small]
    gathered = gather_all(digits, shards_in)
    fulls = [g.reshape((-1, w.shape[1])) for g, w in zip(gathered, weights)]
    smalls, parts, used = gathered[4].reshape(-1, 2048), [], 0
    for v in small_parts:
        block = smalls[:, used : used + v.size].reshape((-1,) + (v.shape if v.ndim == 2 else (1,) + v.shape))
        parts.append(block.transpose(1, 0, 2).reshape(block.shape[1], -1).astype(jnp.float32))
        used += v.size
    par = jnp.pad(jnp.concatenate(parts[:2]), ((0, 6), (0, 0)))
    table = jnp.pad(jnp.concatenate(parts[2:]), ((10, 3), (0, 0)))
    return fulls, par, table


def plain_reduce(digits, weights, grads, small_parts, small_grads):
    total = digits[0] * digits[1] * digits[2] * digits[3]
    block = [v.reshape(v.shape[0], total, -1).transpose(1, 0, 2).reshape(total, -1) for v in small_grads[:-1]]
    block.append(jnp.broadcast_to(small_grads[-1][None], (total, small_grads[-1].shape[0])))
    block = jnp.concatenate(block, axis=1)
    block = jnp.pad(block, ((0, 0), (0, 1024 - block.shape[1]))).reshape(digits + (8, 128))
    blocks = [to_bf16(g).reshape(digits + tiled_rows(*w.shape)) for g, w in zip(grads, weights)]
    summed = reduce_all(digits, blocks + [block])
    flat, used, owned = summed[4].reshape(-1), 0, []
    for v in small_parts:
        owned.append(flat[used : used + v.size].reshape(v.shape))
        used += v.size
    return [g.reshape(w.shape) for g, w in zip(summed[:4], weights)] + owned


def shards(
    digits, tokens, lengths, cotangent, w_qkv, w_out, w_fc1, w_fc2, norm_gain, norm_bias, mid_gain, ff_bias, head_scale
):
    weights = (w_qkv, w_out, w_fc1, w_fc2)
    small_parts = (norm_gain, norm_bias, mid_gain, ff_bias)
    heads = head_scale.shape[0]
    total = digits[0] * digits[1] * digits[2] * digits[3]
    tiled = w_qkv.shape[0] % 16 == 0
    if tiled:
        normed_in, qkv, mixed, logs, full_qkv, full_out, full_fc1, full_fc2, par, table = front(
            digits, lengths, head_scale, tokens, weights, (norm_gain, norm_bias, mid_gain[None], ff_bias)
        )
        full_qkv, full_out, full_fc1, full_fc2 = (
            g.reshape((-1, g.shape[-1])) for g in (full_qkv, full_out, full_fc1, full_fc2)
        )
    else:
        (full_qkv, full_out, full_fc1, full_fc2), par, table = plain_gather(digits, weights, small_parts)
        scale_row = jnp.repeat(head_scale, tokens.shape[1] // heads)[None]
        par = jnp.concatenate((par[:SCALE_ROW], scale_row, par[SCALE_ROW + 1 :]))
        normed_in, qkv = project(tokens, full_qkv, par[0:3], par[3:10])
        mixed, logs = attend(lengths, head_scale, qkv)
    result, normed_ff, normed_mid, grad_pre, grad_projection, grad_residual, grad_attended, sums, wide = ffn(
        lengths, tokens, mixed, cotangent, full_out, full_fc1, full_fc2, par, table
    )
    positions = jnp.arange(tokens.shape[0], dtype=jnp.int32)[:, None]
    grad_branch = jnp.where(positions < lengths, cotangent, jnp.zeros_like(cotangent))
    grad_fc2 = to_bf16(dot_tn(normed_mid, grad_branch))
    if tiled:
        d_qkv, dots, grad_out_w, sum_fc1, sum_fc2 = back(
            digits, lengths, qkv, grad_attended, logs, normed_ff, grad_pre, mixed, grad_projection,
            grad_fc2.reshape(digits + w_fc2.shape),
        )
        grad_tokens, sum_qkv, sum_out, d_gain, d_bias, d_mid, d_ffb, d_scale = last(
            digits, normed_in, d_qkv, full_qkv, tokens, grad_residual, par, sums, wide, dots, head_scale[None],
            grad_out_w.reshape(digits + w_out.shape),
        )
        grad_tokens, sum_qkv, sum_out, sum_fc1, sum_fc2, d_gain, d_bias, d_mid, d_ffb, d_scale = settle(
            (grad_tokens, sum_qkv, sum_out, sum_fc1, sum_fc2, d_gain, d_bias, d_mid, d_ffb, d_scale)
        )
        summed = (sum_qkv, sum_out, sum_fc1, sum_fc2, d_gain, d_bias, d_mid[0], d_ffb, d_scale[0])
    else:
        grad_fc1 = to_bf16(dot_tn(normed_ff, grad_pre))
        grad_out_w = to_bf16(dot_tn(mixed, grad_projection))
        d_qkv, dots = attend_back(lengths, qkv, grad_attended, logs)
        grad_tokens, first_sums = project_back(d_qkv, tokens, grad_residual, full_qkv, par[0:3])
        grad_qkv = jnp.concatenate([dot_tn(normed_in, d_qkv[k]) for k in range(3)], axis=1)
        sums, wide, first_sums = sums.sum(1), wide.sum(1), first_sums.sum(1)
        small_grads = (
            jnp.concatenate((first_sums[0:1], sums[1:3])),
            jnp.concatenate((first_sums[1:4], sums[3:7])),
            wide[0:1],
            wide[1:3],
            dots.sum(-1).reshape(heads) / head_scale,
        )
        summed = plain_reduce(
            digits, weights, (grad_qkv, grad_out_w, grad_fc1, grad_fc2), small_parts + (head_scale,), small_grads
        )
    return (result, grad_tokens) + tuple(summed)


def solution(mesh):
    placed = (
        P(("dp", "fsdp"), None),
        P(("dp", "fsdp")),
        P(("dp", "fsdp"), None),
        P(("dp", "fsdp"), None),
        P(("dp", "fsdp"), None),
        P(("dp", "fsdp"), None),
        P(("dp", "fsdp"), None),
        P(None, ("dp", "fsdp")),
        P(None, ("dp", "fsdp")),
        P(("dp", "fsdp")),
        P(None, ("dp", "fsdp")),
        P(),
    )
    return jax.shard_map(
        functools.partial(shards, digits_of(mesh)),
        mesh=mesh,
        in_specs=placed,
        out_specs=(
            P(("dp", "fsdp"), None),
            P(("dp", "fsdp"), None),
            P(("dp", "fsdp"), None),
            P(("dp", "fsdp"), None),
            P(("dp", "fsdp"), None),
            P(("dp", "fsdp"), None),
            P(None, ("dp", "fsdp")),
            P(None, ("dp", "fsdp")),
            P(("dp", "fsdp")),
            P(None, ("dp", "fsdp")),
            P(),
        ),
        check_vma=False,
    )
```

```python
import functools
import heapq

import jax
import jax.numpy as jnp
from jax import lax
from jax.experimental import pallas as pl
from jax.experimental.pallas import tpu as pltpu
from jax.sharding import PartitionSpec as P

epsilon = 1e-05
mask_fill = -1e30
MESH = pl.DeviceIdType.MESH
ORDERS = ((1, 2, 0), (2, 1, 0), (0, 1, 2), (0, 2, 1))


def digits_of(mesh):
    dp, fsdp = mesh.shape["dp"], mesh.shape["fsdp"]
    minor = 2 if dp <= 8 else 8
    return (dp // minor, minor, fsdp // 2, 2)


class Place:
    def __init__(self, digits):
        self.digits = digits
        dp, fs = lax.axis_index("dp"), lax.axis_index("fsdp")
        self.at = (dp // digits[1], dp % digits[1], fs // digits[3], fs % digits[3])

    def digit(self, axis, shift):
        n = self.digits[axis]
        return (self.at[axis] + shift + n) % n

    def peer(self, axis, shift):
        at = list(self.at)
        at[axis] = self.digit(axis, shift)
        return (at[0] * self.digits[1] + at[1], at[2] * self.digits[3] + at[3])

    def greet(self):
        barrier = pltpu.get_barrier_semaphore()
        peers = []
        for axis, n in enumerate(self.digits):
            if n > 1:
                peers.append(self.peer(axis, 1))
            if n > 2:
                peers.append(self.peer(axis, -1))
        for peer in peers:
            pl.semaphore_signal(barrier, inc=1, device_id=peer, device_id_type=MESH)
        pl.semaphore_wait(barrier, len(peers))


class Sems:
    def __init__(self, send, recv, local):
        self.send, self.recv, self.local = send, recv, local
        self.remotes = self.locals = 0

    def remote(self, src, dst, peer):
        copy = pltpu.make_async_remote_copy(
            src_ref=src,
            dst_ref=dst,
            send_sem=self.send.at[self.remotes],
            recv_sem=self.recv.at[self.remotes],
            device_id=peer,
            device_id_type=MESH,
        )
        self.remotes += 1
        copy.start()
        return copy

    def copy(self, src, dst):
        copy = pltpu.make_async_copy(src, dst, self.local.at[self.locals])
        self.locals += 1
        copy.start()
        return copy


def hops(n):
    if n == 1:
        return []
    if n == 2:
        return [(0, (1,), False)]
    return [(s, (1, -1), s == n // 2 - 1) for s in range(n // 2)]


def column_part(start, size, direction, halved):
    if not halved:
        return start, size
    first = size // 256 * 128
    if first == 0:
        return (start, size) if direction > 0 else (start, 0)
    return (start, first) if direction > 0 else (start + first, size - first)


def slots(place, view, axis, slot, part):
    index = []
    for other, n in enumerate(place.digits):
        if other == axis:
            index.append(slot)
        elif other in view:
            index.append(pl.ds(0, n))
        else:
            index.append(place.at[other])
    return tuple(index) + (slice(None), pl.ds(*part))


def gather_piece(place, sems, shard, full, start, size, order):
    held, sends, cores = set(), [], []
    own = sems.copy(
        shard.at[:, pl.ds(start, size)], full.at[slots(place, (), None, None, (start, size))]
    )
    core = place.peer(3, 1)

    def forward(axis, slot, part):
        view = full.at[slots(place, held, axis, slot, part)]
        cores.append(sems.remote(view, view, core))

    first = True
    for axis in order:
        n = place.digits[axis]
        for step, directions, last in hops(n):
            started = []
            for direction in directions:
                part = column_part(start, size, direction, last)
                if part[1] == 0:
                    continue
                index = slots(place, held, axis, place.digit(axis, -step * direction), part)
                src = shard.at[:, pl.ds(*part)] if first and step == 0 else full.at[index]
                started.append(
                    (direction, sems.remote(src, full.at[index], place.peer(axis, direction)))
                )
            yield
            for direction, copy in started:
                copy.wait_recv()
                sends.append(copy)
                if not first and not last and n > 2:
                    forward(axis, place.digit(axis, -(step + 1) * direction), (start, size))
            if not first and (last or n == 2):
                forward(axis, place.digit(axis, n // 2), (start, size))
        if n > 1:
            held.add(axis)
            if first:
                own.wait()
                forward(None, None, (start, size))
                first = False
    if first:
        own.wait()
        forward(None, None, (start, size))
    yield
    for copy in cores:
        copy.wait()
    for copy in sends:
        copy.wait_send()


def accumulate(target, source, result=None):
    lead, dims = target.shape[:-2], target.shape
    count = 1
    for n in lead:
        count *= n

    def index_of(flat):
        index = []
        for n in reversed(lead):
            index.append(flat % n)
            flat = flat // n
        return tuple(reversed(index)) + (slice(None), slice(None))

    def body(flat, carry):
        index = index_of(flat)
        total = target[index].astype(jnp.float32) + source[index].astype(jnp.float32)
        target[index] = total.astype(target.dtype)
        return carry

    if lead:
        lax.fori_loop(0, count, body, 0)
    else:
        body(0, 0)


def reduce_steps(digits, start, size, order):
    left, plan = [0, 1, 2], []
    for axis in order:
        n = digits[axis]
        left.remove(axis)
        lead = tuple(digits[a] for a in left)
        for step, directions, last in reversed(hops(n)):
            batch = []
            for direction in directions:
                part = column_part(start, size, direction, last)
                if part[1] > 0:
                    batch.append((axis, direction, step, part, lead))
            plan.append((tuple(left), batch))
    return plan


def reduce_piece(place, sems, grad, acc, landed, slabs, out, start, size, order):
    sends = []
    lead = (slice(None),) * 3
    whole = (slice(None), pl.ds(start, size))
    mine = acc.at[lead + whole]
    other = landed.at[lead + whole]
    own = sems.copy(grad.at[lead + (place.at[3],) + whole], mine)
    sent = sems.remote(grad.at[lead + (place.digit(3, 1),) + whole], other, place.peer(3, 1))
    yield
    own.wait()
    sent.wait_recv()
    sends.append(sent)
    accumulate(mine, other)
    slabs = iter(slabs)
    for left, batch in reduce_steps(place.digits, start, size, order):
        started = []
        for axis, direction, step, part, _ in batch:
            slot = place.digit(axis, (step + 1) * direction)
            src = acc.at[slots(place, left, axis, slot, part)[:3] + (slice(None), pl.ds(*part))]
            dst = next(slabs)
            sent = sems.remote(src, dst, place.peer(axis, direction))
            started.append((axis, direction * step, part, dst, sent))
        yield
        for axis, shift, part, dst, sent in started:
            sent.wait_recv()
            sends.append(sent)
            slot = place.digit(axis, shift)
            view = slots(place, left, axis, slot, part)[:3] + (slice(None), pl.ds(*part))
            accumulate(acc.at[view], dst)
    out[:, pl.ds(start, size)] = acc[place.at[:3] + whole].astype(jnp.float32)
    for sent in sends:
        sent.wait_send()
    yield


def pieces_of(cols, wanted=4):
    tiles = cols // 128
    count = wanted
    while tiles % count:
        count -= 1
    size = tiles // count * 128
    return [(k * size, size) for k in range(count)]


def run_all(generators):
    live = list(generators)
    while live:
        still = []
        for generator in live:
            try:
                next(generator)
                still.append(generator)
            except StopIteration:
                pass
        live = still


def gather_kernel(digits, count, *refs):
    shards, fulls = refs[:count], refs[count : 2 * count]
    send, recv, local = refs[2 * count :]
    place = Place(digits)
    sems = Sems(send, recv, local)
    place.greet()
    run_all(
        gather_piece(place, sems, shard, full, start, size, ORDERS[k % 4])
        for shard, full in zip(shards, fulls)
        for k, (start, size) in enumerate(pieces_of(shard.shape[1]))
    )


def gather_all(digits, shards):
    count = len(shards)
    copies = 16 * 4 * count * max(1, max(digits) // 4)
    whole = [jax.ShapeDtypeStruct(digits + s.shape, s.dtype) for s in shards]
    return pl.pallas_call(
        functools.partial(gather_kernel, digits, count),
        out_shape=whole,
        in_specs=[pl.BlockSpec(memory_space=pl.ANY)] * count,
        out_specs=[pl.BlockSpec(memory_space=pl.ANY)] * count,
        scratch_shapes=[
            pltpu.SemaphoreType.DMA((copies,)),
            pltpu.SemaphoreType.DMA((copies,)),
            pltpu.SemaphoreType.DMA((4 * count,)),
        ],
        compiler_params=pltpu.CompilerParams(collective_id=0, has_side_effects=True),
        name="gather_all",
    )(*shards)


def reduce_plan(digits, grads):
    plan = []
    for g, grad in enumerate(grads):
        for k, (start, size) in enumerate(pieces_of(grad.shape[-1])):
            plan.append((g, start, size, ORDERS[k % 4]))
    return plan


def reduce_kernel(digits, plan, slab_counts, count, *refs):
    grads, outs = refs[:count], refs[count : 2 * count]
    accs, landed = refs[2 * count : 3 * count], refs[3 * count : 4 * count]
    slabs = refs[4 * count : -3]
    send, recv, local = refs[-3:]
    place = Place(digits)
    sems = Sems(send, recv, local)
    place.greet()
    generators, used = [], 0
    for (g, start, size, order), many in zip(plan, slab_counts):
        own = slabs[used : used + many]
        used += many
        generators.append(
            reduce_piece(place, sems, grads[g], accs[g], landed[g], own, outs[g], start, size, order)
        )
    run_all(generators)


def reduce_all(digits, grads):
    count = len(grads)
    plan = reduce_plan(digits, grads)
    slabs, slab_counts = [], []
    for g, start, size, order in plan:
        shapes = [
            pltpu.VMEM(lead + (grads[g].shape[-2], part[1]), grads[g].dtype)
            for _, batch in reduce_steps(digits, start, size, order)
            for _, _, _, part, lead in batch
        ]
        slabs += shapes
        slab_counts.append(len(shapes))
    blocks = [pltpu.VMEM(digits[:3] + g.shape[-2:], g.dtype) for g in grads]
    copies = len(slabs) + len(plan)
    return pl.pallas_call(
        functools.partial(reduce_kernel, digits, plan, slab_counts, count),
        out_shape=[jax.ShapeDtypeStruct(g.shape[-2:], jnp.float32) for g in grads],
        in_specs=[pl.BlockSpec(memory_space=pl.ANY)] * count,
        out_specs=[pl.BlockSpec(memory_space=pltpu.VMEM)] * count,
        scratch_shapes=blocks
        + blocks
        + slabs
        + [
            pltpu.SemaphoreType.DMA((copies,)),
            pltpu.SemaphoreType.DMA((copies,)),
            pltpu.SemaphoreType.DMA((len(plan),)),
        ],
        compiler_params=pltpu.CompilerParams(
            collective_id=1, has_side_effects=True, vmem_limit_bytes=58 << 20
        ),
        name="reduce_all",
    )(*grads)


def tiled_rows(rows, cols):
    return (rows, cols) if rows % 16 == 0 else (16, rows * cols // 16)


def to_bf16(values):
    return values.astype(jnp.bfloat16)


def dot_nn(a, b):
    return lax.dot_general(a, b, (((1,), (0,)), ((), ())), preferred_element_type=jnp.float32)


def dot_nt(a, b):
    return lax.dot_general(a, b, (((1,), (1,)), ((), ())), preferred_element_type=jnp.float32)


def dot_tn(a, b):
    return lax.dot_general(a, b, (((0,), (0,)), ((), ())), preferred_element_type=jnp.float32)


def row_mean(v):
    return jnp.mean(v, axis=-1, keepdims=True)


def norm_parts(v):
    centered = v - row_mean(v)
    inverse = lax.rsqrt(row_mean(centered * centered) + epsilon)
    return centered * inverse, inverse


def norm_back(grad, gain, normed, inverse):
    scaled = grad * gain
    return (scaled - row_mean(scaled) - normed * row_mean(scaled * normed)) * inverse


def fold(v):
    return v.reshape(v.shape[0] // 8, 8, v.shape[1]).sum(0)


def normal_parts(v):
    return 0.5 * (1.0 + lax.erf(v * 0.5**0.5)), jnp.exp(v * v * -0.5) * 0.3989422804014327


def ffn_kernel(
    chunk,
    len_ref, x_ref, z_ref, cot_ref, wo_hbm, w1_hbm, w2_hbm, par_ref, table_ref,
    out_ref, c_ref, m_ref, df_ref, dy_ref, dr_ref, do_ref, sums_ref, wide_ref,
    act_ref, slope_ref, wo_ref, w1_ref, w2_ref, fixed_ref, sems,
):
    step = pl.program_id(0)
    rows, width = x_ref.shape
    hidden = w1_ref.shape[1]
    f32, bf16 = jnp.float32, jnp.bfloat16
    chunks = [slice(j, j + chunk) for j in range(0, hidden, chunk)]
    loads = [pltpu.make_async_copy(wo_hbm, wo_ref, sems.at[0]), pltpu.make_async_copy(w2_hbm, w2_ref, sems.at[1])]
    for k, at in enumerate(chunks):
        loads.append(pltpu.make_async_copy(w1_hbm.at[:, at], w1_ref.at[:, at], sems.at[2 + k]))

    def arrived(k):
        @pl.when(step == 0)
        def _():
            loads[k].wait()

    @pl.when(step == 0)
    def _():
        for k in [0, *range(2, len(loads)), 1]:
            loads[k].start()
        sums_ref[...] = jnp.zeros_like(sums_ref)
        wide_ref[...] = jnp.zeros_like(wide_ref)

    gain = lambda k: par_ref[k : k + 1, :]
    bias = lambda k: par_ref[3 + k : 4 + k, :]
    arrived(0)
    y_norm, y_inv = norm_parts(dot_nn(z_ref[...], wo_ref[...]) + bias(3))
    residual = x_ref[...].astype(f32) + (y_norm * gain(1) + bias(4))
    r_norm, r_inv = norm_parts(residual)
    normed = (r_norm * gain(2) + bias(5)).astype(bf16)
    c_ref[...] = normed

    @pl.when(step == 0)
    def _():
        for k in range(2, len(loads)):
            loads[k].wait()

    total = jnp.zeros((rows, 1), f32)
    ahead = dot_nn(normed, w1_ref[:, chunks[0]])
    for k, at in enumerate(chunks):
        pre = ahead + table_ref[11:12, at]
        if k + 1 < len(chunks):
            ahead = dot_nn(normed, w1_ref[:, chunks[k + 1]])
        cdf, pdf = normal_parts(pre)
        act = pre * cdf
        act_ref[:, at] = act
        slope_ref[:, at] = cdf + pre * pdf
        total = total + jnp.sum(act, axis=-1, keepdims=True)
    average = total / hidden
    total = jnp.zeros((rows, 1), f32)
    for at in chunks:
        centered = act_ref[:, at] - average
        total = total + jnp.sum(centered * centered, axis=-1, keepdims=True)
    m_inv = lax.rsqrt(total / hidden + epsilon)

    @pl.when(step == 0)
    def _():
        loads[1].wait()
        fixed_ref[...] = dot_nn(table_ref[8:16, :].astype(bf16), w2_ref[...])

    branch = jnp.zeros((rows, width), f32)
    for k in range(len(chunks) + 1):
        if k < len(chunks):
            at = chunks[k]
            n = (act_ref[:, at] - average) * m_inv
            act_ref[:, at] = n
            m_ref[:, at] = (n * table_ref[10:11, at] + table_ref[12:13, at]).astype(bf16)
        if k > 0:
            branch = branch + dot_nn(m_ref[:, chunks[k - 1]], w2_ref[chunks[k - 1], :])
    out_ref[...] = (residual + (branch + bias(6))).astype(bf16)

    position = step * rows + lax.broadcasted_iota(jnp.int32, (rows, 1), 0)
    d_out = jnp.where(position < len_ref[0], cot_ref[...].astype(f32), 0.0)
    d_w = d_out.astype(bf16)
    sums_ref[6] += fold(d_out)
    first = jnp.sum(d_out * fixed_ref[2:3, :], axis=-1, keepdims=True) / hidden
    second = jnp.sum(d_out * (branch - fixed_ref[4:5, :]), axis=-1, keepdims=True) / hidden
    d_c = jnp.zeros((rows, width), f32)
    ahead = dot_nt(d_w, w2_ref[chunks[0], :])
    for k in range(len(chunks) + 1):
        dm = ahead
        if k + 1 < len(chunks):
            ahead = dot_nt(d_w, w2_ref[chunks[k + 1], :])
        if k > 0:
            d_c = d_c + dot_nt(df_ref[:, chunks[k - 1]], w1_ref[:, chunks[k - 1]])
        if k < len(chunks):
            at = chunks[k]
            n = act_ref[:, at]
            wide_ref[0, :, at] += fold(dm * n)
            wide_ref[2, :, at] += fold(dm)
            du = (dm * table_ref[10:11, at] - first - n * second) * m_inv
            df = (du * slope_ref[:, at]).astype(bf16)
            df_ref[:, at] = df
            wide_ref[1, :, at] += fold(df.astype(f32))
    sums_ref[2] += fold(d_c * r_norm)
    sums_ref[5] += fold(d_c)
    d_r = d_out + norm_back(d_c, gain(2), r_norm, r_inv)
    dr_ref[...] = d_r
    sums_ref[1] += fold(d_r * y_norm)
    sums_ref[4] += fold(d_r)
    d_y = norm_back(d_r, gain(1), y_norm, y_inv).astype(bf16)
    dy_ref[...] = d_y
    sums_ref[3] += fold(d_y.astype(f32))
    do_ref[...] = (dot_nt(d_y, wo_ref[...]) * par_ref[SCALE_ROW : SCALE_ROW + 1, :]).astype(bf16)


def ffn(lengths, x, z, cot, wo, w1, w2, par, table, rows=256, chunk=512):
    tokens, width = x.shape
    hidden = w1.shape[1]
    by_row = lambda n: pl.BlockSpec((rows, n), lambda i: (i, 0))
    whole = lambda a: pl.BlockSpec(a.shape, lambda i: (0,) * a.ndim, pipeline_mode=pl.Buffered(1))
    anywhere = pl.BlockSpec(memory_space=pl.ANY)
    sds = jax.ShapeDtypeStruct
    bf16, f32 = jnp.bfloat16, jnp.float32
    outs = [(width, bf16), (width, bf16), (hidden, bf16), (hidden, bf16), (width, bf16), (width, f32), (width, bf16)]
    return pl.pallas_call(
        functools.partial(ffn_kernel, chunk),
        grid=(tokens // rows,),
        in_specs=[pl.BlockSpec(memory_space=pltpu.SMEM)]
        + [by_row(width)] * 3
        + [anywhere] * 3
        + [whole(par), whole(table)],
        out_specs=[by_row(n) for n, _ in outs]
        + [pl.BlockSpec((7, 8, width), lambda i: (0, 0, 0)), pl.BlockSpec((3, 8, hidden), lambda i: (0, 0, 0))],
        out_shape=[sds((tokens, n), d) for n, d in outs] + [sds((7, 8, width), f32), sds((3, 8, hidden), f32)],
        scratch_shapes=[pltpu.VMEM((rows, hidden), f32)] * 2
        + [pltpu.VMEM(w.shape, bf16) for w in (wo, w1, w2)]
        + [pltpu.VMEM((8, width), f32), pltpu.SemaphoreType.DMA((2 + hidden // chunk,))],
        compiler_params=pltpu.CompilerParams(vmem_limit_bytes=60 << 20),
        name="ffn_both",
    )(lengths, x, z, cot, wo, w1, w2, par, table)


head_size = 64


def head_lanes(values, second):
    lane = lax.broadcasted_iota(jnp.int32, values.shape, 1)
    keep = lane >= head_size if second else lane < head_size
    return jnp.where(keep, values, jnp.zeros_like(values))


def masked_scores(keys, queries, first, length):
    scores = dot_nt(keys, queries)
    key_pos = lax.broadcasted_iota(jnp.int32, scores.shape, 0)
    near = key_pos[first:]
    query_pos = first + lax.broadcasted_iota(jnp.int32, near.shape, 1)
    last = jnp.where((near <= query_pos) & (near < length), scores[first:], mask_fill)
    if first == 0:
        return last
    return jnp.concatenate((jnp.where(key_pos[:first] < length, scores[:first], mask_fill), last), axis=0)


def attend_unit(length, scale_ref, head, first, block, q_ref, k_ref, v_ref, z_ref, log_ref):
    rows, seen = slice(first, first + block), first + block
    scaling = jnp.bfloat16(head_size**-0.5)
    keys, values = k_ref[:seen, :], v_ref[:seen, :]
    mixed = []
    for h in range(2):
        queries = head_lanes(q_ref[rows, :], h) * scaling
        scores = masked_scores(keys, queries, first, length)
        top = jnp.max(scores, axis=0, keepdims=True)
        shifted = jnp.exp(scores - top)
        total = jnp.sum(shifted, axis=0, keepdims=True)
        log_ref[h : h + 1, rows] = top + jnp.log(total)
        attended = dot_tn(shifted.astype(jnp.bfloat16), values)
        mixed.append(attended * (scale_ref[head + h] / total).T)
    lane = lax.broadcasted_iota(jnp.int32, mixed[0].shape, 1)
    z_ref[rows, :] = jnp.where(lane < head_size, mixed[0], mixed[1]).astype(jnp.bfloat16)


def attend_kernel(block, len_ref, scale_ref, q_ref, k_ref, v_ref, z_ref, log_ref):
    for first in range(0, q_ref.shape[1], block):
        attend_unit(
            len_ref[0], scale_ref, pl.program_id(0) * 2, first, block,
            q_ref.at[0], k_ref.at[0], v_ref.at[0], z_ref, log_ref.at[0],
        )


def attend(lengths, head_scale, qkv, block=256):
    _, tokens, width = qkv.shape
    pairs = width // 128
    cols = lambda part: pl.BlockSpec((1, tokens, 128), lambda p: (part, 0, p))
    smem = pl.BlockSpec(memory_space=pltpu.SMEM)
    return pl.pallas_call(
        functools.partial(attend_kernel, min(block, tokens)),
        grid=(pairs,),
        in_specs=[smem, smem, cols(0), cols(1), cols(2)],
        out_specs=[
            pl.BlockSpec((tokens, 128), lambda p: (0, p)),
            pl.BlockSpec((1, 2, tokens), lambda p: (p, 0, 0)),
        ],
        out_shape=[
            jax.ShapeDtypeStruct((tokens, width), jnp.bfloat16),
            jax.ShapeDtypeStruct((pairs, 2, tokens), jnp.float32),
        ],
        compiler_params=pltpu.CompilerParams(vmem_limit_bytes=56 << 20),
        name="attend",
    )(lengths, head_scale, qkv, qkv, qkv)


def attend_back_unit(
    length, first, block, q_ref, k_ref, v_ref, do_ref, log_ref, dq_ref, dot_ref, dk_ref, dv_ref
):
    rows, seen = slice(first, first + block), first + block
    bf16, scaling = jnp.bfloat16, head_size**-0.5
    keys, values = k_ref[:seen, :], v_ref[:seen, :]
    mixed = []
    for h in range(2):
        queries = head_lanes(q_ref[rows, :], h) * bf16(scaling)
        grads = head_lanes(do_ref[rows, :], h)
        scores = masked_scores(keys, queries, first, length)
        weights = jnp.exp(scores - log_ref[h : h + 1, rows])
        products = weights * dot_nt(values, grads)
        total = jnp.sum(products, axis=0, keepdims=True)
        dot_ref[h : h + 1, rows] = total
        d_scores = (products - weights * total).astype(bf16)
        for ref, left, right in ((dv_ref, weights.astype(bf16), grads), (dk_ref, d_scores, queries)):
            part = dot_nn(left, right)
            if h == 0:
                ref[rows, :] = part[first:]
                if first:
                    ref[:first, :] += part[:first]
            else:
                ref[:seen, :] += part
        mixed.append(dot_tn(d_scores, keys))
    lane = lax.broadcasted_iota(jnp.int32, mixed[0].shape, 1)
    dq_ref[rows, :] = (jnp.where(lane < head_size, mixed[0], mixed[1]) * scaling).astype(bf16)


def attend_back_kernel(block, len_ref, q_ref, k_ref, v_ref, do_ref, log_ref, dqkv_ref, dot_ref, dk_ref, dv_ref):
    for first in range(0, do_ref.shape[0], block):
        attend_back_unit(
            len_ref[0], first, block, q_ref.at[0], k_ref.at[0], v_ref.at[0], do_ref, log_ref.at[0],
            dqkv_ref.at[0], dot_ref.at[0], dk_ref, dv_ref,
        )
    dqkv_ref[1] = dk_ref[...].astype(jnp.bfloat16)
    dqkv_ref[2] = dv_ref[...].astype(jnp.bfloat16)


def attend_back(lengths, qkv, d_attended, logs, block=256):
    _, tokens, width = qkv.shape
    pairs = width // 128
    cols = lambda part: pl.BlockSpec((1, tokens, 128), lambda p: (part, 0, p))
    per_pair = pl.BlockSpec((1, 2, tokens), lambda p: (p, 0, 0))
    return pl.pallas_call(
        functools.partial(attend_back_kernel, min(block, tokens)),
        grid=(pairs,),
        in_specs=[
            pl.BlockSpec(memory_space=pltpu.SMEM),
            cols(0),
            cols(1),
            cols(2),
            pl.BlockSpec((tokens, 128), lambda p: (0, p)),
            per_pair,
        ],
        out_specs=[pl.BlockSpec((3, tokens, 128), lambda p: (0, 0, p)), per_pair],
        out_shape=[
            jax.ShapeDtypeStruct((3, tokens, width), jnp.bfloat16),
            jax.ShapeDtypeStruct((pairs, 2, tokens), jnp.float32),
        ],
        scratch_shapes=[pltpu.VMEM((tokens, 128), jnp.float32)] * 2,
        compiler_params=pltpu.CompilerParams(vmem_limit_bytes=56 << 20),
        name="attend_back",
    )(lengths, qkv, qkv, qkv, d_attended, logs)


def project_kernel(x_ref, w_ref, gain_ref, bias_ref, a_ref, qkv_ref):
    width = x_ref.shape[1]
    normed, _ = norm_parts(x_ref[...].astype(jnp.float32))
    a = (normed * gain_ref[0:1, :] + bias_ref[0:1, :]).astype(jnp.bfloat16)
    a_ref[...] = a
    for part, row in ((0, 1), (1, None), (2, 2)):
        at = slice(part * width, (part + 1) * width)
        value = dot_nn(a, w_ref[:, at])
        if row is not None:
            value = value + bias_ref[row : row + 1, :]
        qkv_ref[part] = value.astype(jnp.bfloat16)


def project(x, w, gains, biases, rows=256):
    tokens, width = x.shape
    by_row = lambda n: pl.BlockSpec((rows, n), lambda i: (i, 0))
    whole = lambda a: pl.BlockSpec(a.shape, lambda i: (0,) * a.ndim, pipeline_mode=pl.Buffered(1))
    return pl.pallas_call(
        project_kernel,
        grid=(tokens // rows,),
        in_specs=[by_row(width), whole(w), whole(gains), whole(biases)],
        out_specs=[by_row(width), pl.BlockSpec((3, rows, width), lambda i: (0, i, 0))],
        out_shape=[
            jax.ShapeDtypeStruct((tokens, width), jnp.bfloat16),
            jax.ShapeDtypeStruct((3, tokens, width), jnp.bfloat16),
        ],
        compiler_params=pltpu.CompilerParams(vmem_limit_bytes=56 << 20),
        name="project",
    )(x, w, gains, biases)


def project_back_kernel(d_ref, x_ref, dr_ref, w_ref, gain_ref, dx_ref, sums_ref):
    @pl.when(pl.program_id(0) == 0)
    def _():
        sums_ref[...] = jnp.zeros_like(sums_ref)

    width = x_ref.shape[1]
    d_a = sum(dot_nt(d_ref[k], w_ref[:, k * width : (k + 1) * width]) for k in range(3))
    normed, inverse = norm_parts(x_ref[...].astype(jnp.float32))
    sums_ref[0] += fold(d_a * normed)
    sums_ref[1] += fold(d_a)
    sums_ref[2] += fold(d_ref[0].astype(jnp.float32))
    sums_ref[3] += fold(d_ref[2].astype(jnp.float32))
    back = norm_back(d_a, gain_ref[0:1, :], normed, inverse)
    dx_ref[...] = (dr_ref[...] + back).astype(jnp.bfloat16)


def project_back(d_qkv, x, d_r, w, gains, rows=256):
    tokens, width = x.shape
    by_row = pl.BlockSpec((rows, width), lambda i: (i, 0))
    whole = lambda a: pl.BlockSpec(a.shape, lambda i: (0,) * a.ndim, pipeline_mode=pl.Buffered(1))
    return pl.pallas_call(
        project_back_kernel,
        grid=(tokens // rows,),
        in_specs=[pl.BlockSpec((3, rows, width), lambda i: (0, i, 0)), by_row, by_row, whole(w), whole(gains)],
        out_specs=[by_row, pl.BlockSpec((4, 8, width), lambda i: (0, 0, 0))],
        out_shape=[
            jax.ShapeDtypeStruct((tokens, width), jnp.bfloat16),
            jax.ShapeDtypeStruct((4, 8, width), jnp.float32),
        ],
        compiler_params=pltpu.CompilerParams(vmem_limit_bytes=56 << 20),
        name="project_back",
    )(d_qkv, x, d_r, w, gains)


class Ops:
    def __init__(self, send, recv, local, place):
        self.send, self.recv, self.local, self.place = send, recv, local, place
        self.remotes = self.locals = 0
        self.now = []

    def do(self, action):
        self.now.append(action)

    def remote(self, src, dst, peer):
        k = self.remotes
        self.remotes += 1
        copy = pltpu.make_async_remote_copy(
            src_ref=src,
            dst_ref=dst,
            send_sem=self.send.at[k],
            recv_sem=self.recv.at[k],
            device_id=peer,
            device_id_type=MESH,
        )
        self.do(copy.start)
        return copy

    def copy(self, src, dst):
        copy = pltpu.make_async_copy(src, dst, self.local.at[self.locals])
        self.locals += 1
        self.do(copy.start)
        return copy


class FixedPlace(Place):
    def __init__(self, digits):
        super().__init__(digits)
        self.shifted = {}
        self.peers = {}
        for axis, n in enumerate(digits):
            for shift in range(-n, n + 1):
                self.shifted[axis, shift] = super().digit(axis, shift)
            for shift in (-1, 1):
                self.peers[axis, shift] = super().peer(axis, shift)

    def device(self, shifts):
        at = [self.shifted[axis, shift] for axis, shift in enumerate(shifts)]
        return (at[0] * self.digits[1] + at[1], at[2] * self.digits[3] + at[3])

    def greet_group(self, group):
        barrier = pltpu.get_barrier_semaphore()
        for shifts in group:
            pl.semaphore_signal(barrier, inc=1, device_id=self.device(shifts), device_id_type=MESH)
        pl.semaphore_wait(barrier, len(group))

    def digit(self, axis, shift):
        return self.shifted[axis, shift]

    def peer(self, axis, shift):
        return self.peers[axis, shift]


def plan_ticks(ops, pieces, stride):
    queue = [(start, 0, k) for k, (start, _) in enumerate(pieces)]
    heapq.heapify(queue)
    ticks, ends = [], {}
    while queue:
        at, age, k = heapq.heappop(queue)
        ops.now = []
        alive = next(pieces[k][1], "end") != "end"
        if ops.now:
            ticks.append(ops.now)
        if alive:
            heapq.heappush(queue, (at + stride, age - 1, k))
        else:
            ends[k] = len(ticks)
    return ticks, ends


def schedule(ops, pieces, stride, moments, times, scale):
    queue = [(start, 0, k) for k, (start, _, _) in enumerate(pieces)]
    floor = [earliest for _, earliest, _ in pieces]
    heapq.heapify(queue)
    parts = []
    while queue:
        at, age, k = heapq.heappop(queue)
        ops.now = []
        if next(pieces[k][2], "end") != "end":
            heapq.heappush(queue, (at + stride, age - 1, k))
        where = next((m for m, time in enumerate(times) if time >= at * scale), len(times) - 1)
        floor[k] = max(floor[k], where)
        parts.append((floor[k], at, len(parts), ops.now))
    parts.sort(key=lambda part: part[:3])
    ticks = [actions for _, _, _, actions in parts]
    table = {moment: [] for moment in moments}
    for number, (where, _, _, _) in enumerate(parts):
        table[moments[where]].append(number)
    return Hooks(ticks, table)


class Hooks:
    def __init__(self, ticks, moments):
        self.ticks, self.moments = ticks, moments

    def run(self, step, hook):
        for at in sorted(s for s, h in self.moments if h == hook):
            numbers = self.moments[at, hook]
            if numbers:

                @pl.when(step == at)
                def _(numbers=numbers):
                    for number in numbers:
                        for action in self.ticks[number]:
                            action()


def spread_ticks(first, count, moments, weights=None):
    weights = weights or [1] * len(moments)
    table, todo, used, past = {}, list(range(first, count)), 0, 0
    for moment, weight in zip(moments, weights):
        past += weight
        upto = len(todo) * past // sum(weights)
        table[moment] = todo[used:upto]
        used = upto
    return table


def rect(rows, cols):
    return (pl.ds(*rows), pl.ds(*cols))


def ways(n, turn):
    if n == 1:
        return []
    return [(s, (turn,) if n == 2 or s == n // 2 - 1 else (1, -1)) for s in range(n // 2)]


def copies_of(digits):
    return 1 + sum(len(directions) for n in digits[:3] for _, directions in ways(n, 1))


def gather_steps(ops, shard, full, rows, cols, order, turn):
    place = ops.place
    held, sends = set(), []

    def index(axis, slot):
        return slots(place, held, axis, slot, cols)[:4] + rect(rows, cols)

    own = ops.copy(shard.at[rect(rows, cols)], full.at[index(None, None)])
    first = True
    for axis in order:
        n = place.digits[axis]
        for step, directions in ways(n, turn):
            started = []
            for direction in directions:
                at = index(axis, place.digit(axis, -step * direction))
                src = shard.at[rect(rows, cols)] if first and step == 0 else full.at[at]
                started.append(ops.remote(src, full.at[at], place.peer(axis, direction)))
            yield
            for copy in started:
                ops.do(copy.wait_recv)
            sends += started
        held.add(axis)
        if first:
            ops.do(own.wait)
            first = False
    view = full.at[index(None, None)]
    copy = ops.remote(view, view, place.peer(3, 1))
    yield
    ops.do(copy.wait_recv)
    for copy in sends + [copy]:
        ops.do(copy.wait_send)


def add_into(target, source):
    return lambda: accumulate(target, source)


def staged_sums(digits, order, turn):
    left, plan = [0, 1, 2], []
    for axis in order:
        left.remove(axis)
        lead = tuple(digits[a] for a in left)
        for step, directions in reversed(ways(digits[axis], turn)):
            plan.append((tuple(left), [(axis, direction, step) for direction in directions], lead))
    return plan


def reduce_steps_of(ops, own, sent, stage, landed, slabs, finish, order, turn):
    place, sends = ops.place, []
    if stage is not None:
        local = ops.copy(own, stage)
    copy = ops.remote(sent, landed, place.peer(3, 1))
    yield
    if stage is not None:
        ops.do(local.wait)
    ops.do(copy.wait_recv)
    sends.append(copy)
    ops.do(add_into(landed, own if stage is None else stage))
    slabs = iter(slabs)
    every = (slice(None), slice(None))
    for left, batch, _ in staged_sums(place.digits, order, turn):
        started = []
        for axis, direction, step in batch:
            slot = place.digit(axis, (step + 1) * direction)
            src = landed.at[slots(place, left, axis, slot, (0, 0))[:3] + every]
            dst = next(slabs)
            copy = ops.remote(src, dst, place.peer(axis, direction))
            started.append((axis, direction * step, dst, copy))
        yield
        for axis, shift, dst, copy in started:
            ops.do(copy.wait_recv)
            sends.append(copy)
            view = slots(place, left, axis, place.digit(axis, shift), (0, 0))[:3] + every
            ops.do(add_into(landed.at[view], dst))
    ops.do(lambda: finish(landed[place.at[:3]].astype(jnp.float32)))
    for copy in sends:
        ops.do(copy.wait_send)
    yield


def slab_shapes(digits, rows, cols, order, turn, dtype):
    return [
        pltpu.VMEM(lead + (rows, cols), dtype) for _, batch, lead in staged_sums(digits, order, turn) for _ in batch
    ]


GATHER_ORDERS = ((0, 1, 2), (0, 2, 1), (0, 1, 2), (0, 2, 1), (1, 2, 0), (0, 2, 1), (0, 1, 2), (0, 2, 1), (2, 1, 0))
X, Y, Z, W = (1, 2, 0), (2, 1, 0), (0, 1, 2), (0, 2, 1)
REDUCE_ORDERS = (Z, X, Y, Z, X, W, Y, X, Z, (2, 0, 1), X, (2, 0, 1), X, X, Y, X)
LAST_ROUNDS = 2.5
OUT_PACE = 0.0
BACK_HOOKS = (1, 2, 3)
LAST_HOOKS = (0, 1, 2, 3)
LAST_ORDERS = (W, Y, X, Y, X, Z, Z, Y, X, X, Z, Y, X, Y)


def blocks_of(shape, rows, cols):
    rows, cols = min(rows, shape[0]), min(cols, shape[1])
    return [((r, rows), (c, cols)) for r in range(0, shape[0], rows) for c in range(0, shape[1], cols)]


def semaphores(copies, local):
    return [
        pltpu.SemaphoreType.DMA((copies,)),
        pltpu.SemaphoreType.DMA((copies,)),
        pltpu.SemaphoreType.DMA((local,)),
    ]


HEADS_WIDE = 256
QUERY_BLOCK = 256
SCALE_ROW = 13


def front_kernel(
    digits, counts,
    len_ref, scale_ref, x_ref, w_qkv, w_out, w_fc1, w_fc2, gain_ref, bias_ref, mid_ref, ffb_ref,
    a_ref, qkv_ref, z_ref, log_ref, wqkv_out, wout_ref, w1_ref, w2_ref, par_ref, wide_ref,
    wqkv_ref, small_ref, qkv_shard, out_shard, fc1_shard, fc2_shard, small_shard, mine_ref, send, recv, local,
):
    step = pl.program_id(0)
    steps = counts["steps"]
    f32, bf16 = jnp.float32, jnp.bfloat16
    tokens, width = x_ref.shape
    place = FixedPlace(digits)
    ops = Ops(send, recv, local, place)
    pieces, number, start = [], 0, 0.0
    whole = lambda ref: ((0, ref.shape[0]), (0, ref.shape[1]))
    pieces.append((0.0, gather_steps(ops, small_shard, small_ref, *whole(small_shard), GATHER_ORDERS[0], 1)))
    for s in range(steps):
        for part in range(3):
            cols = (part * width + s * HEADS_WIDE, HEADS_WIDE)
            order, turn = GATHER_ORDERS[number % 9], 1 - number % 2 * 2
            number += 1
            pieces.append((start, gather_steps(ops, qkv_shard, wqkv_ref, (0, qkv_shard.shape[0]), cols, order, turn)))
            start += 0.5
    for shard, full in ((out_shard, wout_ref), (fc1_shard, w1_ref), (fc2_shard, w2_ref)):
        for rows, cols in blocks_of(shard.shape, 32, 512):
            order, turn = GATHER_ORDERS[number % 9], 1 - number % 2 * 2
            number += 1
            pieces.append((start, gather_steps(ops, shard, full, rows, cols, order, turn)))
            start += 1.0
    ticks, ends = plan_ticks(ops, pieces, 3.0)
    ready = [max(ends[k] for k in range(4 + 3 * s)) for s in range(steps)]
    blocks = tokens // QUERY_BLOCK
    units = 2 * blocks
    table = {(s, "head"): [] for s in range(steps)}
    moments = [(s, u) for s in range(steps) for u in range(units)]
    spread = spread_ticks(ready[0], len(ticks), moments, [u % blocks + 1 for _, u in moments])
    table.update(spread)
    table[0, "head"] = list(range(ready[0]))
    for s in range(1, steps):
        late = [(m, t) for m in moments if m[0] >= s for t in table[m] if t < ready[s]]
        for moment, t in late:
            table[moment].remove(t)
            table[s, "head"].append(t)
    hooks = Hooks(ticks, table)

    total = digits[0] * digits[1] * digits[2] * digits[3]

    @pl.when(step == 0)
    def _():
        for shard, w in ((qkv_shard, w_qkv), (out_shard, w_out), (fc1_shard, w_fc1), (fc2_shard, w_fc2)):
            shard[...] = w[...].astype(bf16)
        me = ((place.at[0] * digits[1] + place.at[1]) * digits[2] + place.at[2]) * digits[3] + place.at[3]
        mine_ref[...] = jnp.zeros_like(mine_ref)
        for k, (row, ref) in enumerate(((0, gain_ref), (3, bias_ref), (10, mid_ref), (11, ffb_ref))):
            mine_ref[k // 2, row : row + ref.shape[0], 0 : ref.shape[1]] = ref[...]
        narrow = pltpu.roll(mine_ref[0], me * gain_ref.shape[1] % 128, 1)
        wide = pltpu.roll(mine_ref[1], me * mid_ref.shape[1] % 128, 1)
        small_shard[...] = (narrow + wide).astype(bf16)
        place.greet()

    hooks.run(step, "head")

    @pl.when(step == 0)
    def _():
        for ref in (par_ref, wide_ref):
            own = ref.shape[1] // total
            for lane in range(0, ref.shape[1], 128):
                block = None
                for d in range(lane // own, max((lane + 128) // own, lane // own + 1)):
                    i3, rest = d % digits[3], d // digits[3]
                    i2, rest = rest % digits[2], rest // digits[2]
                    i1, i0 = rest % digits[1], rest // digits[1]
                    value = small_ref[i0, i1, i2, i3].astype(f32)
                    block = value if block is None else block + value
                ref[:, lane : lane + 128] = block
        lane = lax.broadcasted_iota(jnp.int32, (1, 128), 1)
        for pair in range(width // 128):
            scales = jnp.where(lane < head_size, scale_ref[2 * pair], scale_ref[2 * pair + 1])
            par_ref[SCALE_ROW : SCALE_ROW + 1, pair * 128 : pair * 128 + 128] = scales
        for first in range(0, tokens, QUERY_BLOCK):
            rows = slice(first, first + QUERY_BLOCK)
            normed, _ = norm_parts(x_ref[rows, :].astype(f32))
            a_ref[rows, :] = (normed * par_ref[0:1, :] + par_ref[3:4, :]).astype(bf16)

    keep = pltpu.make_async_copy(wqkv_ref, wqkv_out, local.at[local.shape[0] - 1])

    @pl.when(step == steps - 1)
    def _():
        keep.start()

    at = pl.multiple_of(step * HEADS_WIDE, HEADS_WIDE)
    for part, row in ((0, 4), (1, None), (2, 5)):
        cols = pl.ds(pl.multiple_of(part * width + at, HEADS_WIDE), HEADS_WIDE)
        value = dot_nn(a_ref[...], wqkv_ref[:, :, :, :, :, cols].reshape(width, HEADS_WIDE))
        if row is not None:
            value = value + par_ref[row : row + 1, pl.ds(at, HEADS_WIDE)]
        qkv_ref[part] = value.astype(bf16)
    unit = 0
    for pair in range(HEADS_WIDE // 128):
        lanes = slice(pair * 128, pair * 128 + 128)
        for first in range(0, tokens, QUERY_BLOCK):
            attend_unit(
                len_ref[0], scale_ref, (step * (HEADS_WIDE // 128) + pair) * 2, first, QUERY_BLOCK,
                qkv_ref.at[0, :, lanes], qkv_ref.at[1, :, lanes], qkv_ref.at[2, :, lanes],
                z_ref.at[:, lanes], log_ref.at[pair],
            )
            hooks.run(step, unit)
            unit += 1

    @pl.when(step == steps - 1)
    def _():
        keep.wait()


def front(digits, lengths, head_scale, x, weights, small_parts):
    tokens, width = x.shape
    hidden = weights[2].shape[1]
    steps = width // HEADS_WIDE
    bf16, f32 = jnp.bfloat16, jnp.float32
    sds = jax.ShapeDtypeStruct
    anywhere = pl.BlockSpec(memory_space=pl.ANY)
    smem = pl.BlockSpec(memory_space=pltpu.SMEM)
    fixed = lambda shape: pl.BlockSpec(shape, lambda s: (0,) * len(shape), pipeline_mode=pl.Buffered(1))
    per_step = HEADS_WIDE // 128
    pieces = 1 + 3 * steps + sum(len(blocks_of(w.shape, 32, 512)) for w in weights[1:])
    return pl.pallas_call(
        functools.partial(front_kernel, digits, {"steps": steps}),
        grid=(steps,),
        in_specs=[smem, smem] + [fixed(v.shape) for v in (x, *weights, *small_parts)],
        out_specs=[
            fixed((tokens, width)),
            pl.BlockSpec((3, tokens, HEADS_WIDE), lambda s: (0, 0, s)),
            pl.BlockSpec((tokens, HEADS_WIDE), lambda s: (0, s)),
            pl.BlockSpec((per_step, 2, tokens), lambda s: (s, 0, 0)),
            anywhere,
            anywhere,
            anywhere,
            anywhere,
            fixed((16, width)),
            fixed((16, hidden)),
        ],
        out_shape=[
            sds((tokens, width), bf16),
            sds((3, tokens, width), bf16),
            sds((tokens, width), bf16),
            sds((width // 128, 2, tokens), f32),
        ]
        + [sds(digits + w.shape, bf16) for w in weights]
        + [sds((16, width), f32), sds((16, hidden), f32)],
        scratch_shapes=[pltpu.VMEM(digits + weights[0].shape, bf16), pltpu.VMEM(digits + (16, 128), bf16)]
        + [pltpu.VMEM(w.shape, bf16) for w in weights]
        + [pltpu.VMEM((16, 128), bf16), pltpu.VMEM((2, 16, 128), f32)]
        + semaphores(pieces * copies_of(digits), pieces + 1),
        compiler_params=pltpu.CompilerParams(
            collective_id=2, has_side_effects=True, vmem_limit_bytes=60 << 20
        ),
        name="front",
    )(lengths, head_scale, x, *weights, *small_parts)


def back_kernel(
    digits, stages,
    len_ref, q_ref, k_ref, v_ref, do_ref, log_ref, c_ref, df_ref, z_ref, dy_ref, g2_ref,
    dqkv_ref, dot_ref, gout_ref, s1_ref, s2_ref,
    dk_ref, dv_ref, made_ref, *scratch,
):
    step, steps = pl.program_id(0), stages["steps"]
    half = steps // 2
    bf16 = jnp.bfloat16
    place = FixedPlace(digits)
    send, recv, local = scratch[-3:]
    ops = Ops(send, recv, local, place)
    staging, rest = scratch[:4], list(scratch[4:-3])
    tokens = q_ref.shape[1]
    units = tokens // QUERY_BLOCK
    moments, times, now = [(0, "head")], [0.0], 0.0
    for s in range(steps):
        if s < half:
            now += 2.7
            moments.append((s, "made"))
            times.append(now)
        else:
            now += 1.3
        for u in range(units):
            now += 0.52 * (u + 1)
            if u in BACK_HOOKS:
                moments.append((s, u))
                times.append(now)
    pieces, staged = [], 0
    all_slots = (slice(None),) * 3
    for start, which, rows, cols, order, turn, many in stages["pieces"]:
        grad, out = ((g2_ref, s2_ref), (made_ref, s1_ref))[which]
        landed, slabs = rest[0], rest[1 : 1 + many]
        del rest[: 1 + many]
        own = grad.at[all_slots + (place.at[3],) + rect(rows, cols)]
        sent = grad.at[all_slots + (place.digit(3, 1),) + rect(rows, cols)]
        stage, earliest = None, 0
        if which == 0:
            stage = staging[staged % 4]
            staged += 1
        else:
            earliest = moments.index((cols[0] // (made_ref.shape[-1] // half), "made"))

        def finish(value, out=out, rows=rows, cols=cols):
            out[rows[0] : rows[0] + rows[1], cols[0] : cols[0] + cols[1]] = value

        pieces.append(
            (start, earliest, reduce_steps_of(ops, own, sent, stage, landed, slabs, finish, order, turn))
        )
    stride = stages["stride"]
    span = max(start for start, _, _ in pieces) + 5 * stride
    hooks = schedule(ops, pieces, stride, moments, times, now / span)

    @pl.when(step == 0)
    def _():
        place.greet()

    hooks.run(step, "head")

    @pl.when(step < half)
    def _():
        wide = df_ref.shape[1]
        made = dot_tn(c_ref[...], df_ref[...]).astype(bf16)
        cols = pl.ds(pl.multiple_of(step * wide, wide), wide)
        made_ref[:, :, :, :, :, cols] = made.reshape(made_ref.shape[:5] + (wide,))

    hooks.run(step, "made")

    @pl.when(step >= half)
    def _():
        gout_ref[...] = dot_tn(z_ref[...], dy_ref[...]).astype(bf16)

    for unit in range(units):
        attend_back_unit(
            len_ref[0], unit * QUERY_BLOCK, QUERY_BLOCK, q_ref.at[0], k_ref.at[0], v_ref.at[0], do_ref, log_ref.at[0],
            dqkv_ref.at[0], dot_ref.at[0], dk_ref, dv_ref,
        )
        if unit == units - 1:
            dqkv_ref[1] = dk_ref[...].astype(bf16)
            dqkv_ref[2] = dv_ref[...].astype(bf16)
        hooks.run(step, unit)


def back(digits, lengths, qkv, d_attended, logs, c, d_f, z, d_y, grad_fc2):
    _, tokens, width = qkv.shape
    hidden = d_f.shape[1]
    pairs = width // 128
    half = pairs // 2
    bf16, f32 = jnp.bfloat16, jnp.float32
    sds = jax.ShapeDtypeStruct
    anywhere = pl.BlockSpec(memory_space=pl.ANY)
    cols = lambda part: pl.BlockSpec((1, tokens, 128), lambda p: (part, 0, p))
    per_pair = pl.BlockSpec((1, 2, tokens), lambda p: (p, 0, 0))
    fixed = lambda shape: pl.BlockSpec(shape, lambda s: (0,) * len(shape), pipeline_mode=pl.Buffered(1))
    early = pl.BlockSpec((tokens, hidden // half), lambda p: (0, jnp.minimum(p, half - 1)))
    late = pl.BlockSpec((tokens, width // half), lambda p: (0, jnp.maximum(p - half, 0)))
    total = digits[0] * digits[1] * digits[2] * digits[3]
    shapes = (grad_fc2.shape[4:], (width // total, hidden))
    listed = [[(which, *piece) for piece in blocks_of(shape, 32, 512)] for which, shape in enumerate(shapes)]
    mixed = []
    while any(listed):
        for some in listed:
            mixed += some[:2]
            del some[:2]
    pieces, scratch = [], []
    for number, (which, rows, at) in enumerate(mixed):
        order, turn = REDUCE_ORDERS[number % len(REDUCE_ORDERS)], 1 - number % 2 * 2
        slabs = slab_shapes(digits, rows[1], at[1], order, turn, bf16)
        pieces.append((float(number), which, rows, at, order, turn, len(slabs)))
        scratch += [pltpu.VMEM(digits[:3] + (rows[1], at[1]), bf16)] + slabs
    stage = pltpu.VMEM(digits[:3] + (mixed[0][1][1], mixed[0][2][1]), bf16)
    return pl.pallas_call(
        functools.partial(back_kernel, digits, {"steps": pairs, "pieces": pieces, "stride": 4.0}),
        grid=(pairs,),
        in_specs=[
            pl.BlockSpec(memory_space=pltpu.SMEM),
            cols(0),
            cols(1),
            cols(2),
            pl.BlockSpec((tokens, 128), lambda p: (0, p)),
            per_pair,
            fixed(c.shape),
            early,
            fixed(z.shape),
            late,
            anywhere,
        ],
        out_specs=[
            pl.BlockSpec((3, tokens, 128), lambda p: (0, 0, p)),
            per_pair,
            pl.BlockSpec((width, width // half), lambda p: (0, jnp.maximum(p - half, 0))),
            fixed(shapes[1]),
            fixed(shapes[0]),
        ],
        out_shape=[
            sds((3, tokens, width), bf16),
            sds((pairs, 2, tokens), f32),
            sds((width, width), bf16),
            sds(shapes[1], f32),
            sds(shapes[0], f32),
        ],
        scratch_shapes=[pltpu.VMEM((tokens, 128), f32)] * 2
        + [pltpu.VMEM(digits + shapes[1], bf16)]
        + [stage] * 4
        + scratch
        + semaphores(len(scratch), len(pieces)),
        compiler_params=pltpu.CompilerParams(
            collective_id=3, has_side_effects=True, vmem_limit_bytes=60 << 20
        ),
        name="back",
    )(lengths, qkv, qkv, qkv, d_attended, logs, c, d_f, z, d_y, grad_fc2)


def sum_direct(ops, block, first, second, result):
    place = ops.place
    digits = place.digits
    plane = [(0, a, b, c) for a in range(digits[1]) for b in range(digits[2]) for c in range(digits[3])][1:]
    copies = []
    for k, shifts in enumerate(plane):
        to = [place.digit(axis, shift) for axis, shift in enumerate(shifts)]
        src = block.at[:, to[1], to[2], to[3]]
        copies.append(ops.remote(src, first.at[k], place.device(shifts)))
    yield
    for copy in copies:
        ops.do(copy.wait_recv)

    def add_plane():
        total = block[:, place.at[1], place.at[2], place.at[3]]
        for k in range(len(plane)):
            total = total + first[k]
        result[...] = total

    ops.do(add_plane)
    others = []
    for shift in range(1, digits[0]):
        src = result.at[place.digit(0, shift)]
        others.append(ops.remote(src, second.at[shift - 1], place.device((shift, 0, 0, 0))))
    yield
    for copy in others:
        ops.do(copy.wait_recv)
    for copy in copies + others:
        ops.do(copy.wait_send)
    yield


def direct_group(digits):
    plane = [(0, a, b, c) for a in range(digits[1]) for b in range(digits[2]) for c in range(digits[3])][1:]
    return plane + [(shift, 0, 0, 0) for shift in range(1, digits[0])]


def last_kernel(
    digits, stages,
    a_ref, d_ref, wq_ref, wk_ref, wv_ref, x_hbm, dr_hbm, par_ref, sums_ref, wide_ref, dot_ref, scale_ref, gout_ref,
    dx_ref, sqkv_ref, sout_ref, gain_ref, bias_ref, mid_ref, ffb_ref, dscale_ref,
    da_ref, made_ref, rows_ref, block_ref, late_ref, first_ref, second_ref, plane_ref, found_ref, stage_ref, x_ref, dr_ref, load_sems, *scratch,
):
    step, steps = pl.program_id(0), stages["steps"]
    half = steps // 2
    f32, bf16 = jnp.float32, jnp.bfloat16
    place = FixedPlace(digits)
    send, recv, local = scratch[-3:]
    ops = Ops(send, recv, local, place)
    rest = list(scratch[:-3])
    tokens, width = x_ref.shape
    blocks = tokens // QUERY_BLOCK
    moments, times, now = [(0, "head"), (0, "block")], [0.0, 0.01], 0.0
    for s in range(half):
        now += 3.0
        moments.append((s, "made"))
        times.append(now)
    for s in range(half, steps):
        for b in range(blocks):
            now += 0.85
            if b in LAST_HOOKS:
                moments.append((s, b))
                times.append(now)
    for b in range(blocks):
        now += 1.0
        moments.append((steps - 1, "norm%d" % b))
        times.append(now)
    moments.append((steps - 1, "end"))
    times.append(1e9)
    pieces = []
    all_slots = (slice(None),) * 3
    sources = {"small": block_ref, "qkv": made_ref, "out": gout_ref}
    for start, name, cols, order, turn, many in stages["pieces"]:
        landed, slabs = rest[0], rest[1 : 1 + many]
        del rest[: 1 + many]
        source = sources[name]
        view = (slice(None), pl.ds(*cols))
        own = source.at[all_slots + (place.at[3],) + view]
        sent = source.at[all_slots + (place.digit(3, 1),) + view]
        stage, earliest = None, int(name == "small")
        if name == "out":
            stage = stage_ref.at[cols[0] // cols[1]]
        if name == "qkv":
            earliest = moments.index((cols[0] % width // HEADS_WIDE, "made"))
        out = {"small": found_ref, "qkv": sqkv_ref, "out": sout_ref}[name]

        def finish(value, out=out, cols=cols):
            out[:, cols[0] : cols[0] + cols[1]] = value

        pieces.append(
            (start, earliest, reduce_steps_of(ops, own, sent, stage, landed, slabs, finish, order, turn))
        )
    stride = stages["stride"]
    span = max(start for start, _, _ in pieces) + LAST_ROUNDS * stride
    late_key = span + 0.01
    pieces.append((late_key, len(moments) - 1, sum_direct(ops, late_ref, first_ref, second_ref, plane_ref)))
    hooks = schedule(ops, pieces, stride, moments, times, now / span)

    loads = [
        pltpu.make_async_copy(src, dst, load_sems.at[n])
        for n, (src, dst) in enumerate(((x_hbm, x_ref), (dr_hbm, dr_ref)))
    ]

    @pl.when(step == 0)
    def _():
        place.greet_group(direct_group(digits))
        da_ref[...] = jnp.zeros_like(da_ref)
        rows_ref[...] = jnp.zeros_like(rows_ref)

    hooks.run(step, "head")

    @pl.when(step == 0)
    def _():
        for row, k in ((1, 1), (2, 2), (6, 3), (7, 4), (8, 5), (9, 6)):
            rows_ref[row : row + 1, :] = jnp.sum(sums_ref[k], axis=0, keepdims=True)
        wide = [jnp.sum(wide_ref[k], axis=0, keepdims=True) for k in range(3)]
        dots = [sum(dot_ref[p, :, lane : lane + 128] for lane in range(0, tokens, 128)) for p in range(dot_ref.shape[0])]
        for d, slot, lane, lane_wide in small_slots(digits, width, wide_ref.shape[2]):
            block_ref[slot + (slice(0, 16),)] = rows_ref[:, lane : lane + 128]
            for k in range(3):
                block_ref[slot + (slice(10 + k, 11 + k),)] = wide[k][:, lane_wide : lane_wide + 128]
            for p, value in enumerate(dots):
                block_ref[slot + (slice(16 + 2 * p, 18 + 2 * p),)] = value

    hooks.run(step, "block")

    @pl.when(step == 0)
    def _():
        for load in loads:
            load.start()


    @pl.when(step < half)
    def _():
        at = pl.multiple_of(step * HEADS_WIDE, HEADS_WIDE)
        for part in range(3):
            made = dot_tn(a_ref[...], d_ref[part]).astype(bf16)
            cols = pl.ds(pl.multiple_of(part * width + at, HEADS_WIDE), HEADS_WIDE)
            made_ref[:, :, :, :, :, cols] = made.reshape(made_ref.shape[:5] + (HEADS_WIDE,))
        for part, row in ((0, 4), (2, 5)):
            rows_ref[row : row + 1, pl.ds(at, HEADS_WIDE)] = jnp.sum(d_ref[part].astype(f32), axis=0, keepdims=True)

    hooks.run(step, "made")
    end = step == steps - 1

    @pl.when(end)
    def _():
        for load in loads:
            load.wait()

    for b in range(blocks):

        @pl.when(step >= half)
        def _(b=b):
            rows = slice(b * QUERY_BLOCK, (b + 1) * QUERY_BLOCK)
            total = da_ref[rows, :]
            for part, w_ref in enumerate((wq_ref, wk_ref, wv_ref)):
                total = total + dot_nt(d_ref[part, rows, :], w_ref[...])
            da_ref[rows, :] = total

        hooks.run(step, b)
    for b in range(blocks):

        @pl.when(end)
        def _(b=b):
            rows = slice(b * QUERY_BLOCK, (b + 1) * QUERY_BLOCK)
            normed, inverse = norm_parts(x_ref[rows, :].astype(f32))
            d_a = da_ref[rows, :]
            rows_ref[0:1, :] += jnp.sum(d_a * normed, axis=0, keepdims=True)
            rows_ref[3:4, :] += jnp.sum(d_a, axis=0, keepdims=True)
            dx_ref[rows, :] = (dr_ref[rows, :] + norm_back(d_a, par_ref[0:1, :], normed, inverse)).astype(bf16)

        hooks.run(step, "norm%d" % b)

    @pl.when(end)
    def _():
        for d, slot, lane, _ in small_slots(digits, width, wide_ref.shape[2]):
            late_ref[slot] = rows_ref[0:8, lane : lane + 128]

    hooks.run(step, "end")

    @pl.when(end)
    def _():
        late = plane_ref[place.at[0]]
        for k in range(digits[0] - 1):
            late = late + second_ref[k]
        me = ((place.at[0] * digits[1] + place.at[1]) * digits[2] + place.at[2]) * digits[3] + place.at[3]
        row = lax.broadcasted_iota(jnp.int32, (8, 128), 0)
        swapped = (row == 0) | ((row >= 3) & (row <= 5))
        found_ref[0:8, :] = jnp.where(swapped, late, found_ref[0:8, :])
        own, own_wide = gain_ref.shape[1], mid_ref.shape[1]
        narrow = pltpu.roll(found_ref[0:16, :], (128 - me * own % 128) % 128, 1)
        broad = pltpu.roll(found_ref[0:16, :], (128 - me * own_wide % 128) % 128, 1)
        gain_ref[...] = narrow[0:3, 0:own]
        bias_ref[...] = narrow[3:10, 0:own]
        mid_ref[...] = broad[10:11, 0:own_wide]
        ffb_ref[...] = broad[11:13, 0:own_wide]
        heads = dscale_ref.shape[1]
        dscale_ref[...] = jnp.sum(found_ref[16 : 16 + heads, :].T, axis=0, keepdims=True) / scale_ref[...]


def small_slots(digits, width, hidden):
    total = digits[0] * digits[1] * digits[2] * digits[3]
    listed = []
    for d in range(total):
        i3, left = d % digits[3], d // digits[3]
        i2, left = left % digits[2], left // digits[2]
        slot = (left // digits[1], left % digits[1], i2, i3)
        listed.append((d, slot, d * (width // total) // 128 * 128, d * (hidden // total) // 128 * 128))
    return listed


def last(digits, a, d_qkv, w_qkv, x, d_r, par, sums, wide, dots, head_scale, grad_out):
    tokens, width = x.shape
    hidden = wide.shape[2]
    half = width // HEADS_WIDE
    bf16, f32 = jnp.bfloat16, jnp.float32
    sds = jax.ShapeDtypeStruct
    fixed = lambda shape: pl.BlockSpec(shape, lambda s: (0,) * len(shape), pipeline_mode=pl.Buffered(1))
    total = digits[0] * digits[1] * digits[2] * digits[3]
    rows = width // total
    small_rows = 16 + 2 * dots.shape[0]
    pieces, scratch = [], []

    def add(start, name, height, cols, order, kind):
        turn = 1 - len(pieces) % 2 * 2
        slabs = slab_shapes(digits, height, cols[1], order, turn, kind)
        pieces.append((start, name, cols, order, turn, len(slabs)))
        scratch.extend([pltpu.VMEM(digits[:3] + (height, cols[1]), kind)] + slabs)

    for k in range(2):
        add(OUT_PACE * k, "out", rows, (k * (width // 2), width // 2), LAST_ORDERS[k], bf16)
    add(1.0, "small", small_rows, (0, 128), X, f32)
    number = 2
    for s in range(half):
        for part in range(3):
            cols = (part * width + s * HEADS_WIDE, HEADS_WIDE)
            add(0.5 * number + 0.5, "qkv", rows, cols, LAST_ORDERS[number % len(LAST_ORDERS)], bf16)
            number += 1
    weight = lambda part: pl.BlockSpec((width, HEADS_WIDE), lambda s: (0, part * half + jnp.maximum(s - half, 0)))
    smalls = [(3, rows), (7, rows), (1, hidden // total), (2, hidden // total), (1, head_scale.shape[1])]
    plane = digits[1] * digits[2] * digits[3]
    return pl.pallas_call(
        functools.partial(last_kernel, digits, {"steps": 2 * half, "pieces": pieces, "stride": 3.0}),
        grid=(2 * half,),
        in_specs=[fixed(a.shape), pl.BlockSpec((3, tokens, HEADS_WIDE), lambda s: (0, 0, s % half))]
        + [weight(part) for part in range(3)]
        + [pl.BlockSpec(memory_space=pl.ANY)] * 2
        + [fixed(v.shape) for v in (par, sums, wide, dots, head_scale)]
        + [pl.BlockSpec(memory_space=pl.ANY)],
        out_specs=[fixed(s) for s in [(tokens, width), (rows, 3 * width), (rows, width)] + smalls],
        out_shape=[sds((tokens, width), bf16), sds((rows, 3 * width), f32), sds((rows, width), f32)]
        + [sds(s, f32) for s in smalls],
        scratch_shapes=[
            pltpu.VMEM((tokens, width), f32),
            pltpu.VMEM(digits + (rows, 3 * width), bf16),
            pltpu.VMEM((16, width), f32),
            pltpu.VMEM(digits + (small_rows, 128), f32),
            pltpu.VMEM(digits + (8, 128), f32),
            pltpu.VMEM((plane - 1, digits[0], 8, 128), f32),
            pltpu.VMEM((digits[0] - 1, 8, 128), f32),
            pltpu.VMEM((digits[0], 8, 128), f32),
            pltpu.VMEM((small_rows, 128), f32),
            pltpu.VMEM((2,) + digits[:3] + (rows, width // 2), bf16),
            pltpu.VMEM(x.shape, bf16),
            pltpu.VMEM(d_r.shape, f32),
            pltpu.SemaphoreType.DMA((2,)),
        ]
        + scratch
        + semaphores(len(scratch) + plane + digits[0], 2),
        compiler_params=pltpu.CompilerParams(
            collective_id=4, has_side_effects=True, vmem_limit_bytes=60 << 20
        ),
        name="last",
    )(a, d_qkv, w_qkv, w_qkv, w_qkv, x, d_r, par, sums, wide, dots, head_scale, grad_out)


def settle_kernel(count, *refs):
    for k in range(count):
        refs[count + k][...] = refs[k][...]


def settle(arrays, steps=4):
    def block(shape):
        if shape[0] % (8 * steps) == 0:
            return pl.BlockSpec((shape[0] // steps, shape[1]), lambda s: (s, 0))
        return pl.BlockSpec(shape, lambda s: (0, 0))

    blocks = [block(a.shape) for a in arrays]
    return pl.pallas_call(
        functools.partial(settle_kernel, len(arrays)),
        grid=(steps,),
        in_specs=blocks,
        out_specs=blocks,
        out_shape=[jax.ShapeDtypeStruct(a.shape, a.dtype) for a in arrays],
        compiler_params=pltpu.CompilerParams(vmem_limit_bytes=60 << 20),
        name="settle",
    )(*arrays)


def plain_gather(digits, weights, small_parts):
    small = jnp.concatenate([to_bf16(v).reshape(-1) for v in small_parts])
    small = jnp.pad(small, (0, 2048 - small.shape[0])).reshape(16, 128)
    shards_in = [to_bf16(w).reshape(tiled_rows(*w.shape)) for w in weights] + [small]
    gathered = gather_all(digits, shards_in)
    fulls = [g.reshape((-1, w.shape[1])) for g, w in zip(gathered, weights)]
    smalls, parts, used = gathered[4].reshape(-1, 2048), [], 0
    for v in small_parts:
        block = smalls[:, used : used + v.size].reshape((-1,) + (v.shape if v.ndim == 2 else (1,) + v.shape))
        parts.append(block.transpose(1, 0, 2).reshape(block.shape[1], -1).astype(jnp.float32))
        used += v.size
    par = jnp.pad(jnp.concatenate(parts[:2]), ((0, 6), (0, 0)))
    table = jnp.pad(jnp.concatenate(parts[2:]), ((10, 3), (0, 0)))
    return fulls, par, table


def plain_reduce(digits, weights, grads, small_parts, small_grads):
    total = digits[0] * digits[1] * digits[2] * digits[3]
    block = [v.reshape(v.shape[0], total, -1).transpose(1, 0, 2).reshape(total, -1) for v in small_grads[:-1]]
    block.append(jnp.broadcast_to(small_grads[-1][None], (total, small_grads[-1].shape[0])))
    block = jnp.concatenate(block, axis=1)
    block = jnp.pad(block, ((0, 0), (0, 1024 - block.shape[1]))).reshape(digits + (8, 128))
    blocks = [to_bf16(g).reshape(digits + tiled_rows(*w.shape)) for g, w in zip(grads, weights)]
    summed = reduce_all(digits, blocks + [block])
    flat, used, owned = summed[4].reshape(-1), 0, []
    for v in small_parts:
        owned.append(flat[used : used + v.size].reshape(v.shape))
        used += v.size
    return [g.reshape(w.shape) for g, w in zip(summed[:4], weights)] + owned


def shards(
    digits, tokens, lengths, cotangent, w_qkv, w_out, w_fc1, w_fc2, norm_gain, norm_bias, mid_gain, ff_bias, head_scale
):
    weights = (w_qkv, w_out, w_fc1, w_fc2)
    small_parts = (norm_gain, norm_bias, mid_gain, ff_bias)
    heads = head_scale.shape[0]
    total = digits[0] * digits[1] * digits[2] * digits[3]
    tiled = w_qkv.shape[0] % 16 == 0
    if tiled:
        normed_in, qkv, mixed, logs, full_qkv, full_out, full_fc1, full_fc2, par, table = front(
            digits, lengths, head_scale, tokens, weights, (norm_gain, norm_bias, mid_gain[None], ff_bias)
        )
        full_qkv, full_out, full_fc1, full_fc2 = (
            g.reshape((-1, g.shape[-1])) for g in (full_qkv, full_out, full_fc1, full_fc2)
        )
    else:
        (full_qkv, full_out, full_fc1, full_fc2), par, table = plain_gather(digits, weights, small_parts)
        scale_row = jnp.repeat(head_scale, tokens.shape[1] // heads)[None]
        par = jnp.concatenate((par[:SCALE_ROW], scale_row, par[SCALE_ROW + 1 :]))
        normed_in, qkv = project(tokens, full_qkv, par[0:3], par[3:10])
        mixed, logs = attend(lengths, head_scale, qkv)
    result, normed_ff, normed_mid, grad_pre, grad_projection, grad_residual, grad_attended, sums, wide = ffn(
        lengths, tokens, mixed, cotangent, full_out, full_fc1, full_fc2, par, table
    )
    positions = jnp.arange(tokens.shape[0], dtype=jnp.int32)[:, None]
    grad_branch = jnp.where(positions < lengths, cotangent, jnp.zeros_like(cotangent))
    grad_fc2 = to_bf16(dot_tn(normed_mid, grad_branch))
    if tiled:
        d_qkv, dots, grad_out_w, sum_fc1, sum_fc2 = back(
            digits, lengths, qkv, grad_attended, logs, normed_ff, grad_pre, mixed, grad_projection,
            grad_fc2.reshape(digits + w_fc2.shape),
        )
        grad_tokens, sum_qkv, sum_out, d_gain, d_bias, d_mid, d_ffb, d_scale = last(
            digits, normed_in, d_qkv, full_qkv, tokens, grad_residual, par, sums, wide, dots, head_scale[None],
            grad_out_w.reshape(digits + w_out.shape),
        )
        grad_tokens, sum_qkv, sum_out, sum_fc1, sum_fc2, d_gain, d_bias, d_mid, d_ffb, d_scale = settle(
            (grad_tokens, sum_qkv, sum_out, sum_fc1, sum_fc2, d_gain, d_bias, d_mid, d_ffb, d_scale)
        )
        summed = (sum_qkv, sum_out, sum_fc1, sum_fc2, d_gain, d_bias, d_mid[0], d_ffb, d_scale[0])
    else:
        grad_fc1 = to_bf16(dot_tn(normed_ff, grad_pre))
        grad_out_w = to_bf16(dot_tn(mixed, grad_projection))
        d_qkv, dots = attend_back(lengths, qkv, grad_attended, logs)
        grad_tokens, first_sums = project_back(d_qkv, tokens, grad_residual, full_qkv, par[0:3])
        grad_qkv = jnp.concatenate([dot_tn(normed_in, d_qkv[k]) for k in range(3)], axis=1)
        sums, wide, first_sums = sums.sum(1), wide.sum(1), first_sums.sum(1)
        small_grads = (
            jnp.concatenate((first_sums[0:1], sums[1:3])),
            jnp.concatenate((first_sums[1:4], sums[3:7])),
            wide[0:1],
            wide[1:3],
            dots.sum(-1).reshape(heads) / head_scale,
        )
        summed = plain_reduce(
            digits, weights, (grad_qkv, grad_out_w, grad_fc1, grad_fc2), small_parts + (head_scale,), small_grads
        )
    return (result, grad_tokens) + tuple(summed)


def solution(mesh):
    placed = (
        P(("dp", "fsdp"), None),
        P(("dp", "fsdp")),
        P(("dp", "fsdp"), None),
        P(("dp", "fsdp"), None),
        P(("dp", "fsdp"), None),
        P(("dp", "fsdp"), None),
        P(("dp", "fsdp"), None),
        P(None, ("dp", "fsdp")),
        P(None, ("dp", "fsdp")),
        P(("dp", "fsdp")),
        P(None, ("dp", "fsdp")),
        P(),
    )
    return jax.shard_map(
        functools.partial(shards, digits_of(mesh)),
        mesh=mesh,
        in_specs=placed,
        out_specs=(
            P(("dp", "fsdp"), None),
            P(("dp", "fsdp"), None),
            P(("dp", "fsdp"), None),
            P(("dp", "fsdp"), None),
            P(("dp", "fsdp"), None),
            P(("dp", "fsdp"), None),
            P(None, ("dp", "fsdp")),
            P(None, ("dp", "fsdp")),
            P(("dp", "fsdp")),
            P(None, ("dp", "fsdp")),
            P(),
        ),
        check_vma=False,
    )
```

```python
import functools
import heapq

import jax
import jax.numpy as jnp
from jax import lax
from jax.experimental import pallas as pl
from jax.experimental.pallas import tpu as pltpu
from jax.sharding import PartitionSpec as P

epsilon = 1e-05
mask_fill = -1e30
MESH = pl.DeviceIdType.MESH
ORDERS = ((1, 2, 0), (2, 1, 0), (0, 1, 2), (0, 2, 1))


def digits_of(mesh):
    dp, fsdp = mesh.shape["dp"], mesh.shape["fsdp"]
    minor = 2 if dp <= 8 else 8
    return (dp // minor, minor, fsdp // 2, 2)


class Place:
    def __init__(self, digits):
        self.digits = digits
        dp, fs = lax.axis_index("dp"), lax.axis_index("fsdp")
        self.at = (dp // digits[1], dp % digits[1], fs // digits[3], fs % digits[3])

    def digit(self, axis, shift):
        n = self.digits[axis]
        return (self.at[axis] + shift + n) % n

    def peer(self, axis, shift):
        at = list(self.at)
        at[axis] = self.digit(axis, shift)
        return (at[0] * self.digits[1] + at[1], at[2] * self.digits[3] + at[3])

    def greet(self):
        barrier = pltpu.get_barrier_semaphore()
        peers = []
        for axis, n in enumerate(self.digits):
            if n > 1:
                peers.append(self.peer(axis, 1))
            if n > 2:
                peers.append(self.peer(axis, -1))
        for peer in peers:
            pl.semaphore_signal(barrier, inc=1, device_id=peer, device_id_type=MESH)
        pl.semaphore_wait(barrier, len(peers))


class Sems:
    def __init__(self, send, recv, local):
        self.send, self.recv, self.local = send, recv, local
        self.remotes = self.locals = 0

    def remote(self, src, dst, peer):
        copy = pltpu.make_async_remote_copy(
            src_ref=src,
            dst_ref=dst,
            send_sem=self.send.at[self.remotes],
            recv_sem=self.recv.at[self.remotes],
            device_id=peer,
            device_id_type=MESH,
        )
        self.remotes += 1
        copy.start()
        return copy

    def copy(self, src, dst):
        copy = pltpu.make_async_copy(src, dst, self.local.at[self.locals])
        self.locals += 1
        copy.start()
        return copy


def hops(n):
    if n == 1:
        return []
    if n == 2:
        return [(0, (1,), False)]
    return [(s, (1, -1), s == n // 2 - 1) for s in range(n // 2)]


def column_part(start, size, direction, halved):
    if not halved:
        return start, size
    first = size // 256 * 128
    if first == 0:
        return (start, size) if direction > 0 else (start, 0)
    return (start, first) if direction > 0 else (start + first, size - first)


def slots(place, view, axis, slot, part):
    index = []
    for other, n in enumerate(place.digits):
        if other == axis:
            index.append(slot)
        elif other in view:
            index.append(pl.ds(0, n))
        else:
            index.append(place.at[other])
    return tuple(index) + (slice(None), pl.ds(*part))


def gather_piece(place, sems, shard, full, start, size, order):
    held, sends, cores = set(), [], []
    own = sems.copy(
        shard.at[:, pl.ds(start, size)], full.at[slots(place, (), None, None, (start, size))]
    )
    core = place.peer(3, 1)

    def forward(axis, slot, part):
        view = full.at[slots(place, held, axis, slot, part)]
        cores.append(sems.remote(view, view, core))

    first = True
    for axis in order:
        n = place.digits[axis]
        for step, directions, last in hops(n):
            started = []
            for direction in directions:
                part = column_part(start, size, direction, last)
                if part[1] == 0:
                    continue
                index = slots(place, held, axis, place.digit(axis, -step * direction), part)
                src = shard.at[:, pl.ds(*part)] if first and step == 0 else full.at[index]
                started.append(
                    (direction, sems.remote(src, full.at[index], place.peer(axis, direction)))
                )
            yield
            for direction, copy in started:
                copy.wait_recv()
                sends.append(copy)
                if not first and not last and n > 2:
                    forward(axis, place.digit(axis, -(step + 1) * direction), (start, size))
            if not first and (last or n == 2):
                forward(axis, place.digit(axis, n // 2), (start, size))
        if n > 1:
            held.add(axis)
            if first:
                own.wait()
                forward(None, None, (start, size))
                first = False
    if first:
        own.wait()
        forward(None, None, (start, size))
    yield
    for copy in cores:
        copy.wait()
    for copy in sends:
        copy.wait_send()


def accumulate(target, source, result=None):
    lead, dims = target.shape[:-2], target.shape
    count = 1
    for n in lead:
        count *= n

    def index_of(flat):
        index = []
        for n in reversed(lead):
            index.append(flat % n)
            flat = flat // n
        return tuple(reversed(index)) + (slice(None), slice(None))

    def body(flat, carry):
        index = index_of(flat)
        total = target[index].astype(jnp.float32) + source[index].astype(jnp.float32)
        target[index] = total.astype(target.dtype)
        return carry

    if lead:
        lax.fori_loop(0, count, body, 0)
    else:
        body(0, 0)


def reduce_steps(digits, start, size, order):
    left, plan = [0, 1, 2], []
    for axis in order:
        n = digits[axis]
        left.remove(axis)
        lead = tuple(digits[a] for a in left)
        for step, directions, last in reversed(hops(n)):
            batch = []
            for direction in directions:
                part = column_part(start, size, direction, last)
                if part[1] > 0:
                    batch.append((axis, direction, step, part, lead))
            plan.append((tuple(left), batch))
    return plan


def reduce_piece(place, sems, grad, acc, landed, slabs, out, start, size, order):
    sends = []
    lead = (slice(None),) * 3
    whole = (slice(None), pl.ds(start, size))
    mine = acc.at[lead + whole]
    other = landed.at[lead + whole]
    own = sems.copy(grad.at[lead + (place.at[3],) + whole], mine)
    sent = sems.remote(grad.at[lead + (place.digit(3, 1),) + whole], other, place.peer(3, 1))
    yield
    own.wait()
    sent.wait_recv()
    sends.append(sent)
    accumulate(mine, other)
    slabs = iter(slabs)
    for left, batch in reduce_steps(place.digits, start, size, order):
        started = []
        for axis, direction, step, part, _ in batch:
            slot = place.digit(axis, (step + 1) * direction)
            src = acc.at[slots(place, left, axis, slot, part)[:3] + (slice(None), pl.ds(*part))]
            dst = next(slabs)
            sent = sems.remote(src, dst, place.peer(axis, direction))
            started.append((axis, direction * step, part, dst, sent))
        yield
        for axis, shift, part, dst, sent in started:
            sent.wait_recv()
            sends.append(sent)
            slot = place.digit(axis, shift)
            view = slots(place, left, axis, slot, part)[:3] + (slice(None), pl.ds(*part))
            accumulate(acc.at[view], dst)
    out[:, pl.ds(start, size)] = acc[place.at[:3] + whole].astype(jnp.float32)
    for sent in sends:
        sent.wait_send()
    yield


def pieces_of(cols, wanted=4):
    tiles = cols // 128
    count = wanted
    while tiles % count:
        count -= 1
    size = tiles // count * 128
    return [(k * size, size) for k in range(count)]


def run_all(generators):
    live = list(generators)
    while live:
        still = []
        for generator in live:
            try:
                next(generator)
                still.append(generator)
            except StopIteration:
                pass
        live = still


def gather_kernel(digits, count, *refs):
    shards, fulls = refs[:count], refs[count : 2 * count]
    send, recv, local = refs[2 * count :]
    place = Place(digits)
    sems = Sems(send, recv, local)
    place.greet()
    run_all(
        gather_piece(place, sems, shard, full, start, size, ORDERS[k % 4])
        for shard, full in zip(shards, fulls)
        for k, (start, size) in enumerate(pieces_of(shard.shape[1]))
    )


def gather_all(digits, shards):
    count = len(shards)
    copies = 16 * 4 * count * max(1, max(digits) // 4)
    whole = [jax.ShapeDtypeStruct(digits + s.shape, s.dtype) for s in shards]
    return pl.pallas_call(
        functools.partial(gather_kernel, digits, count),
        out_shape=whole,
        in_specs=[pl.BlockSpec(memory_space=pl.ANY)] * count,
        out_specs=[pl.BlockSpec(memory_space=pl.ANY)] * count,
        scratch_shapes=[
            pltpu.SemaphoreType.DMA((copies,)),
            pltpu.SemaphoreType.DMA((copies,)),
            pltpu.SemaphoreType.DMA((4 * count,)),
        ],
        compiler_params=pltpu.CompilerParams(collective_id=0, has_side_effects=True),
        name="gather_all",
    )(*shards)


def reduce_plan(digits, grads):
    plan = []
    for g, grad in enumerate(grads):
        for k, (start, size) in enumerate(pieces_of(grad.shape[-1])):
            plan.append((g, start, size, ORDERS[k % 4]))
    return plan


def reduce_kernel(digits, plan, slab_counts, count, *refs):
    grads, outs = refs[:count], refs[count : 2 * count]
    accs, landed = refs[2 * count : 3 * count], refs[3 * count : 4 * count]
    slabs = refs[4 * count : -3]
    send, recv, local = refs[-3:]
    place = Place(digits)
    sems = Sems(send, recv, local)
    place.greet()
    generators, used = [], 0
    for (g, start, size, order), many in zip(plan, slab_counts):
        own = slabs[used : used + many]
        used += many
        generators.append(
            reduce_piece(place, sems, grads[g], accs[g], landed[g], own, outs[g], start, size, order)
        )
    run_all(generators)


def reduce_all(digits, grads):
    count = len(grads)
    plan = reduce_plan(digits, grads)
    slabs, slab_counts = [], []
    for g, start, size, order in plan:
        shapes = [
            pltpu.VMEM(lead + (grads[g].shape[-2], part[1]), grads[g].dtype)
            for _, batch in reduce_steps(digits, start, size, order)
            for _, _, _, part, lead in batch
        ]
        slabs += shapes
        slab_counts.append(len(shapes))
    blocks = [pltpu.VMEM(digits[:3] + g.shape[-2:], g.dtype) for g in grads]
    copies = len(slabs) + len(plan)
    return pl.pallas_call(
        functools.partial(reduce_kernel, digits, plan, slab_counts, count),
        out_shape=[jax.ShapeDtypeStruct(g.shape[-2:], jnp.float32) for g in grads],
        in_specs=[pl.BlockSpec(memory_space=pl.ANY)] * count,
        out_specs=[pl.BlockSpec(memory_space=pltpu.VMEM)] * count,
        scratch_shapes=blocks
        + blocks
        + slabs
        + [
            pltpu.SemaphoreType.DMA((copies,)),
            pltpu.SemaphoreType.DMA((copies,)),
            pltpu.SemaphoreType.DMA((len(plan),)),
        ],
        compiler_params=pltpu.CompilerParams(
            collective_id=1, has_side_effects=True, vmem_limit_bytes=58 << 20
        ),
        name="reduce_all",
    )(*grads)


def tiled_rows(rows, cols):
    return (rows, cols) if rows % 16 == 0 else (16, rows * cols // 16)


def to_bf16(values):
    return values.astype(jnp.bfloat16)


def dot_nn(a, b):
    return lax.dot_general(a, b, (((1,), (0,)), ((), ())), preferred_element_type=jnp.float32)


def dot_nt(a, b):
    return lax.dot_general(a, b, (((1,), (1,)), ((), ())), preferred_element_type=jnp.float32)


def dot_tn(a, b):
    return lax.dot_general(a, b, (((0,), (0,)), ((), ())), preferred_element_type=jnp.float32)


def row_mean(v):
    return jnp.mean(v, axis=-1, keepdims=True)


def norm_parts(v):
    centered = v - row_mean(v)
    inverse = lax.rsqrt(row_mean(centered * centered) + epsilon)
    return centered * inverse, inverse


def norm_back(grad, gain, normed, inverse):
    scaled = grad * gain
    return (scaled - row_mean(scaled) - normed * row_mean(scaled * normed)) * inverse


def fold(v):
    return v.reshape(v.shape[0] // 8, 8, v.shape[1]).sum(0)


def normal_parts(v):
    return 0.5 * (1.0 + lax.erf(v * 0.5**0.5)), jnp.exp(v * v * -0.5) * 0.3989422804014327


def ffn_kernel(
    chunk,
    len_ref, x_ref, z_ref, cot_ref, wo_hbm, w1_hbm, w2_hbm, par_ref, table_ref,
    out_ref, c_ref, m_ref, df_ref, dy_ref, dr_ref, do_ref, sums_ref, wide_ref,
    act_ref, slope_ref, wo_ref, w1_ref, w2_ref, fixed_ref, sems,
):
    step = pl.program_id(0)
    rows, width = x_ref.shape
    hidden = w1_ref.shape[1]
    f32, bf16 = jnp.float32, jnp.bfloat16
    chunks = [slice(j, j + chunk) for j in range(0, hidden, chunk)]
    loads = [pltpu.make_async_copy(wo_hbm, wo_ref, sems.at[0]), pltpu.make_async_copy(w2_hbm, w2_ref, sems.at[1])]
    for k, at in enumerate(chunks):
        loads.append(pltpu.make_async_copy(w1_hbm.at[:, at], w1_ref.at[:, at], sems.at[2 + k]))

    def arrived(k):
        @pl.when(step == 0)
        def _():
            loads[k].wait()

    @pl.when(step == 0)
    def _():
        for k in [0, *range(2, len(loads)), 1]:
            loads[k].start()
        sums_ref[...] = jnp.zeros_like(sums_ref)
        wide_ref[...] = jnp.zeros_like(wide_ref)

    gain = lambda k: par_ref[k : k + 1, :]
    bias = lambda k: par_ref[3 + k : 4 + k, :]
    arrived(0)
    y_norm, y_inv = norm_parts(dot_nn(z_ref[...], wo_ref[...]) + bias(3))
    residual = x_ref[...].astype(f32) + (y_norm * gain(1) + bias(4))
    r_norm, r_inv = norm_parts(residual)
    normed = (r_norm * gain(2) + bias(5)).astype(bf16)
    c_ref[...] = normed

    @pl.when(step == 0)
    def _():
        for k in range(2, len(loads)):
            loads[k].wait()

    total = jnp.zeros((rows, 1), f32)
    ahead = dot_nn(normed, w1_ref[:, chunks[0]])
    for k, at in enumerate(chunks):
        pre = ahead + table_ref[11:12, at]
        if k + 1 < len(chunks):
            ahead = dot_nn(normed, w1_ref[:, chunks[k + 1]])
        cdf, pdf = normal_parts(pre)
        act = pre * cdf
        act_ref[:, at] = act
        slope_ref[:, at] = cdf + pre * pdf
        total = total + jnp.sum(act, axis=-1, keepdims=True)
    average = total / hidden
    total = jnp.zeros((rows, 1), f32)
    for at in chunks:
        centered = act_ref[:, at] - average
        total = total + jnp.sum(centered * centered, axis=-1, keepdims=True)
    m_inv = lax.rsqrt(total / hidden + epsilon)

    @pl.when(step == 0)
    def _():
        loads[1].wait()
        fixed_ref[...] = dot_nn(table_ref[8:16, :].astype(bf16), w2_ref[...])

    branch = jnp.zeros((rows, width), f32)
    for k in range(len(chunks) + 1):
        if k < len(chunks):
            at = chunks[k]
            n = (act_ref[:, at] - average) * m_inv
            act_ref[:, at] = n
            m_ref[:, at] = (n * table_ref[10:11, at] + table_ref[12:13, at]).astype(bf16)
        if k > 0:
            branch = branch + dot_nn(m_ref[:, chunks[k - 1]], w2_ref[chunks[k - 1], :])
    out_ref[...] = (residual + (branch + bias(6))).astype(bf16)

    position = step * rows + lax.broadcasted_iota(jnp.int32, (rows, 1), 0)
    d_out = jnp.where(position < len_ref[0], cot_ref[...].astype(f32), 0.0)
    d_w = d_out.astype(bf16)
    sums_ref[6] += fold(d_out)
    first = jnp.sum(d_out * fixed_ref[2:3, :], axis=-1, keepdims=True) / hidden
    second = jnp.sum(d_out * (branch - fixed_ref[4:5, :]), axis=-1, keepdims=True) / hidden
    d_c = jnp.zeros((rows, width), f32)
    ahead = dot_nt(d_w, w2_ref[chunks[0], :])
    for k in range(len(chunks) + 1):
        dm = ahead
        if k + 1 < len(chunks):
            ahead = dot_nt(d_w, w2_ref[chunks[k + 1], :])
        if k > 0:
            d_c = d_c + dot_nt(df_ref[:, chunks[k - 1]], w1_ref[:, chunks[k - 1]])
        if k < len(chunks):
            at = chunks[k]
            n = act_ref[:, at]
            wide_ref[0, :, at] += fold(dm * n)
            wide_ref[2, :, at] += fold(dm)
            du = (dm * table_ref[10:11, at] - first - n * second) * m_inv
            df = (du * slope_ref[:, at]).astype(bf16)
            df_ref[:, at] = df
            wide_ref[1, :, at] += fold(df.astype(f32))
    sums_ref[2] += fold(d_c * r_norm)
    sums_ref[5] += fold(d_c)
    d_r = d_out + norm_back(d_c, gain(2), r_norm, r_inv)
    dr_ref[...] = d_r
    sums_ref[1] += fold(d_r * y_norm)
    sums_ref[4] += fold(d_r)
    d_y = norm_back(d_r, gain(1), y_norm, y_inv).astype(bf16)
    dy_ref[...] = d_y
    sums_ref[3] += fold(d_y.astype(f32))
    do_ref[...] = (dot_nt(d_y, wo_ref[...]) * par_ref[SCALE_ROW : SCALE_ROW + 1, :]).astype(bf16)


def ffn(lengths, x, z, cot, wo, w1, w2, par, table, rows=256, chunk=512):
    tokens, width = x.shape
    hidden = w1.shape[1]
    by_row = lambda n: pl.BlockSpec((rows, n), lambda i: (i, 0))
    whole = lambda a: pl.BlockSpec(a.shape, lambda i: (0,) * a.ndim, pipeline_mode=pl.Buffered(1))
    anywhere = pl.BlockSpec(memory_space=pl.ANY)
    sds = jax.ShapeDtypeStruct
    bf16, f32 = jnp.bfloat16, jnp.float32
    outs = [(width, bf16), (width, bf16), (hidden, bf16), (hidden, bf16), (width, bf16), (width, f32), (width, bf16)]
    return pl.pallas_call(
        functools.partial(ffn_kernel, chunk),
        grid=(tokens // rows,),
        in_specs=[pl.BlockSpec(memory_space=pltpu.SMEM)]
        + [by_row(width)] * 3
        + [anywhere] * 3
        + [whole(par), whole(table)],
        out_specs=[by_row(n) for n, _ in outs]
        + [pl.BlockSpec((7, 8, width), lambda i: (0, 0, 0)), pl.BlockSpec((3, 8, hidden), lambda i: (0, 0, 0))],
        out_shape=[sds((tokens, n), d) for n, d in outs] + [sds((7, 8, width), f32), sds((3, 8, hidden), f32)],
        scratch_shapes=[pltpu.VMEM((rows, hidden), f32)] * 2
        + [pltpu.VMEM(w.shape, bf16) for w in (wo, w1, w2)]
        + [pltpu.VMEM((8, width), f32), pltpu.SemaphoreType.DMA((2 + hidden // chunk,))],
        compiler_params=pltpu.CompilerParams(vmem_limit_bytes=60 << 20),
        name="ffn_both",
    )(lengths, x, z, cot, wo, w1, w2, par, table)


head_size = 64


def head_lanes(values, second):
    lane = lax.broadcasted_iota(jnp.int32, values.shape, 1)
    keep = lane >= head_size if second else lane < head_size
    return jnp.where(keep, values, jnp.zeros_like(values))


def masked_scores(keys, queries, first, length):
    scores = dot_nt(keys, queries)
    key_pos = lax.broadcasted_iota(jnp.int32, scores.shape, 0)
    near = key_pos[first:]
    query_pos = first + lax.broadcasted_iota(jnp.int32, near.shape, 1)
    last = jnp.where((near <= query_pos) & (near < length), scores[first:], mask_fill)
    if first == 0:
        return last
    return jnp.concatenate((jnp.where(key_pos[:first] < length, scores[:first], mask_fill), last), axis=0)


def attend_unit(length, scale_ref, head, first, block, q_ref, k_ref, v_ref, z_ref, log_ref):
    rows, seen = slice(first, first + block), first + block
    scaling = jnp.bfloat16(head_size**-0.5)
    keys, values = k_ref[:seen, :], v_ref[:seen, :]
    mixed = []
    for h in range(2):
        queries = head_lanes(q_ref[rows, :], h) * scaling
        scores = masked_scores(keys, queries, first, length)
        top = jnp.max(scores, axis=0, keepdims=True)
        shifted = jnp.exp(scores - top)
        total = jnp.sum(shifted, axis=0, keepdims=True)
        log_ref[h : h + 1, rows] = top + jnp.log(total)
        attended = dot_tn(shifted.astype(jnp.bfloat16), values)
        mixed.append(attended * (scale_ref[head + h] / total).T)
    lane = lax.broadcasted_iota(jnp.int32, mixed[0].shape, 1)
    z_ref[rows, :] = jnp.where(lane < head_size, mixed[0], mixed[1]).astype(jnp.bfloat16)


def attend_kernel(block, len_ref, scale_ref, q_ref, k_ref, v_ref, z_ref, log_ref):
    for first in range(0, q_ref.shape[1], block):
        attend_unit(
            len_ref[0], scale_ref, pl.program_id(0) * 2, first, block,
            q_ref.at[0], k_ref.at[0], v_ref.at[0], z_ref, log_ref.at[0],
        )


def attend(lengths, head_scale, qkv, block=256):
    _, tokens, width = qkv.shape
    pairs = width // 128
    cols = lambda part: pl.BlockSpec((1, tokens, 128), lambda p: (part, 0, p))
    smem = pl.BlockSpec(memory_space=pltpu.SMEM)
    return pl.pallas_call(
        functools.partial(attend_kernel, min(block, tokens)),
        grid=(pairs,),
        in_specs=[smem, smem, cols(0), cols(1), cols(2)],
        out_specs=[
            pl.BlockSpec((tokens, 128), lambda p: (0, p)),
            pl.BlockSpec((1, 2, tokens), lambda p: (p, 0, 0)),
        ],
        out_shape=[
            jax.ShapeDtypeStruct((tokens, width), jnp.bfloat16),
            jax.ShapeDtypeStruct((pairs, 2, tokens), jnp.float32),
        ],
        compiler_params=pltpu.CompilerParams(vmem_limit_bytes=56 << 20),
        name="attend",
    )(lengths, head_scale, qkv, qkv, qkv)


def attend_back_unit(
    length, first, block, q_ref, k_ref, v_ref, do_ref, log_ref, dq_ref, dot_ref, dk_ref, dv_ref
):
    rows, seen = slice(first, first + block), first + block
    bf16, scaling = jnp.bfloat16, head_size**-0.5
    keys, values = k_ref[:seen, :], v_ref[:seen, :]
    mixed = []
    for h in range(2):
        queries = head_lanes(q_ref[rows, :], h) * bf16(scaling)
        grads = head_lanes(do_ref[rows, :], h)
        scores = masked_scores(keys, queries, first, length)
        weights = jnp.exp(scores - log_ref[h : h + 1, rows])
        products = weights * dot_nt(values, grads)
        total = jnp.sum(products, axis=0, keepdims=True)
        dot_ref[h : h + 1, rows] = total
        d_scores = (products - weights * total).astype(bf16)
        for ref, left, right in ((dv_ref, weights.astype(bf16), grads), (dk_ref, d_scores, queries)):
            part = dot_nn(left, right)
            if h == 0:
                ref[rows, :] = part[first:]
                if first:
                    ref[:first, :] += part[:first]
            else:
                ref[:seen, :] += part
        mixed.append(dot_tn(d_scores, keys))
    lane = lax.broadcasted_iota(jnp.int32, mixed[0].shape, 1)
    dq_ref[rows, :] = (jnp.where(lane < head_size, mixed[0], mixed[1]) * scaling).astype(bf16)


def attend_back_kernel(block, len_ref, q_ref, k_ref, v_ref, do_ref, log_ref, dqkv_ref, dot_ref, dk_ref, dv_ref):
    for first in range(0, do_ref.shape[0], block):
        attend_back_unit(
            len_ref[0], first, block, q_ref.at[0], k_ref.at[0], v_ref.at[0], do_ref, log_ref.at[0],
            dqkv_ref.at[0], dot_ref.at[0], dk_ref, dv_ref,
        )
    dqkv_ref[1] = dk_ref[...].astype(jnp.bfloat16)
    dqkv_ref[2] = dv_ref[...].astype(jnp.bfloat16)


def attend_back(lengths, qkv, d_attended, logs, block=256):
    _, tokens, width = qkv.shape
    pairs = width // 128
    cols = lambda part: pl.BlockSpec((1, tokens, 128), lambda p: (part, 0, p))
    per_pair = pl.BlockSpec((1, 2, tokens), lambda p: (p, 0, 0))
    return pl.pallas_call(
        functools.partial(attend_back_kernel, min(block, tokens)),
        grid=(pairs,),
        in_specs=[
            pl.BlockSpec(memory_space=pltpu.SMEM),
            cols(0),
            cols(1),
            cols(2),
            pl.BlockSpec((tokens, 128), lambda p: (0, p)),
            per_pair,
        ],
        out_specs=[pl.BlockSpec((3, tokens, 128), lambda p: (0, 0, p)), per_pair],
        out_shape=[
            jax.ShapeDtypeStruct((3, tokens, width), jnp.bfloat16),
            jax.ShapeDtypeStruct((pairs, 2, tokens), jnp.float32),
        ],
        scratch_shapes=[pltpu.VMEM((tokens, 128), jnp.float32)] * 2,
        compiler_params=pltpu.CompilerParams(vmem_limit_bytes=56 << 20),
        name="attend_back",
    )(lengths, qkv, qkv, qkv, d_attended, logs)


def project_kernel(x_ref, w_ref, gain_ref, bias_ref, a_ref, qkv_ref):
    width = x_ref.shape[1]
    normed, _ = norm_parts(x_ref[...].astype(jnp.float32))
    a = (normed * gain_ref[0:1, :] + bias_ref[0:1, :]).astype(jnp.bfloat16)
    a_ref[...] = a
    for part, row in ((0, 1), (1, None), (2, 2)):
        at = slice(part * width, (part + 1) * width)
        value = dot_nn(a, w_ref[:, at])
        if row is not None:
            value = value + bias_ref[row : row + 1, :]
        qkv_ref[part] = value.astype(jnp.bfloat16)


def project(x, w, gains, biases, rows=256):
    tokens, width = x.shape
    by_row = lambda n: pl.BlockSpec((rows, n), lambda i: (i, 0))
    whole = lambda a: pl.BlockSpec(a.shape, lambda i: (0,) * a.ndim, pipeline_mode=pl.Buffered(1))
    return pl.pallas_call(
        project_kernel,
        grid=(tokens // rows,),
        in_specs=[by_row(width), whole(w), whole(gains), whole(biases)],
        out_specs=[by_row(width), pl.BlockSpec((3, rows, width), lambda i: (0, i, 0))],
        out_shape=[
            jax.ShapeDtypeStruct((tokens, width), jnp.bfloat16),
            jax.ShapeDtypeStruct((3, tokens, width), jnp.bfloat16),
        ],
        compiler_params=pltpu.CompilerParams(vmem_limit_bytes=56 << 20),
        name="project",
    )(x, w, gains, biases)


def project_back_kernel(d_ref, x_ref, dr_ref, w_ref, gain_ref, dx_ref, sums_ref):
    @pl.when(pl.program_id(0) == 0)
    def _():
        sums_ref[...] = jnp.zeros_like(sums_ref)

    width = x_ref.shape[1]
    d_a = sum(dot_nt(d_ref[k], w_ref[:, k * width : (k + 1) * width]) for k in range(3))
    normed, inverse = norm_parts(x_ref[...].astype(jnp.float32))
    sums_ref[0] += fold(d_a * normed)
    sums_ref[1] += fold(d_a)
    sums_ref[2] += fold(d_ref[0].astype(jnp.float32))
    sums_ref[3] += fold(d_ref[2].astype(jnp.float32))
    back = norm_back(d_a, gain_ref[0:1, :], normed, inverse)
    dx_ref[...] = (dr_ref[...] + back).astype(jnp.bfloat16)


def project_back(d_qkv, x, d_r, w, gains, rows=256):
    tokens, width = x.shape
    by_row = pl.BlockSpec((rows, width), lambda i: (i, 0))
    whole = lambda a: pl.BlockSpec(a.shape, lambda i: (0,) * a.ndim, pipeline_mode=pl.Buffered(1))
    return pl.pallas_call(
        project_back_kernel,
        grid=(tokens // rows,),
        in_specs=[pl.BlockSpec((3, rows, width), lambda i: (0, i, 0)), by_row, by_row, whole(w), whole(gains)],
        out_specs=[by_row, pl.BlockSpec((4, 8, width), lambda i: (0, 0, 0))],
        out_shape=[
            jax.ShapeDtypeStruct((tokens, width), jnp.bfloat16),
            jax.ShapeDtypeStruct((4, 8, width), jnp.float32),
        ],
        compiler_params=pltpu.CompilerParams(vmem_limit_bytes=56 << 20),
        name="project_back",
    )(d_qkv, x, d_r, w, gains)


class Ops:
    def __init__(self, send, recv, local, place):
        self.send, self.recv, self.local, self.place = send, recv, local, place
        self.remotes = self.locals = 0
        self.now = []

    def do(self, action):
        self.now.append(action)

    def remote(self, src, dst, peer):
        k = self.remotes
        self.remotes += 1
        copy = pltpu.make_async_remote_copy(
            src_ref=src,
            dst_ref=dst,
            send_sem=self.send.at[k],
            recv_sem=self.recv.at[k],
            device_id=peer,
            device_id_type=MESH,
        )
        self.do(copy.start)
        return copy

    def copy(self, src, dst):
        copy = pltpu.make_async_copy(src, dst, self.local.at[self.locals])
        self.locals += 1
        self.do(copy.start)
        return copy


class FixedPlace(Place):
    def __init__(self, digits):
        super().__init__(digits)
        self.shifted = {}
        self.peers = {}
        for axis, n in enumerate(digits):
            for shift in range(-n, n + 1):
                self.shifted[axis, shift] = super().digit(axis, shift)
            for shift in (-1, 1):
                self.peers[axis, shift] = super().peer(axis, shift)

    def device(self, shifts):
        at = [self.shifted[axis, shift] for axis, shift in enumerate(shifts)]
        return (at[0] * self.digits[1] + at[1], at[2] * self.digits[3] + at[3])

    def greet_group(self, group):
        barrier = pltpu.get_barrier_semaphore()
        for shifts in group:
            pl.semaphore_signal(barrier, inc=1, device_id=self.device(shifts), device_id_type=MESH)
        pl.semaphore_wait(barrier, len(group))

    def digit(self, axis, shift):
        return self.shifted[axis, shift]

    def peer(self, axis, shift):
        return self.peers[axis, shift]


def plan_ticks(ops, pieces, stride):
    queue = [(start, 0, k) for k, (start, _) in enumerate(pieces)]
    heapq.heapify(queue)
    ticks, ends = [], {}
    while queue:
        at, age, k = heapq.heappop(queue)
        ops.now = []
        alive = next(pieces[k][1], "end") != "end"
        if ops.now:
            ticks.append(ops.now)
        if alive:
            heapq.heappush(queue, (at + stride, age - 1, k))
        else:
            ends[k] = len(ticks)
    return ticks, ends


def schedule(ops, pieces, stride, moments, times, scale):
    queue = [(start, 0, k) for k, (start, _, _) in enumerate(pieces)]
    floor = [earliest for _, earliest, _ in pieces]
    heapq.heapify(queue)
    parts = []
    while queue:
        at, age, k = heapq.heappop(queue)
        ops.now = []
        if next(pieces[k][2], "end") != "end":
            heapq.heappush(queue, (at + stride, age - 1, k))
        where = next((m for m, time in enumerate(times) if time >= at * scale), len(times) - 1)
        floor[k] = max(floor[k], where)
        parts.append((floor[k], at, len(parts), ops.now))
    parts.sort(key=lambda part: part[:3])
    ticks = [actions for _, _, _, actions in parts]
    table = {moment: [] for moment in moments}
    for number, (where, _, _, _) in enumerate(parts):
        table[moments[where]].append(number)
    return Hooks(ticks, table)


class Hooks:
    def __init__(self, ticks, moments):
        self.ticks, self.moments = ticks, moments

    def run(self, step, hook):
        for at in sorted(s for s, h in self.moments if h == hook):
            numbers = self.moments[at, hook]
            if numbers:

                @pl.when(step == at)
                def _(numbers=numbers):
                    for number in numbers:
                        for action in self.ticks[number]:
                            action()


def spread_ticks(first, count, moments, weights=None):
    weights = weights or [1] * len(moments)
    table, todo, used, past = {}, list(range(first, count)), 0, 0
    for moment, weight in zip(moments, weights):
        past += weight
        upto = len(todo) * past // sum(weights)
        table[moment] = todo[used:upto]
        used = upto
    return table


def rect(rows, cols):
    return (pl.ds(*rows), pl.ds(*cols))


def ways(n, turn):
    if n == 1:
        return []
    return [(s, (turn,) if n == 2 or s == n // 2 - 1 else (1, -1)) for s in range(n // 2)]


def copies_of(digits):
    return 1 + sum(len(directions) for n in digits[:3] for _, directions in ways(n, 1))


def gather_steps(ops, shard, full, rows, cols, order, turn):
    place = ops.place
    held, sends = set(), []

    def index(axis, slot):
        return slots(place, held, axis, slot, cols)[:4] + rect(rows, cols)

    own = ops.copy(shard.at[rect(rows, cols)], full.at[index(None, None)])
    first = True
    for axis in order:
        n = place.digits[axis]
        for step, directions in ways(n, turn):
            started = []
            for direction in directions:
                at = index(axis, place.digit(axis, -step * direction))
                src = shard.at[rect(rows, cols)] if first and step == 0 else full.at[at]
                started.append(ops.remote(src, full.at[at], place.peer(axis, direction)))
            yield
            for copy in started:
                ops.do(copy.wait_recv)
            sends += started
        held.add(axis)
        if first:
            ops.do(own.wait)
            first = False
    view = full.at[index(None, None)]
    copy = ops.remote(view, view, place.peer(3, 1))
    yield
    ops.do(copy.wait_recv)
    for copy in sends + [copy]:
        ops.do(copy.wait_send)


def add_into(target, source):
    return lambda: accumulate(target, source)


def staged_sums(digits, order, turn):
    left, plan = [0, 1, 2], []
    for axis in order:
        left.remove(axis)
        lead = tuple(digits[a] for a in left)
        for step, directions in reversed(ways(digits[axis], turn)):
            plan.append((tuple(left), [(axis, direction, step) for direction in directions], lead))
    return plan


def reduce_steps_of(ops, own, sent, stage, landed, slabs, finish, order, turn):
    place, sends = ops.place, []
    if stage is not None:
        local = ops.copy(own, stage)
    copy = ops.remote(sent, landed, place.peer(3, 1))
    yield
    if stage is not None:
        ops.do(local.wait)
    ops.do(copy.wait_recv)
    sends.append(copy)
    ops.do(add_into(landed, own if stage is None else stage))
    slabs = iter(slabs)
    every = (slice(None), slice(None))
    for left, batch, _ in staged_sums(place.digits, order, turn):
        started = []
        for axis, direction, step in batch:
            slot = place.digit(axis, (step + 1) * direction)
            src = landed.at[slots(place, left, axis, slot, (0, 0))[:3] + every]
            dst = next(slabs)
            copy = ops.remote(src, dst, place.peer(axis, direction))
            started.append((axis, direction * step, dst, copy))
        yield
        for axis, shift, dst, copy in started:
            ops.do(copy.wait_recv)
            sends.append(copy)
            view = slots(place, left, axis, place.digit(axis, shift), (0, 0))[:3] + every
            ops.do(add_into(landed.at[view], dst))
    ops.do(lambda: finish(landed[place.at[:3]].astype(jnp.float32)))
    for copy in sends:
        ops.do(copy.wait_send)
    yield


def slab_shapes(digits, rows, cols, order, turn, dtype):
    return [
        pltpu.VMEM(lead + (rows, cols), dtype) for _, batch, lead in staged_sums(digits, order, turn) for _ in batch
    ]


GATHER_ORDERS = ((0, 1, 2), (0, 2, 1), (0, 1, 2), (0, 2, 1), (1, 2, 0), (0, 2, 1), (0, 1, 2), (0, 2, 1), (2, 1, 0))
X, Y, Z, W = (1, 2, 0), (2, 1, 0), (0, 1, 2), (0, 2, 1)
REDUCE_ORDERS = (Z, X, Y, Z, X, W, Y, X, Z, (2, 0, 1), X, (2, 0, 1), X, X, Y, X)
LAST_ROUNDS = 2.5
OUT_PACE = 0.0
BACK_HOOKS = (1, 2, 3)
LAST_HOOKS = (0, 1, 2, 3)
LAST_ORDERS = (W, Y, X, Y, X, Z, Z, Y, X, X, Z, Y, X, Y)


def blocks_of(shape, rows, cols):
    rows, cols = min(rows, shape[0]), min(cols, shape[1])
    return [((r, rows), (c, cols)) for r in range(0, shape[0], rows) for c in range(0, shape[1], cols)]


def semaphores(copies, local):
    return [
        pltpu.SemaphoreType.DMA((copies,)),
        pltpu.SemaphoreType.DMA((copies,)),
        pltpu.SemaphoreType.DMA((local,)),
    ]


HEADS_WIDE = 256
QUERY_BLOCK = 256
SCALE_ROW = 13


def front_kernel(
    digits, counts,
    len_ref, scale_ref, x_ref, w_qkv, w_out, w_fc1, w_fc2, gain_ref, bias_ref, mid_ref, ffb_ref,
    a_ref, qkv_ref, z_ref, log_ref, wqkv_out, wout_ref, w1_ref, w2_ref, par_ref, wide_ref,
    wqkv_ref, small_ref, qkv_shard, out_shard, fc1_shard, fc2_shard, small_shard, mine_ref, send, recv, local,
):
    step = pl.program_id(0)
    steps = counts["steps"]
    f32, bf16 = jnp.float32, jnp.bfloat16
    tokens, width = x_ref.shape
    place = FixedPlace(digits)
    ops = Ops(send, recv, local, place)
    pieces, number, start = [], 0, 0.0
    whole = lambda ref: ((0, ref.shape[0]), (0, ref.shape[1]))
    pieces.append((0.0, gather_steps(ops, small_shard, small_ref, *whole(small_shard), GATHER_ORDERS[0], 1)))
    for s in range(steps):
        for part in range(3):
            cols = (part * width + s * HEADS_WIDE, HEADS_WIDE)
            order, turn = GATHER_ORDERS[number % 9], 1 - number % 2 * 2
            number += 1
            pieces.append((start, gather_steps(ops, qkv_shard, wqkv_ref, (0, qkv_shard.shape[0]), cols, order, turn)))
            start += 0.5
    for shard, full in ((out_shard, wout_ref), (fc1_shard, w1_ref), (fc2_shard, w2_ref)):
        for rows, cols in blocks_of(shard.shape, 32, 512):
            order, turn = GATHER_ORDERS[number % 9], 1 - number % 2 * 2
            number += 1
            pieces.append((start, gather_steps(ops, shard, full, rows, cols, order, turn)))
            start += 1.0
    ticks, ends = plan_ticks(ops, pieces, 3.0)
    ready = [max(ends[k] for k in range(4 + 3 * s)) for s in range(steps)]
    blocks = tokens // QUERY_BLOCK
    units = 2 * blocks
    table = {(s, "head"): [] for s in range(steps)}
    moments = [(s, u) for s in range(steps) for u in range(units)]
    spread = spread_ticks(ready[0], len(ticks), moments, [u % blocks + 1 for _, u in moments])
    table.update(spread)
    table[0, "head"] = list(range(ready[0]))
    for s in range(1, steps):
        late = [(m, t) for m in moments if m[0] >= s for t in table[m] if t < ready[s]]
        for moment, t in late:
            table[moment].remove(t)
            table[s, "head"].append(t)
    hooks = Hooks(ticks, table)

    total = digits[0] * digits[1] * digits[2] * digits[3]

    @pl.when(step == 0)
    def _():
        for shard, w in ((qkv_shard, w_qkv), (out_shard, w_out), (fc1_shard, w_fc1), (fc2_shard, w_fc2)):
            shard[...] = w[...].astype(bf16)
        me = ((place.at[0] * digits[1] + place.at[1]) * digits[2] + place.at[2]) * digits[3] + place.at[3]
        mine_ref[...] = jnp.zeros_like(mine_ref)
        for k, (row, ref) in enumerate(((0, gain_ref), (3, bias_ref), (10, mid_ref), (11, ffb_ref))):
            mine_ref[k // 2, row : row + ref.shape[0], 0 : ref.shape[1]] = ref[...]
        narrow = pltpu.roll(mine_ref[0], me * gain_ref.shape[1] % 128, 1)
        wide = pltpu.roll(mine_ref[1], me * mid_ref.shape[1] % 128, 1)
        small_shard[...] = (narrow + wide).astype(bf16)
        place.greet()

    hooks.run(step, "head")

    @pl.when(step == 0)
    def _():
        for ref in (par_ref, wide_ref):
            own = ref.shape[1] // total
            for lane in range(0, ref.shape[1], 128):
                block = None
                for d in range(lane // own, max((lane + 128) // own, lane // own + 1)):
                    i3, rest = d % digits[3], d // digits[3]
                    i2, rest = rest % digits[2], rest // digits[2]
                    i1, i0 = rest % digits[1], rest // digits[1]
                    value = small_ref[i0, i1, i2, i3].astype(f32)
                    block = value if block is None else block + value
                ref[:, lane : lane + 128] = block
        lane = lax.broadcasted_iota(jnp.int32, (1, 128), 1)
        for pair in range(width // 128):
            scales = jnp.where(lane < head_size, scale_ref[2 * pair], scale_ref[2 * pair + 1])
            par_ref[SCALE_ROW : SCALE_ROW + 1, pair * 128 : pair * 128 + 128] = scales
        for first in range(0, tokens, QUERY_BLOCK):
            rows = slice(first, first + QUERY_BLOCK)
            normed, _ = norm_parts(x_ref[rows, :].astype(f32))
            a_ref[rows, :] = (normed * par_ref[0:1, :] + par_ref[3:4, :]).astype(bf16)

    keep = pltpu.make_async_copy(wqkv_ref, wqkv_out, local.at[local.shape[0] - 1])

    @pl.when(step == steps - 1)
    def _():
        keep.start()

    at = pl.multiple_of(step * HEADS_WIDE, HEADS_WIDE)
    for part, row in ((0, 4), (1, None), (2, 5)):
        cols = pl.ds(pl.multiple_of(part * width + at, HEADS_WIDE), HEADS_WIDE)
        value = dot_nn(a_ref[...], wqkv_ref[:, :, :, :, :, cols].reshape(width, HEADS_WIDE))
        if row is not None:
            value = value + par_ref[row : row + 1, pl.ds(at, HEADS_WIDE)]
        qkv_ref[part] = value.astype(bf16)
    unit = 0
    for pair in range(HEADS_WIDE // 128):
        lanes = slice(pair * 128, pair * 128 + 128)
        for first in range(0, tokens, QUERY_BLOCK):
            attend_unit(
                len_ref[0], scale_ref, (step * (HEADS_WIDE // 128) + pair) * 2, first, QUERY_BLOCK,
                qkv_ref.at[0, :, lanes], qkv_ref.at[1, :, lanes], qkv_ref.at[2, :, lanes],
                z_ref.at[:, lanes], log_ref.at[pair],
            )
            hooks.run(step, unit)
            unit += 1

    @pl.when(step == steps - 1)
    def _():
        keep.wait()


def front(digits, lengths, head_scale, x, weights, small_parts):
    tokens, width = x.shape
    hidden = weights[2].shape[1]
    steps = width // HEADS_WIDE
    bf16, f32 = jnp.bfloat16, jnp.float32
    sds = jax.ShapeDtypeStruct
    anywhere = pl.BlockSpec(memory_space=pl.ANY)
    smem = pl.BlockSpec(memory_space=pltpu.SMEM)
    fixed = lambda shape: pl.BlockSpec(shape, lambda s: (0,) * len(shape), pipeline_mode=pl.Buffered(1))
    per_step = HEADS_WIDE // 128
    pieces = 1 + 3 * steps + sum(len(blocks_of(w.shape, 32, 512)) for w in weights[1:])
    return pl.pallas_call(
        functools.partial(front_kernel, digits, {"steps": steps}),
        grid=(steps,),
        in_specs=[smem, smem] + [fixed(v.shape) for v in (x, *weights, *small_parts)],
        out_specs=[
            fixed((tokens, width)),
            pl.BlockSpec((3, tokens, HEADS_WIDE), lambda s: (0, 0, s)),
            pl.BlockSpec((tokens, HEADS_WIDE), lambda s: (0, s)),
            pl.BlockSpec((per_step, 2, tokens), lambda s: (s, 0, 0)),
            anywhere,
            anywhere,
            anywhere,
            anywhere,
            fixed((16, width)),
            fixed((16, hidden)),
        ],
        out_shape=[
            sds((tokens, width), bf16),
            sds((3, tokens, width), bf16),
            sds((tokens, width), bf16),
            sds((width // 128, 2, tokens), f32),
        ]
        + [sds(digits + w.shape, bf16) for w in weights]
        + [sds((16, width), f32), sds((16, hidden), f32)],
        scratch_shapes=[pltpu.VMEM(digits + weights[0].shape, bf16), pltpu.VMEM(digits + (16, 128), bf16)]
        + [pltpu.VMEM(w.shape, bf16) for w in weights]
        + [pltpu.VMEM((16, 128), bf16), pltpu.VMEM((2, 16, 128), f32)]
        + semaphores(pieces * copies_of(digits), pieces + 1),
        compiler_params=pltpu.CompilerParams(
            collective_id=2, has_side_effects=True, vmem_limit_bytes=60 << 20
        ),
        name="front",
    )(lengths, head_scale, x, *weights, *small_parts)


def back_kernel(
    digits, stages,
    len_ref, q_ref, k_ref, v_ref, do_ref, log_ref, c_ref, df_ref, z_ref, dy_ref, g2_ref,
    dqkv_ref, dot_ref, gout_ref, s1_ref, s2_ref,
    dk_ref, dv_ref, made_ref, *scratch,
):
    step, steps = pl.program_id(0), stages["steps"]
    half = steps // 2
    bf16 = jnp.bfloat16
    place = FixedPlace(digits)
    send, recv, local = scratch[-3:]
    ops = Ops(send, recv, local, place)
    staging, rest = scratch[:4], list(scratch[4:-3])
    tokens = q_ref.shape[1]
    units = tokens // QUERY_BLOCK
    moments, times, now = [(0, "head")], [0.0], 0.0
    for s in range(steps):
        if s < half:
            now += 2.7
            moments.append((s, "made"))
            times.append(now)
        else:
            now += 1.3
        for u in range(units):
            now += 0.52 * (u + 1)
            if u in BACK_HOOKS:
                moments.append((s, u))
                times.append(now)
    pieces, staged = [], 0
    all_slots = (slice(None),) * 3
    for start, which, rows, cols, order, turn, many in stages["pieces"]:
        grad, out = ((g2_ref, s2_ref), (made_ref, s1_ref))[which]
        landed, slabs = rest[0], rest[1 : 1 + many]
        del rest[: 1 + many]
        own = grad.at[all_slots + (place.at[3],) + rect(rows, cols)]
        sent = grad.at[all_slots + (place.digit(3, 1),) + rect(rows, cols)]
        stage, earliest = None, 0
        if which == 0:
            stage = staging[staged % 4]
            staged += 1
        else:
            earliest = moments.index((cols[0] // (made_ref.shape[-1] // half), "made"))

        def finish(value, out=out, rows=rows, cols=cols):
            out[rows[0] : rows[0] + rows[1], cols[0] : cols[0] + cols[1]] = value

        pieces.append(
            (start, earliest, reduce_steps_of(ops, own, sent, stage, landed, slabs, finish, order, turn))
        )
    stride = stages["stride"]
    span = max(start for start, _, _ in pieces) + 5 * stride
    hooks = schedule(ops, pieces, stride, moments, times, now / span)

    @pl.when(step == 0)
    def _():
        place.greet()

    hooks.run(step, "head")

    @pl.when(step < half)
    def _():
        wide = df_ref.shape[1]
        made = dot_tn(c_ref[...], df_ref[...]).astype(bf16)
        cols = pl.ds(pl.multiple_of(step * wide, wide), wide)
        made_ref[:, :, :, :, :, cols] = made.reshape(made_ref.shape[:5] + (wide,))

    hooks.run(step, "made")

    @pl.when(step >= half)
    def _():
        gout_ref[...] = dot_tn(z_ref[...], dy_ref[...]).astype(bf16)

    for unit in range(units):
        attend_back_unit(
            len_ref[0], unit * QUERY_BLOCK, QUERY_BLOCK, q_ref.at[0], k_ref.at[0], v_ref.at[0], do_ref, log_ref.at[0],
            dqkv_ref.at[0], dot_ref.at[0], dk_ref, dv_ref,
        )
        if unit == units - 1:
            dqkv_ref[1] = dk_ref[...].astype(bf16)
            dqkv_ref[2] = dv_ref[...].astype(bf16)
        hooks.run(step, unit)


def back(digits, lengths, qkv, d_attended, logs, c, d_f, z, d_y, grad_fc2):
    _, tokens, width = qkv.shape
    hidden = d_f.shape[1]
    pairs = width // 128
    half = pairs // 2
    bf16, f32 = jnp.bfloat16, jnp.float32
    sds = jax.ShapeDtypeStruct
    anywhere = pl.BlockSpec(memory_space=pl.ANY)
    cols = lambda part: pl.BlockSpec((1, tokens, 128), lambda p: (part, 0, p))
    per_pair = pl.BlockSpec((1, 2, tokens), lambda p: (p, 0, 0))
    fixed = lambda shape: pl.BlockSpec(shape, lambda s: (0,) * len(shape), pipeline_mode=pl.Buffered(1))
    early = pl.BlockSpec((tokens, hidden // half), lambda p: (0, jnp.minimum(p, half - 1)))
    late = pl.BlockSpec((tokens, width // half), lambda p: (0, jnp.maximum(p - half, 0)))
    total = digits[0] * digits[1] * digits[2] * digits[3]
    shapes = (grad_fc2.shape[4:], (width // total, hidden))
    listed = [[(which, *piece) for piece in blocks_of(shape, 32, 512)] for which, shape in enumerate(shapes)]
    mixed = []
    while any(listed):
        for some in listed:
            mixed += some[:2]
            del some[:2]
    pieces, scratch = [], []
    for number, (which, rows, at) in enumerate(mixed):
        order, turn = REDUCE_ORDERS[number % len(REDUCE_ORDERS)], 1 - number % 2 * 2
        slabs = slab_shapes(digits, rows[1], at[1], order, turn, bf16)
        pieces.append((float(number), which, rows, at, order, turn, len(slabs)))
        scratch += [pltpu.VMEM(digits[:3] + (rows[1], at[1]), bf16)] + slabs
    stage = pltpu.VMEM(digits[:3] + (mixed[0][1][1], mixed[0][2][1]), bf16)
    return pl.pallas_call(
        functools.partial(back_kernel, digits, {"steps": pairs, "pieces": pieces, "stride": 4.0}),
        grid=(pairs,),
        in_specs=[
            pl.BlockSpec(memory_space=pltpu.SMEM),
            cols(0),
            cols(1),
            cols(2),
            pl.BlockSpec((tokens, 128), lambda p: (0, p)),
            per_pair,
            fixed(c.shape),
            early,
            fixed(z.shape),
            late,
            anywhere,
        ],
        out_specs=[
            pl.BlockSpec((3, tokens, 128), lambda p: (0, 0, p)),
            per_pair,
            pl.BlockSpec((width, width // half), lambda p: (0, jnp.maximum(p - half, 0))),
            fixed(shapes[1]),
            fixed(shapes[0]),
        ],
        out_shape=[
            sds((3, tokens, width), bf16),
            sds((pairs, 2, tokens), f32),
            sds((width, width), bf16),
            sds(shapes[1], f32),
            sds(shapes[0], f32),
        ],
        scratch_shapes=[pltpu.VMEM((tokens, 128), f32)] * 2
        + [pltpu.VMEM(digits + shapes[1], bf16)]
        + [stage] * 4
        + scratch
        + semaphores(len(scratch), len(pieces)),
        compiler_params=pltpu.CompilerParams(
            collective_id=3, has_side_effects=True, vmem_limit_bytes=60 << 20
        ),
        name="back",
    )(lengths, qkv, qkv, qkv, d_attended, logs, c, d_f, z, d_y, grad_fc2)


def sum_direct(ops, block, first, second, result):
    place = ops.place
    digits = place.digits
    plane = [(0, a, b, c) for a in range(digits[1]) for b in range(digits[2]) for c in range(digits[3])][1:]
    copies = []
    for k, shifts in enumerate(plane):
        to = [place.digit(axis, shift) for axis, shift in enumerate(shifts)]
        src = block.at[:, to[1], to[2], to[3]]
        copies.append(ops.remote(src, first.at[k], place.device(shifts)))
    yield
    for copy in copies:
        ops.do(copy.wait_recv)

    def add_plane():
        total = block[:, place.at[1], place.at[2], place.at[3]]
        for k in range(len(plane)):
            total = total + first[k]
        result[...] = total

    ops.do(add_plane)
    others = []
    for shift in range(1, digits[0]):
        src = result.at[place.digit(0, shift)]
        others.append(ops.remote(src, second.at[shift - 1], place.device((shift, 0, 0, 0))))
    yield
    for copy in others:
        ops.do(copy.wait_recv)
    for copy in copies + others:
        ops.do(copy.wait_send)
    yield


def direct_group(digits):
    plane = [(0, a, b, c) for a in range(digits[1]) for b in range(digits[2]) for c in range(digits[3])][1:]
    return plane + [(shift, 0, 0, 0) for shift in range(1, digits[0])]


def last_kernel(
    digits, stages,
    a_ref, d_ref, wq_ref, wk_ref, wv_ref, x_hbm, dr_hbm, par_ref, sums_ref, wide_ref, dot_ref, scale_ref, gout_ref,
    dx_ref, sqkv_ref, sout_ref, gain_ref, bias_ref, mid_ref, ffb_ref, dscale_ref,
    da_ref, made_ref, rows_ref, block_ref, late_ref, first_ref, second_ref, plane_ref, found_ref, stage_ref, x_ref, dr_ref, load_sems, *scratch,
):
    step, steps = pl.program_id(0), stages["steps"]
    half = steps // 2
    f32, bf16 = jnp.float32, jnp.bfloat16
    place = FixedPlace(digits)
    send, recv, local = scratch[-3:]
    ops = Ops(send, recv, local, place)
    rest = list(scratch[:-3])
    tokens, width = x_ref.shape
    blocks = tokens // QUERY_BLOCK
    moments, times, now = [(0, "head"), (0, "block")], [0.0, 0.01], 0.0
    for s in range(half):
        now += 3.0
        moments.append((s, "made"))
        times.append(now)
    for s in range(half, steps):
        for b in range(blocks):
            now += 0.85
            if b in LAST_HOOKS:
                moments.append((s, b))
                times.append(now)
    for b in range(blocks):
        now += 1.0
        moments.append((steps - 1, "norm%d" % b))
        times.append(now)
    moments.append((steps - 1, "end"))
    times.append(1e9)
    pieces = []
    all_slots = (slice(None),) * 3
    sources = {"small": block_ref, "qkv": made_ref, "out": gout_ref}
    for start, name, cols, order, turn, many in stages["pieces"]:
        landed, slabs = rest[0], rest[1 : 1 + many]
        del rest[: 1 + many]
        source = sources[name]
        view = (slice(None), pl.ds(*cols))
        own = source.at[all_slots + (place.at[3],) + view]
        sent = source.at[all_slots + (place.digit(3, 1),) + view]
        stage, earliest = None, int(name == "small")
        if name == "out":
            stage = stage_ref.at[cols[0] // cols[1]]
        if name == "qkv":
            earliest = moments.index((cols[0] % width // HEADS_WIDE, "made"))
        out = {"small": found_ref, "qkv": sqkv_ref, "out": sout_ref}[name]

        def finish(value, out=out, cols=cols):
            out[:, cols[0] : cols[0] + cols[1]] = value

        pieces.append(
            (start, earliest, reduce_steps_of(ops, own, sent, stage, landed, slabs, finish, order, turn))
        )
    stride = stages["stride"]
    span = max(start for start, _, _ in pieces) + LAST_ROUNDS * stride
    late_key = span + 0.01
    pieces.append((late_key, len(moments) - 1, sum_direct(ops, late_ref, first_ref, second_ref, plane_ref)))
    hooks = schedule(ops, pieces, stride, moments, times, now / span)

    loads = [
        pltpu.make_async_copy(src, dst, load_sems.at[n])
        for n, (src, dst) in enumerate(((x_hbm, x_ref), (dr_hbm, dr_ref)))
    ]

    @pl.when(step == 0)
    def _():
        place.greet_group(direct_group(digits))
        da_ref[...] = jnp.zeros_like(da_ref)
        rows_ref[...] = jnp.zeros_like(rows_ref)

    hooks.run(step, "head")

    @pl.when(step == 0)
    def _():
        for row, k in ((1, 1), (2, 2), (6, 3), (7, 4), (8, 5), (9, 6)):
            rows_ref[row : row + 1, :] = jnp.sum(sums_ref[k], axis=0, keepdims=True)
        wide = [jnp.sum(wide_ref[k], axis=0, keepdims=True) for k in range(3)]
        dots = [sum(dot_ref[p, :, lane : lane + 128] for lane in range(0, tokens, 128)) for p in range(dot_ref.shape[0])]
        for d, slot, lane, lane_wide in small_slots(digits, width, wide_ref.shape[2]):
            block_ref[slot + (slice(0, 16),)] = rows_ref[:, lane : lane + 128]
            for k in range(3):
                block_ref[slot + (slice(10 + k, 11 + k),)] = wide[k][:, lane_wide : lane_wide + 128]
            for p, value in enumerate(dots):
                block_ref[slot + (slice(16 + 2 * p, 18 + 2 * p),)] = value

    hooks.run(step, "block")

    @pl.when(step == 0)
    def _():
        for load in loads:
            load.start()


    @pl.when(step < half)
    def _():
        at = pl.multiple_of(step * HEADS_WIDE, HEADS_WIDE)
        for part in range(3):
            made = dot_tn(a_ref[...], d_ref[part]).astype(bf16)
            cols = pl.ds(pl.multiple_of(part * width + at, HEADS_WIDE), HEADS_WIDE)
            made_ref[:, :, :, :, :, cols] = made.reshape(made_ref.shape[:5] + (HEADS_WIDE,))
        for part, row in ((0, 4), (2, 5)):
            rows_ref[row : row + 1, pl.ds(at, HEADS_WIDE)] = jnp.sum(d_ref[part].astype(f32), axis=0, keepdims=True)

    hooks.run(step, "made")
    end = step == steps - 1

    @pl.when(end)
    def _():
        for load in loads:
            load.wait()

    for b in range(blocks):

        @pl.when(step >= half)
        def _(b=b):
            rows = slice(b * QUERY_BLOCK, (b + 1) * QUERY_BLOCK)
            total = da_ref[rows, :]
            for part, w_ref in enumerate((wq_ref, wk_ref, wv_ref)):
                total = total + dot_nt(d_ref[part, rows, :], w_ref[...])
            da_ref[rows, :] = total

        hooks.run(step, b)
    for b in range(blocks):

        @pl.when(end)
        def _(b=b):
            rows = slice(b * QUERY_BLOCK, (b + 1) * QUERY_BLOCK)
            normed, inverse = norm_parts(x_ref[rows, :].astype(f32))
            d_a = da_ref[rows, :]
            rows_ref[0:1, :] += jnp.sum(d_a * normed, axis=0, keepdims=True)
            rows_ref[3:4, :] += jnp.sum(d_a, axis=0, keepdims=True)
            dx_ref[rows, :] = (dr_ref[rows, :] + norm_back(d_a, par_ref[0:1, :], normed, inverse)).astype(bf16)

        hooks.run(step, "norm%d" % b)

    @pl.when(end)
    def _():
        for d, slot, lane, _ in small_slots(digits, width, wide_ref.shape[2]):
            late_ref[slot] = rows_ref[0:8, lane : lane + 128]

    hooks.run(step, "end")

    @pl.when(end)
    def _():
        late = plane_ref[place.at[0]]
        for k in range(digits[0] - 1):
            late = late + second_ref[k]
        me = ((place.at[0] * digits[1] + place.at[1]) * digits[2] + place.at[2]) * digits[3] + place.at[3]
        row = lax.broadcasted_iota(jnp.int32, (8, 128), 0)
        swapped = (row == 0) | ((row >= 3) & (row <= 5))
        found_ref[0:8, :] = jnp.where(swapped, late, found_ref[0:8, :])
        own, own_wide = gain_ref.shape[1], mid_ref.shape[1]
        narrow = pltpu.roll(found_ref[0:16, :], (128 - me * own % 128) % 128, 1)
        broad = pltpu.roll(found_ref[0:16, :], (128 - me * own_wide % 128) % 128, 1)
        gain_ref[...] = narrow[0:3, 0:own]
        bias_ref[...] = narrow[3:10, 0:own]
        mid_ref[...] = broad[10:11, 0:own_wide]
        ffb_ref[...] = broad[11:13, 0:own_wide]
        heads = dscale_ref.shape[1]
        dscale_ref[...] = jnp.sum(found_ref[16 : 16 + heads, :].T, axis=0, keepdims=True) / scale_ref[...]


def small_slots(digits, width, hidden):
    total = digits[0] * digits[1] * digits[2] * digits[3]
    listed = []
    for d in range(total):
        i3, left = d % digits[3], d // digits[3]
        i2, left = left % digits[2], left // digits[2]
        slot = (left // digits[1], left % digits[1], i2, i3)
        listed.append((d, slot, d * (width // total) // 128 * 128, d * (hidden // total) // 128 * 128))
    return listed


def last(digits, a, d_qkv, w_qkv, x, d_r, par, sums, wide, dots, head_scale, grad_out):
    tokens, width = x.shape
    hidden = wide.shape[2]
    half = width // HEADS_WIDE
    bf16, f32 = jnp.bfloat16, jnp.float32
    sds = jax.ShapeDtypeStruct
    fixed = lambda shape: pl.BlockSpec(shape, lambda s: (0,) * len(shape), pipeline_mode=pl.Buffered(1))
    total = digits[0] * digits[1] * digits[2] * digits[3]
    rows = width // total
    small_rows = 16 + 2 * dots.shape[0]
    pieces, scratch = [], []

    def add(start, name, height, cols, order, kind):
        turn = 1 - len(pieces) % 2 * 2
        slabs = slab_shapes(digits, height, cols[1], order, turn, kind)
        pieces.append((start, name, cols, order, turn, len(slabs)))
        scratch.extend([pltpu.VMEM(digits[:3] + (height, cols[1]), kind)] + slabs)

    for k in range(2):
        add(OUT_PACE * k, "out", rows, (k * (width // 2), width // 2), LAST_ORDERS[k], bf16)
    add(1.0, "small", small_rows, (0, 128), X, f32)
    number = 2
    for s in range(half):
        for part in range(3):
            cols = (part * width + s * HEADS_WIDE, HEADS_WIDE)
            add(0.5 * number + 0.5, "qkv", rows, cols, LAST_ORDERS[number % len(LAST_ORDERS)], bf16)
            number += 1
    weight = lambda part: pl.BlockSpec((width, HEADS_WIDE), lambda s: (0, part * half + jnp.maximum(s - half, 0)))
    smalls = [(3, rows), (7, rows), (1, hidden // total), (2, hidden // total), (1, head_scale.shape[1])]
    plane = digits[1] * digits[2] * digits[3]
    return pl.pallas_call(
        functools.partial(last_kernel, digits, {"steps": 2 * half, "pieces": pieces, "stride": 3.0}),
        grid=(2 * half,),
        in_specs=[fixed(a.shape), pl.BlockSpec((3, tokens, HEADS_WIDE), lambda s: (0, 0, s % half))]
        + [weight(part) for part in range(3)]
        + [pl.BlockSpec(memory_space=pl.ANY)] * 2
        + [fixed(v.shape) for v in (par, sums, wide, dots, head_scale)]
        + [pl.BlockSpec(memory_space=pl.ANY)],
        out_specs=[fixed(s) for s in [(tokens, width), (rows, 3 * width), (rows, width)] + smalls],
        out_shape=[sds((tokens, width), bf16), sds((rows, 3 * width), f32), sds((rows, width), f32)]
        + [sds(s, f32) for s in smalls],
        scratch_shapes=[
            pltpu.VMEM((tokens, width), f32),
            pltpu.VMEM(digits + (rows, 3 * width), bf16),
            pltpu.VMEM((16, width), f32),
            pltpu.VMEM(digits + (small_rows, 128), f32),
            pltpu.VMEM(digits + (8, 128), f32),
            pltpu.VMEM((plane - 1, digits[0], 8, 128), f32),
            pltpu.VMEM((digits[0] - 1, 8, 128), f32),
            pltpu.VMEM((digits[0], 8, 128), f32),
            pltpu.VMEM((small_rows, 128), f32),
            pltpu.VMEM((2,) + digits[:3] + (rows, width // 2), bf16),
            pltpu.VMEM(x.shape, bf16),
            pltpu.VMEM(d_r.shape, f32),
            pltpu.SemaphoreType.DMA((2,)),
        ]
        + scratch
        + semaphores(len(scratch) + plane + digits[0], 2),
        compiler_params=pltpu.CompilerParams(
            collective_id=4, has_side_effects=True, vmem_limit_bytes=60 << 20
        ),
        name="last",
    )(a, d_qkv, w_qkv, w_qkv, w_qkv, x, d_r, par, sums, wide, dots, head_scale, grad_out)


def mid_grad_kernel(len_ref, m_ref, cot_ref, out_ref, dw_ref):
    @pl.when(pl.program_id(0) == 0)
    def _():
        position = lax.broadcasted_iota(jnp.int32, (cot_ref.shape[0], 1), 0)
        dw_ref[...] = jnp.where(position < len_ref[0], cot_ref[...].astype(jnp.float32), 0.0).astype(jnp.bfloat16)

    out_ref[...] = dot_tn(m_ref[...], dw_ref[...]).astype(jnp.bfloat16)


def mid_grad(lengths, m, cot, block=512):
    tokens, hidden = m.shape
    width = cot.shape[1]
    return pl.pallas_call(
        mid_grad_kernel,
        grid=(hidden // block,),
        in_specs=[
            pl.BlockSpec(memory_space=pltpu.SMEM),
            pl.BlockSpec((tokens, block), lambda i: (0, i)),
            pl.BlockSpec(cot.shape, lambda i: (0, 0), pipeline_mode=pl.Buffered(1)),
        ],
        out_specs=pl.BlockSpec((block, width), lambda i: (i, 0)),
        out_shape=jax.ShapeDtypeStruct((hidden, width), jnp.bfloat16),
        scratch_shapes=[pltpu.VMEM(cot.shape, jnp.bfloat16)],
        compiler_params=pltpu.CompilerParams(vmem_limit_bytes=60 << 20),
        name="mid_grad",
    )(lengths, m, cot)


def settle_kernel(count, *refs):
    for k in range(count):
        refs[count + k][...] = refs[k][...]


def settle(arrays, steps=4):
    def block(shape):
        if shape[0] % (8 * steps) == 0:
            return pl.BlockSpec((shape[0] // steps, shape[1]), lambda s: (s, 0))
        return pl.BlockSpec(shape, lambda s: (0, 0))

    blocks = [block(a.shape) for a in arrays]
    return pl.pallas_call(
        functools.partial(settle_kernel, len(arrays)),
        grid=(steps,),
        in_specs=blocks,
        out_specs=blocks,
        out_shape=[jax.ShapeDtypeStruct(a.shape, a.dtype) for a in arrays],
        compiler_params=pltpu.CompilerParams(vmem_limit_bytes=60 << 20),
        name="settle",
    )(*arrays)


def plain_gather(digits, weights, small_parts):
    small = jnp.concatenate([to_bf16(v).reshape(-1) for v in small_parts])
    small = jnp.pad(small, (0, 2048 - small.shape[0])).reshape(16, 128)
    shards_in = [to_bf16(w).reshape(tiled_rows(*w.shape)) for w in weights] + [small]
    gathered = gather_all(digits, shards_in)
    fulls = [g.reshape((-1, w.shape[1])) for g, w in zip(gathered, weights)]
    smalls, parts, used = gathered[4].reshape(-1, 2048), [], 0
    for v in small_parts:
        block = smalls[:, used : used + v.size].reshape((-1,) + (v.shape if v.ndim == 2 else (1,) + v.shape))
        parts.append(block.transpose(1, 0, 2).reshape(block.shape[1], -1).astype(jnp.float32))
        used += v.size
    par = jnp.pad(jnp.concatenate(parts[:2]), ((0, 6), (0, 0)))
    table = jnp.pad(jnp.concatenate(parts[2:]), ((10, 3), (0, 0)))
    return fulls, par, table


def plain_reduce(digits, weights, grads, small_parts, small_grads):
    total = digits[0] * digits[1] * digits[2] * digits[3]
    block = [v.reshape(v.shape[0], total, -1).transpose(1, 0, 2).reshape(total, -1) for v in small_grads[:-1]]
    block.append(jnp.broadcast_to(small_grads[-1][None], (total, small_grads[-1].shape[0])))
    block = jnp.concatenate(block, axis=1)
    block = jnp.pad(block, ((0, 0), (0, 1024 - block.shape[1]))).reshape(digits + (8, 128))
    blocks = [to_bf16(g).reshape(digits + tiled_rows(*w.shape)) for g, w in zip(grads, weights)]
    summed = reduce_all(digits, blocks + [block])
    flat, used, owned = summed[4].reshape(-1), 0, []
    for v in small_parts:
        owned.append(flat[used : used + v.size].reshape(v.shape))
        used += v.size
    return [g.reshape(w.shape) for g, w in zip(summed[:4], weights)] + owned


def shards(
    digits, tokens, lengths, cotangent, w_qkv, w_out, w_fc1, w_fc2, norm_gain, norm_bias, mid_gain, ff_bias, head_scale
):
    weights = (w_qkv, w_out, w_fc1, w_fc2)
    small_parts = (norm_gain, norm_bias, mid_gain, ff_bias)
    heads = head_scale.shape[0]
    total = digits[0] * digits[1] * digits[2] * digits[3]
    tiled = w_qkv.shape[0] % 16 == 0
    if tiled:
        normed_in, qkv, mixed, logs, full_qkv, full_out, full_fc1, full_fc2, par, table = front(
            digits, lengths, head_scale, tokens, weights, (norm_gain, norm_bias, mid_gain[None], ff_bias)
        )
        full_qkv, full_out, full_fc1, full_fc2 = (
            g.reshape((-1, g.shape[-1])) for g in (full_qkv, full_out, full_fc1, full_fc2)
        )
    else:
        (full_qkv, full_out, full_fc1, full_fc2), par, table = plain_gather(digits, weights, small_parts)
        scale_row = jnp.repeat(head_scale, tokens.shape[1] // heads)[None]
        par = jnp.concatenate((par[:SCALE_ROW], scale_row, par[SCALE_ROW + 1 :]))
        normed_in, qkv = project(tokens, full_qkv, par[0:3], par[3:10])
        mixed, logs = attend(lengths, head_scale, qkv)
    result, normed_ff, normed_mid, grad_pre, grad_projection, grad_residual, grad_attended, sums, wide = ffn(
        lengths, tokens, mixed, cotangent, full_out, full_fc1, full_fc2, par, table
    )
    grad_fc2 = mid_grad(lengths, normed_mid, cotangent)
    if tiled:
        d_qkv, dots, grad_out_w, sum_fc1, sum_fc2 = back(
            digits, lengths, qkv, grad_attended, logs, normed_ff, grad_pre, mixed, grad_projection,
            grad_fc2.reshape(digits + w_fc2.shape),
        )
        grad_tokens, sum_qkv, sum_out, d_gain, d_bias, d_mid, d_ffb, d_scale = last(
            digits, normed_in, d_qkv, full_qkv, tokens, grad_residual, par, sums, wide, dots, head_scale[None],
            grad_out_w.reshape(digits + w_out.shape),
        )
        grad_tokens, sum_qkv, sum_out, sum_fc1, sum_fc2, d_gain, d_bias, d_mid, d_ffb, d_scale = settle(
            (grad_tokens, sum_qkv, sum_out, sum_fc1, sum_fc2, d_gain, d_bias, d_mid, d_ffb, d_scale)
        )
        summed = (sum_qkv, sum_out, sum_fc1, sum_fc2, d_gain, d_bias, d_mid[0], d_ffb, d_scale[0])
    else:
        grad_fc1 = to_bf16(dot_tn(normed_ff, grad_pre))
        grad_out_w = to_bf16(dot_tn(mixed, grad_projection))
        d_qkv, dots = attend_back(lengths, qkv, grad_attended, logs)
        grad_tokens, first_sums = project_back(d_qkv, tokens, grad_residual, full_qkv, par[0:3])
        grad_qkv = jnp.concatenate([dot_tn(normed_in, d_qkv[k]) for k in range(3)], axis=1)
        sums, wide, first_sums = sums.sum(1), wide.sum(1), first_sums.sum(1)
        small_grads = (
            jnp.concatenate((first_sums[0:1], sums[1:3])),
            jnp.concatenate((first_sums[1:4], sums[3:7])),
            wide[0:1],
            wide[1:3],
            dots.sum(-1).reshape(heads) / head_scale,
        )
        summed = plain_reduce(
            digits, weights, (grad_qkv, grad_out_w, grad_fc1, grad_fc2), small_parts + (head_scale,), small_grads
        )
    return (result, grad_tokens) + tuple(summed)


def solution(mesh):
    placed = (
        P(("dp", "fsdp"), None),
        P(("dp", "fsdp")),
        P(("dp", "fsdp"), None),
        P(("dp", "fsdp"), None),
        P(("dp", "fsdp"), None),
        P(("dp", "fsdp"), None),
        P(("dp", "fsdp"), None),
        P(None, ("dp", "fsdp")),
        P(None, ("dp", "fsdp")),
        P(("dp", "fsdp")),
        P(None, ("dp", "fsdp")),
        P(),
    )
    return jax.shard_map(
        functools.partial(shards, digits_of(mesh)),
        mesh=mesh,
        in_specs=placed,
        out_specs=(
            P(("dp", "fsdp"), None),
            P(("dp", "fsdp"), None),
            P(("dp", "fsdp"), None),
            P(("dp", "fsdp"), None),
            P(("dp", "fsdp"), None),
            P(("dp", "fsdp"), None),
            P(None, ("dp", "fsdp")),
            P(None, ("dp", "fsdp")),
            P(("dp", "fsdp")),
            P(None, ("dp", "fsdp")),
            P(),
        ),
        check_vma=False,
    )
```
